32 devices in a mesh: region: 2 (over y), blk: 16 (over z, x, core).
Axes of the slice: x: 2, y: 2, z: 4, core: 2. Of those that a mesh axis runs over, the one named last changes fastest.
Arguments:
- u_now: float32 [32, 2, 4, 32, 1024], P('blk', 'region'), may hold values from -6 to 6
- u_prev: float32 [32, 2, 4, 32, 1024], P('blk', 'region'), may hold values from -6 to 6
- coef_store: bfloat16 [16, 2, 2, 4, 32, 1024], P('blk', 'region'), may hold values from 0.019897461 to 0.099609375
- store_map: int32 [16, 2, 8], P('blk', 'region'), may hold values from 0 to 7, each once within a row
- new_owner: int32 [32], P('blk'), may hold values from 0 to 15, as said below
Outputs:
- new_state: float32 [48, 2, 4, 32, 1024], P('blk', 'region')
The draws below stay inside these ranges and needn't reach their ends.
Inputs may be any that keep to these rules, and one draw needn't show every extreme that they name: new_owner[m] is m // 2, except that the last row of an owner may instead go to the next owner, (m // 2 + 1) mod 16; every owner gets 1 to 3 rows, and in every draw some owner gets 3 rows. Each store_map[j, x, :] holds every piece number once.
All inputs are finite; a program needn't handle non-finite values.
Results may differ from the reference program's by a relative error of at most 0.0003.
Values may be sent and summed in bfloat16 or wider, within the bound.
No kernel may reach another device: no remote copies, remote signals or barrier semaphores. Data moves between devices by JAX's collectives and lax.ppermute only.
A program may use at most 64 MiB of HBM per device.

```python
import math
import jax
import jax.numpy as jnp
from jax import lax

EDGE = 32
FIELDS = 4
BLK_DEV = 2
STEPS = 2
CAP = 3
ROWS = 32
COLS = 2
PER = 4
N_REGION = 2
N_BLK = 16


def draw_new_owner(key, part):
    owners = ROWS // BLK_DEV
    random_shift = jax.random.randint(jax.random.fold_in(key, 7), (owners,), 0, 2).astype(jnp.int32)
    boundary = jnp.arange(owners, dtype=jnp.int32)
    half_owner = owners // 2
    forced_on = (boundary == 0) | (boundary == half_owner - 1) | (boundary == half_owner) | (boundary == owners - 1)
    shifted = jnp.where(forced_on, 1, jnp.where(boundary == 1, 0, random_shift)).astype(jnp.int32)
    row_index = jnp.arange(ROWS, dtype=jnp.int32)
    home_owner = row_index // BLK_DEV
    last_row = row_index % BLK_DEV == BLK_DEV - 1
    next_owner = (home_owner + 1) % owners
    moving_row = last_row & (jnp.take(shifted, next_owner) == 1)
    return jnp.where(moving_row, next_owner, home_owner).astype(jnp.int32)


def shard_levels(own_key, shape, split, least, high):
    level = 1.0
    for position, blocks in split:
        heights = jax.random.uniform(jax.random.fold_in(jax.random.fold_in(own_key, 6), position), (blocks,), jnp.float32, least / len(split), high / len(split))
        level = level * jnp.repeat(jnp.exp(heights), shape[position] // blocks).reshape((-1,) + (1,) * (len(shape) - 1 - position))
    return level


def bell_draw(own_key, dims, width, bound, shards=(), held_as=jnp.bfloat16):
    level = shard_levels(own_key, dims, shards, -0.22, 0.18) if shards else 1.0
    values = jax.random.normal(own_key, dims, jnp.float32) * width * level
    return jnp.minimum(jnp.maximum(values, -bound), bound).astype(held_as)


def setup_inputs(seed: int = 0) -> dict:
    key_list = jax.random.split(jax.random.key(seed), 6)
    return {
        "u_now": bell_draw(key_list[0], (ROWS, COLS, FIELDS, EDGE, EDGE * EDGE), 1.0, 6.0, ((0, 16), (1, 2)), jnp.float32),
        "u_prev": bell_draw(key_list[1], (ROWS, COLS, FIELDS, EDGE, EDGE * EDGE), 1.0, 6.0, ((0, 16), (1, 2)), jnp.float32),
        "coef_store": jnp.clip(jnp.exp(math.log(0.099609375) - 1.61066415 * jax.random.uniform(key_list[2], (N_BLK, N_REGION, N_REGION, PER, EDGE, EDGE * EDGE), jnp.float32) ** shard_levels(key_list[2], (N_BLK, N_REGION, N_REGION, PER, EDGE, EDGE * EDGE), ((0, 16), (1, 2)), -0.2, 0.2)), 0.019897461, 0.099609375).astype(jnp.bfloat16),
        "store_map": jax.vmap(lambda own: jax.random.permutation(own, BLK_DEV * FIELDS))(jax.random.split(key_list[3], N_BLK * N_REGION)).reshape((N_BLK, N_REGION, BLK_DEV * FIELDS)).astype(jnp.int32),
        "new_owner": draw_new_owner(jax.random.fold_in(key_list[5], 71), 0),
    }


def to_grid(field_rows):
    shaped = field_rows.reshape(ROWS, COLS, FIELDS, EDGE, EDGE, EDGE)
    shaped = shaped.transpose(2, 1, 3, 0, 4, 5)
    return shaped.reshape(FIELDS, COLS * EDGE, ROWS * EDGE, EDGE)


def from_grid(grid_field):
    shaped = grid_field.reshape(FIELDS, COLS, EDGE, ROWS, EDGE, EDGE)
    shaped = shaped.transpose(3, 1, 0, 2, 4, 5)
    return shaped.reshape(ROWS, COLS, FIELDS, EDGE, EDGE * EDGE)


def leap_step(state_now, state_prev, coefficient):
    wrapped = jnp.pad(state_now, ((0, 0), (1, 1), (0, 0)), mode="wrap")
    padded = jnp.pad(wrapped, ((1, 1), (0, 0), (1, 1)))
    summed = (padded[:, :, :-2] + padded[:, :, 1:-1]) + padded[:, :, 2:]
    summed = (summed[:, :-2] + summed[:, 1:-1]) + summed[:, 2:]
    summed = (summed[:-2] + summed[1:-1]) + summed[2:]
    laplace = summed - 27.0 * state_now
    return (2.0 * state_now - state_prev) + coefficient * laplace


def per_field(members):
    state_now, state_prev, coefficient = members
    coefficient = coefficient.astype(jnp.float32)
    for step_index in range(STEPS):
        state_now, state_prev = leap_step(state_now, state_prev, coefficient), state_now
    return state_now


def reference(u_now, u_prev, coef_store, store_map, new_owner):
    inverse = jnp.argsort(store_map, axis=-1).astype(jnp.int32)
    src_region = inverse // PER
    src_slot = inverse % PER
    owner_index = jnp.arange(N_BLK, dtype=jnp.int32)[:, None, None]
    column_index = jnp.arange(N_REGION, dtype=jnp.int32)[None, :, None]
    picked = coef_store[owner_index, src_region, column_index, src_slot]
    picked = picked.reshape(N_BLK, N_REGION, BLK_DEV, FIELDS, EDGE, EDGE * EDGE)
    coefficient = picked.transpose(0, 2, 1, 3, 4, 5).reshape(ROWS, COLS, FIELDS, EDGE, EDGE * EDGE)
    final_grid = lax.map(per_field, (to_grid(u_now), to_grid(u_prev), to_grid(coefficient)))
    final_rows = from_grid(final_grid)
    row_index = jnp.arange(ROWS, dtype=jnp.int32)
    order_key = (row_index - BLK_DEV * new_owner + 1) % ROWS
    same_owner = new_owner[None, :] == new_owner[:, None]
    earlier = order_key[None, :] < order_key[:, None]
    rank = jnp.sum((same_owner & earlier).astype(jnp.int32), axis=1)
    slot_index = (new_owner * CAP + rank).astype(jnp.int32)
    result = jnp.zeros((N_BLK * CAP, COLS, FIELDS, EDGE, EDGE * EDGE), final_rows.dtype)
    return result.at[slot_index].set(final_rows)
```

```python
import functools

import jax
import jax.numpy as jnp
from jax import lax
from jax.experimental import pallas as pl
from jax.experimental.pallas import tpu as pltpu
from jax.sharding import PartitionSpec as P

STEPS = 2
LANES = 128
F32 = jnp.float32
BF16 = jnp.bfloat16
VMEM = pl.BlockSpec(memory_space=pltpu.VMEM)
SMEM = pl.BlockSpec(memory_space=pltpu.SMEM)
ANY = pl.BlockSpec(memory_space=pl.ANY)


def extended_2(block, sides, width, periodic):
    for axis, dim in sides:
        count = lax.axis_size(axis)
        forward = [(i, i + 1) for i in range(count - 1)]
        if periodic:
            forward.append((count - 1, 0))
        backward = [(target, source) for source, target in forward]
        low = lax.ppermute(
            lax.slice_in_dim(block, block.shape[dim] - width, None, axis=dim), axis, forward
        )
        high = lax.ppermute(lax.slice_in_dim(block, 0, width, axis=dim), axis, backward)
        block = jnp.concatenate([low, block, high], axis=dim)
    return block


def shifted_2(value, axis, by):
    devices = lax.axis_size(axis)
    return lax.ppermute(value, axis, [(i, (i + by) % devices) for i in range(devices)])


def stencil_step(state_now, state_prev, coefficient, live_count):
    slot_count, field_count, edge_cells, plane_cells = state_now.shape
    padded = extended_2(state_now, (("region", 2),), 1, False)
    first_planes = padded[..., :edge_cells]
    last_planes = padded[..., plane_cells - edge_cells :]
    last_live = jnp.take(last_planes, live_count - 1, axis=0)
    rim_pair = jnp.stack([first_planes[0], last_live], axis=2)
    spread = extended_2(rim_pair.astype(jnp.bfloat16), (("blk", 2),), 1, True).astype(
        rim_pair.dtype
    )
    left_rim = spread[:, :, 0]
    right_rim = spread[:, :, 3]
    before_planes = jnp.concatenate([left_rim[None], last_planes[:-1]], axis=0)
    after_planes = jnp.pad(first_planes[1:], ((0, 1), (0, 0), (0, 0), (0, 0)))
    slot_ids = jnp.arange(slot_count)
    after_planes = jnp.where(
        (slot_ids == live_count - 1)[:, None, None, None], right_rim[None], after_planes
    )
    extended = jnp.concatenate([before_planes, padded, after_planes], axis=-1)
    width = extended.shape[-1]
    column = jnp.arange(width) % edge_cells
    lower_mask = (column != 0).astype(jnp.float32)
    upper_mask = (column != edge_cells - 1).astype(jnp.float32)
    margin = ((0, 0), (0, 0), (0, 0), (1, 1))
    shifted = jnp.pad(extended, margin)
    summed = shifted[..., :width] * lower_mask + extended + shifted[..., 2:] * upper_mask
    summed = (
        summed[..., : -2 * edge_cells]
        + summed[..., edge_cells:-edge_cells]
        + summed[..., 2 * edge_cells :]
    )
    box_sum = summed[:, :, :-2] + summed[:, :, 1:-1] + summed[:, :, 2:]
    laplace = box_sum - 27.0 * state_now
    return 2.0 * state_now - state_prev + coefficient.astype(jnp.float32) * laplace


def compact(members, valid_flags):
    slot_count = valid_flags.shape[0]
    place_index = jnp.cumsum(valid_flags) - 1
    target = jnp.arange(slot_count)
    chooser = (valid_flags[None, :] == 1) & (place_index[None, :] == target[:, None])
    source = jnp.sum(jnp.where(chooser, target[None, :], 0), axis=1)
    filled = jnp.sum(chooser.astype(jnp.int32), axis=1) > 0
    placed = tuple(
        (
            jnp.where(
                filled.reshape((slot_count,) + (1,) * (member.ndim - 1)),
                jnp.take(member, source, axis=0),
                jnp.zeros_like(member),
            )
            for member in members
        )
    )
    return (placed, jnp.sum(valid_flags))


def general_on_device(u_now, u_prev, coef_store, store_map, new_owner):
    state_now = u_now[:, 0]
    state_prev = u_prev[:, 0]
    blocks, fields, edge_cells, plane_cells = state_now.shape
    store_local = coef_store[0, 0]
    arrived = lax.all_to_all(store_local, "region", split_axis=0, concat_axis=0, tiled=True)
    flattened = arrived.reshape((-1,) + arrived.shape[2:])
    inverse = jnp.argsort(store_map[0, 0])
    coefficient = jnp.take(flattened, inverse, axis=0).reshape(
        blocks, fields, edge_cells, plane_cells
    )
    own_index = lax.axis_index("blk")
    goes_right = new_owner[blocks - 1] != own_index
    mark_right = goes_right.astype(jnp.float32).reshape(1)
    middle_flags = jnp.ones((blocks - 2,), jnp.int32)
    keep_first = (new_owner[0] == own_index).astype(jnp.int32).reshape(1)
    keep_last = (new_owner[blocks - 1] == own_index).astype(jnp.int32).reshape(1)
    for step_index in range(STEPS):
        state_now, state_prev = (
            stencil_step(state_now, state_prev, coefficient, blocks),
            state_now,
        )
    from_left = shifted_2((state_now[blocks - 1], mark_right), "blk", 1)
    valid_flags = jnp.concatenate(
        [(from_left[1] > 0.5).astype(jnp.int32), keep_first, middle_flags, keep_last]
    )
    stacked_now = jnp.concatenate([from_left[0][None], state_now], axis=0)
    placed, live_count = compact((stacked_now,), valid_flags)
    result = placed[0]
    return result[:, None]


def lane_ids():
    return lax.broadcasted_iota(jnp.int32, (1, LANES), 1)


def pack_body(edge, info, u_ref, p_ref, coef_ref, y_ref, left_ref, right_ref, dleft_ref, dright_ref, rows_ref):
    fields = u_ref.shape[1]
    depth = u_ref.shape[2]
    last = u_ref.shape[3] - LANES
    top = depth - 1
    region = info[0]
    lower = region == 0
    other = 1 - region
    own_edge = jnp.where(lower, top, 0)
    own_next = jnp.where(lower, top - 1, 1)
    lane = lane_ids()

    def own_row(s, lanes):
        piece = coef_ref[region, s, :, lanes].astype(F32)
        return jnp.where(lower, piece[top:depth], piece[0:1])

    def other_row(s, lanes):
        piece = coef_ref[other, s, :, lanes].astype(F32)
        return jnp.where(lower, piece[0:1], piece[top:depth])

    everything = slice(None)
    y_ref[0:4] = coef_ref[other]
    for m in range(2):
        for f in range(fields):
            at = m * fields + f
            near = u_ref[m, f, pl.ds(own_edge, 1), :]
            rows_ref[at : at + 1, :] = near
            rows_ref[8 + at : 9 + at, :] = u_ref[m, f, pl.ds(own_next, 1), :]
            rows_ref[16 + at : 17 + at, :] = 2.0 * near - p_ref[m, f, pl.ds(own_edge, 1), :]
    for s in range(4):
        rows_ref[24 + s : 25 + s, :] = own_row(s, everything)
    tags = []
    for half in range(2):
        for s in range(4):
            at = jnp.where(region == half, s, 4 + s)
            tags.append(info[8 + at].astype(F32))
    held = [info[8 + region * 4 + s].astype(F32) for s in range(4)]
    away = [info[8 + other * 4 + s].astype(F32) for s in range(4)]
    tags = held + away
    for i, tag in enumerate(tags):
        rows_ref[28:29, i * LANES : (i + 1) * LANES] = jnp.full((1, LANES), 0.0, F32) + tag
    rows_ref[29:32, :] = jnp.zeros((3, rows_ref.shape[1]), F32)
    y_ref[4] = rows_ref[...].astype(BF16)

    tag_rows = [jnp.full((1, LANES), 0.0, F32) + tag for tag in tags]
    flag = jnp.full((1, LANES), 0.0, F32) + info[1].astype(F32)
    zero_row = jnp.zeros((1, LANES), F32)
    for m, lanes, straight_ref, diag_ref in (
        (0, slice(0, LANES), left_ref, dleft_ref),
        (1, slice(last, last + LANES), right_ref, dright_ref),
    ):
        for f in range(fields):
            now = u_ref[m, f, :, lanes]
            ahead = 2.0 * now - p_ref[m, f, :, lanes]
            piece = coef_ref[region, f, :, lanes].astype(F32)
            if m == 0:
                tile = jnp.where(
                    lane < 64, now, jnp.where(lane < 96, pltpu.roll(ahead, 64, 1), pltpu.roll(piece, 96, 1))
                )
            else:
                tile = jnp.where(
                    lane >= 64, now, jnp.where(lane < 32, pltpu.roll(ahead, 32, 1), pltpu.roll(piece, 64, 1))
                )
            straight_ref[f * depth : (f + 1) * depth, :] = tile.astype(BF16)
        extra = [other_row(s, lanes) for s in range(4)] + tag_rows + [flag] + [zero_row] * 3
        straight_ref[fields * depth : fields * depth + 16, :] = jnp.concatenate(extra, axis=0).astype(BF16)
        plane = jnp.zeros((depth, LANES), F32)
        for s in range(4):
            piece = coef_ref[other, s, :, lanes].astype(F32)
            shift = (32 * s if m == 0 else 32 + 32 * s) % LANES
            moved = pltpu.roll(piece, shift, 1) if shift else piece
            plane = jnp.where((lane >= 32 * s) & (lane < 32 * s + 32), moved, plane)
        diag_ref[0:depth, :] = plane.astype(BF16)
        extra = (
            [rows_ref[m * fields : m * fields + 4, lanes]]
            + [rows_ref[8 + m * fields : 12 + m * fields, lanes]]
            + [rows_ref[16 + m * fields : 20 + m * fields, lanes]]
            + [rows_ref[24:28, lanes]]
            + tag_rows
            + [zero_row] * 8
        )
        diag_ref[depth : depth + 32, :] = jnp.concatenate(extra, axis=0).astype(BF16)


def nine_sum(tiles, lane, first=0):
    inside = lane % 32
    low = inside != 0
    high = inside != 31
    rows = []
    for tile in tiles:
        rows.append(
            tile
            + jnp.where(low, pltpu.roll(tile, 1, 1), 0.0)
            + jnp.where(high, pltpu.roll(tile, LANES - 1, 1), 0.0)
        )
    up = [pltpu.roll(row, 32, 1) for row in rows]
    down = [pltpu.roll(row, LANES - 32, 1) for row in rows]
    count = len(tiles)
    result = []
    for t in range(count):
        before = up[t] if t == 0 else jnp.where(lane < 32, up[t - 1], up[t])
        after = down[t] if t == count - 1 else jnp.where(lane >= 96, down[t + 1], down[t])
        result.append(rows[t] + before + after)
    return result


def step_body(m, info, u_ref, p_ref, coef_ref, y_ref, straight_ref, diag_ref, out_write, first_ref, edge_ref):
    fields = u_ref.shape[1]
    depth = u_ref.shape[2]
    width = u_ref.shape[3]
    main = width // LANES
    last = width - LANES
    top = depth - 1
    region = info[0]
    lower = region == 0
    other = 1 - region
    lane = lane_ids()
    row_id = lax.broadcasted_iota(jnp.int32, (depth, 1), 0)
    neighbour = 1 - m

    def tile_at(t):
        return slice(t * LANES, (t + 1) * LANES)

    local_lanes = slice(last, width) if m == 1 else slice(0, LANES)
    extra_s = straight_ref[fields * depth : fields * depth + 16, :].astype(F32)
    extra_d = diag_ref[depth : depth + 32, :].astype(F32)
    extra_y = y_ref[4].astype(F32)

    def position(number):
        place = jnp.int32(0)
        for q in range(8):
            place = jnp.where(info[8 + q] == number, q, place)
        return place

    def coef_tile(number, lanes):
        place = position(number)
        slot = place % 4
        held = (place // 4) == region
        mine = coef_ref[region, slot, :, lanes].astype(F32)
        far = y_ref[slot, :, lanes].astype(F32)
        return jnp.where(held, mine, far)

    planes = []
    for s in range(4):
        tile = straight_ref[s * depth : (s + 1) * depth, :].astype(F32)
        planes.append(pltpu.roll(tile, 32 if m == 1 else 64, 1))
    diag_tile = diag_ref[0:depth, :].astype(F32)
    for s in range(4):
        shift = (-32 * s if m == 1 else 96 - 32 * s) % LANES
        planes.append(pltpu.roll(diag_tile, shift, 1) if shift else diag_tile)
    tags_s = [extra_s[4 + i : 5 + i] for i in range(8)]
    tags_d = [extra_d[16 + i : 17 + i] for i in range(8)]
    tags_y = [extra_y[28:29, i * LANES : (i + 1) * LANES] for i in range(8)]
    halo_base = 0 if m == 1 else fields

    def with_sides(local, remote, middle):
        return [local] + middle + [remote] if m == 1 else [remote] + middle + [local]

    def edge_tiles(base_y, base_d):
        middle = [extra_y[base_y + m * fields : base_y + m * fields + 4, tile_at(t)] for t in range(main)]
        local = extra_y[base_y + neighbour * fields : base_y + neighbour * fields + 4, local_lanes]
        return with_sides(local, extra_d[base_d : base_d + 4], middle)

    near = edge_tiles(0, 0)
    beyond = edge_tiles(8, 4)
    ahead = edge_tiles(16, 8)
    field_id = lax.broadcasted_iota(jnp.int32, (4, LANES), 0).astype(F32)

    def other_row(s, lanes):
        piece = coef_ref[other, s, :, lanes].astype(F32)
        return jnp.where(lower, piece[0:1], piece[top:depth])

    def edge_coef(lanes, base):
        total = jnp.zeros((4, LANES), F32)
        for s in range(4):
            total = total + jnp.where(tags_y[s] == field_id + base, extra_y[24 + s : 25 + s, lanes], 0.0)
            total = total + jnp.where(tags_y[4 + s] == field_id + base, other_row(s, lanes), 0.0)
        return total

    corner = jnp.zeros((4, LANES), F32)
    for s in range(4):
        corner = corner + jnp.where(tags_d[s] == field_id + halo_base, extra_d[12 + s : 13 + s], 0.0)
        corner = corner + jnp.where(tags_d[4 + s] == field_id + halo_base, extra_s[s : s + 1], 0.0)
    edge_c = with_sides(
        edge_coef(local_lanes, neighbour * fields),
        corner,
        [edge_coef(tile_at(t), m * fields) for t in range(main)],
    )
    near_sum = nine_sum(near, lane)
    beyond_sum = nine_sum(beyond, lane)

    def column_sum(tile, row):
        above = jnp.where(row_id == 0, jnp.where(lower, 0.0, row), pltpu.roll(tile, 1, 0))
        below = jnp.where(row_id == top, jnp.where(lower, row, 0.0), pltpu.roll(tile, depth - 1, 0))
        return tile + above + below

    def sides_of(f):
        remote = straight_ref[f * depth : (f + 1) * depth, :].astype(F32)
        local = u_ref[neighbour, f, :, local_lanes]
        return local, remote

    for f in range(fields):
        local, remote = sides_of(f)
        now = with_sides(local, remote, [u_ref[m, f, :, tile_at(t)] for t in range(main)])
        sums = nine_sum(now, lane)
        halo_c = jnp.zeros((depth, LANES), F32)
        for i in range(8):
            halo_c = halo_c + jnp.where(tags_s[i] == F32(halo_base + f), planes[i], 0.0)
        coef = with_sides(
            coef_tile(neighbour * fields + f, local_lanes),
            halo_c,
            [coef_tile(m * fields + f, tile_at(t)) for t in range(main)],
        )
        drift = with_sides(
            2.0 * local - p_ref[neighbour, f, :, local_lanes],
            pltpu.roll(remote, 64 if m == 1 else 96, 1),
            [2.0 * now[t + 1] - p_ref[m, f, :, tile_at(t)] for t in range(main)],
        )
        for t in range(main + 2):
            edge_ref[f : f + 1, tile_at(t)] = jnp.where(lower, sums[t][top:depth], sums[t][0:1])
            box = column_sum(sums[t], near_sum[t][f : f + 1])
            first_ref[f, :, tile_at(t)] = drift[t] + coef[t] * (box - 27.0 * now[t])
    stepped = []
    for t in range(main + 2):
        box = near_sum[t] + beyond_sum[t] + edge_ref[0:4, tile_at(t)]
        stepped.append(ahead[t] + edge_c[t] * (box - 27.0 * near[t]))
    stepped_sum = nine_sum(stepped, lane)
    for f in range(fields):
        now = [first_ref[f, :, tile_at(t)] for t in range(main + 2)]
        sums = nine_sum(now, lane)
        for t in range(1, main + 1):
            box = column_sum(sums[t], stepped_sum[t][f : f + 1])
            lanes = tile_at(t - 1)
            coef = coef_tile(m * fields + f, lanes)
            value = 2.0 * now[t] - u_ref[m, f, :, lanes] + coef * (box - 27.0 * now[t])
            out_write(f, lanes, value)


def last_row_body(info, u_ref, p_ref, coef_ref, y_ref, straight_ref, diag_ref, row_ref, first_ref, edge_ref):
    def write(f, lanes, value):
        row_ref[f, :, lanes] = value

    step_body(1, info, u_ref, p_ref, coef_ref, y_ref, straight_ref, diag_ref, write, first_ref, edge_ref)


def first_row_body(
    info, u_ref, p_ref, coef_ref, y_ref, straight_ref, diag_ref, last_ref, out_ref, first_ref, edge_ref
):
    fields = u_ref.shape[1]
    depth = u_ref.shape[2]
    arrives = straight_ref[fields * depth : fields * depth + 16, :].astype(F32)[12:13] > 0.5
    keeps = info[1] == 0

    def write(f, lanes, value):
        kept = jnp.where(keeps, last_ref[f, :, lanes], 0.0)
        out_ref[0, f, :, lanes] = value
        out_ref[1, f, :, lanes] = jnp.where(arrives, value, kept)
        out_ref[2, f, :, lanes] = jnp.where(arrives, kept, 0.0)

    step_body(0, info, u_ref, p_ref, coef_ref, y_ref, straight_ref, diag_ref, write, first_ref, edge_ref)


def place_body(straight_ref, row_ref, partial_ref, out_ref, sem):
    rows = straight_ref.shape[0]
    flag = jnp.max(straight_ref[rows - 16 : rows, :].astype(F32)[12:13])

    @pl.when(flag > 0.5)
    def _():
        copy = pltpu.make_async_copy(row_ref, out_ref.at[0], sem)
        copy.start()
        copy.wait()


def fast_on_device(u_now, u_prev, coef_store, store_map, new_owner):
    blocks, _, fields, depth, width = u_now.shape
    now = u_now.reshape(blocks, fields, depth, width)
    prev = u_prev.reshape(blocks, fields, depth, width)
    coef = coef_store[0, 0]
    count = lax.axis_size("blk")
    region = lax.axis_index("region").astype(jnp.int32)
    owner = lax.axis_index("blk").astype(jnp.int32)
    moves = (new_owner[blocks - 1] != owner).astype(jnp.int32)
    info = jnp.concatenate([jnp.stack([region, moves]), jnp.zeros((6,), jnp.int32), store_map[0, 0]])
    params = pltpu.CompilerParams(vmem_limit_bytes=48 * 1024 * 1024)

    straight = jax.ShapeDtypeStruct((fields * depth + 16, LANES), BF16)
    diag = jax.ShapeDtypeStruct((depth + 32, LANES), BF16)
    y_out, left, right, dleft, dright = pl.pallas_call(
        functools.partial(pack_body, None),
        out_shape=(jax.ShapeDtypeStruct((5, depth, width), BF16), straight, straight, diag, diag),
        in_specs=[SMEM, VMEM, VMEM, VMEM],
        out_specs=(VMEM,) * 5,
        scratch_shapes=[pltpu.VMEM((depth, width), F32)],
        compiler_params=params,
        name="pack",
    )(info, now, prev, coef)

    swap = [(0, 1), (1, 0)]
    forward = [(i, (i + 1) % count) for i in range(count)]
    backward = [(i, (i - 1) % count) for i in range(count)]

    def crossed(by):
        return [(r * count + i, (1 - r) * count + (i + by) % count) for r in range(2) for i in range(count)]

    y_in = lax.ppermute(y_out, "region", swap)
    from_right = lax.ppermute(left, "blk", backward)
    from_dright = lax.ppermute(dleft, ("region", "blk"), crossed(-1))
    from_left = lax.ppermute(right, "blk", forward)
    from_dleft = lax.ppermute(dright, ("region", "blk"), crossed(1))

    scratch = [pltpu.VMEM((fields, depth, width + 2 * LANES), F32), pltpu.VMEM((8, width + 2 * LANES), F32)]
    row = jax.ShapeDtypeStruct((fields, depth, width), F32)
    last_row = pl.pallas_call(
        last_row_body,
        out_shape=row,
        in_specs=[SMEM] + [VMEM] * 6,
        out_specs=VMEM,
        scratch_shapes=scratch,
        compiler_params=params,
        name="last_row",
    )(info, now, prev, coef, y_in, from_right, from_dright)
    arrived = lax.ppermute(last_row, "blk", forward)
    partial = pl.pallas_call(
        first_row_body,
        out_shape=jax.ShapeDtypeStruct((blocks + 1, fields, depth, width), F32),
        in_specs=[SMEM] + [VMEM] * 7,
        out_specs=VMEM,
        scratch_shapes=scratch,
        compiler_params=params,
        name="first_row",
    )(info, now, prev, coef, y_in, from_left, from_dleft, last_row)
    result = pl.pallas_call(
        place_body,
        out_shape=jax.ShapeDtypeStruct((blocks + 1, fields, depth, width), F32),
        in_specs=[VMEM, ANY, ANY],
        out_specs=ANY,
        scratch_shapes=[pltpu.SemaphoreType.DMA],
        input_output_aliases={2: 0},
        compiler_params=params,
        name="place",
    )(from_left, arrived, partial)
    return result[:, None]


def solution(mesh):
    def on_device(*args):
        blocks = args[0].shape[0]
        if lax.axis_size("region") == 2 and blocks == 2:
            return fast_on_device(*args)
        return general_on_device(*args)

    return jax.shard_map(
        on_device,
        mesh=mesh,
        in_specs=(
            P("blk", "region", None, None, None),
            P("blk", "region", None, None, None),
            P("blk", "region", None, None, None, None),
            P("blk", "region", None),
            P("blk"),
        ),
        out_specs=P("blk", "region", None, None, None),
        check_vma=False,
    )
```

```python
import jax
import jax.numpy as jnp
from jax import lax
from jax.experimental import pallas as pl
from jax.experimental.pallas import tpu as pltpu
from jax.sharding import PartitionSpec as P

STEPS = 2
LANES = 128
F32 = jnp.float32
BF16 = jnp.bfloat16
VMEM = pl.BlockSpec(memory_space=pltpu.VMEM)
SMEM = pl.BlockSpec(memory_space=pltpu.SMEM)
ANY = pl.BlockSpec(memory_space=pl.ANY)
HBM = pl.BlockSpec(memory_space=pltpu.HBM)


def extended_2(block, sides, width, periodic):
    for axis, dim in sides:
        count = lax.axis_size(axis)
        forward = [(i, i + 1) for i in range(count - 1)]
        if periodic:
            forward.append((count - 1, 0))
        backward = [(target, source) for source, target in forward]
        low = lax.ppermute(
            lax.slice_in_dim(block, block.shape[dim] - width, None, axis=dim), axis, forward
        )
        high = lax.ppermute(lax.slice_in_dim(block, 0, width, axis=dim), axis, backward)
        block = jnp.concatenate([low, block, high], axis=dim)
    return block


def shifted_2(value, axis, by):
    devices = lax.axis_size(axis)
    return lax.ppermute(value, axis, [(i, (i + by) % devices) for i in range(devices)])


def stencil_step(state_now, state_prev, coefficient, live_count):
    slot_count, field_count, edge_cells, plane_cells = state_now.shape
    padded = extended_2(state_now, (("region", 2),), 1, False)
    first_planes = padded[..., :edge_cells]
    last_planes = padded[..., plane_cells - edge_cells :]
    last_live = jnp.take(last_planes, live_count - 1, axis=0)
    rim_pair = jnp.stack([first_planes[0], last_live], axis=2)
    spread = extended_2(rim_pair.astype(jnp.bfloat16), (("blk", 2),), 1, True).astype(
        rim_pair.dtype
    )
    left_rim = spread[:, :, 0]
    right_rim = spread[:, :, 3]
    before_planes = jnp.concatenate([left_rim[None], last_planes[:-1]], axis=0)
    after_planes = jnp.pad(first_planes[1:], ((0, 1), (0, 0), (0, 0), (0, 0)))
    slot_ids = jnp.arange(slot_count)
    after_planes = jnp.where(
        (slot_ids == live_count - 1)[:, None, None, None], right_rim[None], after_planes
    )
    extended = jnp.concatenate([before_planes, padded, after_planes], axis=-1)
    width = extended.shape[-1]
    column = jnp.arange(width) % edge_cells
    lower_mask = (column != 0).astype(jnp.float32)
    upper_mask = (column != edge_cells - 1).astype(jnp.float32)
    margin = ((0, 0), (0, 0), (0, 0), (1, 1))
    shifted = jnp.pad(extended, margin)
    summed = shifted[..., :width] * lower_mask + extended + shifted[..., 2:] * upper_mask
    summed = (
        summed[..., : -2 * edge_cells]
        + summed[..., edge_cells:-edge_cells]
        + summed[..., 2 * edge_cells :]
    )
    box_sum = summed[:, :, :-2] + summed[:, :, 1:-1] + summed[:, :, 2:]
    laplace = box_sum - 27.0 * state_now
    return 2.0 * state_now - state_prev + coefficient.astype(jnp.float32) * laplace


def compact(members, valid_flags):
    slot_count = valid_flags.shape[0]
    place_index = jnp.cumsum(valid_flags) - 1
    target = jnp.arange(slot_count)
    chooser = (valid_flags[None, :] == 1) & (place_index[None, :] == target[:, None])
    source = jnp.sum(jnp.where(chooser, target[None, :], 0), axis=1)
    filled = jnp.sum(chooser.astype(jnp.int32), axis=1) > 0
    placed = tuple(
        (
            jnp.where(
                filled.reshape((slot_count,) + (1,) * (member.ndim - 1)),
                jnp.take(member, source, axis=0),
                jnp.zeros_like(member),
            )
            for member in members
        )
    )
    return (placed, jnp.sum(valid_flags))


def general_on_device(u_now, u_prev, coef_store, store_map, new_owner):
    state_now = u_now[:, 0]
    state_prev = u_prev[:, 0]
    blocks, fields, edge_cells, plane_cells = state_now.shape
    store_local = coef_store[0, 0]
    arrived = lax.all_to_all(store_local, "region", split_axis=0, concat_axis=0, tiled=True)
    flattened = arrived.reshape((-1,) + arrived.shape[2:])
    inverse = jnp.argsort(store_map[0, 0])
    coefficient = jnp.take(flattened, inverse, axis=0).reshape(
        blocks, fields, edge_cells, plane_cells
    )
    own_index = lax.axis_index("blk")
    goes_right = new_owner[blocks - 1] != own_index
    mark_right = goes_right.astype(jnp.float32).reshape(1)
    middle_flags = jnp.ones((blocks - 2,), jnp.int32)
    keep_first = (new_owner[0] == own_index).astype(jnp.int32).reshape(1)
    keep_last = (new_owner[blocks - 1] == own_index).astype(jnp.int32).reshape(1)
    for step_index in range(STEPS):
        state_now, state_prev = (
            stencil_step(state_now, state_prev, coefficient, blocks),
            state_now,
        )
    from_left = shifted_2((state_now[blocks - 1], mark_right), "blk", 1)
    valid_flags = jnp.concatenate(
        [(from_left[1] > 0.5).astype(jnp.int32), keep_first, middle_flags, keep_last]
    )
    stacked_now = jnp.concatenate([from_left[0][None], state_now], axis=0)
    placed, live_count = compact((stacked_now,), valid_flags)
    result = placed[0]
    return result[:, None]


def lane_ids():
    return lax.broadcasted_iota(jnp.int32, (1, LANES), 1)


def pack_body(
    owner_hbm, map_hbm, u_ref, p_ref, coef_ref, y_ref, left_ref, right_ref, dleft_ref, dright_ref,
    rows_ref, ue_ref, pe_ref, ce_ref, ua_ref, pa_ref, ca_ref, owner_ref, map_ref, sems
):
    fields = u_ref.shape[1]
    depth = u_ref.shape[2]
    last = u_ref.shape[3] - LANES
    top = depth - 1
    region = lax.axis_index("region")
    lower = region == 0
    other = 1 - region
    edge8 = pl.multiple_of(jnp.where(lower, depth - 8, 0), 8)
    edge16 = pl.multiple_of(jnp.where(lower, depth - 16, 0), 16)
    scalars = [
        pltpu.make_async_copy(owner_hbm, owner_ref, sems.at[10]),
        pltpu.make_async_copy(map_hbm, map_ref, sems.at[11]),
    ]
    copies = [
        pltpu.make_async_copy(u_ref.at[:, :, pl.ds(edge8, 8), :], ue_ref, sems.at[0]),
        pltpu.make_async_copy(p_ref.at[:, :, pl.ds(edge8, 8), :], pe_ref, sems.at[1]),
        pltpu.make_async_copy(coef_ref.at[region, :, pl.ds(edge16, 16), :], ce_ref, sems.at[2]),
        pltpu.make_async_copy(u_ref.at[0, :, :, 0:LANES], ua_ref.at[0], sems.at[3]),
        pltpu.make_async_copy(u_ref.at[1, :, :, last : last + LANES], ua_ref.at[1], sems.at[4]),
        pltpu.make_async_copy(p_ref.at[0, :, :, 0:LANES], pa_ref.at[0], sems.at[5]),
        pltpu.make_async_copy(p_ref.at[1, :, :, last : last + LANES], pa_ref.at[1], sems.at[6]),
        pltpu.make_async_copy(coef_ref.at[:, :, :, 0:LANES], ca_ref.at[0], sems.at[7]),
        pltpu.make_async_copy(coef_ref.at[:, :, :, last : last + LANES], ca_ref.at[1], sems.at[8]),
        pltpu.make_async_copy(coef_ref.at[other], y_ref.at[0:4], sems.at[9]),
    ]
    for copy in copies[9:] + scalars + copies[:9]:
        copy.start()
    lane = lane_ids()
    for copy in scalars:
        copy.wait()
    moves = jnp.where(owner_ref[1] != lax.axis_index("blk"), 1.0, 0.0).astype(F32)
    numbers = [map_ref[region * 4 + s] for s in range(4)] + [map_ref[other * 4 + s] for s in range(4)]
    blank = jnp.zeros((1, LANES), F32)
    tag_rows = [blank + number.astype(F32) for number in numbers]
    flag = blank + moves
    for copy in copies[:3]:
        copy.wait()
    own_edge = jnp.where(lower, 7, 0)
    own_next = jnp.where(lower, 6, 1)
    for m in range(2):
        for f in range(fields):
            at = m * fields + f
            near = ue_ref[m, f, pl.ds(own_edge, 1), :]
            rows_ref[at : at + 1, :] = near
            rows_ref[8 + at : 9 + at, :] = ue_ref[m, f, pl.ds(own_next, 1), :]
            rows_ref[16 + at : 17 + at, :] = 2.0 * near - pe_ref[m, f, pl.ds(own_edge, 1), :]
    for s in range(4):
        piece = ce_ref[s].astype(F32)
        rows_ref[24 + s : 25 + s, :] = jnp.where(lower, piece[15:16], piece[0:1])
    for i, row in enumerate(tag_rows):
        rows_ref[28:29, i * LANES : (i + 1) * LANES] = row
    rows_ref[29:32, :] = jnp.zeros((3, rows_ref.shape[1]), F32)
    y_ref[4] = rows_ref[...].astype(BF16)
    for copy in copies[3:9]:
        copy.wait()
    for m, lanes, straight_ref, diag_ref in (
        (0, slice(0, LANES), left_ref, dleft_ref),
        (1, slice(last, last + LANES), right_ref, dright_ref),
    ):
        for f in range(fields):
            now = ua_ref[m, f]
            ahead = 2.0 * now - pa_ref[m, f]
            piece = ca_ref[m, region, f].astype(F32)
            if m == 0:
                tile = jnp.where(
                    lane < 64, now, jnp.where(lane < 96, pltpu.roll(ahead, 64, 1), pltpu.roll(piece, 96, 1))
                )
            else:
                tile = jnp.where(
                    lane >= 64, now, jnp.where(lane < 32, pltpu.roll(ahead, 32, 1), pltpu.roll(piece, 64, 1))
                )
            straight_ref[f * depth : (f + 1) * depth, :] = tile.astype(BF16)
        far = [ca_ref[m, other, s].astype(F32) for s in range(4)]
        extra = [jnp.where(lower, piece[0:1], piece[top:depth]) for piece in far] + tag_rows + [flag] + [blank] * 3
        straight_ref[fields * depth : fields * depth + 16, :] = jnp.concatenate(extra, axis=0).astype(BF16)
        plane = jnp.zeros((depth, LANES), F32)
        for s in range(4):
            shift = (32 * s if m == 0 else 32 + 32 * s) % LANES
            moved = pltpu.roll(far[s], shift, 1) if shift else far[s]
            plane = jnp.where((lane >= 32 * s) & (lane < 32 * s + 32), moved, plane)
        diag_ref[0:depth, :] = plane.astype(BF16)
        extra = (
            [rows_ref[m * fields : m * fields + 4, lanes]]
            + [rows_ref[8 + m * fields : 12 + m * fields, lanes]]
            + [rows_ref[16 + m * fields : 20 + m * fields, lanes]]
            + [rows_ref[24:28, lanes]]
            + tag_rows
            + [blank] * 8
        )
        diag_ref[depth : depth + 32, :] = jnp.concatenate(extra, axis=0).astype(BF16)
    copies[9].wait()


def nine_sum(tiles, lane, first=0):
    inside = lane % 32
    low = inside != 0
    high = inside != 31
    rows = []
    for tile in tiles:
        rows.append(
            tile
            + jnp.where(low, pltpu.roll(tile, 1, 1), 0.0)
            + jnp.where(high, pltpu.roll(tile, LANES - 1, 1), 0.0)
        )
    up = [pltpu.roll(row, 32, 1) for row in rows]
    down = [pltpu.roll(row, LANES - 32, 1) for row in rows]
    count = len(tiles)
    result = []
    for t in range(count):
        before = up[t] if t == 0 else jnp.where(lane < 32, up[t - 1], up[t])
        after = down[t] if t == count - 1 else jnp.where(lane >= 96, down[t + 1], down[t])
        result.append(rows[t] + before + after)
    return result


def step_body(m, map_ref, u_ref, p_ref, coef_ref, y_ref, straight_ref, diag_ref, out_write, first_ref, edge_ref):
    fields = u_ref.shape[1]
    depth = u_ref.shape[2]
    width = u_ref.shape[3]
    main = width // LANES
    last = width - LANES
    top = depth - 1
    region = lax.axis_index("region")
    lower = region == 0
    other = 1 - region
    lane = lane_ids()
    row_id = lax.broadcasted_iota(jnp.int32, (depth, 1), 0)
    neighbour = 1 - m

    def tile_at(t):
        return slice(t * LANES, (t + 1) * LANES)

    local_lanes = slice(last, width) if m == 1 else slice(0, LANES)
    extra_s = straight_ref[fields * depth : fields * depth + 16, :].astype(F32)
    extra_d = diag_ref[depth : depth + 32, :].astype(F32)
    extra_y = y_ref[4].astype(F32)

    numbers = [map_ref[q] for q in range(8)]
    places = []
    for number in range(8):
        place = jnp.int32(0)
        for q in range(8):
            place = jnp.where(numbers[q] == number, q, place)
        places.append((place & 3, (place >> 2) == region))

    def coef_tile(number, lanes):
        slot, held = places[number]
        return jnp.where(held, coef_ref[region, slot, :, lanes], y_ref[slot, :, lanes]).astype(F32)

    planes = []
    for s in range(4):
        tile = straight_ref[s * depth : (s + 1) * depth, :].astype(F32)
        planes.append(pltpu.roll(tile, 32 if m == 1 else 64, 1))
    diag_tile = diag_ref[0:depth, :].astype(F32)
    for s in range(4):
        shift = (-32 * s if m == 1 else 96 - 32 * s) % LANES
        planes.append(pltpu.roll(diag_tile, shift, 1) if shift else diag_tile)
    tags_s = [extra_s[4 + i : 5 + i] for i in range(8)]
    tags_d = [extra_d[16 + i : 17 + i] for i in range(8)]
    tags_y = [extra_y[28:29, i * LANES : (i + 1) * LANES] for i in range(8)]
    halo_base = 0 if m == 1 else fields

    def with_sides(local, remote, middle):
        return [local] + middle + [remote] if m == 1 else [remote] + middle + [local]

    def edge_tiles(base_y, base_d):
        middle = [extra_y[base_y + m * fields : base_y + m * fields + 4, tile_at(t)] for t in range(main)]
        local = extra_y[base_y + neighbour * fields : base_y + neighbour * fields + 4, local_lanes]
        return with_sides(local, extra_d[base_d : base_d + 4], middle)

    near = edge_tiles(0, 0)
    beyond = edge_tiles(8, 4)
    ahead = edge_tiles(16, 8)
    field_id = lax.broadcasted_iota(jnp.int32, (4, LANES), 0).astype(F32)

    def other_row(s, lanes):
        piece = coef_ref[other, s, :, lanes].astype(F32)
        return jnp.where(lower, piece[0:1], piece[top:depth])

    def edge_coef(lanes, base):
        total = jnp.zeros((4, LANES), F32)
        for s in range(4):
            total = total + jnp.where(tags_y[s] == field_id + base, extra_y[24 + s : 25 + s, lanes], 0.0)
            total = total + jnp.where(tags_y[4 + s] == field_id + base, other_row(s, lanes), 0.0)
        return total

    corner = jnp.zeros((4, LANES), F32)
    for s in range(4):
        corner = corner + jnp.where(tags_d[s] == field_id + halo_base, extra_d[12 + s : 13 + s], 0.0)
        corner = corner + jnp.where(tags_d[4 + s] == field_id + halo_base, extra_s[s : s + 1], 0.0)
    edge_c = with_sides(
        edge_coef(local_lanes, neighbour * fields),
        corner,
        [edge_coef(tile_at(t), m * fields) for t in range(main)],
    )
    near_sum = nine_sum(near, lane)
    beyond_sum = nine_sum(beyond, lane)

    def column_sum(tile, row):
        above = jnp.where(row_id == 0, jnp.where(lower, 0.0, row), pltpu.roll(tile, 1, 0))
        below = jnp.where(row_id == top, jnp.where(lower, row, 0.0), pltpu.roll(tile, depth - 1, 0))
        return tile + above + below

    def sides_of(f):
        remote = straight_ref[f * depth : (f + 1) * depth, :].astype(F32)
        local = u_ref[neighbour, f, :, local_lanes]
        return local, remote

    for f in range(fields):
        local, remote = sides_of(f)
        now = with_sides(local, remote, [u_ref[m, f, :, tile_at(t)] for t in range(main)])
        sums = nine_sum(now, lane)
        halo_c = jnp.zeros((depth, LANES), F32)
        for i in range(8):
            halo_c = halo_c + jnp.where(tags_s[i] == F32(halo_base + f), planes[i], 0.0)
        coef = with_sides(
            coef_tile(neighbour * fields + f, local_lanes),
            halo_c,
            [coef_tile(m * fields + f, tile_at(t)) for t in range(main)],
        )
        drift = with_sides(
            2.0 * local - p_ref[neighbour, f, :, local_lanes],
            pltpu.roll(remote, 64 if m == 1 else 96, 1),
            [2.0 * now[t + 1] - p_ref[m, f, :, tile_at(t)] for t in range(main)],
        )
        for t in range(main + 2):
            edge_ref[f : f + 1, tile_at(t)] = jnp.where(lower, sums[t][top:depth], sums[t][0:1])
            box = column_sum(sums[t], near_sum[t][f : f + 1])
            first_ref[f, :, tile_at(t)] = drift[t] + coef[t] * (box - 27.0 * now[t])
    stepped = []
    for t in range(main + 2):
        box = near_sum[t] + beyond_sum[t] + edge_ref[0:4, tile_at(t)]
        stepped.append(ahead[t] + edge_c[t] * (box - 27.0 * near[t]))
    stepped_sum = nine_sum(stepped, lane)
    for f in range(fields):
        now = [first_ref[f, :, tile_at(t)] for t in range(main + 2)]
        sums = nine_sum(now, lane)
        for t in range(1, main + 1):
            box = column_sum(sums[t], stepped_sum[t][f : f + 1])
            lanes = tile_at(t - 1)
            coef = coef_tile(m * fields + f, lanes)
            value = 2.0 * now[t] - u_ref[m, f, :, lanes] + coef * (box - 27.0 * now[t])
            out_write(f, lanes, value)


CODES = 32000.0


def last_row_body(
    map_ref, u_ref, p_ref, coef_ref, y_ref, straight_ref, diag_ref, early_a, early_b, row_ref, code_ref,
    first_ref, edge_ref
):
    depth = u_ref.shape[2]
    fields = u_ref.shape[1]

    def write(f, lanes, value):
        row_ref[f, :, lanes] = value
        size = jnp.maximum(jnp.max(jnp.abs(value), axis=0, keepdims=True), 1e-30)
        power = jnp.ceil(jnp.log2(size))
        code = jnp.floor(value * (CODES * jnp.exp2(-power)) + 0.5)
        code_ref[f * depth : (f + 1) * depth, lanes] = code.astype(jnp.int32).astype(jnp.int16)
        edge_ref[f : f + 1, lanes] = power

    step_body(1, map_ref, u_ref, p_ref, coef_ref, y_ref, straight_ref, diag_ref, write, first_ref, edge_ref)
    edge_ref[4:8, :] = jnp.zeros((4, edge_ref.shape[1]), F32)
    powers = edge_ref[:, 0 : row_ref.shape[2]]
    code_ref[fields * depth : fields * depth + 8, :] = powers.astype(jnp.int32).astype(jnp.int16)


def first_row_body(
    owner_ref, map_ref, u_ref, p_ref, coef_ref, y_ref, straight_ref, diag_ref, last_ref, out_ref, first_ref, edge_ref
):
    fields = u_ref.shape[1]
    depth = u_ref.shape[2]
    arrives = straight_ref[fields * depth : fields * depth + 16, :].astype(F32)[12:13] > 0.5
    keeps = owner_ref[1] == lax.axis_index("blk")

    def write(f, lanes, value):
        kept = jnp.where(keeps, last_ref[f, :, lanes], 0.0)
        out_ref[0, f, :, lanes] = value
        out_ref[1, f, :, lanes] = jnp.where(arrives, value, kept)
        out_ref[2, f, :, lanes] = jnp.where(arrives, kept, 0.0)

    step_body(0, map_ref, u_ref, p_ref, coef_ref, y_ref, straight_ref, diag_ref, write, first_ref, edge_ref)


def place_body(straight_ref, code_ref, partial_ref, out_ref, row_ref, sems):
    fields, depth, width = row_ref.shape
    flag = jnp.max(straight_ref[fields * depth : fields * depth + 16, :].astype(F32)[12:13])

    @pl.when(flag > 0.5)
    def _():
        scale = jnp.exp2(code_ref[fields * depth : fields * depth + 8, :].astype(jnp.int32).astype(F32)) * (1.0 / CODES)
        copies = []
        for f in range(fields):
            code = code_ref[f * depth : (f + 1) * depth, :].astype(jnp.int32).astype(F32)
            row_ref[f] = code * scale[f : f + 1]
            copy = pltpu.make_async_copy(row_ref.at[f], out_ref.at[0, f], sems.at[f])
            copy.start()
            copies.append(copy)
        for copy in copies:
            copy.wait()


def fast_on_device(u_now, u_prev, coef_store, store_map, new_owner):
    blocks, _, fields, depth, width = u_now.shape
    now = u_now.reshape(blocks, fields, depth, width)
    prev = u_prev.reshape(blocks, fields, depth, width)
    coef = coef_store[0, 0]
    count = lax.axis_size("blk")
    order = store_map.reshape(-1)
    owner_hbm, order_hbm, now_hbm, prev_hbm, coef_hbm = (
        pltpu.with_memory_space_constraint(array, pltpu.HBM) for array in (new_owner, order, now, prev, coef)
    )
    params = pltpu.CompilerParams(vmem_limit_bytes=48 * 1024 * 1024)

    straight = jax.ShapeDtypeStruct((fields * depth + 16, LANES), BF16)
    diag = jax.ShapeDtypeStruct((depth + 32, LANES), BF16)
    y_out, left, right, dleft, dright = pl.pallas_call(
        pack_body,
        out_shape=(jax.ShapeDtypeStruct((5, depth, width), BF16), straight, straight, diag, diag),
        in_specs=[HBM] * 5,
        out_specs=(VMEM,) * 5,
        scratch_shapes=[
            pltpu.VMEM((depth, width), F32),
            pltpu.VMEM((blocks, fields, 8, width), F32),
            pltpu.VMEM((blocks, fields, 8, width), F32),
            pltpu.VMEM((4, 16, width), BF16),
            pltpu.VMEM((2, fields, depth, LANES), F32),
            pltpu.VMEM((2, fields, depth, LANES), F32),
            pltpu.VMEM((2, 2, 4, depth, LANES), BF16),
            pltpu.SMEM(new_owner.shape, jnp.int32),
            pltpu.SMEM(order.shape, jnp.int32),
            pltpu.SemaphoreType.DMA((12,)),
        ],
        compiler_params=params,
        name="pack",
    )(owner_hbm, order_hbm, now_hbm, prev_hbm, coef_hbm)

    swap = [(0, 1), (1, 0)]
    forward = [(i, (i + 1) % count) for i in range(count)]
    backward = [(i, (i - 1) % count) for i in range(count)]

    def crossed(by):
        return [(r * count + i, (1 - r) * count + (i + by) % count) for r in range(2) for i in range(count)]

    y_in = lax.ppermute(y_out, "region", swap)
    from_right = lax.ppermute(left, "blk", backward)
    from_dright = lax.ppermute(dleft, ("region", "blk"), crossed(-1))
    from_left = lax.ppermute(right, "blk", forward)
    from_dleft = lax.ppermute(dright, ("region", "blk"), crossed(1))

    scratch = [pltpu.VMEM((fields, depth, width + 2 * LANES), F32), pltpu.VMEM((8, width + 2 * LANES), F32)]
    last_row, code = pl.pallas_call(
        last_row_body,
        out_shape=(
            jax.ShapeDtypeStruct((fields, depth, width), F32),
            jax.ShapeDtypeStruct((fields * depth + 8, width), jnp.int16),
        ),
        in_specs=[SMEM] + [VMEM] * 6 + [ANY] * 2,
        out_specs=(VMEM, VMEM),
        scratch_shapes=scratch,
        compiler_params=params,
        name="last_row",
    )(order, now, prev, coef, y_in, from_right, from_dright, from_left, from_dleft)
    arrived = lax.ppermute(code, "blk", forward)
    partial = pl.pallas_call(
        first_row_body,
        out_shape=jax.ShapeDtypeStruct((blocks + 1, fields, depth, width), F32),
        in_specs=[SMEM] * 2 + [VMEM] * 7,
        out_specs=VMEM,
        scratch_shapes=scratch,
        compiler_params=params,
        name="first_row",
    )(new_owner, order, now, prev, coef, y_in, from_left, from_dleft, last_row)
    result = pl.pallas_call(
        place_body,
        out_shape=jax.ShapeDtypeStruct((blocks + 1, fields, depth, width), F32),
        in_specs=[VMEM, VMEM, ANY],
        out_specs=ANY,
        scratch_shapes=[pltpu.VMEM((fields, depth, width), F32), pltpu.SemaphoreType.DMA((fields,))],
        input_output_aliases={2: 0},
        compiler_params=params,
        name="place",
    )(from_left, arrived, partial)
    return result[:, None]


def solution(mesh):
    def on_device(*args):
        blocks = args[0].shape[0]
        if lax.axis_size("region") == 2 and blocks == 2:
            return fast_on_device(*args)
        return general_on_device(*args)

    return jax.shard_map(
        on_device,
        mesh=mesh,
        in_specs=(
            P("blk", "region", None, None, None),
            P("blk", "region", None, None, None),
            P("blk", "region", None, None, None, None),
            P("blk", "region", None),
            P("blk"),
        ),
        out_specs=P("blk", "region", None, None, None),
        check_vma=False,
    )
```

```python
import functools

import jax
import jax.numpy as jnp
from jax import lax
from jax.experimental import pallas as pl
from jax.experimental.pallas import tpu as pltpu
from jax.sharding import PartitionSpec as P

STEPS = 2
LANES = 128
F32 = jnp.float32
BF16 = jnp.bfloat16
VMEM = pl.BlockSpec(memory_space=pltpu.VMEM)
SMEM = pl.BlockSpec(memory_space=pltpu.SMEM)
ANY = pl.BlockSpec(memory_space=pl.ANY)
HBM = pl.BlockSpec(memory_space=pltpu.HBM)


def extended_2(block, sides, width, periodic):
    for axis, dim in sides:
        count = lax.axis_size(axis)
        forward = [(i, i + 1) for i in range(count - 1)]
        if periodic:
            forward.append((count - 1, 0))
        backward = [(target, source) for source, target in forward]
        low = lax.ppermute(
            lax.slice_in_dim(block, block.shape[dim] - width, None, axis=dim), axis, forward
        )
        high = lax.ppermute(lax.slice_in_dim(block, 0, width, axis=dim), axis, backward)
        block = jnp.concatenate([low, block, high], axis=dim)
    return block


def shifted_2(value, axis, by):
    devices = lax.axis_size(axis)
    return lax.ppermute(value, axis, [(i, (i + by) % devices) for i in range(devices)])


def stencil_step(state_now, state_prev, coefficient, live_count):
    slot_count, field_count, edge_cells, plane_cells = state_now.shape
    padded = extended_2(state_now, (("region", 2),), 1, False)
    first_planes = padded[..., :edge_cells]
    last_planes = padded[..., plane_cells - edge_cells :]
    last_live = jnp.take(last_planes, live_count - 1, axis=0)
    rim_pair = jnp.stack([first_planes[0], last_live], axis=2)
    spread = extended_2(rim_pair.astype(jnp.bfloat16), (("blk", 2),), 1, True).astype(
        rim_pair.dtype
    )
    left_rim = spread[:, :, 0]
    right_rim = spread[:, :, 3]
    before_planes = jnp.concatenate([left_rim[None], last_planes[:-1]], axis=0)
    after_planes = jnp.pad(first_planes[1:], ((0, 1), (0, 0), (0, 0), (0, 0)))
    slot_ids = jnp.arange(slot_count)
    after_planes = jnp.where(
        (slot_ids == live_count - 1)[:, None, None, None], right_rim[None], after_planes
    )
    extended = jnp.concatenate([before_planes, padded, after_planes], axis=-1)
    width = extended.shape[-1]
    column = jnp.arange(width) % edge_cells
    lower_mask = (column != 0).astype(jnp.float32)
    upper_mask = (column != edge_cells - 1).astype(jnp.float32)
    margin = ((0, 0), (0, 0), (0, 0), (1, 1))
    shifted = jnp.pad(extended, margin)
    summed = shifted[..., :width] * lower_mask + extended + shifted[..., 2:] * upper_mask
    summed = (
        summed[..., : -2 * edge_cells]
        + summed[..., edge_cells:-edge_cells]
        + summed[..., 2 * edge_cells :]
    )
    box_sum = summed[:, :, :-2] + summed[:, :, 1:-1] + summed[:, :, 2:]
    laplace = box_sum - 27.0 * state_now
    return 2.0 * state_now - state_prev + coefficient.astype(jnp.float32) * laplace


def compact(members, valid_flags):
    slot_count = valid_flags.shape[0]
    place_index = jnp.cumsum(valid_flags) - 1
    target = jnp.arange(slot_count)
    chooser = (valid_flags[None, :] == 1) & (place_index[None, :] == target[:, None])
    source = jnp.sum(jnp.where(chooser, target[None, :], 0), axis=1)
    filled = jnp.sum(chooser.astype(jnp.int32), axis=1) > 0
    placed = tuple(
        (
            jnp.where(
                filled.reshape((slot_count,) + (1,) * (member.ndim - 1)),
                jnp.take(member, source, axis=0),
                jnp.zeros_like(member),
            )
            for member in members
        )
    )
    return (placed, jnp.sum(valid_flags))


def general_on_device(u_now, u_prev, coef_store, store_map, new_owner):
    state_now = u_now[:, 0]
    state_prev = u_prev[:, 0]
    blocks, fields, edge_cells, plane_cells = state_now.shape
    store_local = coef_store[0, 0]
    arrived = lax.all_to_all(store_local, "region", split_axis=0, concat_axis=0, tiled=True)
    flattened = arrived.reshape((-1,) + arrived.shape[2:])
    inverse = jnp.argsort(store_map[0, 0])
    coefficient = jnp.take(flattened, inverse, axis=0).reshape(
        blocks, fields, edge_cells, plane_cells
    )
    own_index = lax.axis_index("blk")
    goes_right = new_owner[blocks - 1] != own_index
    mark_right = goes_right.astype(jnp.float32).reshape(1)
    middle_flags = jnp.ones((blocks - 2,), jnp.int32)
    keep_first = (new_owner[0] == own_index).astype(jnp.int32).reshape(1)
    keep_last = (new_owner[blocks - 1] == own_index).astype(jnp.int32).reshape(1)
    for step_index in range(STEPS):
        state_now, state_prev = (
            stencil_step(state_now, state_prev, coefficient, blocks),
            state_now,
        )
    from_left = shifted_2((state_now[blocks - 1], mark_right), "blk", 1)
    valid_flags = jnp.concatenate(
        [(from_left[1] > 0.5).astype(jnp.int32), keep_first, middle_flags, keep_last]
    )
    stacked_now = jnp.concatenate([from_left[0][None], state_now], axis=0)
    placed, live_count = compact((stacked_now,), valid_flags)
    result = placed[0]
    return result[:, None]


def lane_ids():
    return lax.broadcasted_iota(jnp.int32, (1, LANES), 1)


def edge_start(lower, depth, size):
    return pl.multiple_of(jnp.where(lower, depth - size, 0), size)


def tag_values(map_ref, region):
    numbers = [map_ref[region * 4 + s] for s in range(4)] + [map_ref[(1 - region) * 4 + s] for s in range(4)]
    return [jnp.zeros((1, LANES), F32) + number.astype(F32) for number in numbers]


def load_edges(u_ref, p_ref, coef_ref, ue_ref, pe_ref, ce_ref, region, lower, depth, sems):
    edge8 = edge_start(lower, depth, 8)
    edge16 = edge_start(lower, depth, 16)
    return [
        pltpu.make_async_copy(u_ref.at[:, :, pl.ds(edge8, 8), :], ue_ref, sems.at[0]),
        pltpu.make_async_copy(p_ref.at[:, :, pl.ds(edge8, 8), :], pe_ref, sems.at[1]),
        pltpu.make_async_copy(coef_ref.at[region, :, pl.ds(edge16, 16), :], ce_ref, sems.at[2]),
    ]


def pack_region_body(
    map_hbm, u_ref, p_ref, coef_ref, y_ref, edges_ref, rows_ref, ue_ref, pe_ref, ce_ref, map_ref, sems
):
    fields = u_ref.shape[1]
    depth = u_ref.shape[2]
    region = lax.axis_index("region")
    lower = region == 0
    scalars = pltpu.make_async_copy(map_hbm, map_ref, sems.at[3])
    bulk = pltpu.make_async_copy(coef_ref.at[1 - region], y_ref.at[0:4], sems.at[4])
    copies = load_edges(u_ref, p_ref, coef_ref, ue_ref, pe_ref, ce_ref, region, lower, depth, sems)
    for copy in [bulk, scalars] + copies:
        copy.start()
    for copy in copies:
        copy.wait()
    own_edge = jnp.where(lower, 7, 0)
    own_next = jnp.where(lower, 6, 1)
    for m in range(2):
        for f in range(fields):
            at = m * fields + f
            near = ue_ref[m, f, pl.ds(own_edge, 1), :]
            rows_ref[at : at + 1, :] = near
            rows_ref[8 + at : 9 + at, :] = ue_ref[m, f, pl.ds(own_next, 1), :]
            rows_ref[16 + at : 17 + at, :] = 2.0 * near - pe_ref[m, f, pl.ds(own_edge, 1), :]
    for s in range(4):
        piece = ce_ref[s].astype(F32)
        rows_ref[24 + s : 25 + s, :] = jnp.where(lower, piece[15:16], piece[0:1])
    scalars.wait()
    for i, row in enumerate(tag_values(map_ref, region)):
        rows_ref[28:29, i * LANES : (i + 1) * LANES] = row
    rows_ref[29:32, :] = jnp.zeros((3, rows_ref.shape[1]), F32)
    y_ref[4] = rows_ref[...].astype(BF16)
    edges_ref[...] = rows_ref[...]
    bulk.wait()


def pack_ring_body(
    owner_hbm, map_hbm, u_ref, p_ref, coef_ref, edges_ref, left_ref, right_ref, dleft_ref, dright_ref,
    ua_ref, pa_ref, ca_ref, owner_ref, map_ref, sems
):
    fields = u_ref.shape[1]
    depth = u_ref.shape[2]
    last = u_ref.shape[3] - LANES
    top = depth - 1
    region = lax.axis_index("region")
    lower = region == 0
    other = 1 - region
    copies = [
        pltpu.make_async_copy(owner_hbm, owner_ref, sems.at[0]),
        pltpu.make_async_copy(map_hbm, map_ref, sems.at[1]),
        pltpu.make_async_copy(u_ref.at[0, :, :, 0:LANES], ua_ref.at[0], sems.at[2]),
        pltpu.make_async_copy(u_ref.at[1, :, :, last : last + LANES], ua_ref.at[1], sems.at[3]),
        pltpu.make_async_copy(p_ref.at[0, :, :, 0:LANES], pa_ref.at[0], sems.at[4]),
        pltpu.make_async_copy(p_ref.at[1, :, :, last : last + LANES], pa_ref.at[1], sems.at[5]),
        pltpu.make_async_copy(coef_ref.at[:, :, :, 0:LANES], ca_ref.at[0], sems.at[6]),
        pltpu.make_async_copy(coef_ref.at[:, :, :, last : last + LANES], ca_ref.at[1], sems.at[7]),
    ]
    for copy in copies:
        copy.start()
    for copy in copies:
        copy.wait()
    lane = lane_ids()
    tag_rows = tag_values(map_ref, region)
    blank = jnp.zeros((1, LANES), F32)
    flag = blank + jnp.where(owner_ref[1] != lax.axis_index("blk"), 1.0, 0.0).astype(F32)
    for m, lanes, straight_ref, diag_ref in (
        (0, slice(0, LANES), left_ref, dleft_ref),
        (1, slice(last, last + LANES), right_ref, dright_ref),
    ):
        for f in range(fields):
            now = ua_ref[m, f]
            ahead = 2.0 * now - pa_ref[m, f]
            piece = ca_ref[m, region, f].astype(F32)
            if m == 0:
                tile = jnp.where(
                    lane < 64, now, jnp.where(lane < 96, pltpu.roll(ahead, 64, 1), pltpu.roll(piece, 96, 1))
                )
            else:
                tile = jnp.where(
                    lane >= 64, now, jnp.where(lane < 32, pltpu.roll(ahead, 32, 1), pltpu.roll(piece, 64, 1))
                )
            straight_ref[f * depth : (f + 1) * depth, :] = tile.astype(BF16)
        far = [ca_ref[m, other, s].astype(F32) for s in range(4)]
        extra = [jnp.where(lower, piece[0:1], piece[top:depth]) for piece in far] + tag_rows + [flag] + [blank] * 3
        straight_ref[fields * depth : fields * depth + 16, :] = jnp.concatenate(extra, axis=0).astype(BF16)
        plane = jnp.zeros((depth, LANES), F32)
        for s in range(4):
            shift = (32 * s if m == 0 else 32 + 32 * s) % LANES
            moved = pltpu.roll(far[s], shift, 1) if shift else far[s]
            plane = jnp.where((lane >= 32 * s) & (lane < 32 * s + 32), moved, plane)
        diag_ref[0:depth, :] = plane.astype(BF16)
        extra = (
            [edges_ref[m * fields : m * fields + 4, lanes]]
            + [edges_ref[8 + m * fields : 12 + m * fields, lanes]]
            + [edges_ref[16 + m * fields : 20 + m * fields, lanes]]
            + [edges_ref[24:28, lanes]]
            + tag_rows
            + [blank] * 8
        )
        diag_ref[depth : depth + 32, :] = jnp.concatenate(extra, axis=0).astype(BF16)


def nine_sum(tiles, lane, first=0):
    inside = lane % 32
    low = inside != 0
    high = inside != 31
    rows = []
    for tile in tiles:
        rows.append(
            tile
            + jnp.where(low, pltpu.roll(tile, 1, 1), 0.0)
            + jnp.where(high, pltpu.roll(tile, LANES - 1, 1), 0.0)
        )
    up = [pltpu.roll(row, 32, 1) for row in rows]
    down = [pltpu.roll(row, LANES - 32, 1) for row in rows]
    count = len(tiles)
    result = []
    for t in range(count):
        before = up[t] if t == 0 else jnp.where(lane < 32, up[t - 1], up[t])
        after = down[t] if t == count - 1 else jnp.where(lane >= 96, down[t + 1], down[t])
        result.append(rows[t] + before + after)
    return result


def column_sum(tile, row_id, low_row, high_row):
    depth = tile.shape[0]
    above = pltpu.roll(tile, 1, 0)
    below = pltpu.roll(tile, depth - 1, 0)
    return tile + jnp.where(row_id == 0, low_row, above) + jnp.where(row_id == depth - 1, high_row, below)


def local_body(u_ref, box_ref, rim_ref):
    fields, depth, width = u_ref.shape[1:]
    main = width // LANES
    lower = lax.axis_index("region") == 0
    lane = lane_ids()
    row_id = lax.broadcasted_iota(jnp.int32, (depth, 1), 0)
    for f in range(fields):
        now = [u_ref[m, f, :, t * LANES : (t + 1) * LANES] for m in range(2) for t in range(main)]
        sums = nine_sum(now, lane)
        for i, (tile, total) in enumerate(zip(now, sums)):
            m, t = divmod(i, main)
            lanes = slice(t * LANES, (t + 1) * LANES)
            rim_ref[m, f : f + 1, lanes] = jnp.where(lower, total[depth - 1 : depth], total[0:1])
            box_ref[m, f, :, lanes] = column_sum(total, row_id, 0.0, 0.0) - 27.0 * tile
    rim_ref[:, 4:8, :] = jnp.zeros((2, 4, width), F32)


def tile_at(t):
    return slice(t * LANES, (t + 1) * LANES)


class Row:
    def __init__(self, m, map_ref, u_ref, p_ref, coef_ref, y_ref, straight_ref, diag_ref, box_ref):
        self.m = m
        self.u, self.p, self.coef, self.y, self.box = u_ref, p_ref, coef_ref, y_ref, box_ref
        self.straight, self.diag = straight_ref, diag_ref
        self.fields, self.depth, self.width = u_ref.shape[1:]
        self.main = self.width // LANES
        self.region = lax.axis_index("region")
        self.lower = self.region == 0
        self.lane = lane_ids()
        self.row_id = lax.broadcasted_iota(jnp.int32, (self.depth, 1), 0)
        self.beside = 1 - m
        self.local_lanes = slice(self.width - LANES, self.width) if m == 1 else slice(0, LANES)
        fields, depth = self.fields, self.depth
        self.extra_s = straight_ref[fields * depth : fields * depth + 16, :].astype(F32)
        numbers = [map_ref[q] for q in range(8)]
        self.places = []
        for number in range(8):
            place = jnp.int32(0)
            for q in range(8):
                place = jnp.where(numbers[q] == number, q, place)
            self.places.append((place & 3, (place >> 2) == self.region))
        planes = []
        for s in range(4):
            tile = straight_ref[s * depth : (s + 1) * depth, :].astype(F32)
            planes.append(pltpu.roll(tile, 32 if m == 1 else 64, 1))
        diag_tile = diag_ref[0:depth, :].astype(F32)
        for s in range(4):
            shift = (-32 * s if m == 1 else 96 - 32 * s) % LANES
            planes.append(pltpu.roll(diag_tile, shift, 1) if shift else diag_tile)
        self.planes = planes
        self.tags = [self.extra_s[4 + i : 5 + i] for i in range(8)]
        self.halo_base = 0 if m == 1 else fields

    def with_sides(self, local, remote, middle):
        return [local] + middle + [remote] if self.m == 1 else [remote] + middle + [local]

    def coef_tile(self, number, lanes):
        slot, held = self.places[number]
        return jnp.where(held, self.coef[self.region, slot, :, lanes], self.y[slot, :, lanes]).astype(F32)

    def other_column(self, rim_ref, near_ref, stepped_ref):
        m, fields, depth, main = self.m, self.fields, self.depth, self.main
        lane, lower = self.lane, self.lower
        extra_y = self.y[4].astype(F32)
        extra_d = self.diag[depth : depth + 32, :].astype(F32)
        tags_d = [extra_d[16 + i : 17 + i] for i in range(8)]
        tags_y = [extra_y[28:29, i * LANES : (i + 1) * LANES] for i in range(8)]
        field_id = lax.broadcasted_iota(jnp.int32, (4, LANES), 0).astype(F32)

        def edge_tiles(base_y, base_d):
            middle = [extra_y[base_y + m * fields : base_y + m * fields + 4, tile_at(t)] for t in range(main)]
            local = extra_y[base_y + self.beside * fields : base_y + self.beside * fields + 4, self.local_lanes]
            return self.with_sides(local, extra_d[base_d : base_d + 4], middle)

        near = edge_tiles(0, 0)
        beyond = edge_tiles(8, 4)
        ahead = edge_tiles(16, 8)

        def other_row(s, lanes):
            piece = self.coef[1 - self.region, s, :, lanes].astype(F32)
            return jnp.where(lower, piece[0:1], piece[depth - 1 : depth])

        def edge_coef(lanes, base):
            total = jnp.zeros((4, LANES), F32)
            for s in range(4):
                total = total + jnp.where(tags_y[s] == field_id + base, extra_y[24 + s : 25 + s, lanes], 0.0)
                total = total + jnp.where(tags_y[4 + s] == field_id + base, other_row(s, lanes), 0.0)
            return total

        corner = jnp.zeros((4, LANES), F32)
        for s in range(4):
            corner = corner + jnp.where(tags_d[s] == field_id + self.halo_base, extra_d[12 + s : 13 + s], 0.0)
            corner = corner + jnp.where(tags_d[4 + s] == field_id + self.halo_base, self.extra_s[s : s + 1], 0.0)
        edge_c = self.with_sides(
            edge_coef(self.local_lanes, self.beside * fields),
            corner,
            [edge_coef(tile_at(t), m * fields) for t in range(main)],
        )
        near_sum = nine_sum(near, lane)
        beyond_sum = nine_sum(beyond, lane)
        border = main - 1 if m == 1 else 0
        rims = self.with_sides(
            rim_ref[self.beside, 0:4, self.local_lanes],
            jnp.zeros((4, LANES), F32),
            [rim_ref[m, 0:4, tile_at(t)] for t in range(main)],
        )
        own, outer = [], []
        for f in range(fields):
            tiles = self.border_tiles(f)
            own.append(jnp.where(lower, tiles[0][depth - 1 : depth], tiles[0][0:1]))
            outer.append(jnp.where(lower, tiles[1][depth - 1 : depth], tiles[1][0:1]))
        pair = [jnp.concatenate(own, axis=0), jnp.concatenate(outer, axis=0)]
        sums = nine_sum(pair if m == 1 else pair[::-1], lane)
        side = main + 1 if m == 1 else 0
        rims[side] = sums[1] if m == 1 else sums[0]
        touched = sums[0] if m == 1 else sums[1]
        facing = lane >= 96 if m == 1 else lane < 32
        rims[border + 1] = jnp.where(facing, touched, rims[border + 1])
        stepped = []
        for t in range(main + 2):
            box = near_sum[t] + beyond_sum[t] + rims[t]
            stepped.append(ahead[t] + edge_c[t] * (box - 27.0 * near[t]))
        stepped_sum = nine_sum(stepped, lane)
        for t in range(main + 2):
            near_ref[0:4, tile_at(t)] = near_sum[t]
            stepped_ref[0:4, tile_at(t)] = stepped_sum[t]

    def border_tiles(self, f):
        border = self.main - 1 if self.m == 1 else 0
        remote = self.straight[f * self.depth : (f + 1) * self.depth, :].astype(F32)
        return self.u[self.m, f, :, tile_at(border)], remote

    def rows(self, row):
        return jnp.where(self.lower, 0.0, row), jnp.where(self.lower, row, 0.0)

    def first_step(self, f, near_ref):
        m, main, lane, fields = self.m, self.main, self.lane, self.fields
        inner, remote = self.border_tiles(f)
        local = self.u[self.beside, f, :, self.local_lanes]
        pair = [inner, remote] if m == 1 else [remote, inner]
        sums = nine_sum(pair, lane)
        inner_sum, remote_sum = (sums[0], sums[1]) if m == 1 else (sums[1], sums[0])
        facing = lane >= 96 if m == 1 else lane < 32
        border = main - 1 if m == 1 else 0
        now = self.with_sides(local, remote, [self.u[m, f, :, tile_at(t)] for t in range(main)])
        halo_c = jnp.zeros((self.depth, LANES), F32)
        for i in range(8):
            halo_c = halo_c + jnp.where(self.tags[i] == F32(self.halo_base + f), self.planes[i], 0.0)
        coef = self.with_sides(
            self.coef_tile(self.beside * fields + f, self.local_lanes),
            halo_c,
            [self.coef_tile(m * fields + f, tile_at(t)) for t in range(main)],
        )
        drift = self.with_sides(
            2.0 * local - self.p[self.beside, f, :, self.local_lanes],
            pltpu.roll(remote, 64 if m == 1 else 96, 1),
            [2.0 * now[t + 1] - self.p[m, f, :, tile_at(t)] for t in range(main)],
        )
        result = []
        for t in range(main + 2):
            remote_side = t == (main + 1 if m == 1 else 0)
            low_row, high_row = self.rows(near_ref[f : f + 1, tile_at(t)])
            if remote_side:
                lap = column_sum(remote_sum, self.row_id, low_row, high_row) - 27.0 * remote
            else:
                if t == (0 if m == 1 else main + 1):
                    lap = self.box[self.beside, f, :, self.local_lanes]
                else:
                    lap = self.box[m, f, :, tile_at(t - 1)]
                lap = lap + jnp.where(self.row_id == 0, low_row, 0.0)
                lap = lap + jnp.where(self.row_id == self.depth - 1, high_row, 0.0)
                if t == border + 1:
                    whole = column_sum(inner_sum, self.row_id, low_row, high_row) - 27.0 * inner
                    lap = jnp.where(facing, whole, lap)
            result.append(drift[t] + coef[t] * lap)
        return result

    def second_step(self, f, now, stepped_ref, write):
        sums = nine_sum(now, self.lane)
        for t in range(1, self.main + 1):
            low_row, high_row = self.rows(stepped_ref[f : f + 1, tile_at(t)])
            lanes = tile_at(t - 1)
            lap = column_sum(sums[t], self.row_id, low_row, high_row) - 27.0 * now[t]
            coef = self.coef_tile(self.m * self.fields + f, lanes)
            write(f, lanes, 2.0 * now[t] - self.u[self.m, f, :, lanes] + coef * lap)


CODES = 32000.0


def code_writer(row_ref, code_ref, power_ref, first, count, depth):
    def write(f, lanes, value):
        at = f - first
        row_ref[at, :, lanes] = value
        size = jnp.maximum(jnp.max(jnp.abs(value), axis=0, keepdims=True), 1e-30)
        power = jnp.ceil(jnp.log2(size))
        code = jnp.floor(value * (CODES * jnp.exp2(-power)) + 0.5)
        code_ref[at * depth : (at + 1) * depth, lanes] = code.astype(jnp.int32).astype(jnp.int16)
        power_ref[at : at + 1, lanes] = power

    return write


def write_powers(power_ref, code_ref, count, depth):
    power_ref[count:8, :] = jnp.zeros((8 - count, power_ref.shape[1]), F32)
    code_ref[count * depth : count * depth + 8, :] = power_ref[...].astype(jnp.int32).astype(jnp.int16)


def last_row_a_body(
    map_ref, u_ref, p_ref, coef_ref, y_ref, straight_ref, diag_ref, box_ref, rim_ref,
    row_ref, code_ref, near_ref, stepped_ref, power_ref
):
    count = row_ref.shape[0]
    row = Row(1, map_ref, u_ref, p_ref, coef_ref, y_ref, straight_ref, diag_ref, box_ref)
    row.other_column(rim_ref, near_ref, stepped_ref)
    write = code_writer(row_ref, code_ref, power_ref, 0, count, row.depth)
    for f in range(count):
        row.second_step(f, row.first_step(f, near_ref), stepped_ref, write)
    write_powers(power_ref, code_ref, count, row.depth)


def last_row_b_body(
    map_ref, u_ref, p_ref, coef_ref, y_ref, straight_ref, diag_ref, box_ref, near_ref, stepped_ref, early_a, early_b,
    row_ref, code_ref, power_ref
):
    count = row_ref.shape[0]
    row = Row(1, map_ref, u_ref, p_ref, coef_ref, y_ref, straight_ref, diag_ref, box_ref)
    write = code_writer(row_ref, code_ref, power_ref, row.fields - count, count, row.depth)
    for f in range(row.fields - count, row.fields):
        row.second_step(f, row.first_step(f, near_ref), stepped_ref, write)
    write_powers(power_ref, code_ref, count, row.depth)


def first_row_body(
    owner_ref, map_ref, u_ref, p_ref, coef_ref, y_ref, straight_ref, diag_ref, box_ref, rim_ref, last_a_ref, last_b_ref,
    out_ref, near_ref, stepped_ref
):
    row = Row(0, map_ref, u_ref, p_ref, coef_ref, y_ref, straight_ref, diag_ref, box_ref)
    arrives = row.extra_s[12:13] > 0.5
    keeps = owner_ref[1] == lax.axis_index("blk")
    half = last_a_ref.shape[0]

    def write(f, lanes, value):
        mine = last_a_ref[f, :, lanes] if f < half else last_b_ref[f - half, :, lanes]
        kept = jnp.where(keeps, mine, 0.0)
        out_ref[0, f, :, lanes] = value
        out_ref[1, f, :, lanes] = jnp.where(arrives, value, kept)
        out_ref[2, f, :, lanes] = jnp.where(arrives, kept, 0.0)

    row.other_column(rim_ref, near_ref, stepped_ref)
    for f in range(row.fields):
        row.second_step(f, row.first_step(f, near_ref), stepped_ref, write)


def place_body(first, straight_ref, code_ref, partial_ref, out_ref, row_ref, sems):
    count, depth, width = row_ref.shape
    rows = straight_ref.shape[0]
    flag = jnp.max(straight_ref[rows - 16 : rows, :].astype(F32)[12:13])

    @pl.when(flag > 0.5)
    def _():
        scale = jnp.exp2(code_ref[count * depth : count * depth + 8, :].astype(jnp.int32).astype(F32)) * (1.0 / CODES)
        copies = []
        for f in range(count):
            code = code_ref[f * depth : (f + 1) * depth, :].astype(jnp.int32).astype(F32)
            row_ref[f] = code * scale[f : f + 1]
            copy = pltpu.make_async_copy(row_ref.at[f], out_ref.at[0, first + f], sems.at[f])
            copy.start()
            copies.append(copy)
        for copy in copies:
            copy.wait()


def fast_on_device(u_now, u_prev, coef_store, store_map, new_owner):
    blocks, _, fields, depth, width = u_now.shape
    now = u_now.reshape(blocks, fields, depth, width)
    prev = u_prev.reshape(blocks, fields, depth, width)
    coef = coef_store[0, 0]
    count = lax.axis_size("blk")
    order = store_map.reshape(-1)
    owner_hbm, order_hbm, now_hbm, prev_hbm, coef_hbm = (
        pltpu.with_memory_space_constraint(array, pltpu.HBM) for array in (new_owner, order, now, prev, coef)
    )
    params = pltpu.CompilerParams(vmem_limit_bytes=48 * 1024 * 1024)

    def call(body, name, out_shape, in_specs, out_specs, scratch, args, **options):
        return pl.pallas_call(
            body,
            out_shape=out_shape,
            in_specs=in_specs,
            out_specs=out_specs,
            scratch_shapes=scratch,
            compiler_params=params,
            name=name,
            **options,
        )(*args)

    straight = jax.ShapeDtypeStruct((fields * depth + 16, LANES), BF16)
    diag = jax.ShapeDtypeStruct((depth + 32, LANES), BF16)
    y_out, edges = call(
        pack_region_body,
        "pack_region",
        (jax.ShapeDtypeStruct((5, depth, width), BF16), jax.ShapeDtypeStruct((depth, width), F32)),
        [HBM] * 4,
        (VMEM, VMEM),
        [
            pltpu.VMEM((depth, width), F32),
            pltpu.VMEM((blocks, fields, 8, width), F32),
            pltpu.VMEM((blocks, fields, 8, width), F32),
            pltpu.VMEM((4, 16, width), BF16),
            pltpu.SMEM(order.shape, jnp.int32),
            pltpu.SemaphoreType.DMA((5,)),
        ],
        (order_hbm, now_hbm, prev_hbm, coef_hbm),
    )
    left, right, dleft, dright = call(
        pack_ring_body,
        "pack_ring",
        (straight, straight, diag, diag),
        [HBM] * 5 + [VMEM],
        (VMEM,) * 4,
        [
            pltpu.VMEM((2, fields, depth, LANES), F32),
            pltpu.VMEM((2, fields, depth, LANES), F32),
            pltpu.VMEM((2, 2, 4, depth, LANES), BF16),
            pltpu.SMEM(new_owner.shape, jnp.int32),
            pltpu.SMEM(order.shape, jnp.int32),
            pltpu.SemaphoreType.DMA((8,)),
        ],
        (owner_hbm, order_hbm, now_hbm, prev_hbm, coef_hbm, edges),
    )

    swap = [(0, 1), (1, 0)]
    forward = [(i, (i + 1) % count) for i in range(count)]
    backward = [(i, (i - 1) % count) for i in range(count)]

    def crossed(by):
        return [(r * count + i, (1 - r) * count + (i + by) % count) for r in range(2) for i in range(count)]

    y_in = lax.ppermute(y_out, "region", swap)
    from_right = lax.ppermute(left, "blk", backward)
    from_dright = lax.ppermute(dleft, ("region", "blk"), crossed(-1))
    from_left = lax.ppermute(right, "blk", forward)
    from_dleft = lax.ppermute(dright, ("region", "blk"), crossed(1))

    box, rim = call(
        local_body,
        "local",
        (jax.ShapeDtypeStruct(now.shape, F32), jax.ShapeDtypeStruct((blocks, 8, width), F32)),
        [VMEM],
        (VMEM, VMEM),
        [],
        (now,),
    )
    half = fields // 2
    part = jax.ShapeDtypeStruct((half, depth, width), F32)
    codes = jax.ShapeDtypeStruct((half * depth + 8, width), jnp.int16)
    sums = jax.ShapeDtypeStruct((8, width + 2 * LANES), F32)
    powers = pltpu.VMEM((8, width), F32)
    last_a, code_a, near, stepped = call(
        last_row_a_body,
        "last_row_a",
        (part, codes, sums, sums),
        [SMEM] + [VMEM] * 8,
        (VMEM,) * 4,
        [powers],
        (order, now, prev, coef, y_in, from_right, from_dright, box, rim),
    )
    arrived_a = lax.ppermute(code_a, "blk", forward)
    last_b, code_b = call(
        last_row_b_body,
        "last_row_b",
        (part, codes),
        [SMEM] + [VMEM] * 9 + [ANY] * 2,
        (VMEM,) * 2,
        [powers],
        (order, now, prev, coef, y_in, from_right, from_dright, box, near, stepped, from_left, from_dleft),
    )
    arrived_b = lax.ppermute(code_b, "blk", forward)
    whole = jax.ShapeDtypeStruct((blocks + 1, fields, depth, width), F32)
    result = call(
        first_row_body,
        "first_row",
        whole,
        [SMEM] * 2 + [VMEM] * 10,
        VMEM,
        [pltpu.VMEM((8, width + 2 * LANES), F32)] * 2,
        (new_owner, order, now, prev, coef, y_in, from_left, from_dleft, box, rim, last_a, last_b),
    )
    for first, arrived in ((0, arrived_a), (half, arrived_b)):
        result = call(
            functools.partial(place_body, first),
            "place",
            whole,
            [VMEM, VMEM, ANY],
            ANY,
            [pltpu.VMEM((half, depth, width), F32), pltpu.SemaphoreType.DMA((half,))],
            (from_left, arrived, result),
            input_output_aliases={2: 0},
        )
    return result[:, None]


def solution(mesh):
    def on_device(*args):
        blocks = args[0].shape[0]
        if lax.axis_size("region") == 2 and blocks == 2:
            return fast_on_device(*args)
        return general_on_device(*args)

    return jax.shard_map(
        on_device,
        mesh=mesh,
        in_specs=(
            P("blk", "region", None, None, None),
            P("blk", "region", None, None, None),
            P("blk", "region", None, None, None, None),
            P("blk", "region", None),
            P("blk"),
        ),
        out_specs=P("blk", "region", None, None, None),
        check_vma=False,
    )
```

```python
import functools

import jax
import jax.numpy as jnp
from jax import lax
from jax.experimental import pallas as pl
from jax.experimental.pallas import tpu as pltpu
from jax.sharding import PartitionSpec as P

STEPS = 2
LANES = 128
F32 = jnp.float32
BF16 = jnp.bfloat16
VMEM = pl.BlockSpec(memory_space=pltpu.VMEM)
SMEM = pl.BlockSpec(memory_space=pltpu.SMEM)
ANY = pl.BlockSpec(memory_space=pl.ANY)
HBM = pl.BlockSpec(memory_space=pltpu.HBM)


def extended_2(block, sides, width, periodic):
    for axis, dim in sides:
        count = lax.axis_size(axis)
        forward = [(i, i + 1) for i in range(count - 1)]
        if periodic:
            forward.append((count - 1, 0))
        backward = [(target, source) for source, target in forward]
        low = lax.ppermute(
            lax.slice_in_dim(block, block.shape[dim] - width, None, axis=dim), axis, forward
        )
        high = lax.ppermute(lax.slice_in_dim(block, 0, width, axis=dim), axis, backward)
        block = jnp.concatenate([low, block, high], axis=dim)
    return block


def shifted_2(value, axis, by):
    devices = lax.axis_size(axis)
    return lax.ppermute(value, axis, [(i, (i + by) % devices) for i in range(devices)])


def stencil_step(state_now, state_prev, coefficient, live_count):
    slot_count, field_count, edge_cells, plane_cells = state_now.shape
    padded = extended_2(state_now, (("region", 2),), 1, False)
    first_planes = padded[..., :edge_cells]
    last_planes = padded[..., plane_cells - edge_cells :]
    last_live = jnp.take(last_planes, live_count - 1, axis=0)
    rim_pair = jnp.stack([first_planes[0], last_live], axis=2)
    spread = extended_2(rim_pair.astype(jnp.bfloat16), (("blk", 2),), 1, True).astype(
        rim_pair.dtype
    )
    left_rim = spread[:, :, 0]
    right_rim = spread[:, :, 3]
    before_planes = jnp.concatenate([left_rim[None], last_planes[:-1]], axis=0)
    after_planes = jnp.pad(first_planes[1:], ((0, 1), (0, 0), (0, 0), (0, 0)))
    slot_ids = jnp.arange(slot_count)
    after_planes = jnp.where(
        (slot_ids == live_count - 1)[:, None, None, None], right_rim[None], after_planes
    )
    extended = jnp.concatenate([before_planes, padded, after_planes], axis=-1)
    width = extended.shape[-1]
    column = jnp.arange(width) % edge_cells
    lower_mask = (column != 0).astype(jnp.float32)
    upper_mask = (column != edge_cells - 1).astype(jnp.float32)
    margin = ((0, 0), (0, 0), (0, 0), (1, 1))
    shifted = jnp.pad(extended, margin)
    summed = shifted[..., :width] * lower_mask + extended + shifted[..., 2:] * upper_mask
    summed = (
        summed[..., : -2 * edge_cells]
        + summed[..., edge_cells:-edge_cells]
        + summed[..., 2 * edge_cells :]
    )
    box_sum = summed[:, :, :-2] + summed[:, :, 1:-1] + summed[:, :, 2:]
    laplace = box_sum - 27.0 * state_now
    return 2.0 * state_now - state_prev + coefficient.astype(jnp.float32) * laplace


def compact(members, valid_flags):
    slot_count = valid_flags.shape[0]
    place_index = jnp.cumsum(valid_flags) - 1
    target = jnp.arange(slot_count)
    chooser = (valid_flags[None, :] == 1) & (place_index[None, :] == target[:, None])
    source = jnp.sum(jnp.where(chooser, target[None, :], 0), axis=1)
    filled = jnp.sum(chooser.astype(jnp.int32), axis=1) > 0
    placed = tuple(
        (
            jnp.where(
                filled.reshape((slot_count,) + (1,) * (member.ndim - 1)),
                jnp.take(member, source, axis=0),
                jnp.zeros_like(member),
            )
            for member in members
        )
    )
    return (placed, jnp.sum(valid_flags))


def general_on_device(u_now, u_prev, coef_store, store_map, new_owner):
    state_now = u_now[:, 0]
    state_prev = u_prev[:, 0]
    blocks, fields, edge_cells, plane_cells = state_now.shape
    store_local = coef_store[0, 0]
    arrived = lax.all_to_all(store_local, "region", split_axis=0, concat_axis=0, tiled=True)
    flattened = arrived.reshape((-1,) + arrived.shape[2:])
    inverse = jnp.argsort(store_map[0, 0])
    coefficient = jnp.take(flattened, inverse, axis=0).reshape(
        blocks, fields, edge_cells, plane_cells
    )
    own_index = lax.axis_index("blk")
    goes_right = new_owner[blocks - 1] != own_index
    mark_right = goes_right.astype(jnp.float32).reshape(1)
    middle_flags = jnp.ones((blocks - 2,), jnp.int32)
    keep_first = (new_owner[0] == own_index).astype(jnp.int32).reshape(1)
    keep_last = (new_owner[blocks - 1] == own_index).astype(jnp.int32).reshape(1)
    for step_index in range(STEPS):
        state_now, state_prev = (
            stencil_step(state_now, state_prev, coefficient, blocks),
            state_now,
        )
    from_left = shifted_2((state_now[blocks - 1], mark_right), "blk", 1)
    valid_flags = jnp.concatenate(
        [(from_left[1] > 0.5).astype(jnp.int32), keep_first, middle_flags, keep_last]
    )
    stacked_now = jnp.concatenate([from_left[0][None], state_now], axis=0)
    placed, live_count = compact((stacked_now,), valid_flags)
    result = placed[0]
    return result[:, None]


def lane_ids():
    return lax.broadcasted_iota(jnp.int32, (1, LANES), 1)


def edge_start(lower, depth, size):
    return pl.multiple_of(jnp.where(lower, depth - size, 0), size)


def tag_values(map_ref, region):
    numbers = [map_ref[region * 4 + s] for s in range(4)] + [map_ref[(1 - region) * 4 + s] for s in range(4)]
    return [jnp.zeros((1, LANES), F32) + number.astype(F32) for number in numbers]


def pack_slab_body(coef_ref, slab_ref, sem):
    copy = pltpu.make_async_copy(coef_ref.at[1 - lax.axis_index("region")], slab_ref, sem)
    copy.start()
    copy.wait()


def pack_edges_body(
    owner_hbm, map_hbm, u_ref, p_ref, coef_ref, y_ref, left_ref, right_ref, dleft_ref, dright_ref,
    rows_ref, ue_ref, pe_ref, ce_ref, ua_ref, pa_ref, ca_ref, owner_ref, map_ref, sems
):
    fields = u_ref.shape[1]
    depth = u_ref.shape[2]
    last = u_ref.shape[3] - LANES
    top = depth - 1
    region = lax.axis_index("region")
    lower = region == 0
    other = 1 - region
    edge8 = edge_start(lower, depth, 8)
    edge16 = edge_start(lower, depth, 16)
    copies = [
        pltpu.make_async_copy(map_hbm, map_ref, sems.at[0]),
        pltpu.make_async_copy(u_ref.at[:, :, pl.ds(edge8, 8), :], ue_ref, sems.at[1]),
        pltpu.make_async_copy(p_ref.at[:, :, pl.ds(edge8, 8), :], pe_ref, sems.at[2]),
        pltpu.make_async_copy(coef_ref.at[region, :, pl.ds(edge16, 16), :], ce_ref, sems.at[3]),
        pltpu.make_async_copy(owner_hbm, owner_ref, sems.at[4]),
        pltpu.make_async_copy(u_ref.at[0, :, :, 0:LANES], ua_ref.at[0], sems.at[5]),
        pltpu.make_async_copy(u_ref.at[1, :, :, last : last + LANES], ua_ref.at[1], sems.at[6]),
        pltpu.make_async_copy(p_ref.at[0, :, :, 0:LANES], pa_ref.at[0], sems.at[7]),
        pltpu.make_async_copy(p_ref.at[1, :, :, last : last + LANES], pa_ref.at[1], sems.at[8]),
        pltpu.make_async_copy(coef_ref.at[:, :, :, 0:LANES], ca_ref.at[0], sems.at[9]),
        pltpu.make_async_copy(coef_ref.at[:, :, :, last : last + LANES], ca_ref.at[1], sems.at[10]),
    ]
    for copy in copies:
        copy.start()
    for copy in copies[:4]:
        copy.wait()
    lane = lane_ids()
    own_edge = jnp.where(lower, 7, 0)
    own_next = jnp.where(lower, 6, 1)
    for m in range(2):
        for f in range(fields):
            at = m * fields + f
            near = ue_ref[m, f, pl.ds(own_edge, 1), :]
            rows_ref[at : at + 1, :] = near
            rows_ref[8 + at : 9 + at, :] = ue_ref[m, f, pl.ds(own_next, 1), :]
            rows_ref[16 + at : 17 + at, :] = 2.0 * near - pe_ref[m, f, pl.ds(own_edge, 1), :]
    for s in range(4):
        piece = ce_ref[s].astype(F32)
        rows_ref[24 + s : 25 + s, :] = jnp.where(lower, piece[15:16], piece[0:1])
    tag_rows = tag_values(map_ref, region)
    for i, row in enumerate(tag_rows):
        rows_ref[28:29, i * LANES : (i + 1) * LANES] = row
    rows_ref[29:32, :] = jnp.zeros((3, rows_ref.shape[1]), F32)
    y_ref[...] = rows_ref[...].astype(BF16)
    for copy in copies[4:]:
        copy.wait()
    blank = jnp.zeros((1, LANES), F32)
    flag = blank + jnp.where(owner_ref[1] != lax.axis_index("blk"), 1.0, 0.0).astype(F32)
    for m, lanes, straight_ref, diag_ref in (
        (0, slice(0, LANES), left_ref, dleft_ref),
        (1, slice(last, last + LANES), right_ref, dright_ref),
    ):
        for f in range(fields):
            now = ua_ref[m, f]
            ahead = 2.0 * now - pa_ref[m, f]
            piece = ca_ref[m, region, f].astype(F32)
            if m == 0:
                tile = jnp.where(
                    lane < 64, now, jnp.where(lane < 96, pltpu.roll(ahead, 64, 1), pltpu.roll(piece, 96, 1))
                )
            else:
                tile = jnp.where(
                    lane >= 64, now, jnp.where(lane < 32, pltpu.roll(ahead, 32, 1), pltpu.roll(piece, 64, 1))
                )
            straight_ref[f * depth : (f + 1) * depth, :] = tile.astype(BF16)
        far = [ca_ref[m, other, s].astype(F32) for s in range(4)]
        extra = [jnp.where(lower, piece[0:1], piece[top:depth]) for piece in far] + tag_rows + [flag] + [blank] * 3
        straight_ref[fields * depth : fields * depth + 16, :] = jnp.concatenate(extra, axis=0).astype(BF16)
        plane = jnp.zeros((depth, LANES), F32)
        for s in range(4):
            shift = (32 * s if m == 0 else 32 + 32 * s) % LANES
            moved = pltpu.roll(far[s], shift, 1) if shift else far[s]
            plane = jnp.where((lane >= 32 * s) & (lane < 32 * s + 32), moved, plane)
        diag_ref[0:depth, :] = plane.astype(BF16)
        extra = (
            [rows_ref[m * fields : m * fields + 4, lanes]]
            + [rows_ref[8 + m * fields : 12 + m * fields, lanes]]
            + [rows_ref[16 + m * fields : 20 + m * fields, lanes]]
            + [rows_ref[24:28, lanes]]
            + tag_rows
            + [blank] * 8
        )
        diag_ref[depth : depth + 32, :] = jnp.concatenate(extra, axis=0).astype(BF16)
        rest = diag_ref.shape[0] - depth - 32
        diag_ref[depth + 32 :, :] = jnp.zeros((rest, LANES), BF16)


def nine_sum(tiles, lane, first=0):
    inside = lane % 32
    low = inside != 0
    high = inside != 31
    rows = []
    for tile in tiles:
        rows.append(
            tile
            + jnp.where(low, pltpu.roll(tile, 1, 1), 0.0)
            + jnp.where(high, pltpu.roll(tile, LANES - 1, 1), 0.0)
        )
    up = [pltpu.roll(row, 32, 1) for row in rows]
    down = [pltpu.roll(row, LANES - 32, 1) for row in rows]
    count = len(tiles)
    result = []
    for t in range(count):
        before = up[t] if t == 0 else jnp.where(lane < 32, up[t - 1], up[t])
        after = down[t] if t == count - 1 else jnp.where(lane >= 96, down[t + 1], down[t])
        result.append(rows[t] + before + after)
    return result


def column_sum(tile, row_id, low_row, high_row):
    depth = tile.shape[0]
    above = pltpu.roll(tile, 1, 0)
    below = pltpu.roll(tile, depth - 1, 0)
    return tile + jnp.where(row_id == 0, low_row, above) + jnp.where(row_id == depth - 1, high_row, below)


def local_body(u_ref, p_ref, box0_ref, box1_ref, drift_ref, rim_ref):
    fields, depth, width = u_ref.shape[1:]
    main = width // LANES
    lower = lax.axis_index("region") == 0
    lane = lane_ids()
    row_id = lax.broadcasted_iota(jnp.int32, (depth, 1), 0)
    boxes = (box0_ref, box1_ref)
    for f in range(fields):
        now = [u_ref[m, f, :, tile_at(t)] for m in range(2) for t in range(main)]
        sums = nine_sum(now, lane)
        for i, (tile, total) in enumerate(zip(now, sums)):
            m, t = divmod(i, main)
            lanes = tile_at(t)
            rim_ref[m, f : f + 1, lanes] = jnp.where(lower, total[depth - 1 : depth], total[0:1])
            boxes[m][f, :, lanes] = column_sum(total, row_id, 0.0, 0.0) - 27.0 * tile
            drift_ref[m, f, :, lanes] = 2.0 * tile - p_ref[m, f, :, lanes]
    rim_ref[:, 4:8, :] = jnp.zeros((2, 4, width), F32)


def tile_at(t):
    return slice(t * LANES, (t + 1) * LANES)


def with_sides(m, local, remote, middle):
    return [local] + middle + [remote] if m == 1 else [remote] + middle + [local]


def edge_body(
    m, u_ref, coef_ref, y_ref, straight_ref, diag_ref, beside_ref, rim_ref, box_in, box_ref, lap_ref, side_ref, stepped_ref
):
    fields, depth, width = u_ref.shape[1:]
    main = width // LANES
    region = lax.axis_index("region")
    lower = region == 0
    lane = lane_ids()
    row_id = lax.broadcasted_iota(jnp.int32, (depth, 1), 0)
    beside = 1 - m
    local_lanes = slice(width - LANES, width) if m == 1 else slice(0, LANES)
    border = main - 1 if m == 1 else 0
    side = main + 1 if m == 1 else 0
    facing = lane >= 96 if m == 1 else lane < 32
    halo_base = 0 if m == 1 else fields
    extra_s = straight_ref[fields * depth : fields * depth + 16, :].astype(F32)
    extra_d = diag_ref[depth : depth + 32, :].astype(F32)
    extra_y = y_ref[...].astype(F32)
    tags_s = [extra_s[4 + i : 5 + i] for i in range(8)]
    tags_d = [extra_d[16 + i : 17 + i] for i in range(8)]
    tags_y = [extra_y[28:29, i * LANES : (i + 1) * LANES] for i in range(8)]
    field_id = lax.broadcasted_iota(jnp.int32, (4, LANES), 0).astype(F32)

    planes = []
    for s in range(4):
        tile = straight_ref[s * depth : (s + 1) * depth, :].astype(F32)
        planes.append(pltpu.roll(tile, 32 if m == 1 else 64, 1))
    diag_tile = diag_ref[0:depth, :].astype(F32)
    for s in range(4):
        shift = (-32 * s if m == 1 else 96 - 32 * s) % LANES
        planes.append(pltpu.roll(diag_tile, shift, 1) if shift else diag_tile)

    def edge_tiles(base_y, base_d):
        middle = [extra_y[base_y + m * fields : base_y + m * fields + 4, tile_at(t)] for t in range(main)]
        local = extra_y[base_y + beside * fields : base_y + beside * fields + 4, local_lanes]
        return with_sides(m, local, extra_d[base_d : base_d + 4], middle)

    near = edge_tiles(0, 0)
    beyond = edge_tiles(8, 4)
    ahead = edge_tiles(16, 8)

    def other_row(s, lanes):
        piece = coef_ref[1 - region, s, :, lanes].astype(F32)
        return jnp.where(lower, piece[0:1], piece[depth - 1 : depth])

    def edge_coef(lanes, base):
        total = jnp.zeros((4, LANES), F32)
        for s in range(4):
            total = total + jnp.where(tags_y[s] == field_id + base, extra_y[24 + s : 25 + s, lanes], 0.0)
            total = total + jnp.where(tags_y[4 + s] == field_id + base, other_row(s, lanes), 0.0)
        return total

    corner = jnp.zeros((4, LANES), F32)
    for s in range(4):
        corner = corner + jnp.where(tags_d[s] == field_id + halo_base, extra_d[12 + s : 13 + s], 0.0)
        corner = corner + jnp.where(tags_d[4 + s] == field_id + halo_base, extra_s[s : s + 1], 0.0)
    edge_c = with_sides(
        m, edge_coef(local_lanes, beside * fields), corner, [edge_coef(tile_at(t), m * fields) for t in range(main)]
    )
    near_sum = nine_sum(near, lane)
    beyond_sum = nine_sum(beyond, lane)

    def rows(t, f):
        row = near_sum[t][f : f + 1]
        return jnp.where(lower, 0.0, row), jnp.where(lower, row, 0.0)

    own, outer = [], []
    for f in range(fields):
        inner = u_ref[m, f, :, tile_at(border)]
        remote = straight_ref[f * depth : (f + 1) * depth, :].astype(F32)
        sums = nine_sum(with_sides(m, remote, remote, [inner])[1:] if m == 1 else [remote, inner], lane)
        inner_sum, remote_sum = (sums[0], sums[1]) if m == 1 else (sums[1], sums[0])
        own.append(jnp.where(lower, inner_sum[depth - 1 : depth], inner_sum[0:1]))
        outer.append(jnp.where(lower, remote_sum[depth - 1 : depth], remote_sum[0:1]))
        halo_c = jnp.zeros((depth, LANES), F32)
        for i in range(8):
            halo_c = halo_c + jnp.where(tags_s[i] == F32(halo_base + f), planes[i], 0.0)
        low_row, high_row = rows(side, f)
        lap = column_sum(remote_sum, row_id, low_row, high_row) - 27.0 * remote
        side_ref[f] = pltpu.roll(remote, 64 if m == 1 else 96, 1) + halo_c * lap
        for t in range(main):
            low_row, high_row = rows(t + 1, f)
            if t == border:
                box = box_in[f, :, tile_at(t)]
                box = box + jnp.where(row_id == 0, low_row, 0.0) + jnp.where(row_id == depth - 1, high_row, 0.0)
                whole = column_sum(inner_sum, row_id, low_row, high_row) - 27.0 * inner
                box_ref[f, :, tile_at(t)] = jnp.where(facing, whole, box)
            else:
                box_ref[f, 0:1, tile_at(t)] = box_in[f, 0:1, tile_at(t)] + low_row
                box_ref[f, depth - 1 : depth, tile_at(t)] = box_in[f, depth - 1 : depth, tile_at(t)] + high_row
        lap = beside_ref[f, :, local_lanes]
        if m == 1:
            low_row, high_row = rows(0, f)
            lap = lap + jnp.where(row_id == 0, low_row, 0.0) + jnp.where(row_id == depth - 1, high_row, 0.0)
        lap_ref[f] = lap
    rims = with_sides(
        m,
        rim_ref[beside, 0:4, local_lanes],
        jnp.concatenate(outer, axis=0),
        [rim_ref[m, 0:4, tile_at(t)] for t in range(main)],
    )
    rims[border + 1] = jnp.where(facing, jnp.concatenate(own, axis=0), rims[border + 1])
    stepped = []
    for t in range(main + 2):
        box = near_sum[t] + beyond_sum[t] + rims[t]
        stepped.append(ahead[t] + edge_c[t] * (box - 27.0 * near[t]))
    stepped_sum = nine_sum(stepped, lane)
    for t in range(main + 2):
        stepped_ref[0:4, tile_at(t)] = stepped_sum[t]
    stepped_ref[4:8, :] = jnp.zeros((4, width + 2 * LANES), F32)


def steps(m, some, map_ref, u_ref, coef_ref, slab_ref, box_ref, drift_ref, lap_ref, side_ref, stepped_ref, write):
    fields, depth, width = u_ref.shape[1:]
    main = width // LANES
    region = lax.axis_index("region")
    lower = region == 0
    lane = lane_ids()
    row_id = lax.broadcasted_iota(jnp.int32, (depth, 1), 0)
    beside = 1 - m
    local_lanes = slice(width - LANES, width) if m == 1 else slice(0, LANES)
    numbers = [map_ref[q] for q in range(8)]

    def piece_of(number):
        place = jnp.int32(0)
        for q in range(8):
            place = jnp.where(numbers[q] == number, q, place)
        slot = place & 3
        held = (place >> 2) == region

        def tile(lanes):
            return jnp.where(held, coef_ref[region, slot, :, lanes], slab_ref[slot, :, lanes]).astype(F32)

        return tile

    for f in some:
        coef = piece_of(m * fields + f)
        coefs = [coef(tile_at(t)) for t in range(main)]
        local = drift_ref[beside, f, :, local_lanes] + piece_of(beside * fields + f)(local_lanes) * lap_ref[f]
        middle = [drift_ref[m, f, :, tile_at(t)] + coefs[t] * box_ref[f, :, tile_at(t)] for t in range(main)]
        now = with_sides(m, local, side_ref[f], middle)
        sums = nine_sum(now, lane)
        for t in range(main):
            row = stepped_ref[f : f + 1, tile_at(t + 1)]
            low_row, high_row = jnp.where(lower, 0.0, row), jnp.where(lower, row, 0.0)
            lap = column_sum(sums[t + 1], row_id, low_row, high_row) - 27.0 * middle[t]
            write(f, tile_at(t), 2.0 * middle[t] - u_ref[m, f, :, tile_at(t)] + coefs[t] * lap)


CODES = 32000.0


def code_writer(row_ref, code_ref, power_ref, first, count, depth):
    def write(f, lanes, value):
        at = f - first
        row_ref[at, :, lanes] = value
        size = jnp.maximum(jnp.max(jnp.abs(value), axis=0, keepdims=True), 1e-30)
        power = jnp.ceil(jnp.log2(size))
        code = jnp.floor(value * (CODES * jnp.exp2(-power)) + 0.5)
        code_ref[at * depth : (at + 1) * depth, lanes] = code.astype(jnp.int32).astype(jnp.int16)
        power_ref[at : at + 1, lanes] = power

    return write


def write_powers(power_ref, code_ref, count, depth):
    power_ref[count:8, :] = jnp.zeros((8 - count, power_ref.shape[1]), F32)
    code_ref[count * depth : count * depth + 8, :] = power_ref[...].astype(jnp.int32).astype(jnp.int16)


def last_row_body(
    first, map_ref, u_ref, coef_ref, slab_ref, box_ref, drift_ref, lap_ref, side_ref, stepped_ref, *rest
):
    row_ref, code_ref, power_ref = rest[-3:]
    count, depth, _ = row_ref.shape
    write = code_writer(row_ref, code_ref, power_ref, first, count, depth)
    some = range(first, first + count)
    steps(1, some, map_ref, u_ref, coef_ref, slab_ref, box_ref, drift_ref, lap_ref, side_ref, stepped_ref, write)
    write_powers(power_ref, code_ref, count, depth)


def first_row_body(
    owner_ref, map_ref, u_ref, coef_ref, slab_ref, box_ref, drift_ref, lap_ref, side_ref, stepped_ref, straight_ref,
    last_a_ref, last_b_ref, out_ref
):
    fields, depth = u_ref.shape[1:3]
    extra = straight_ref[fields * depth : fields * depth + 16, :].astype(F32)
    arrives = extra[12:13] > 0.5
    keeps = owner_ref[1] == lax.axis_index("blk")
    half = last_a_ref.shape[0]

    def write(f, lanes, value):
        mine = last_a_ref[f, :, lanes] if f < half else last_b_ref[f - half, :, lanes]
        kept = jnp.where(keeps, mine, 0.0)
        out_ref[0, f, :, lanes] = value
        out_ref[1, f, :, lanes] = jnp.where(arrives, value, kept)
        out_ref[2, f, :, lanes] = jnp.where(arrives, kept, 0.0)

    some = range(fields)
    steps(0, some, map_ref, u_ref, coef_ref, slab_ref, box_ref, drift_ref, lap_ref, side_ref, stepped_ref, write)


def place_body(first, straight_ref, code_ref, partial_ref, out_ref, row_ref, sems):
    count, depth, width = row_ref.shape
    rows = straight_ref.shape[0]
    flag = jnp.max(straight_ref[rows - 16 : rows, :].astype(F32)[12:13])

    @pl.when(flag > 0.5)
    def _():
        scale = jnp.exp2(code_ref[count * depth : count * depth + 8, :].astype(jnp.int32).astype(F32)) * (1.0 / CODES)
        copies = []
        for f in range(count):
            code = code_ref[f * depth : (f + 1) * depth, :].astype(jnp.int32).astype(F32)
            row_ref[f] = code * scale[f : f + 1]
            copy = pltpu.make_async_copy(row_ref.at[f], out_ref.at[0, first + f], sems.at[f])
            copy.start()
            copies.append(copy)
        for copy in copies:
            copy.wait()


def fast_on_device(u_now, u_prev, coef_store, store_map, new_owner):
    blocks, _, fields, depth, width = u_now.shape
    now = u_now.reshape(blocks, fields, depth, width)
    prev = u_prev.reshape(blocks, fields, depth, width)
    coef = coef_store[0, 0]
    count = lax.axis_size("blk")
    order = store_map.reshape(-1)
    owner_hbm, order_hbm, now_hbm, prev_hbm, coef_hbm = (
        pltpu.with_memory_space_constraint(array, pltpu.HBM) for array in (new_owner, order, now, prev, coef)
    )
    params = pltpu.CompilerParams(vmem_limit_bytes=48 * 1024 * 1024)

    def call(body, name, out_shape, in_specs, out_specs, scratch, args, **options):
        return pl.pallas_call(
            body,
            out_shape=out_shape,
            in_specs=in_specs,
            out_specs=out_specs,
            scratch_shapes=scratch,
            compiler_params=params,
            name=name,
            **options,
        )(*args)

    slab_shape = jax.ShapeDtypeStruct(coef.shape[1:], BF16)
    slab_out = call(pack_slab_body, "pack_slab", slab_shape, [HBM], VMEM, [pltpu.SemaphoreType.DMA], (coef_hbm,))
    message = jax.ShapeDtypeStruct((fields * depth + 16, LANES), BF16)
    y_out, left, right, dleft, dright = call(
        pack_edges_body,
        "pack_edges",
        (jax.ShapeDtypeStruct((depth, width), BF16),) + (message,) * 4,
        [HBM] * 5,
        (VMEM,) * 5,
        [
            pltpu.VMEM((depth, width), F32),
            pltpu.VMEM((blocks, fields, 8, width), F32),
            pltpu.VMEM((blocks, fields, 8, width), F32),
            pltpu.VMEM((4, 16, width), BF16),
            pltpu.VMEM((2, fields, depth, LANES), F32),
            pltpu.VMEM((2, fields, depth, LANES), F32),
            pltpu.VMEM((2, 2, 4, depth, LANES), BF16),
            pltpu.SMEM(new_owner.shape, jnp.int32),
            pltpu.SMEM(order.shape, jnp.int32),
            pltpu.SemaphoreType.DMA((11,)),
        ],
        (owner_hbm, order_hbm, now_hbm, prev_hbm, coef_hbm),
    )

    swap = [(0, 1), (1, 0)]
    forward = [(i, (i + 1) % count) for i in range(count)]
    backward = [(i, (i - 1) % count) for i in range(count)]

    def crossed(by):
        return [(r * count + i, (1 - r) * count + (i + by) % count) for r in range(2) for i in range(count)]

    slab = lax.ppermute(slab_out, "region", swap)
    y_in = lax.ppermute(y_out, "region", swap)
    from_right = lax.ppermute(left, "blk", backward)
    from_dright = lax.ppermute(dleft, ("region", "blk"), crossed(-1))
    from_left = lax.ppermute(right, "blk", forward)
    from_dleft = lax.ppermute(dright, ("region", "blk"), crossed(1))

    row = jax.ShapeDtypeStruct((fields, depth, width), F32)
    box0, box1, drift, rim = call(
        local_body,
        "local",
        (row, row, jax.ShapeDtypeStruct(now.shape, F32), jax.ShapeDtypeStruct((blocks, 8, width), F32)),
        [VMEM] * 2,
        (VMEM,) * 4,
        [],
        (now, prev),
    )
    tiles = jax.ShapeDtypeStruct((fields, depth, LANES), F32)
    edge_outs = (row, tiles, tiles, jax.ShapeDtypeStruct((8, width + 2 * LANES), F32))

    def edges(m, straight, diag, beside, own):
        return call(
            functools.partial(edge_body, m),
            "edges",
            edge_outs,
            [VMEM] * 8,
            (VMEM,) * 4,
            [],
            (now, coef, y_in, straight, diag, beside, rim, own),
            input_output_aliases={7: 0},
        )

    half = fields // 2
    part = jax.ShapeDtypeStruct((half, depth, width), F32)
    codes = jax.ShapeDtypeStruct((half * depth + 8, width), jnp.int16)

    def last_row(first, *early):
        return call(
            functools.partial(last_row_body, first),
            "last_row",
            (part, codes),
            [SMEM] + [VMEM] * 8 + [ANY] * len(early),
            (VMEM,) * 2,
            [pltpu.VMEM((8, width), F32)],
            (order, now, coef, slab, box1, drift, lap1, side1, stepped1) + early,
        )

    box1, lap1, side1, stepped1 = edges(1, from_right, from_dright, box0, box1)
    last_a, code_a = last_row(0)
    arrived_a = lax.ppermute(code_a, "blk", forward)
    last_b, code_b = last_row(half, from_left, from_dleft)
    arrived_b = lax.ppermute(code_b, "blk", forward)
    box0, lap0, side0, stepped0 = edges(0, from_left, from_dleft, box1, box0)
    whole = jax.ShapeDtypeStruct((blocks + 1, fields, depth, width), F32)
    result = call(
        first_row_body,
        "first_row",
        whole,
        [SMEM] * 2 + [VMEM] * 11,
        VMEM,
        [],
        (new_owner, order, now, coef, slab, box0, drift, lap0, side0, stepped0, from_left, last_a, last_b),
    )
    for first, arrived in ((0, arrived_a), (half, arrived_b)):
        result = call(
            functools.partial(place_body, first),
            "place",
            whole,
            [VMEM, VMEM, ANY],
            ANY,
            [pltpu.VMEM((half, depth, width), F32), pltpu.SemaphoreType.DMA((half,))],
            (from_left, arrived, result),
            input_output_aliases={2: 0},
        )
    return result[:, None]


def solution(mesh):
    def on_device(*args):
        blocks = args[0].shape[0]
        if lax.axis_size("region") == 2 and blocks == 2:
            return fast_on_device(*args)
        return general_on_device(*args)

    return jax.shard_map(
        on_device,
        mesh=mesh,
        in_specs=(
            P("blk", "region", None, None, None),
            P("blk", "region", None, None, None),
            P("blk", "region", None, None, None, None),
            P("blk", "region", None),
            P("blk"),
        ),
        out_specs=P("blk", "region", None, None, None),
        check_vma=False,
    )
```

```python
import functools

import jax
import jax.numpy as jnp
from jax import lax
from jax.experimental import pallas as pl
from jax.experimental.pallas import tpu as pltpu
from jax.sharding import PartitionSpec as P

STEPS = 2
LANES = 128
F32 = jnp.float32
BF16 = jnp.bfloat16
VMEM = pl.BlockSpec(memory_space=pltpu.VMEM)
SMEM = pl.BlockSpec(memory_space=pltpu.SMEM)
ANY = pl.BlockSpec(memory_space=pl.ANY)
HBM = pl.BlockSpec(memory_space=pltpu.HBM)


def extended_2(block, sides, width, periodic):
    for axis, dim in sides:
        count = lax.axis_size(axis)
        forward = [(i, i + 1) for i in range(count - 1)]
        if periodic:
            forward.append((count - 1, 0))
        backward = [(target, source) for source, target in forward]
        low = lax.ppermute(
            lax.slice_in_dim(block, block.shape[dim] - width, None, axis=dim), axis, forward
        )
        high = lax.ppermute(lax.slice_in_dim(block, 0, width, axis=dim), axis, backward)
        block = jnp.concatenate([low, block, high], axis=dim)
    return block


def shifted_2(value, axis, by):
    devices = lax.axis_size(axis)
    return lax.ppermute(value, axis, [(i, (i + by) % devices) for i in range(devices)])


def stencil_step(state_now, state_prev, coefficient, live_count):
    slot_count, field_count, edge_cells, plane_cells = state_now.shape
    padded = extended_2(state_now, (("region", 2),), 1, False)
    first_planes = padded[..., :edge_cells]
    last_planes = padded[..., plane_cells - edge_cells :]
    last_live = jnp.take(last_planes, live_count - 1, axis=0)
    rim_pair = jnp.stack([first_planes[0], last_live], axis=2)
    spread = extended_2(rim_pair.astype(jnp.bfloat16), (("blk", 2),), 1, True).astype(
        rim_pair.dtype
    )
    left_rim = spread[:, :, 0]
    right_rim = spread[:, :, 3]
    before_planes = jnp.concatenate([left_rim[None], last_planes[:-1]], axis=0)
    after_planes = jnp.pad(first_planes[1:], ((0, 1), (0, 0), (0, 0), (0, 0)))
    slot_ids = jnp.arange(slot_count)
    after_planes = jnp.where(
        (slot_ids == live_count - 1)[:, None, None, None], right_rim[None], after_planes
    )
    extended = jnp.concatenate([before_planes, padded, after_planes], axis=-1)
    width = extended.shape[-1]
    column = jnp.arange(width) % edge_cells
    lower_mask = (column != 0).astype(jnp.float32)
    upper_mask = (column != edge_cells - 1).astype(jnp.float32)
    margin = ((0, 0), (0, 0), (0, 0), (1, 1))
    shifted = jnp.pad(extended, margin)
    summed = shifted[..., :width] * lower_mask + extended + shifted[..., 2:] * upper_mask
    summed = (
        summed[..., : -2 * edge_cells]
        + summed[..., edge_cells:-edge_cells]
        + summed[..., 2 * edge_cells :]
    )
    box_sum = summed[:, :, :-2] + summed[:, :, 1:-1] + summed[:, :, 2:]
    laplace = box_sum - 27.0 * state_now
    return 2.0 * state_now - state_prev + coefficient.astype(jnp.float32) * laplace


def compact(members, valid_flags):
    slot_count = valid_flags.shape[0]
    place_index = jnp.cumsum(valid_flags) - 1
    target = jnp.arange(slot_count)
    chooser = (valid_flags[None, :] == 1) & (place_index[None, :] == target[:, None])
    source = jnp.sum(jnp.where(chooser, target[None, :], 0), axis=1)
    filled = jnp.sum(chooser.astype(jnp.int32), axis=1) > 0
    placed = tuple(
        (
            jnp.where(
                filled.reshape((slot_count,) + (1,) * (member.ndim - 1)),
                jnp.take(member, source, axis=0),
                jnp.zeros_like(member),
            )
            for member in members
        )
    )
    return (placed, jnp.sum(valid_flags))


def general_on_device(u_now, u_prev, coef_store, store_map, new_owner):
    state_now = u_now[:, 0]
    state_prev = u_prev[:, 0]
    blocks, fields, edge_cells, plane_cells = state_now.shape
    store_local = coef_store[0, 0]
    arrived = lax.all_to_all(store_local, "region", split_axis=0, concat_axis=0, tiled=True)
    flattened = arrived.reshape((-1,) + arrived.shape[2:])
    inverse = jnp.argsort(store_map[0, 0])
    coefficient = jnp.take(flattened, inverse, axis=0).reshape(
        blocks, fields, edge_cells, plane_cells
    )
    own_index = lax.axis_index("blk")
    goes_right = new_owner[blocks - 1] != own_index
    mark_right = goes_right.astype(jnp.float32).reshape(1)
    middle_flags = jnp.ones((blocks - 2,), jnp.int32)
    keep_first = (new_owner[0] == own_index).astype(jnp.int32).reshape(1)
    keep_last = (new_owner[blocks - 1] == own_index).astype(jnp.int32).reshape(1)
    for step_index in range(STEPS):
        state_now, state_prev = (
            stencil_step(state_now, state_prev, coefficient, blocks),
            state_now,
        )
    from_left = shifted_2((state_now[blocks - 1], mark_right), "blk", 1)
    valid_flags = jnp.concatenate(
        [(from_left[1] > 0.5).astype(jnp.int32), keep_first, middle_flags, keep_last]
    )
    stacked_now = jnp.concatenate([from_left[0][None], state_now], axis=0)
    placed, live_count = compact((stacked_now,), valid_flags)
    result = placed[0]
    return result[:, None]


def lane_ids():
    return lax.broadcasted_iota(jnp.int32, (1, LANES), 1)


def edge_start(lower, depth, size):
    return pl.multiple_of(jnp.where(lower, depth - size, 0), size)


def tag_values(map_ref, region):
    numbers = [map_ref[region * 4 + s] for s in range(4)] + [map_ref[(1 - region) * 4 + s] for s in range(4)]
    return [jnp.zeros((1, LANES), F32) + number.astype(F32) for number in numbers]


def pack_slab_body(coef_ref, slab_ref, sems):
    other = 1 - lax.axis_index("region")
    half = coef_ref.shape[2] // 2
    copies = []
    for s in range(4):
        for h in range(2):
            part = slice(h * half, (h + 1) * half)
            copies.append(
                pltpu.make_async_copy(coef_ref.at[other, s, part], slab_ref.at[s, part], sems.at[2 * s + h])
            )
    for copy in copies:
        copy.start()
    for copy in copies:
        copy.wait()


def pack_edges_body(
    map_hbm, u_ref, p_ref, coef_ref, y_ref, straight_ref, diag_ref,
    rows_ref, ue_ref, pe_ref, ce_ref, ua_ref, pa_ref, ca_ref, map_ref, sems
):
    fields = u_ref.shape[1]
    depth = u_ref.shape[2]
    top = depth - 1
    region = lax.axis_index("region")
    lower = region == 0
    other = 1 - region
    edge8 = edge_start(lower, depth, 8)
    edge16 = edge_start(lower, depth, 16)
    copies = [
        pltpu.make_async_copy(map_hbm, map_ref, sems.at[0]),
        pltpu.make_async_copy(u_ref.at[:, :, pl.ds(edge8, 8), :], ue_ref, sems.at[1]),
        pltpu.make_async_copy(p_ref.at[:, :, pl.ds(edge8, 8), :], pe_ref, sems.at[2]),
        pltpu.make_async_copy(coef_ref.at[region, :, pl.ds(edge16, 16), :], ce_ref, sems.at[3]),
        pltpu.make_async_copy(u_ref.at[0, :, :, 0:LANES], ua_ref, sems.at[4]),
        pltpu.make_async_copy(p_ref.at[0, :, :, 0:LANES], pa_ref, sems.at[5]),
        pltpu.make_async_copy(coef_ref.at[:, :, :, 0:LANES], ca_ref, sems.at[6]),
    ]
    for copy in copies:
        copy.start()
    for copy in copies[:4]:
        copy.wait()
    lane = lane_ids()
    own_edge = jnp.where(lower, 7, 0)
    own_next = jnp.where(lower, 6, 1)
    for m in range(2):
        for f in range(fields):
            at = m * fields + f
            near = ue_ref[m, f, pl.ds(own_edge, 1), :]
            rows_ref[at : at + 1, :] = near
            rows_ref[8 + at : 9 + at, :] = ue_ref[m, f, pl.ds(own_next, 1), :]
            rows_ref[16 + at : 17 + at, :] = 2.0 * near - pe_ref[m, f, pl.ds(own_edge, 1), :]
    for s in range(4):
        piece = ce_ref[s].astype(F32)
        rows_ref[24 + s : 25 + s, :] = jnp.where(lower, piece[15:16], piece[0:1])
    tag_rows = tag_values(map_ref, region)
    for i, row in enumerate(tag_rows):
        rows_ref[28:29, i * LANES : (i + 1) * LANES] = row
    rows_ref[29:32, :] = jnp.zeros((3, rows_ref.shape[1]), F32)
    y_ref[...] = rows_ref[...].astype(BF16)
    for copy in copies[4:]:
        copy.wait()
    blank = jnp.zeros((1, LANES), F32)
    for f in range(fields):
        now = ua_ref[f]
        ahead = 2.0 * now - pa_ref[f]
        piece = ca_ref[region, f].astype(F32)
        tile = jnp.where(
            lane < 64, now, jnp.where(lane < 96, pltpu.roll(ahead, 64, 1), pltpu.roll(piece, 96, 1))
        )
        straight_ref[f * depth : (f + 1) * depth, :] = tile.astype(BF16)
    far = [ca_ref[other, s].astype(F32) for s in range(4)]
    extra = [jnp.where(lower, piece[0:1], piece[top:depth]) for piece in far] + tag_rows + [blank] * 4
    straight_ref[fields * depth : fields * depth + 16, :] = jnp.concatenate(extra, axis=0).astype(BF16)
    plane = jnp.zeros((depth, LANES), F32)
    for s in range(4):
        moved = pltpu.roll(far[s], 32 * s, 1) if s else far[s]
        plane = jnp.where((lane >= 32 * s) & (lane < 32 * s + 32), moved, plane)
    diag_ref[0:depth, :] = plane.astype(BF16)
    edges = [rows_ref[base : base + 4, 0:LANES] for base in (0, 8, 16, 24)]
    extra = edges + tag_rows + [blank] * 8
    diag_ref[depth : depth + 32, :] = jnp.concatenate(extra, axis=0).astype(BF16)


def nine_sum(tiles, lane, first=0):
    inside = lane % 32
    low = inside != 0
    high = inside != 31
    rows = []
    for tile in tiles:
        rows.append(
            tile
            + jnp.where(low, pltpu.roll(tile, 1, 1), 0.0)
            + jnp.where(high, pltpu.roll(tile, LANES - 1, 1), 0.0)
        )
    up = [pltpu.roll(row, 32, 1) for row in rows]
    down = [pltpu.roll(row, LANES - 32, 1) for row in rows]
    count = len(tiles)
    result = []
    for t in range(count):
        before = up[t] if t == 0 else jnp.where(lane < 32, up[t - 1], up[t])
        after = down[t] if t == count - 1 else jnp.where(lane >= 96, down[t + 1], down[t])
        result.append(rows[t] + before + after)
    return result


def column_sum(tile, row_id, low_row, high_row):
    depth = tile.shape[0]
    above = pltpu.roll(tile, 1, 0)
    below = pltpu.roll(tile, depth - 1, 0)
    return tile + jnp.where(row_id == 0, low_row, above) + jnp.where(row_id == depth - 1, high_row, below)


def local_body(u_ref, p_ref, box0_ref, box1_ref, drift_ref, rim_ref):
    fields, depth, width = u_ref.shape[1:]
    main = width // LANES
    lower = lax.axis_index("region") == 0
    lane = lane_ids()
    row_id = lax.broadcasted_iota(jnp.int32, (depth, 1), 0)
    boxes = (box0_ref, box1_ref)
    for f in range(fields):
        now = [u_ref[m, f, :, tile_at(t)] for m in range(2) for t in range(main)]
        sums = nine_sum(now, lane)
        for i, (tile, total) in enumerate(zip(now, sums)):
            m, t = divmod(i, main)
            lanes = tile_at(t)
            rim_ref[m, f : f + 1, lanes] = jnp.where(lower, total[depth - 1 : depth], total[0:1])
            boxes[m][f, :, lanes] = column_sum(total, row_id, 0.0, 0.0) - 27.0 * tile
            drift_ref[m, f, :, lanes] = 2.0 * tile - p_ref[m, f, :, lanes]
    rim_ref[:, 4:8, :] = jnp.zeros((2, 4, width), F32)


def tile_at(t):
    return slice(t * LANES, (t + 1) * LANES)


class ColumnEdge:
    def __init__(self, coef_ref, y_ref):
        self.region = lax.axis_index("region")
        self.lower = self.region == 0
        self.coef = coef_ref
        self.depth = coef_ref.shape[2]
        self.extra = y_ref[...].astype(F32)
        self.tags = [self.extra[28:29, i * LANES : (i + 1) * LANES] for i in range(8)]
        self.field_id = lax.broadcasted_iota(jnp.int32, (4, LANES), 0).astype(F32)

    def near(self, m, lanes):
        return self.extra[4 * m : 4 * m + 4, lanes]

    def beyond(self, m, lanes):
        return self.extra[8 + 4 * m : 12 + 4 * m, lanes]

    def ahead(self, m, lanes):
        return self.extra[16 + 4 * m : 20 + 4 * m, lanes]

    def coefs(self, m, lanes):
        total = jnp.zeros((4, LANES), F32)
        for s in range(4):
            piece = self.coef[1 - self.region, s, :, lanes].astype(F32)
            held = jnp.where(self.lower, piece[0:1], piece[self.depth - 1 : self.depth])
            total = total + jnp.where(self.tags[s] == self.field_id + 4 * m, self.extra[24 + s : 25 + s, lanes], 0.0)
            total = total + jnp.where(self.tags[4 + s] == self.field_id + 4 * m, held, 0.0)
        return total

    def own(self, tile):
        return jnp.where(self.lower, tile[self.depth - 1 : self.depth], tile[0:1])

    def rows(self, row):
        return jnp.where(self.lower, 0.0, row), jnp.where(self.lower, row, 0.0)


def last_edges_body(
    u_ref, coef_ref, y_ref, straight_ref, diag_ref, box0_ref, rim_ref, box_in, box_ref, lap_ref, side_ref, sums_ref, tail_ref
):
    fields, depth, width = u_ref.shape[1:]
    main = width // LANES
    lane = lane_ids()
    row_id = lax.broadcasted_iota(jnp.int32, (depth, 1), 0)
    column = ColumnEdge(coef_ref, y_ref)
    before = slice(width - LANES, width)
    facing = lane >= 96
    extra_s = straight_ref[fields * depth : fields * depth + 16, :].astype(F32)
    extra_d = diag_ref[depth : depth + 32, :].astype(F32)
    tags_s = [extra_s[4 + i : 5 + i] for i in range(8)]
    tags_d = [extra_d[16 + i : 17 + i] for i in range(8)]

    planes = []
    for s in range(4):
        planes.append(pltpu.roll(straight_ref[s * depth : (s + 1) * depth, :].astype(F32), 32, 1))
    diag_tile = diag_ref[0:depth, :].astype(F32)
    for s in range(4):
        planes.append(pltpu.roll(diag_tile, LANES - 32 * s, 1) if s else diag_tile)

    def edge_tiles(of, base):
        return [of(0, before)] + [of(1, tile_at(t)) for t in range(main)] + [extra_d[base : base + 4]]

    near = edge_tiles(column.near, 0)
    beyond = edge_tiles(column.beyond, 4)
    ahead = edge_tiles(column.ahead, 8)
    corner = jnp.zeros((4, LANES), F32)
    for s in range(4):
        corner = corner + jnp.where(tags_d[s] == column.field_id, extra_d[12 + s : 13 + s], 0.0)
        corner = corner + jnp.where(tags_d[4 + s] == column.field_id, extra_s[s : s + 1], 0.0)
    edge_c = [column.coefs(0, before)] + [column.coefs(1, tile_at(t)) for t in range(main)] + [corner]
    near_sum = nine_sum(near, lane)
    beyond_sum = nine_sum(beyond, lane)

    own, outer = [], []
    for f in range(fields):
        inner = u_ref[1, f, :, tile_at(main - 1)]
        remote = straight_ref[f * depth : (f + 1) * depth, :].astype(F32)
        inner_sum, remote_sum = nine_sum([inner, remote], lane)
        own.append(column.own(inner_sum))
        outer.append(column.own(remote_sum))
        halo_c = jnp.zeros((depth, LANES), F32)
        for i in range(8):
            halo_c = halo_c + jnp.where(tags_s[i] == F32(f), planes[i], 0.0)
        low_row, high_row = column.rows(near_sum[main + 1][f : f + 1])
        lap = column_sum(remote_sum, row_id, low_row, high_row) - 27.0 * remote
        side_ref[f] = pltpu.roll(remote, 64, 1) + halo_c * lap
        for t in range(main):
            low_row, high_row = column.rows(near_sum[t + 1][f : f + 1])
            lanes = tile_at(t)
            if t == main - 1:
                box = box_in[f, :, lanes]
                box = box + jnp.where(row_id == 0, low_row, 0.0) + jnp.where(row_id == depth - 1, high_row, 0.0)
                whole = column_sum(inner_sum, row_id, low_row, high_row) - 27.0 * inner
                box_ref[f, :, lanes] = jnp.where(facing, whole, box)
            else:
                box_ref[f, 0:1, lanes] = box_in[f, 0:1, lanes] + low_row
                box_ref[f, depth - 1 : depth, lanes] = box_in[f, depth - 1 : depth, lanes] + high_row
        low_row, high_row = column.rows(near_sum[0][f : f + 1])
        lap = box0_ref[f, :, before]
        lap_ref[f] = lap + jnp.where(row_id == 0, low_row, 0.0) + jnp.where(row_id == depth - 1, high_row, 0.0)
    rims = [rim_ref[0, 0:4, before]] + [rim_ref[1, 0:4, tile_at(t)] for t in range(main)]
    rims.append(jnp.concatenate(outer, axis=0))
    rims[main] = jnp.where(facing, jnp.concatenate(own, axis=0), rims[main])
    stepped = []
    for t in range(main + 2):
        box = near_sum[t] + beyond_sum[t] + rims[t]
        stepped.append(ahead[t] + edge_c[t] * (box - 27.0 * near[t]))
    stepped_sum = nine_sum(stepped, lane)
    for t in range(main):
        sums_ref[0:4, tile_at(t)] = stepped_sum[t + 1]
    sums_ref[4:8, :] = jnp.zeros((4, width), F32)
    tail_ref[0:4, :] = stepped[main]
    tail_ref[4:8, :] = jnp.zeros((4, LANES), F32)


def first_edges_body(
    u_ref, coef_ref, y_ref, box1_ref, rim_ref, box_in, box_ref, sums_ref, tail_ref
):
    fields, depth, width = u_ref.shape[1:]
    main = width // LANES
    lane = lane_ids()
    column = ColumnEdge(coef_ref, y_ref)
    after = slice(0, LANES)

    def edge_tiles(of):
        return [of(0, tile_at(t)) for t in range(main)] + [of(1, after)]

    near = edge_tiles(column.near)
    near_sum = nine_sum(near, lane)
    beyond_sum = nine_sum(edge_tiles(column.beyond), lane)
    ahead = edge_tiles(column.ahead)
    edge_c = edge_tiles(column.coefs)
    for f in range(fields):
        for t in range(main):
            low_row, high_row = column.rows(near_sum[t][f : f + 1])
            lanes = tile_at(t)
            box_ref[f, 0:1, lanes] = box_in[f, 0:1, lanes] + low_row
            box_ref[f, depth - 1 : depth, lanes] = box_in[f, depth - 1 : depth, lanes] + high_row
    rims = [rim_ref[0, 0:4, tile_at(t)] for t in range(main)] + [rim_ref[1, 0:4, after]]
    stepped = []
    for t in range(main + 1):
        box = near_sum[t] + beyond_sum[t] + rims[t]
        stepped.append(ahead[t] + edge_c[t] * (box - 27.0 * near[t]))
    stepped_sum = nine_sum(stepped, lane)
    for t in range(main):
        sums_ref[0:4, tile_at(t)] = stepped_sum[t]
    sums_ref[4:8, :] = jnp.zeros((4, width), F32)
    tail_ref[0:4, :] = stepped[1]
    tail_ref[4:8, :] = jnp.zeros((4, LANES), F32)


class Pieces:
    def __init__(self, map_ref, coef_ref, slab_ref):
        self.coef, self.slab = coef_ref, slab_ref
        self.region = lax.axis_index("region")
        self.numbers = [map_ref[q] for q in range(8)]

    def piece(self, number):
        place = jnp.int32(0)
        for q in range(8):
            place = jnp.where(self.numbers[q] == number, q, place)
        slot = place & 3
        held = (place >> 2) == self.region

        def tile(lanes):
            return jnp.where(held, self.coef[self.region, slot, :, lanes], self.slab[slot, :, lanes]).astype(F32)

        return tile


def second_step(now, before, total, coef, row_id, row, lower):
    low_row, high_row = jnp.where(lower, 0.0, row), jnp.where(lower, row, 0.0)
    lap = column_sum(total, row_id, low_row, high_row) - 27.0 * now
    return 2.0 * now - before + coef * lap


CODES = 32000.0


def power_of(size):
    return jnp.ceil(jnp.log2(jnp.maximum(size, 1e-30)))


def coded(value, power):
    return jnp.floor(value * (CODES * jnp.exp2(-power)) + 0.5)


def narrow(value):
    return value.astype(jnp.int32).astype(jnp.int16)


def wide(code):
    return code.astype(jnp.int32).astype(F32)


def scale_of(power):
    return jnp.exp2(power) * (1.0 / CODES)


def last_row_body(
    first, map_ref, u_ref, coef_ref, slab_ref, box_ref, drift_ref, lap_ref, side_ref, sums_ref, *rest
):
    if first == 0:
        owner_ref, y_ref, tail_ref, row_ref, code_ref, power_ref, extra_ref = rest
    else:
        row_ref, code_ref, power_ref = rest
    count, depth, width = row_ref.shape
    fields = u_ref.shape[1]
    main = width // LANES
    lane = lane_ids()
    row_id = lax.broadcasted_iota(jnp.int32, (depth, 1), 0)
    pieces = Pieces(map_ref, coef_ref, slab_ref)
    lower = pieces.region == 0
    before = slice(width - LANES, width)
    base = count * depth
    last_tiles = []
    for f in range(first, first + count):
        coef = pieces.piece(fields + f)
        coefs = [coef(tile_at(t)) for t in range(main)]
        middle = [drift_ref[1, f, :, tile_at(t)] + coefs[t] * box_ref[f, :, tile_at(t)] for t in range(main)]
        local = drift_ref[0, f, :, before] + pieces.piece(f)(before) * lap_ref[f]
        sums = nine_sum([local] + middle + [side_ref[f]], lane)
        at = f - first
        for t in range(main):
            lanes = tile_at(t)
            row = sums_ref[f : f + 1, lanes]
            value = second_step(middle[t], u_ref[1, f, :, lanes], sums[t + 1], coefs[t], row_id, row, lower)
            row_ref[at, :, lanes] = value
            power = power_of(jnp.max(jnp.abs(value), axis=0, keepdims=True))
            code_ref[at * depth : (at + 1) * depth, lanes] = narrow(coded(value, power))
            power_ref[at : at + 1, lanes] = power
        last_tiles.append(middle[main - 1])
    power_ref[count:8, :] = jnp.zeros((8 - count, width), F32)
    code_ref[base : base + 8, :] = narrow(power_ref[...])
    if first == 0:
        near = y_ref[0:16, before].astype(F32)
        extra_ref[2:3, :] = jnp.zeros((1, width), F32) + jnp.where(owner_ref[1] != lax.axis_index("blk"), 1.0, 0.0)
        extra_ref[3:8, :] = jnp.zeros((5, width), F32)
        for f in range(fields):
            if f < count:
                stepped = last_tiles[f]
            else:
                stepped = drift_ref[1, f, :, before] + pieces.piece(fields + f)(before) * box_ref[f, :, before]
            both = jnp.where(lane >= 96, u_ref[1, f, :, before], pltpu.roll(stepped, 96, 1))
            rows = [near[4 + f : 5 + f], near[12 + f : 13 + f], tail_ref[f : f + 1, :]]
            size = jnp.max(jnp.abs(both), axis=0, keepdims=True)
            for row in rows:
                size = jnp.maximum(size, jnp.abs(row))
            power = power_of(size)
            codes = narrow(coded(both, power))
            here, there = tile_at(f), tile_at(fields + f)
            code_ref[base + 8 : base + 8 + depth // 2, here] = codes[0 : depth // 2]
            code_ref[base + 8 : base + 8 + depth // 2, there] = codes[depth // 2 : depth]
            extra_ref[0:1, here] = power
            extra_ref[0:1, there] = coded(rows[0], power)
            extra_ref[1:2, here] = coded(rows[1], power)
            extra_ref[1:2, there] = coded(rows[2], power)
        code_ref[base + 8 + depth // 2 : base + 16 + depth // 2, :] = narrow(extra_ref[...])


def first_row_body(map_ref, u_ref, coef_ref, slab_ref, box_ref, box1_ref, drift_ref, sums_ref, row_ref):
    fields, depth, width = u_ref.shape[1:]
    main = width // LANES
    lane = lane_ids()
    row_id = lax.broadcasted_iota(jnp.int32, (depth, 1), 0)
    pieces = Pieces(map_ref, coef_ref, slab_ref)
    lower = pieces.region == 0
    after = slice(0, LANES)
    for f in range(fields):
        coef = pieces.piece(f)
        coefs = [coef(tile_at(t)) for t in range(main)]
        now = [drift_ref[0, f, :, tile_at(t)] + coefs[t] * box_ref[f, :, tile_at(t)] for t in range(main)]
        local = drift_ref[1, f, :, after] + pieces.piece(fields + f)(after) * box1_ref[f, :, after]
        sums = nine_sum(now + [local], lane)
        for t in range(1, main):
            lanes = tile_at(t)
            row = sums_ref[f : f + 1, lanes]
            row_ref[f, :, lanes] = second_step(now[t], u_ref[0, f, :, lanes], sums[t], coefs[t], row_id, row, lower)


def arrival(code_ref):
    rows = code_ref.shape[0]
    return jnp.max(wide(code_ref[rows - 8 : rows, :])[2:3]) > 0.5


def place_codes(code_ref, first, count, depth, row_ref, out_ref, sems, base):
    scale = scale_of(wide(code_ref[count * depth : count * depth + 8, :]))
    part = depth // 2
    copies = []
    for f in range(count):
        for h in range(2):
            rows = slice(h * part, (h + 1) * part)
            start = f * depth + h * part
            row_ref[f, rows] = wide(code_ref[start : start + part, :]) * scale[f : f + 1]
            sem = sems.at[base + 2 * f + h]
            copies.append(pltpu.make_async_copy(row_ref.at[f, rows], out_ref.at[0, first + f, rows], sem))
            copies[-1].start()
    return copies


def finish_body(
    owner_ref, map_ref, u_ref, coef_ref, slab_ref, y_ref, box_ref, drift_ref, tail_ref, code_ref, row_ref,
    last_a_ref, last_b_ref, out_ref, tile_ref, zero_ref, arrived_ref, sems
):
    fields, depth, width = u_ref.shape[1:]
    half = last_a_ref.shape[0]
    base = half * depth
    lane = lane_ids()
    row_id = lax.broadcasted_iota(jnp.int32, (depth, 1), 0)
    arrives = arrival(code_ref)
    slot = jnp.where(arrives, 1, 0)
    keeps = owner_ref[1] == lax.axis_index("blk")

    def row_copies(at, sources, base):
        return [
            pltpu.make_async_copy(source, out_ref.at[at, f], sems.at[base + f]) for f, source in enumerate(sources)
        ]

    mine = [last_a_ref.at[f] for f in range(half)] + [last_b_ref.at[f] for f in range(fields - half)]
    kept = row_copies(slot + 1, mine, 0)
    blank = row_copies(slot + 1, [zero_ref] * fields, 0)
    third = row_copies(2, [zero_ref] * fields, fields)
    rest = slice(LANES, width)
    firsts = [
        pltpu.make_async_copy(row_ref.at[f, :, rest], out_ref.at[slot, f, :, rest], sems.at[2 * fields + f])
        for f in range(fields)
    ]
    for copy in firsts:
        copy.start()

    @pl.when(keeps)
    def _():
        for copy in kept:
            copy.start()

    zero_ref[...] = jnp.zeros(zero_ref.shape, F32)

    @pl.when(jnp.logical_not(keeps))
    def _():
        for copy in blank:
            copy.start()

    @pl.when(jnp.logical_not(arrives))
    def _():
        for copy in third:
            copy.start()

    column = ColumnEdge(coef_ref, y_ref)
    pieces = Pieces(map_ref, coef_ref, slab_ref)
    extra = wide(code_ref[base + 8 + depth // 2 : base + 16 + depth // 2, :])
    tile0, tile1 = tile_at(0), tile_at(1)
    near = column.near(0, tile0)
    corners = [[], [], []]
    rims, before, stepped, nexts, coefs = [], [], [], [], []
    for f in range(fields):
        here, there = tile_at(f), tile_at(fields + f)
        scale = scale_of(extra[0:1, here])
        corners[0].append(extra[0:1, there] * scale)
        corners[1].append(extra[1:2, here] * scale)
        corners[2].append(extra[1:2, there] * scale)
        upper = wide(code_ref[base + 8 : base + 8 + depth // 2, here])
        under = wide(code_ref[base + 8 : base + 8 + depth // 2, there])
        before.append(jnp.concatenate([upper, under], axis=0) * scale)
    corners = [jnp.concatenate(rows, axis=0) for rows in corners]
    near_sum = nine_sum([corners[0], near, column.near(0, tile1)], lane)[1]
    beyond_sum = nine_sum([corners[1], column.beyond(0, tile0), column.beyond(0, tile1)], lane)[1]
    for f in range(fields):
        now = u_ref[0, f, :, tile0]
        total = nine_sum([before[f], now, u_ref[0, f, :, tile1]], lane)[1]
        rims.append(column.own(total))
        low_row, high_row = column.rows(near_sum[f : f + 1])
        lap = column_sum(total, row_id, low_row, high_row) - 27.0 * now
        coef = pieces.piece(f)
        coefs.append(coef(tile0))
        stepped.append(drift_ref[0, f, :, tile0] + coefs[f] * lap)
        nexts.append(drift_ref[0, f, :, tile1] + coef(tile1) * box_ref[f, :, tile1])
    box = near_sum + beyond_sum + jnp.concatenate(rims, axis=0)
    edge = column.ahead(0, tile0) + column.coefs(0, tile0) * (box - 27.0 * near)
    edge_sum = nine_sum([corners[2], edge, tail_ref[0:4, :]], lane)[1]
    for f in range(fields):
        total = nine_sum([pltpu.roll(before[f], 32, 1), stepped[f], nexts[f]], lane)[1]
        row = edge_sum[f : f + 1]
        tile_ref[f] = second_step(stepped[f], u_ref[0, f, :, tile0], total, coefs[f], row_id, row, column.lower)
    last = pltpu.make_async_copy(tile_ref, out_ref.at[slot, :, :, tile0], sems.at[3 * fields])
    last.start()

    @pl.when(arrives)
    def _():
        for copy in place_codes(code_ref, 0, half, depth, arrived_ref, out_ref, sems, 3 * fields + 1):
            copy.wait()

    @pl.when(keeps)
    def _():
        for copy in kept:
            copy.wait()

    @pl.when(jnp.logical_not(keeps))
    def _():
        for copy in blank:
            copy.wait()

    @pl.when(jnp.logical_not(arrives))
    def _():
        for copy in third:
            copy.wait()

    for copy in firsts:
        copy.wait()
    last.wait()


def place_body(first, code_a_ref, code_ref, partial_ref, out_ref, row_ref, sems):
    count, depth, _ = row_ref.shape

    @pl.when(arrival(code_a_ref))
    def _():
        for copy in place_codes(code_ref, first, count, depth, row_ref, out_ref, sems, 0):
            copy.wait()


def fast_on_device(u_now, u_prev, coef_store, store_map, new_owner):
    blocks, _, fields, depth, width = u_now.shape
    now = u_now.reshape(blocks, fields, depth, width)
    prev = u_prev.reshape(blocks, fields, depth, width)
    coef = coef_store[0, 0]
    count = lax.axis_size("blk")
    order = store_map.reshape(-1)
    owner_hbm, order_hbm, now_hbm, prev_hbm, coef_hbm = (
        pltpu.with_memory_space_constraint(array, pltpu.HBM) for array in (new_owner, order, now, prev, coef)
    )
    params = pltpu.CompilerParams(vmem_limit_bytes=48 * 1024 * 1024)

    def call(body, name, out_shape, in_specs, out_specs, scratch, args, **options):
        return pl.pallas_call(
            body,
            out_shape=out_shape,
            in_specs=in_specs,
            out_specs=out_specs,
            scratch_shapes=scratch,
            compiler_params=params,
            name=name,
            **options,
        )(*args)

    slab_shape = jax.ShapeDtypeStruct(coef.shape[1:], BF16)
    slab_out = call(pack_slab_body, "pack_slab", slab_shape, [HBM], VMEM, [pltpu.SemaphoreType.DMA((8,))], (coef_hbm,))
    straight = jax.ShapeDtypeStruct((fields * depth + 16, LANES), BF16)
    diag = jax.ShapeDtypeStruct((depth + 32, LANES), BF16)
    y_out, left, dleft = call(
        pack_edges_body,
        "pack_edges",
        (jax.ShapeDtypeStruct((depth, width), BF16), straight, diag),
        [HBM] * 4,
        (VMEM,) * 3,
        [
            pltpu.VMEM((depth, width), F32),
            pltpu.VMEM((blocks, fields, 8, width), F32),
            pltpu.VMEM((blocks, fields, 8, width), F32),
            pltpu.VMEM((4, 16, width), BF16),
            pltpu.VMEM((fields, depth, LANES), F32),
            pltpu.VMEM((fields, depth, LANES), F32),
            pltpu.VMEM((2, 4, depth, LANES), BF16),
            pltpu.SMEM(order.shape, jnp.int32),
            pltpu.SemaphoreType.DMA((7,)),
        ],
        (order_hbm, now_hbm, prev_hbm, coef_hbm),
    )

    swap = [(0, 1), (1, 0)]
    forward = [(i, (i + 1) % count) for i in range(count)]
    backward = [(i, (i - 1) % count) for i in range(count)]
    crossed = [(r * count + i, (1 - r) * count + (i - 1) % count) for r in range(2) for i in range(count)]
    slab = lax.ppermute(slab_out, "region", swap)
    y_in = lax.ppermute(y_out, "region", swap)
    from_right = lax.ppermute(left, "blk", backward)
    from_dright = lax.ppermute(dleft, ("region", "blk"), crossed)

    row = jax.ShapeDtypeStruct((fields, depth, width), F32)
    box0, box1, drift, rim = call(
        local_body,
        "local",
        (row, row, jax.ShapeDtypeStruct(now.shape, F32), jax.ShapeDtypeStruct((blocks, 8, width), F32)),
        [VMEM] * 2,
        (VMEM,) * 4,
        [],
        (now, prev),
    )
    tiles = jax.ShapeDtypeStruct((fields, depth, LANES), F32)
    sums = jax.ShapeDtypeStruct((8, width), F32)
    tail = jax.ShapeDtypeStruct((8, LANES), F32)
    box1, lap1, side1, sums1, tail1 = call(
        last_edges_body,
        "last_edges",
        (row, tiles, tiles, sums, tail),
        [VMEM] * 8,
        (VMEM,) * 5,
        [],
        (now, coef, y_in, from_right, from_dright, box0, rim, box1),
        input_output_aliases={7: 0},
    )
    half = fields // 2
    part = jax.ShapeDtypeStruct((half, depth, width), F32)
    codes = jax.ShapeDtypeStruct((half * depth + 8, width), jnp.int16)
    more_codes = jax.ShapeDtypeStruct((half * depth + depth // 2 + 16, width), jnp.int16)
    stepping = (order, now, coef, slab, box1, drift, lap1, side1, sums1)
    powers = pltpu.VMEM((8, width), F32)
    last_a, code_a = call(
        functools.partial(last_row_body, 0),
        "last_row",
        (part, more_codes),
        [SMEM] + [VMEM] * 8 + [SMEM] + [VMEM] * 2,
        (VMEM,) * 2,
        [powers, powers],
        stepping + (new_owner, y_in, tail1),
    )
    arrived_a = lax.ppermute(code_a, "blk", forward)
    last_b, code_b = call(
        functools.partial(last_row_body, half), "last_row", (part, codes), [SMEM] + [VMEM] * 8, (VMEM,) * 2, [powers], stepping
    )
    arrived_b = lax.ppermute(code_b, "blk", forward)
    box0, sums0, tail0 = call(
        first_edges_body,
        "first_edges",
        (row, sums, tail),
        [VMEM] * 6,
        (VMEM,) * 3,
        [],
        (now, coef, y_in, box1, rim, box0),
        input_output_aliases={5: 0},
    )
    first = call(
        first_row_body,
        "first_row",
        row,
        [SMEM] + [VMEM] * 7,
        VMEM,
        [],
        (order, now, coef, slab, box0, box1, drift, sums0),
    )
    whole = jax.ShapeDtypeStruct((blocks + 1, fields, depth, width), F32)
    result = call(
        finish_body,
        "finish",
        whole,
        [SMEM] * 2 + [VMEM] * 11,
        ANY,
        [
            pltpu.VMEM((fields, depth, LANES), F32),
            pltpu.VMEM((depth, width), F32),
            pltpu.VMEM((half, depth, width), F32),
            pltpu.SemaphoreType.DMA((3 * fields + 1 + 2 * half,)),
        ],
        (new_owner, order, now, coef, slab, y_in, box0, drift, tail0, arrived_a, first, last_a, last_b),
    )
    result = call(
        functools.partial(place_body, half),
        "place",
        whole,
        [VMEM, VMEM, ANY],
        ANY,
        [pltpu.VMEM((half, depth, width), F32), pltpu.SemaphoreType.DMA((2 * half,))],
        (arrived_a, arrived_b, result),
        input_output_aliases={2: 0},
    )
    return result[:, None]


def solution(mesh):
    def on_device(*args):
        blocks = args[0].shape[0]
        if lax.axis_size("region") == 2 and blocks == 2:
            return fast_on_device(*args)
        return general_on_device(*args)

    return jax.shard_map(
        on_device,
        mesh=mesh,
        in_specs=(
            P("blk", "region", None, None, None),
            P("blk", "region", None, None, None),
            P("blk", "region", None, None, None, None),
            P("blk", "region", None),
            P("blk"),
        ),
        out_specs=P("blk", "region", None, None, None),
        check_vma=False,
    )
```

```python
import functools

import jax
import jax.numpy as jnp
from jax import lax
from jax.experimental import pallas as pl
from jax.experimental.pallas import tpu as pltpu
from jax.sharding import PartitionSpec as P

STEPS = 2
LANES = 128
F32 = jnp.float32
BF16 = jnp.bfloat16
VMEM = pl.BlockSpec(memory_space=pltpu.VMEM)
SMEM = pl.BlockSpec(memory_space=pltpu.SMEM)
ANY = pl.BlockSpec(memory_space=pl.ANY)
HBM = pl.BlockSpec(memory_space=pltpu.HBM)


def extended_2(block, sides, width, periodic):
    for axis, dim in sides:
        count = lax.axis_size(axis)
        forward = [(i, i + 1) for i in range(count - 1)]
        if periodic:
            forward.append((count - 1, 0))
        backward = [(target, source) for source, target in forward]
        low = lax.ppermute(
            lax.slice_in_dim(block, block.shape[dim] - width, None, axis=dim), axis, forward
        )
        high = lax.ppermute(lax.slice_in_dim(block, 0, width, axis=dim), axis, backward)
        block = jnp.concatenate([low, block, high], axis=dim)
    return block


def shifted_2(value, axis, by):
    devices = lax.axis_size(axis)
    return lax.ppermute(value, axis, [(i, (i + by) % devices) for i in range(devices)])


def stencil_step(state_now, state_prev, coefficient, live_count):
    slot_count, field_count, edge_cells, plane_cells = state_now.shape
    padded = extended_2(state_now, (("region", 2),), 1, False)
    first_planes = padded[..., :edge_cells]
    last_planes = padded[..., plane_cells - edge_cells :]
    last_live = jnp.take(last_planes, live_count - 1, axis=0)
    rim_pair = jnp.stack([first_planes[0], last_live], axis=2)
    spread = extended_2(rim_pair.astype(jnp.bfloat16), (("blk", 2),), 1, True).astype(
        rim_pair.dtype
    )
    left_rim = spread[:, :, 0]
    right_rim = spread[:, :, 3]
    before_planes = jnp.concatenate([left_rim[None], last_planes[:-1]], axis=0)
    after_planes = jnp.pad(first_planes[1:], ((0, 1), (0, 0), (0, 0), (0, 0)))
    slot_ids = jnp.arange(slot_count)
    after_planes = jnp.where(
        (slot_ids == live_count - 1)[:, None, None, None], right_rim[None], after_planes
    )
    extended = jnp.concatenate([before_planes, padded, after_planes], axis=-1)
    width = extended.shape[-1]
    column = jnp.arange(width) % edge_cells
    lower_mask = (column != 0).astype(jnp.float32)
    upper_mask = (column != edge_cells - 1).astype(jnp.float32)
    margin = ((0, 0), (0, 0), (0, 0), (1, 1))
    shifted = jnp.pad(extended, margin)
    summed = shifted[..., :width] * lower_mask + extended + shifted[..., 2:] * upper_mask
    summed = (
        summed[..., : -2 * edge_cells]
        + summed[..., edge_cells:-edge_cells]
        + summed[..., 2 * edge_cells :]
    )
    box_sum = summed[:, :, :-2] + summed[:, :, 1:-1] + summed[:, :, 2:]
    laplace = box_sum - 27.0 * state_now
    return 2.0 * state_now - state_prev + coefficient.astype(jnp.float32) * laplace


def compact(members, valid_flags):
    slot_count = valid_flags.shape[0]
    place_index = jnp.cumsum(valid_flags) - 1
    target = jnp.arange(slot_count)
    chooser = (valid_flags[None, :] == 1) & (place_index[None, :] == target[:, None])
    source = jnp.sum(jnp.where(chooser, target[None, :], 0), axis=1)
    filled = jnp.sum(chooser.astype(jnp.int32), axis=1) > 0
    placed = tuple(
        (
            jnp.where(
                filled.reshape((slot_count,) + (1,) * (member.ndim - 1)),
                jnp.take(member, source, axis=0),
                jnp.zeros_like(member),
            )
            for member in members
        )
    )
    return (placed, jnp.sum(valid_flags))


def general_on_device(u_now, u_prev, coef_store, store_map, new_owner):
    state_now = u_now[:, 0]
    state_prev = u_prev[:, 0]
    blocks, fields, edge_cells, plane_cells = state_now.shape
    store_local = coef_store[0, 0]
    arrived = lax.all_to_all(store_local, "region", split_axis=0, concat_axis=0, tiled=True)
    flattened = arrived.reshape((-1,) + arrived.shape[2:])
    inverse = jnp.argsort(store_map[0, 0])
    coefficient = jnp.take(flattened, inverse, axis=0).reshape(
        blocks, fields, edge_cells, plane_cells
    )
    own_index = lax.axis_index("blk")
    goes_right = new_owner[blocks - 1] != own_index
    mark_right = goes_right.astype(jnp.float32).reshape(1)
    middle_flags = jnp.ones((blocks - 2,), jnp.int32)
    keep_first = (new_owner[0] == own_index).astype(jnp.int32).reshape(1)
    keep_last = (new_owner[blocks - 1] == own_index).astype(jnp.int32).reshape(1)
    for step_index in range(STEPS):
        state_now, state_prev = (
            stencil_step(state_now, state_prev, coefficient, blocks),
            state_now,
        )
    from_left = shifted_2((state_now[blocks - 1], mark_right), "blk", 1)
    valid_flags = jnp.concatenate(
        [(from_left[1] > 0.5).astype(jnp.int32), keep_first, middle_flags, keep_last]
    )
    stacked_now = jnp.concatenate([from_left[0][None], state_now], axis=0)
    placed, live_count = compact((stacked_now,), valid_flags)
    result = placed[0]
    return result[:, None]


def lane_ids():
    return lax.broadcasted_iota(jnp.int32, (1, LANES), 1)


def edge_start(lower, depth, size):
    return pl.multiple_of(jnp.where(lower, depth - size, 0), size)


def tag_values(map_ref, region):
    numbers = [map_ref[region * 4 + s] for s in range(4)] + [map_ref[(1 - region) * 4 + s] for s in range(4)]
    return [jnp.zeros((1, LANES), F32) + number.astype(F32) for number in numbers]


def edge_copies(u_ref, p_ref, coef_ref, ue_ref, pe_ref, ce_ref, some, region, sems):
    lower = region == 0
    depth = u_ref.shape[2]
    edge8 = edge_start(lower, depth, 8)
    edge16 = edge_start(lower, depth, 16)
    rows, lanes = some
    return [
        pltpu.make_async_copy(u_ref.at[rows, :, pl.ds(edge8, 8), lanes], ue_ref, sems.at[0]),
        pltpu.make_async_copy(p_ref.at[rows, :, pl.ds(edge8, 8), lanes], pe_ref, sems.at[1]),
        pltpu.make_async_copy(coef_ref.at[region, :, pl.ds(edge16, 16), lanes], ce_ref, sems.at[2]),
    ]


def edge_rows(ue_ref, pe_ref, m, f, lower):
    own_edge = jnp.where(lower, 7, 0)
    own_next = jnp.where(lower, 6, 1)
    near = ue_ref[m, f, pl.ds(own_edge, 1), :]
    return near, ue_ref[m, f, pl.ds(own_next, 1), :], 2.0 * near - pe_ref[m, f, pl.ds(own_edge, 1), :]


def edge_piece(ce_ref, s, lower):
    piece = ce_ref[s].astype(F32)
    return jnp.where(lower, piece[15:16], piece[0:1])


def pack_back_body(
    map_hbm, u_ref, p_ref, coef_ref, straight_ref, diag_ref, ue_ref, pe_ref, ce_ref, ua_ref, pa_ref, ca_ref, map_ref, sems
):
    fields = u_ref.shape[1]
    depth = u_ref.shape[2]
    region = lax.axis_index("region")
    lower = region == 0
    other = 1 - region
    front = slice(0, LANES)
    copies = [
        pltpu.make_async_copy(map_hbm, map_ref, sems.at[3]),
        pltpu.make_async_copy(u_ref.at[0, :, :, front], ua_ref, sems.at[4]),
        pltpu.make_async_copy(p_ref.at[0, :, :, front], pa_ref, sems.at[5]),
        pltpu.make_async_copy(coef_ref.at[:, :, :, front], ca_ref, sems.at[6]),
    ] + edge_copies(u_ref, p_ref, coef_ref, ue_ref, pe_ref, ce_ref, (slice(0, 1), front), region, sems)
    for copy in copies:
        copy.start()
    for copy in copies:
        copy.wait()
    lane = lane_ids()
    tag_rows = tag_values(map_ref, region)
    blank = jnp.zeros((1, LANES), F32)
    for f in range(fields):
        now = ua_ref[f]
        ahead = 2.0 * now - pa_ref[f]
        piece = ca_ref[region, f].astype(F32)
        tile = jnp.where(
            lane < 64, now, jnp.where(lane < 96, pltpu.roll(ahead, 64, 1), pltpu.roll(piece, 96, 1))
        )
        straight_ref[f * depth : (f + 1) * depth, :] = tile.astype(BF16)
    far = [ca_ref[other, s].astype(F32) for s in range(4)]
    extra = [jnp.where(lower, piece[0:1], piece[depth - 1 : depth]) for piece in far] + tag_rows + [blank] * 4
    straight_ref[fields * depth : fields * depth + 16, :] = jnp.concatenate(extra, axis=0).astype(BF16)
    plane = jnp.zeros((depth, LANES), F32)
    for s in range(4):
        moved = pltpu.roll(far[s], 32 * s, 1) if s else far[s]
        plane = jnp.where((lane >= 32 * s) & (lane < 32 * s + 32), moved, plane)
    diag_ref[0:depth, :] = plane.astype(BF16)
    rows = [edge_rows(ue_ref, pe_ref, 0, f, lower) for f in range(fields)]
    extra = [row[kind] for kind in range(3) for row in rows]
    extra += [edge_piece(ce_ref, s, lower) for s in range(4)] + tag_rows + [blank] * 8
    diag_ref[depth : depth + 32, :] = jnp.concatenate(extra, axis=0).astype(BF16)


def pack_region_body(map_hbm, u_ref, p_ref, coef_ref, y_ref, rows_ref, ue_ref, pe_ref, ce_ref, map_ref, sems):
    fields, depth, width = u_ref.shape[1:]
    region = lax.axis_index("region")
    lower = region == 0
    other = 1 - region
    half = depth // 2
    slab = []
    for s in range(4):
        for h in range(2):
            part = slice(h * half, (h + 1) * half)
            slab.append(pltpu.make_async_copy(coef_ref.at[other, s, part], y_ref.at[s, part], sems.at[4 + 2 * s + h]))
    copies = [pltpu.make_async_copy(map_hbm, map_ref, sems.at[3])]
    copies += edge_copies(u_ref, p_ref, coef_ref, ue_ref, pe_ref, ce_ref, (slice(0, 2), slice(0, width)), region, sems)
    for copy in copies + slab:
        copy.start()
    for copy in copies:
        copy.wait()
    for m in range(2):
        for f in range(fields):
            for kind, row in enumerate(edge_rows(ue_ref, pe_ref, m, f, lower)):
                at = 8 * kind + m * fields + f
                rows_ref[at : at + 1, :] = row
    for s in range(4):
        rows_ref[24 + s : 25 + s, :] = edge_piece(ce_ref, s, lower)
    for i, row in enumerate(tag_values(map_ref, region)):
        rows_ref[28:29, i * LANES : (i + 1) * LANES] = row
    rows_ref[29:32, :] = jnp.zeros((3, width), F32)
    y_ref[4] = rows_ref[...].astype(BF16)
    for copy in slab:
        copy.wait()


def nine_sum(tiles, lane, first=0):
    inside = lane % 32
    low = inside != 0
    high = inside != 31
    rows = []
    for tile in tiles:
        rows.append(
            tile
            + jnp.where(low, pltpu.roll(tile, 1, 1), 0.0)
            + jnp.where(high, pltpu.roll(tile, LANES - 1, 1), 0.0)
        )
    up = [pltpu.roll(row, 32, 1) for row in rows]
    down = [pltpu.roll(row, LANES - 32, 1) for row in rows]
    count = len(tiles)
    result = []
    for t in range(count):
        before = up[t] if t == 0 else jnp.where(lane < 32, up[t - 1], up[t])
        after = down[t] if t == count - 1 else jnp.where(lane >= 96, down[t + 1], down[t])
        result.append(rows[t] + before + after)
    return result


def column_sum(tile, row_id, low_row, high_row):
    depth = tile.shape[0]
    above = pltpu.roll(tile, 1, 0)
    below = pltpu.roll(tile, depth - 1, 0)
    return tile + jnp.where(row_id == 0, low_row, above) + jnp.where(row_id == depth - 1, high_row, below)


def local_body(u_ref, p_ref, box0_ref, box1_ref, drift_ref, rim_ref):
    fields, depth, width = u_ref.shape[1:]
    main = width // LANES
    lower = lax.axis_index("region") == 0
    lane = lane_ids()
    row_id = lax.broadcasted_iota(jnp.int32, (depth, 1), 0)
    boxes = (box0_ref, box1_ref)
    for f in range(fields):
        now = [u_ref[m, f, :, tile_at(t)] for m in range(2) for t in range(main)]
        sums = nine_sum(now, lane)
        for i, (tile, total) in enumerate(zip(now, sums)):
            m, t = divmod(i, main)
            lanes = tile_at(t)
            rim_ref[m, f : f + 1, lanes] = jnp.where(lower, total[depth - 1 : depth], total[0:1])
            boxes[m][f, :, lanes] = column_sum(total, row_id, 0.0, 0.0) - 27.0 * tile
            drift_ref[m, f, :, lanes] = 2.0 * tile - p_ref[m, f, :, lanes]
    rim_ref[:, 4:8, :] = jnp.zeros((2, 4, width), F32)


def tile_at(t):
    return slice(t * LANES, (t + 1) * LANES)


class ColumnEdge:
    def __init__(self, coef_ref, y_ref):
        self.region = lax.axis_index("region")
        self.lower = self.region == 0
        self.coef = coef_ref
        self.depth = coef_ref.shape[2]
        self.extra = y_ref[4].astype(F32)
        self.tags = [self.extra[28:29, i * LANES : (i + 1) * LANES] for i in range(8)]
        self.field_id = lax.broadcasted_iota(jnp.int32, (4, LANES), 0).astype(F32)

    def near(self, m, lanes):
        return self.extra[4 * m : 4 * m + 4, lanes]

    def beyond(self, m, lanes):
        return self.extra[8 + 4 * m : 12 + 4 * m, lanes]

    def ahead(self, m, lanes):
        return self.extra[16 + 4 * m : 20 + 4 * m, lanes]

    def coefs(self, m, lanes):
        total = jnp.zeros((4, LANES), F32)
        for s in range(4):
            piece = self.coef[1 - self.region, s, :, lanes].astype(F32)
            held = jnp.where(self.lower, piece[0:1], piece[self.depth - 1 : self.depth])
            total = total + jnp.where(self.tags[s] == self.field_id + 4 * m, self.extra[24 + s : 25 + s, lanes], 0.0)
            total = total + jnp.where(self.tags[4 + s] == self.field_id + 4 * m, held, 0.0)
        return total

    def own(self, tile):
        return jnp.where(self.lower, tile[self.depth - 1 : self.depth], tile[0:1])

    def rows(self, row):
        return jnp.where(self.lower, 0.0, row), jnp.where(self.lower, row, 0.0)


def border_body(u_ref, straight_ref, diag_ref, box_in, box_ref, side_lap_ref, side_coef_ref, rim_ref):
    fields, depth, width = u_ref.shape[1:]
    lane = lane_ids()
    row_id = lax.broadcasted_iota(jnp.int32, (depth, 1), 0)
    lower = lax.axis_index("region") == 0
    before = slice(width - LANES, width)
    facing = lane >= 96
    tags = [straight_ref[fields * depth : fields * depth + 16, :].astype(F32)[4 + i : 5 + i] for i in range(8)]
    planes = []
    for s in range(4):
        planes.append(pltpu.roll(straight_ref[s * depth : (s + 1) * depth, :].astype(F32), 32, 1))
    diag_tile = diag_ref[0:depth, :].astype(F32)
    for s in range(4):
        planes.append(pltpu.roll(diag_tile, LANES - 32 * s, 1) if s else diag_tile)
    for f in range(fields):
        inner = u_ref[1, f, :, before]
        remote = straight_ref[f * depth : (f + 1) * depth, :].astype(F32)
        inner_sum, remote_sum = nine_sum([inner, remote], lane)
        for i, tile in enumerate((inner_sum, remote_sum)):
            rim_ref[i, f : f + 1, :] = jnp.where(lower, tile[depth - 1 : depth], tile[0:1])
        halo_c = jnp.zeros((depth, LANES), F32)
        for i in range(8):
            halo_c = halo_c + jnp.where(tags[i] == F32(f), planes[i], 0.0)
        side_coef_ref[f] = halo_c
        side_lap_ref[f] = column_sum(remote_sum, row_id, 0.0, 0.0) - 27.0 * remote
        whole = column_sum(inner_sum, row_id, 0.0, 0.0) - 27.0 * inner
        box_ref[f, :, before] = jnp.where(facing, whole, box_in[f, :, before])
    rim_ref[:, 4:8, :] = jnp.zeros((2, 4, LANES), F32)


def last_edges(
    coef_ref, y_ref, straight_ref, diag_ref, box0_ref, rim_ref, side_lap_ref, side_coef_ref, side_rim_ref, box_in,
    box_ref, lap_ref, side_ref, sums_ref
):
    fields, depth, width = box_in.shape
    main = width // LANES
    lane = lane_ids()
    column = ColumnEdge(coef_ref, y_ref)
    before = slice(width - LANES, width)
    extra_s = straight_ref[fields * depth : fields * depth + 16, :].astype(F32)
    extra_d = diag_ref[depth : depth + 32, :].astype(F32)
    tags_d = [extra_d[16 + i : 17 + i] for i in range(8)]

    def edge_tiles(of, base):
        return [of(0, before)] + [of(1, tile_at(t)) for t in range(main)] + [extra_d[base : base + 4]]

    near = edge_tiles(column.near, 0)
    beyond = edge_tiles(column.beyond, 4)
    ahead = edge_tiles(column.ahead, 8)
    corner = jnp.zeros((4, LANES), F32)
    for s in range(4):
        corner = corner + jnp.where(tags_d[s] == column.field_id, extra_d[12 + s : 13 + s], 0.0)
        corner = corner + jnp.where(tags_d[4 + s] == column.field_id, extra_s[s : s + 1], 0.0)
    edge_c = [column.coefs(0, before)] + [column.coefs(1, tile_at(t)) for t in range(main)] + [corner]
    near_sum = nine_sum(near, lane)
    beyond_sum = nine_sum(beyond, lane)
    top = slice(0, 1)
    bottom = slice(depth - 1, depth)
    for f in range(fields):
        for t in range(main):
            low_row, high_row = column.rows(near_sum[t + 1][f : f + 1])
            lanes = tile_at(t)
            box_ref[f, top, lanes] = box_in[f, top, lanes] + low_row
            box_ref[f, bottom, lanes] = box_in[f, bottom, lanes] + high_row
        remote = straight_ref[f * depth : (f + 1) * depth, :].astype(F32)
        side_ref[f] = pltpu.roll(remote, 64, 1) + side_coef_ref[f] * side_lap_ref[f]
        low_row, high_row = column.rows(near_sum[main + 1][f : f + 1])
        side_ref[f, top] += side_coef_ref[f, top] * low_row
        side_ref[f, bottom] += side_coef_ref[f, bottom] * high_row
        low_row, high_row = column.rows(near_sum[0][f : f + 1])
        lap_ref[f] = box0_ref[f, :, before]
        lap_ref[f, top] += low_row
        lap_ref[f, bottom] += high_row
    rims = [rim_ref[0, 0:4, before]] + [rim_ref[1, 0:4, tile_at(t)] for t in range(main)] + [side_rim_ref[1, 0:4, :]]
    rims[main] = jnp.where(lane >= 96, side_rim_ref[0, 0:4, :], rims[main])
    stepped = []
    for t in range(main + 2):
        box = near_sum[t] + beyond_sum[t] + rims[t]
        stepped.append(ahead[t] + edge_c[t] * (box - 27.0 * near[t]))
    stepped_sum = nine_sum(stepped, lane)
    for t in range(main):
        sums_ref[0:4, tile_at(t)] = stepped_sum[t + 1]
    sums_ref[4:8, :] = jnp.zeros((4, width), F32)
    return stepped[main]


def first_edges_body(
    u_ref, coef_ref, y_ref, box1_ref, rim_ref, box_in, box_ref, sums_ref, tail_ref
):
    fields, depth, width = u_ref.shape[1:]
    main = width // LANES
    lane = lane_ids()
    column = ColumnEdge(coef_ref, y_ref)
    after = slice(0, LANES)

    def edge_tiles(of):
        return [of(0, tile_at(t)) for t in range(main)] + [of(1, after)]

    near = edge_tiles(column.near)
    near_sum = nine_sum(near, lane)
    beyond_sum = nine_sum(edge_tiles(column.beyond), lane)
    ahead = edge_tiles(column.ahead)
    edge_c = edge_tiles(column.coefs)
    for f in range(fields):
        for t in range(main):
            low_row, high_row = column.rows(near_sum[t][f : f + 1])
            lanes = tile_at(t)
            box_ref[f, 0:1, lanes] = box_in[f, 0:1, lanes] + low_row
            box_ref[f, depth - 1 : depth, lanes] = box_in[f, depth - 1 : depth, lanes] + high_row
    rims = [rim_ref[0, 0:4, tile_at(t)] for t in range(main)] + [rim_ref[1, 0:4, after]]
    stepped = []
    for t in range(main + 1):
        box = near_sum[t] + beyond_sum[t] + rims[t]
        stepped.append(ahead[t] + edge_c[t] * (box - 27.0 * near[t]))
    stepped_sum = nine_sum(stepped, lane)
    for t in range(main):
        sums_ref[0:4, tile_at(t)] = stepped_sum[t]
    sums_ref[4:8, :] = jnp.zeros((4, width), F32)
    tail_ref[0:4, :] = stepped[1]
    tail_ref[4:8, :] = jnp.zeros((4, LANES), F32)


class Pieces:
    def __init__(self, map_ref, coef_ref, slab_ref):
        self.coef, self.slab = coef_ref, slab_ref
        self.region = lax.axis_index("region")
        self.numbers = [map_ref[q] for q in range(8)]

    def piece(self, number):
        place = jnp.int32(0)
        for q in range(8):
            place = jnp.where(self.numbers[q] == number, q, place)
        slot = place & 3
        held = (place >> 2) == self.region

        def tile(lanes):
            return jnp.where(held, self.coef[self.region, slot, :, lanes], self.slab[slot, :, lanes]).astype(F32)

        return tile


def second_step(now, before, total, coef, row_id, row, lower):
    low_row, high_row = jnp.where(lower, 0.0, row), jnp.where(lower, row, 0.0)
    lap = column_sum(total, row_id, low_row, high_row) - 27.0 * now
    return 2.0 * now - before + coef * lap


CODES = 32000.0


def power_of(size):
    return jnp.ceil(jnp.log2(jnp.maximum(size, 1e-30)))


def coded(value, power):
    return jnp.floor(value * (CODES * jnp.exp2(-power)) + 0.5)


def narrow(value):
    return value.astype(jnp.int32).astype(jnp.int16)


def wide(code):
    return code.astype(jnp.int32).astype(F32)


def scale_of(power):
    return jnp.exp2(power) * (1.0 / CODES)


def last_row_a_body(
    map_ref, owner_ref, u_ref, coef_ref, y_ref, straight_ref, diag_ref, box0_ref, rim_ref, side_lap_ref, side_coef_ref,
    side_rim_ref, drift_ref, box_in, box_ref, lap_ref, side_ref, sums_ref, row_ref, code_ref, power_ref, extra_ref
):
    tail = last_edges(
        coef_ref, y_ref, straight_ref, diag_ref, box0_ref, rim_ref, side_lap_ref, side_coef_ref, side_rim_ref, box_in,
        box_ref, lap_ref, side_ref, sums_ref
    )
    more = (owner_ref, tail, extra_ref)
    refs = (map_ref, u_ref, coef_ref, y_ref, box_ref, drift_ref, lap_ref, side_ref, sums_ref, row_ref, code_ref, power_ref)
    last_row(0, *refs, more=more)


def last_row_b_body(first, *refs):
    last_row(first, *refs)


def last_row(
    first, map_ref, u_ref, coef_ref, y_ref, box_ref, drift_ref, lap_ref, side_ref, sums_ref, row_ref, code_ref, power_ref,
    more=None
):
    count, depth, width = row_ref.shape
    fields = u_ref.shape[1]
    main = width // LANES
    lane = lane_ids()
    row_id = lax.broadcasted_iota(jnp.int32, (depth, 1), 0)
    pieces = Pieces(map_ref, coef_ref, y_ref)
    lower = pieces.region == 0
    before = slice(width - LANES, width)
    base = count * depth
    last_tiles = []
    for f in range(first, first + count):
        coef = pieces.piece(fields + f)
        coefs = [coef(tile_at(t)) for t in range(main)]
        middle = [drift_ref[1, f, :, tile_at(t)] + coefs[t] * box_ref[f, :, tile_at(t)] for t in range(main)]
        local = drift_ref[0, f, :, before] + pieces.piece(f)(before) * lap_ref[f]
        sums = nine_sum([local] + middle + [side_ref[f]], lane)
        at = f - first
        for t in range(main):
            lanes = tile_at(t)
            row = sums_ref[f : f + 1, lanes]
            value = second_step(middle[t], u_ref[1, f, :, lanes], sums[t + 1], coefs[t], row_id, row, lower)
            row_ref[at, :, lanes] = value
            power = power_of(jnp.max(jnp.abs(value), axis=0, keepdims=True))
            code_ref[at * depth : (at + 1) * depth, lanes] = narrow(coded(value, power))
            power_ref[at : at + 1, lanes] = power
        last_tiles.append(middle[main - 1])
    power_ref[count:8, :] = jnp.zeros((8 - count, width), F32)
    code_ref[base : base + 8, :] = narrow(power_ref[...])
    if more is not None:
        owner_ref, tail, extra_ref = more
        near = y_ref[4, 0:16, before].astype(F32)
        extra_ref[2:3, :] = jnp.zeros((1, width), F32) + jnp.where(owner_ref[1] != lax.axis_index("blk"), 1.0, 0.0)
        extra_ref[3:8, :] = jnp.zeros((5, width), F32)
        for f in range(fields):
            if f < count:
                stepped = last_tiles[f]
            else:
                stepped = drift_ref[1, f, :, before] + pieces.piece(fields + f)(before) * box_ref[f, :, before]
            both = jnp.where(lane >= 96, u_ref[1, f, :, before], pltpu.roll(stepped, 96, 1))
            rows = [near[4 + f : 5 + f], near[12 + f : 13 + f], tail[f : f + 1]]
            size = jnp.max(jnp.abs(both), axis=0, keepdims=True)
            for row in rows:
                size = jnp.maximum(size, jnp.abs(row))
            power = power_of(size)
            codes = narrow(coded(both, power))
            here, there = tile_at(f), tile_at(fields + f)
            code_ref[base + 8 : base + 8 + depth // 2, here] = codes[0 : depth // 2]
            code_ref[base + 8 : base + 8 + depth // 2, there] = codes[depth // 2 : depth]
            extra_ref[0:1, here] = power
            extra_ref[0:1, there] = coded(rows[0], power)
            extra_ref[1:2, here] = coded(rows[1], power)
            extra_ref[1:2, there] = coded(rows[2], power)
        code_ref[base + 8 + depth // 2 : base + 16 + depth // 2, :] = narrow(extra_ref[...])


def first_row_body(map_ref, u_ref, coef_ref, y_ref, box_ref, box1_ref, drift_ref, sums_ref, row_ref):
    fields, depth, width = u_ref.shape[1:]
    main = width // LANES
    lane = lane_ids()
    row_id = lax.broadcasted_iota(jnp.int32, (depth, 1), 0)
    pieces = Pieces(map_ref, coef_ref, y_ref)
    lower = pieces.region == 0
    after = slice(0, LANES)
    for f in range(fields):
        coef = pieces.piece(f)
        coefs = [coef(tile_at(t)) for t in range(main)]
        now = [drift_ref[0, f, :, tile_at(t)] + coefs[t] * box_ref[f, :, tile_at(t)] for t in range(main)]
        local = drift_ref[1, f, :, after] + pieces.piece(fields + f)(after) * box1_ref[f, :, after]
        sums = nine_sum(now + [local], lane)
        for t in range(1, main):
            lanes = tile_at(t)
            row = sums_ref[f : f + 1, lanes]
            row_ref[f, :, lanes] = second_step(now[t], u_ref[0, f, :, lanes], sums[t], coefs[t], row_id, row, lower)


def arrival(code_ref):
    rows = code_ref.shape[0]
    return jnp.max(wide(code_ref[rows - 8 : rows, 0:LANES])[2:3]) > 0.5


def code_copies(first, count, depth, row_ref, out_ref, sems, base):
    part = depth // 2
    copies = []
    for f in range(count):
        for h in range(2):
            rows = slice(h * part, (h + 1) * part)
            sem = sems.at[base + 2 * f + h]
            copies.append(pltpu.make_async_copy(row_ref.at[f, rows], out_ref.at[0, first + f, rows], sem))
    return copies


def place_codes(code_ref, first, count, depth, row_ref, out_ref, sems, base):
    scale = scale_of(wide(code_ref[count * depth : count * depth + 8, :]))
    part = depth // 2
    for i, copy in enumerate(code_copies(first, count, depth, row_ref, out_ref, sems, base)):
        f, h = divmod(i, 2)
        row_ref[f, h * part : (h + 1) * part] = wide(code_ref[i * part : (i + 1) * part, :]) * scale[f : f + 1]
        copy.start()


def first_copies(row_ref, out_ref, at, sems, base):
    fields, _, width = row_ref.shape
    rest = slice(LANES, width)
    return [
        pltpu.make_async_copy(row_ref.at[f, :, rest], out_ref.at[at, f, :, rest], sems.at[base + f])
        for f in range(fields)
    ]


def last_copies(last_a_ref, last_b_ref, out_ref, at, sems, base):
    half = last_a_ref.shape[0]
    sources = [last_a_ref.at[f] for f in range(half)] + [last_b_ref.at[f] for f in range(half)]
    return [pltpu.make_async_copy(source, out_ref.at[at, f], sems.at[base + f]) for f, source in enumerate(sources)]


def rows_body(owner_ref, row_ref, last_a_ref, last_b_ref, out_ref, zero_ref, sems):
    fields = row_ref.shape[0]
    keeps = owner_ref[1] == lax.axis_index("blk")
    zero_ref[...] = jnp.zeros(zero_ref.shape, F32)

    def zeros(at, base):
        return [pltpu.make_async_copy(zero_ref, out_ref.at[at, f], sems.at[base + f]) for f in range(fields)]

    always = first_copies(row_ref, out_ref, 0, sems, 0) + zeros(2, fields)
    kept = last_copies(last_a_ref, last_b_ref, out_ref, 1, sems, 2 * fields)
    gone = zeros(1, 2 * fields)

    def all_of(act):
        for copy in always:
            act(copy)

        @pl.when(keeps)
        def _():
            for copy in kept:
                act(copy)

        @pl.when(jnp.logical_not(keeps))
        def _():
            for copy in gone:
                act(copy)

    all_of(lambda copy: copy.start())
    all_of(lambda copy: copy.wait())


def finish_body(
    owner_ref, map_ref, u_ref, coef_ref, y_ref, box_ref, drift_ref, tail_ref, code_ref, row_ref,
    last_a_ref, last_b_ref, partial_ref, out_ref, tile_ref, arrived_ref, sems
):
    fields, depth, width = u_ref.shape[1:]
    half = arrived_ref.shape[0]
    base = half * depth
    lane = lane_ids()
    row_id = lax.broadcasted_iota(jnp.int32, (depth, 1), 0)
    arrives = arrival(code_ref)
    slot = jnp.where(arrives, 1, 0)
    moves_on = jnp.logical_and(arrives, owner_ref[1] == lax.axis_index("blk"))
    firsts = first_copies(row_ref, out_ref, 1, sems, 1 + 2 * half)
    lasts = last_copies(last_a_ref, last_b_ref, out_ref, 2, sems, 1 + 2 * half + fields)

    @pl.when(arrives)
    def _():
        for copy in firsts:
            copy.start()

    @pl.when(moves_on)
    def _():
        for copy in lasts:
            copy.start()

    @pl.when(arrives)
    def _():
        place_codes(code_ref, 0, half, depth, arrived_ref, out_ref, sems, 1)

    column = ColumnEdge(coef_ref, y_ref)
    pieces = Pieces(map_ref, coef_ref, y_ref)
    extra = wide(code_ref[base + 8 + depth // 2 : base + 16 + depth // 2, :])
    tile0, tile1 = tile_at(0), tile_at(1)
    near = column.near(0, tile0)
    corners = [[], [], []]
    rims, before, stepped, nexts, coefs = [], [], [], [], []
    for f in range(fields):
        here, there = tile_at(f), tile_at(fields + f)
        scale = scale_of(extra[0:1, here])
        corners[0].append(extra[0:1, there] * scale)
        corners[1].append(extra[1:2, here] * scale)
        corners[2].append(extra[1:2, there] * scale)
        upper = wide(code_ref[base + 8 : base + 8 + depth // 2, here])
        under = wide(code_ref[base + 8 : base + 8 + depth // 2, there])
        before.append(jnp.concatenate([upper, under], axis=0) * scale)
    corners = [jnp.concatenate(rows, axis=0) for rows in corners]
    near_sum = nine_sum([corners[0], near, column.near(0, tile1)], lane)[1]
    beyond_sum = nine_sum([corners[1], column.beyond(0, tile0), column.beyond(0, tile1)], lane)[1]
    for f in range(fields):
        now = u_ref[0, f, :, tile0]
        total = nine_sum([before[f], now, u_ref[0, f, :, tile1]], lane)[1]
        rims.append(column.own(total))
        low_row, high_row = column.rows(near_sum[f : f + 1])
        lap = column_sum(total, row_id, low_row, high_row) - 27.0 * now
        coef = pieces.piece(f)
        coefs.append(coef(tile0))
        stepped.append(drift_ref[0, f, :, tile0] + coefs[f] * lap)
        nexts.append(drift_ref[0, f, :, tile1] + coef(tile1) * box_ref[f, :, tile1])
    box = near_sum + beyond_sum + jnp.concatenate(rims, axis=0)
    edge = column.ahead(0, tile0) + column.coefs(0, tile0) * (box - 27.0 * near)
    edge_sum = nine_sum([corners[2], edge, tail_ref[0:4, :]], lane)[1]
    for f in range(fields):
        total = nine_sum([pltpu.roll(before[f], 32, 1), stepped[f], nexts[f]], lane)[1]
        row = edge_sum[f : f + 1]
        tile_ref[f] = second_step(stepped[f], u_ref[0, f, :, tile0], total, coefs[f], row_id, row, column.lower)
    last = pltpu.make_async_copy(tile_ref, out_ref.at[slot, :, :, tile0], sems.at[0])
    last.start()

    @pl.when(arrives)
    def _():
        for copy in code_copies(0, half, depth, arrived_ref, out_ref, sems, 1):
            copy.wait()
        for copy in firsts:
            copy.wait()

    @pl.when(moves_on)
    def _():
        for copy in lasts:
            copy.wait()

    last.wait()


def place_body(first, code_a_ref, code_ref, partial_ref, out_ref, row_ref, sems):
    count, depth, _ = row_ref.shape

    @pl.when(arrival(code_a_ref))
    def _():
        place_codes(code_ref, first, count, depth, row_ref, out_ref, sems, 0)
        for copy in code_copies(first, count, depth, row_ref, out_ref, sems, 0):
            copy.wait()


def fast_on_device(u_now, u_prev, coef_store, store_map, new_owner):
    blocks, _, fields, depth, width = u_now.shape
    now = u_now.reshape(blocks, fields, depth, width)
    prev = u_prev.reshape(blocks, fields, depth, width)
    coef = coef_store[0, 0]
    count = lax.axis_size("blk")
    order = store_map.reshape(-1)
    order_hbm, now_hbm, prev_hbm, coef_hbm = (
        pltpu.with_memory_space_constraint(array, pltpu.HBM) for array in (order, now, prev, coef)
    )
    params = pltpu.CompilerParams(vmem_limit_bytes=48 * 1024 * 1024)

    def call(body, name, out_shape, in_specs, out_specs, scratch, args, **options):
        return pl.pallas_call(
            body,
            out_shape=out_shape,
            in_specs=in_specs,
            out_specs=out_specs,
            scratch_shapes=scratch,
            compiler_params=params,
            name=name,
            **options,
        )(*args)

    straight = jax.ShapeDtypeStruct((fields * depth + 16, LANES), BF16)
    diag = jax.ShapeDtypeStruct((depth + 32, LANES), BF16)
    sources = (order_hbm, now_hbm, prev_hbm, coef_hbm)
    y_out = call(
        pack_region_body,
        "pack_region",
        jax.ShapeDtypeStruct((5, depth, width), BF16),
        [HBM] * 4,
        VMEM,
        [
            pltpu.VMEM((depth, width), F32),
            pltpu.VMEM((blocks, fields, 8, width), F32),
            pltpu.VMEM((blocks, fields, 8, width), F32),
            pltpu.VMEM((4, 16, width), BF16),
            pltpu.SMEM(order.shape, jnp.int32),
            pltpu.SemaphoreType.DMA((12,)),
        ],
        sources,
    )
    left, dleft = call(
        pack_back_body,
        "pack_back",
        (straight, diag),
        [HBM] * 4,
        (VMEM,) * 2,
        [
            pltpu.VMEM((1, fields, 8, LANES), F32),
            pltpu.VMEM((1, fields, 8, LANES), F32),
            pltpu.VMEM((4, 16, LANES), BF16),
            pltpu.VMEM((fields, depth, LANES), F32),
            pltpu.VMEM((fields, depth, LANES), F32),
            pltpu.VMEM((2, 4, depth, LANES), BF16),
            pltpu.SMEM(order.shape, jnp.int32),
            pltpu.SemaphoreType.DMA((7,)),
        ],
        sources,
    )
    swap = [(0, 1), (1, 0)]
    forward = [(i, (i + 1) % count) for i in range(count)]
    backward = [(i, (i - 1) % count) for i in range(count)]
    crossed = [(r * count + i, (1 - r) * count + (i - 1) % count) for r in range(2) for i in range(count)]
    y_in = lax.ppermute(y_out, "region", swap)
    from_right = lax.ppermute(left, "blk", backward)
    from_dright = lax.ppermute(dleft, ("region", "blk"), crossed)

    row = jax.ShapeDtypeStruct((fields, depth, width), F32)
    box0, box1, drift, rim = call(
        local_body,
        "local",
        (row, row, jax.ShapeDtypeStruct(now.shape, F32), jax.ShapeDtypeStruct((blocks, 8, width), F32)),
        [VMEM] * 2,
        (VMEM,) * 4,
        [],
        (now, prev),
    )
    tiles = jax.ShapeDtypeStruct((fields, depth, LANES), F32)
    sums = jax.ShapeDtypeStruct((8, width), F32)
    tail = jax.ShapeDtypeStruct((8, LANES), F32)
    box1, side_lap, side_coef, side_rim = call(
        border_body,
        "border",
        (row, tiles, tiles, jax.ShapeDtypeStruct((2, 8, LANES), F32)),
        [VMEM] * 4,
        (VMEM,) * 4,
        [],
        (now, from_right, from_dright, box1),
        input_output_aliases={3: 0},
        cost_estimate=pl.CostEstimate(flops=0, transcendentals=0, bytes_accessed=40_000_000),
    )
    half = fields // 2
    part = jax.ShapeDtypeStruct((half, depth, width), F32)
    codes = jax.ShapeDtypeStruct((half * depth + 8, width), jnp.int16)
    more_codes = jax.ShapeDtypeStruct((half * depth + depth // 2 + 16, width), jnp.int16)
    powers = pltpu.VMEM((8, width), F32)
    box1, lap1, side1, sums1, last_a, code_a = call(
        last_row_a_body,
        "last_row",
        (row, tiles, tiles, sums, part, more_codes),
        [SMEM] * 2 + [VMEM] * 12,
        (VMEM,) * 6,
        [powers, powers],
        (order, new_owner, now, coef, y_in, from_right, from_dright, box0, rim, side_lap, side_coef, side_rim, drift, box1),
        input_output_aliases={13: 0},
    )
    arrived_a = lax.ppermute(code_a, "blk", forward)
    last_b, code_b = call(
        functools.partial(last_row_b_body, half),
        "last_row",
        (part, codes),
        [SMEM] + [VMEM] * 8,
        (VMEM,) * 2,
        [powers],
        (order, now, coef, y_in, box1, drift, lap1, side1, sums1),
    )
    arrived_b = lax.ppermute(code_b, "blk", forward)
    box0, sums0, tail0 = call(
        first_edges_body,
        "first_edges",
        (row, sums, tail),
        [VMEM] * 6,
        (VMEM,) * 3,
        [],
        (now, coef, y_in, box1, rim, box0),
        input_output_aliases={5: 0},
    )
    first = call(
        first_row_body,
        "first_row",
        row,
        [SMEM] + [VMEM] * 7,
        VMEM,
        [],
        (order, now, coef, y_in, box0, box1, drift, sums0),
    )
    whole = jax.ShapeDtypeStruct((blocks + 1, fields, depth, width), F32)
    placed = call(
        rows_body,
        "rows",
        whole,
        [SMEM] + [VMEM] * 3,
        ANY,
        [pltpu.VMEM((depth, width), F32), pltpu.SemaphoreType.DMA((3 * fields,))],
        (new_owner, first, last_a, last_b),
    )
    arrived_half = pltpu.VMEM((half, depth, width), F32)
    placed = call(
        finish_body,
        "finish",
        whole,
        [SMEM] * 2 + [VMEM] * 10 + [ANY],
        ANY,
        [
            pltpu.VMEM((fields, depth, LANES), F32),
            arrived_half,
            pltpu.SemaphoreType.DMA((1 + 2 * half + 2 * fields,)),
        ],
        (new_owner, order, now, coef, y_in, box0, drift, tail0, arrived_a, first, last_a, last_b, placed),
        input_output_aliases={12: 0},
    )
    placed = call(
        functools.partial(place_body, half),
        "place",
        whole,
        [VMEM, VMEM, ANY],
        ANY,
        [arrived_half, pltpu.SemaphoreType.DMA((2 * half,))],
        (arrived_a, arrived_b, placed),
        input_output_aliases={2: 0},
    )
    return placed[:, None]


def solution(mesh):
    def on_device(*args):
        blocks = args[0].shape[0]
        if lax.axis_size("region") == 2 and blocks == 2:
            return fast_on_device(*args)
        return general_on_device(*args)

    return jax.shard_map(
        on_device,
        mesh=mesh,
        in_specs=(
            P("blk", "region", None, None, None),
            P("blk", "region", None, None, None),
            P("blk", "region", None, None, None, None),
            P("blk", "region", None),
            P("blk"),
        ),
        out_specs=P("blk", "region", None, None, None),
        check_vma=False,
    )
```

```python
import functools

import jax
import jax.numpy as jnp
from jax import lax
from jax.experimental import pallas as pl
from jax.experimental.pallas import tpu as pltpu
from jax.sharding import PartitionSpec as P

STEPS = 2
LANES = 128
F32 = jnp.float32
BF16 = jnp.bfloat16
VMEM = pl.BlockSpec(memory_space=pltpu.VMEM)
SMEM = pl.BlockSpec(memory_space=pltpu.SMEM)
ANY = pl.BlockSpec(memory_space=pl.ANY)
HBM = pl.BlockSpec(memory_space=pltpu.HBM)


def extended_2(block, sides, width, periodic):
    for axis, dim in sides:
        count = lax.axis_size(axis)
        forward = [(i, i + 1) for i in range(count - 1)]
        if periodic:
            forward.append((count - 1, 0))
        backward = [(target, source) for source, target in forward]
        low = lax.ppermute(
            lax.slice_in_dim(block, block.shape[dim] - width, None, axis=dim), axis, forward
        )
        high = lax.ppermute(lax.slice_in_dim(block, 0, width, axis=dim), axis, backward)
        block = jnp.concatenate([low, block, high], axis=dim)
    return block


def shifted_2(value, axis, by):
    devices = lax.axis_size(axis)
    return lax.ppermute(value, axis, [(i, (i + by) % devices) for i in range(devices)])


def stencil_step(state_now, state_prev, coefficient, live_count):
    slot_count, field_count, edge_cells, plane_cells = state_now.shape
    padded = extended_2(state_now, (("region", 2),), 1, False)
    first_planes = padded[..., :edge_cells]
    last_planes = padded[..., plane_cells - edge_cells :]
    last_live = jnp.take(last_planes, live_count - 1, axis=0)
    rim_pair = jnp.stack([first_planes[0], last_live], axis=2)
    spread = extended_2(rim_pair.astype(jnp.bfloat16), (("blk", 2),), 1, True).astype(
        rim_pair.dtype
    )
    left_rim = spread[:, :, 0]
    right_rim = spread[:, :, 3]
    before_planes = jnp.concatenate([left_rim[None], last_planes[:-1]], axis=0)
    after_planes = jnp.pad(first_planes[1:], ((0, 1), (0, 0), (0, 0), (0, 0)))
    slot_ids = jnp.arange(slot_count)
    after_planes = jnp.where(
        (slot_ids == live_count - 1)[:, None, None, None], right_rim[None], after_planes
    )
    extended = jnp.concatenate([before_planes, padded, after_planes], axis=-1)
    width = extended.shape[-1]
    column = jnp.arange(width) % edge_cells
    lower_mask = (column != 0).astype(jnp.float32)
    upper_mask = (column != edge_cells - 1).astype(jnp.float32)
    margin = ((0, 0), (0, 0), (0, 0), (1, 1))
    shifted = jnp.pad(extended, margin)
    summed = shifted[..., :width] * lower_mask + extended + shifted[..., 2:] * upper_mask
    summed = (
        summed[..., : -2 * edge_cells]
        + summed[..., edge_cells:-edge_cells]
        + summed[..., 2 * edge_cells :]
    )
    box_sum = summed[:, :, :-2] + summed[:, :, 1:-1] + summed[:, :, 2:]
    laplace = box_sum - 27.0 * state_now
    return 2.0 * state_now - state_prev + coefficient.astype(jnp.float32) * laplace


def compact(members, valid_flags):
    slot_count = valid_flags.shape[0]
    place_index = jnp.cumsum(valid_flags) - 1
    target = jnp.arange(slot_count)
    chooser = (valid_flags[None, :] == 1) & (place_index[None, :] == target[:, None])
    source = jnp.sum(jnp.where(chooser, target[None, :], 0), axis=1)
    filled = jnp.sum(chooser.astype(jnp.int32), axis=1) > 0
    placed = tuple(
        (
            jnp.where(
                filled.reshape((slot_count,) + (1,) * (member.ndim - 1)),
                jnp.take(member, source, axis=0),
                jnp.zeros_like(member),
            )
            for member in members
        )
    )
    return (placed, jnp.sum(valid_flags))


def general_on_device(u_now, u_prev, coef_store, store_map, new_owner):
    state_now = u_now[:, 0]
    state_prev = u_prev[:, 0]
    blocks, fields, edge_cells, plane_cells = state_now.shape
    store_local = coef_store[0, 0]
    arrived = lax.all_to_all(store_local, "region", split_axis=0, concat_axis=0, tiled=True)
    flattened = arrived.reshape((-1,) + arrived.shape[2:])
    inverse = jnp.argsort(store_map[0, 0])
    coefficient = jnp.take(flattened, inverse, axis=0).reshape(
        blocks, fields, edge_cells, plane_cells
    )
    own_index = lax.axis_index("blk")
    goes_right = new_owner[blocks - 1] != own_index
    mark_right = goes_right.astype(jnp.float32).reshape(1)
    middle_flags = jnp.ones((blocks - 2,), jnp.int32)
    keep_first = (new_owner[0] == own_index).astype(jnp.int32).reshape(1)
    keep_last = (new_owner[blocks - 1] == own_index).astype(jnp.int32).reshape(1)
    for step_index in range(STEPS):
        state_now, state_prev = (
            stencil_step(state_now, state_prev, coefficient, blocks),
            state_now,
        )
    from_left = shifted_2((state_now[blocks - 1], mark_right), "blk", 1)
    valid_flags = jnp.concatenate(
        [(from_left[1] > 0.5).astype(jnp.int32), keep_first, middle_flags, keep_last]
    )
    stacked_now = jnp.concatenate([from_left[0][None], state_now], axis=0)
    placed, live_count = compact((stacked_now,), valid_flags)
    result = placed[0]
    return result[:, None]


def lane_ids():
    return lax.broadcasted_iota(jnp.int32, (1, LANES), 1)


def edge_start(lower, depth, size):
    return pl.multiple_of(jnp.where(lower, depth - size, 0), size)


def tag_values(map_ref, region):
    numbers = [map_ref[region * 4 + s] for s in range(4)] + [map_ref[(1 - region) * 4 + s] for s in range(4)]
    return [jnp.zeros((1, LANES), F32) + number.astype(F32) for number in numbers]


def edge_copies(u_ref, p_ref, coef_ref, ue_ref, pe_ref, ce_ref, some, region, sems):
    lower = region == 0
    depth = u_ref.shape[2]
    edge8 = edge_start(lower, depth, 8)
    edge16 = edge_start(lower, depth, 16)
    rows, lanes = some
    return [
        pltpu.make_async_copy(u_ref.at[rows, :, pl.ds(edge8, 8), lanes], ue_ref, sems.at[0]),
        pltpu.make_async_copy(p_ref.at[rows, :, pl.ds(edge8, 8), lanes], pe_ref, sems.at[1]),
        pltpu.make_async_copy(coef_ref.at[region, :, pl.ds(edge16, 16), lanes], ce_ref, sems.at[2]),
    ]


def edge_rows(ue_ref, pe_ref, m, f, lower):
    own_edge = jnp.where(lower, 7, 0)
    own_next = jnp.where(lower, 6, 1)
    near = ue_ref[m, f, pl.ds(own_edge, 1), :]
    return near, ue_ref[m, f, pl.ds(own_next, 1), :], 2.0 * near - pe_ref[m, f, pl.ds(own_edge, 1), :]


def edge_piece(ce_ref, s, lower):
    piece = ce_ref[s].astype(F32)
    return jnp.where(lower, piece[15:16], piece[0:1])


def pack_back_body(
    map_hbm, u_ref, p_ref, coef_ref, straight_ref, diag_ref, ue_ref, pe_ref, ce_ref, ua_ref, pa_ref, ca_ref, map_ref, sems
):
    fields = u_ref.shape[1]
    depth = u_ref.shape[2]
    region = lax.axis_index("region")
    lower = region == 0
    other = 1 - region
    front = slice(0, LANES)
    copies = [
        pltpu.make_async_copy(map_hbm, map_ref, sems.at[3]),
        pltpu.make_async_copy(u_ref.at[0, :, :, front], ua_ref, sems.at[4]),
        pltpu.make_async_copy(p_ref.at[0, :, :, front], pa_ref, sems.at[5]),
        pltpu.make_async_copy(coef_ref.at[:, :, :, front], ca_ref, sems.at[6]),
    ] + edge_copies(u_ref, p_ref, coef_ref, ue_ref, pe_ref, ce_ref, (slice(0, 1), front), region, sems)
    for copy in copies:
        copy.start()
    for copy in copies:
        copy.wait()
    lane = lane_ids()
    tag_rows = tag_values(map_ref, region)
    blank = jnp.zeros((1, LANES), F32)
    for f in range(fields):
        now = ua_ref[f]
        ahead = 2.0 * now - pa_ref[f]
        piece = ca_ref[region, f].astype(F32)
        tile = jnp.where(
            lane < 64, now, jnp.where(lane < 96, pltpu.roll(ahead, 64, 1), pltpu.roll(piece, 96, 1))
        )
        straight_ref[f * depth : (f + 1) * depth, :] = tile.astype(BF16)
    far = [ca_ref[other, s].astype(F32) for s in range(4)]
    extra = [jnp.where(lower, piece[0:1], piece[depth - 1 : depth]) for piece in far] + tag_rows + [blank] * 4
    straight_ref[fields * depth : fields * depth + 16, :] = jnp.concatenate(extra, axis=0).astype(BF16)
    plane = jnp.zeros((depth, LANES), F32)
    for s in range(4):
        moved = pltpu.roll(far[s], 32 * s, 1) if s else far[s]
        plane = jnp.where((lane >= 32 * s) & (lane < 32 * s + 32), moved, plane)
    diag_ref[0:depth, :] = plane.astype(BF16)
    rows = [edge_rows(ue_ref, pe_ref, 0, f, lower) for f in range(fields)]
    extra = [row[kind] for kind in range(3) for row in rows]
    extra += [edge_piece(ce_ref, s, lower) for s in range(4)] + tag_rows + [blank] * 8
    diag_ref[depth : depth + 32, :] = jnp.concatenate(extra, axis=0).astype(BF16)


def pack_region_body(map_hbm, u_ref, p_ref, coef_ref, y_ref, rows_ref, ue_ref, pe_ref, ce_ref, map_ref, sems):
    fields, depth, width = u_ref.shape[1:]
    region = lax.axis_index("region")
    lower = region == 0
    other = 1 - region
    half = depth // 2
    slab = []
    for s in range(4):
        for h in range(2):
            part = slice(h * half, (h + 1) * half)
            slab.append(pltpu.make_async_copy(coef_ref.at[other, s, part], y_ref.at[s, part], sems.at[4 + 2 * s + h]))
    copies = [pltpu.make_async_copy(map_hbm, map_ref, sems.at[3])]
    copies += edge_copies(u_ref, p_ref, coef_ref, ue_ref, pe_ref, ce_ref, (slice(0, 2), slice(0, width)), region, sems)
    for copy in copies + slab:
        copy.start()
    for copy in copies:
        copy.wait()
    for m in range(2):
        for f in range(fields):
            for kind, row in enumerate(edge_rows(ue_ref, pe_ref, m, f, lower)):
                at = 8 * kind + m * fields + f
                rows_ref[at : at + 1, :] = row
    for s in range(4):
        rows_ref[24 + s : 25 + s, :] = edge_piece(ce_ref, s, lower)
    for i, row in enumerate(tag_values(map_ref, region)):
        rows_ref[28:29, i * LANES : (i + 1) * LANES] = row
    rows_ref[29:32, :] = jnp.zeros((3, width), F32)
    y_ref[4] = rows_ref[...].astype(BF16)
    for copy in slab:
        copy.wait()


def nine_sum(tiles, lane, first=0):
    inside = lane % 32
    low = inside != 0
    high = inside != 31
    rows = []
    for tile in tiles:
        rows.append(
            tile
            + jnp.where(low, pltpu.roll(tile, 1, 1), 0.0)
            + jnp.where(high, pltpu.roll(tile, LANES - 1, 1), 0.0)
        )
    up = [pltpu.roll(row, 32, 1) for row in rows]
    down = [pltpu.roll(row, LANES - 32, 1) for row in rows]
    count = len(tiles)
    result = []
    for t in range(count):
        before = up[t] if t == 0 else jnp.where(lane < 32, up[t - 1], up[t])
        after = down[t] if t == count - 1 else jnp.where(lane >= 96, down[t + 1], down[t])
        result.append(rows[t] + before + after)
    return result


def column_sum(tile, row_id, low_row, high_row):
    depth = tile.shape[0]
    above = pltpu.roll(tile, 1, 0)
    below = pltpu.roll(tile, depth - 1, 0)
    return tile + jnp.where(row_id == 0, low_row, above) + jnp.where(row_id == depth - 1, high_row, below)


def local_body(u_ref, p_ref, box0_ref, box1_ref, drift_ref, rim_ref):
    fields, depth, width = u_ref.shape[1:]
    main = width // LANES
    lower = lax.axis_index("region") == 0
    lane = lane_ids()
    row_id = lax.broadcasted_iota(jnp.int32, (depth, 1), 0)
    boxes = (box0_ref, box1_ref)
    for f in range(fields):
        now = [u_ref[m, f, :, tile_at(t)] for m in range(2) for t in range(main)]
        sums = nine_sum(now, lane)
        for i, (tile, total) in enumerate(zip(now, sums)):
            m, t = divmod(i, main)
            lanes = tile_at(t)
            rim_ref[m, f : f + 1, lanes] = jnp.where(lower, total[depth - 1 : depth], total[0:1])
            boxes[m][f, :, lanes] = column_sum(total, row_id, 0.0, 0.0) - 27.0 * tile
            drift_ref[m, f, :, lanes] = 2.0 * tile - p_ref[m, f, :, lanes]
    rim_ref[:, 4:8, :] = jnp.zeros((2, 4, width), F32)


def tile_at(t):
    return slice(t * LANES, (t + 1) * LANES)


class ColumnEdge:
    def __init__(self, coef_ref, y_ref):
        self.region = lax.axis_index("region")
        self.lower = self.region == 0
        self.coef = coef_ref
        self.depth = coef_ref.shape[2]
        self.extra = y_ref[4].astype(F32)
        self.tags = [self.extra[28:29, i * LANES : (i + 1) * LANES] for i in range(8)]
        self.field_id = lax.broadcasted_iota(jnp.int32, (4, LANES), 0).astype(F32)

    def near(self, m, lanes):
        return self.extra[4 * m : 4 * m + 4, lanes]

    def beyond(self, m, lanes):
        return self.extra[8 + 4 * m : 12 + 4 * m, lanes]

    def ahead(self, m, lanes):
        return self.extra[16 + 4 * m : 20 + 4 * m, lanes]

    def coefs(self, m, lanes):
        total = jnp.zeros((4, LANES), F32)
        for s in range(4):
            piece = self.coef[1 - self.region, s, :, lanes].astype(F32)
            held = jnp.where(self.lower, piece[0:1], piece[self.depth - 1 : self.depth])
            total = total + jnp.where(self.tags[s] == self.field_id + 4 * m, self.extra[24 + s : 25 + s, lanes], 0.0)
            total = total + jnp.where(self.tags[4 + s] == self.field_id + 4 * m, held, 0.0)
        return total

    def own(self, tile):
        return jnp.where(self.lower, tile[self.depth - 1 : self.depth], tile[0:1])

    def rows(self, row):
        return jnp.where(self.lower, 0.0, row), jnp.where(self.lower, row, 0.0)


def border_body(u_ref, straight_ref, diag_ref, box_in, box_ref, side_lap_ref, side_coef_ref, rim_ref):
    fields, depth, width = u_ref.shape[1:]
    lane = lane_ids()
    row_id = lax.broadcasted_iota(jnp.int32, (depth, 1), 0)
    lower = lax.axis_index("region") == 0
    before = slice(width - LANES, width)
    facing = lane >= 96
    tags = [straight_ref[fields * depth : fields * depth + 16, :].astype(F32)[4 + i : 5 + i] for i in range(8)]
    planes = []
    for s in range(4):
        planes.append(pltpu.roll(straight_ref[s * depth : (s + 1) * depth, :].astype(F32), 32, 1))
    diag_tile = diag_ref[0:depth, :].astype(F32)
    for s in range(4):
        planes.append(pltpu.roll(diag_tile, LANES - 32 * s, 1) if s else diag_tile)
    for f in range(fields):
        inner = u_ref[1, f, :, before]
        remote = straight_ref[f * depth : (f + 1) * depth, :].astype(F32)
        inner_sum, remote_sum = nine_sum([inner, remote], lane)
        for i, tile in enumerate((inner_sum, remote_sum)):
            rim_ref[i, f : f + 1, :] = jnp.where(lower, tile[depth - 1 : depth], tile[0:1])
        halo_c = jnp.zeros((depth, LANES), F32)
        for i in range(8):
            halo_c = halo_c + jnp.where(tags[i] == F32(f), planes[i], 0.0)
        side_coef_ref[f] = halo_c
        side_lap_ref[f] = column_sum(remote_sum, row_id, 0.0, 0.0) - 27.0 * remote
        whole = column_sum(inner_sum, row_id, 0.0, 0.0) - 27.0 * inner
        box_ref[f, :, before] = jnp.where(facing, whole, box_in[f, :, before])
    rim_ref[:, 4:8, :] = jnp.zeros((2, 4, LANES), F32)


def last_edges(
    coef_ref, y_ref, straight_ref, diag_ref, box0_ref, rim_ref, side_lap_ref, side_coef_ref, side_rim_ref, box_in,
    box_ref, lap_ref, side_ref, sums_ref
):
    fields, depth, width = box_in.shape
    main = width // LANES
    lane = lane_ids()
    column = ColumnEdge(coef_ref, y_ref)
    before = slice(width - LANES, width)
    extra_s = straight_ref[fields * depth : fields * depth + 16, :].astype(F32)
    extra_d = diag_ref[depth : depth + 32, :].astype(F32)
    tags_d = [extra_d[16 + i : 17 + i] for i in range(8)]

    def edge_tiles(of, base):
        return [of(0, before)] + [of(1, tile_at(t)) for t in range(main)] + [extra_d[base : base + 4]]

    near = edge_tiles(column.near, 0)
    beyond = edge_tiles(column.beyond, 4)
    ahead = edge_tiles(column.ahead, 8)
    corner = jnp.zeros((4, LANES), F32)
    for s in range(4):
        corner = corner + jnp.where(tags_d[s] == column.field_id, extra_d[12 + s : 13 + s], 0.0)
        corner = corner + jnp.where(tags_d[4 + s] == column.field_id, extra_s[s : s + 1], 0.0)
    edge_c = [column.coefs(0, before)] + [column.coefs(1, tile_at(t)) for t in range(main)] + [corner]
    near_sum = nine_sum(near, lane)
    beyond_sum = nine_sum(beyond, lane)
    top = slice(0, 1)
    bottom = slice(depth - 1, depth)
    for f in range(fields):
        for t in range(main):
            low_row, high_row = column.rows(near_sum[t + 1][f : f + 1])
            lanes = tile_at(t)
            box_ref[f, top, lanes] = box_in[f, top, lanes] + low_row
            box_ref[f, bottom, lanes] = box_in[f, bottom, lanes] + high_row
        remote = straight_ref[f * depth : (f + 1) * depth, :].astype(F32)
        side_ref[f] = pltpu.roll(remote, 64, 1) + side_coef_ref[f] * side_lap_ref[f]
        low_row, high_row = column.rows(near_sum[main + 1][f : f + 1])
        side_ref[f, top] += side_coef_ref[f, top] * low_row
        side_ref[f, bottom] += side_coef_ref[f, bottom] * high_row
        low_row, high_row = column.rows(near_sum[0][f : f + 1])
        lap_ref[f] = box0_ref[f, :, before]
        lap_ref[f, top] += low_row
        lap_ref[f, bottom] += high_row
    rims = [rim_ref[0, 0:4, before]] + [rim_ref[1, 0:4, tile_at(t)] for t in range(main)] + [side_rim_ref[1, 0:4, :]]
    rims[main] = jnp.where(lane >= 96, side_rim_ref[0, 0:4, :], rims[main])
    stepped = []
    for t in range(main + 2):
        box = near_sum[t] + beyond_sum[t] + rims[t]
        stepped.append(ahead[t] + edge_c[t] * (box - 27.0 * near[t]))
    stepped_sum = nine_sum(stepped, lane)
    for t in range(main):
        sums_ref[0:4, tile_at(t)] = stepped_sum[t + 1]
    sums_ref[4:8, :] = jnp.zeros((4, width), F32)
    return stepped[main]


def first_edges_body(
    u_ref, coef_ref, y_ref, box1_ref, rim_ref, box_in, box_ref, sums_ref, tail_ref
):
    fields, depth, width = u_ref.shape[1:]
    main = width // LANES
    lane = lane_ids()
    column = ColumnEdge(coef_ref, y_ref)
    after = slice(0, LANES)

    def edge_tiles(of):
        return [of(0, tile_at(t)) for t in range(main)] + [of(1, after)]

    near = edge_tiles(column.near)
    near_sum = nine_sum(near, lane)
    beyond_sum = nine_sum(edge_tiles(column.beyond), lane)
    ahead = edge_tiles(column.ahead)
    edge_c = edge_tiles(column.coefs)
    for f in range(fields):
        for t in range(main):
            low_row, high_row = column.rows(near_sum[t][f : f + 1])
            lanes = tile_at(t)
            box_ref[f, 0:1, lanes] = box_in[f, 0:1, lanes] + low_row
            box_ref[f, depth - 1 : depth, lanes] = box_in[f, depth - 1 : depth, lanes] + high_row
    rims = [rim_ref[0, 0:4, tile_at(t)] for t in range(main)] + [rim_ref[1, 0:4, after]]
    stepped = []
    for t in range(main + 1):
        box = near_sum[t] + beyond_sum[t] + rims[t]
        stepped.append(ahead[t] + edge_c[t] * (box - 27.0 * near[t]))
    stepped_sum = nine_sum(stepped, lane)
    for t in range(main):
        sums_ref[0:4, tile_at(t)] = stepped_sum[t]
    sums_ref[4:8, :] = jnp.zeros((4, width), F32)
    tail_ref[0:4, :] = stepped[1]
    tail_ref[4:8, :] = jnp.zeros((4, LANES), F32)


def load_map(map_any, map_ref, sem):
    copy = pltpu.make_async_copy(map_any, map_ref, sem)
    copy.start()
    return copy


class Pieces:
    def __init__(self, map_ref, coef_ref, slab_ref):
        self.coef, self.slab = coef_ref, slab_ref
        self.region = lax.axis_index("region")
        self.numbers = [map_ref[q] for q in range(8)]

    def piece(self, number):
        place = jnp.int32(0)
        for q in range(8):
            place = jnp.where(self.numbers[q] == number, q, place)
        slot = place & 3
        held = (place >> 2) == self.region

        def tile(lanes):
            return jnp.where(held, self.coef[self.region, slot, :, lanes], self.slab[slot, :, lanes]).astype(F32)

        return tile


def second_step(now, before, total, coef, row_id, row, lower):
    low_row, high_row = jnp.where(lower, 0.0, row), jnp.where(lower, row, 0.0)
    lap = column_sum(total, row_id, low_row, high_row) - 27.0 * now
    return 2.0 * now - before + coef * lap


CODES = 32000.0


def power_of(size):
    return jnp.ceil(jnp.log2(jnp.maximum(size, 1e-30)))


def coded(value, power):
    return jnp.floor(value * (CODES * jnp.exp2(-power)) + 0.5)


def narrow(value):
    return value.astype(jnp.int32).astype(jnp.int16)


def wide(code):
    return code.astype(jnp.int32).astype(F32)


def scale_of(power):
    return jnp.exp2(power) * (1.0 / CODES)


def last_row_a_body(
    map_any, owner_any, u_ref, coef_ref, y_ref, straight_ref, diag_ref, box0_ref, rim_ref, side_lap_ref, side_coef_ref,
    side_rim_ref, drift_ref, box_in, box_ref, lap_ref, side_ref, sums_ref, row_ref, code_ref, power_ref, extra_ref,
    map_ref, owner_ref, sems
):
    copies = [load_map(map_any, map_ref, sems.at[0]), load_map(owner_any, owner_ref, sems.at[1])]
    tail = last_edges(
        coef_ref, y_ref, straight_ref, diag_ref, box0_ref, rim_ref, side_lap_ref, side_coef_ref, side_rim_ref, box_in,
        box_ref, lap_ref, side_ref, sums_ref
    )
    for copy in copies:
        copy.wait()
    more = (owner_ref, tail, extra_ref)
    refs = (map_ref, u_ref, coef_ref, y_ref, box_ref, drift_ref, lap_ref, side_ref, sums_ref, row_ref, code_ref, power_ref)
    last_row(0, *refs, more=more)


def last_row_b_body(first, map_any, *refs):
    map_ref, sem = refs[-2:]
    load_map(map_any, map_ref, sem).wait()
    last_row(first, map_ref, *refs[:-2])


def last_row(
    first, map_ref, u_ref, coef_ref, y_ref, box_ref, drift_ref, lap_ref, side_ref, sums_ref, row_ref, code_ref, power_ref,
    more=None
):
    count, depth, width = row_ref.shape
    fields = u_ref.shape[1]
    main = width // LANES
    lane = lane_ids()
    row_id = lax.broadcasted_iota(jnp.int32, (depth, 1), 0)
    pieces = Pieces(map_ref, coef_ref, y_ref)
    lower = pieces.region == 0
    before = slice(width - LANES, width)
    last_tiles = []
    for f in range(first, first + count):
        coef = pieces.piece(fields + f)
        coefs = [coef(tile_at(t)) for t in range(main)]
        middle = [drift_ref[1, f, :, tile_at(t)] + coefs[t] * box_ref[f, :, tile_at(t)] for t in range(main)]
        local = drift_ref[0, f, :, before] + pieces.piece(f)(before) * lap_ref[f]
        sums = nine_sum([local] + middle + [side_ref[f]], lane)
        for t in range(main):
            lanes = tile_at(t)
            row = sums_ref[f : f + 1, lanes]
            value = second_step(middle[t], u_ref[1, f, :, lanes], sums[t + 1], coefs[t], row_id, row, lower)
            row_ref[f - first, :, lanes] = value
            power = power_of(jnp.max(jnp.abs(value), axis=0, keepdims=True))
            at = (f - first) * main + t
            code_ref[at * depth : (at + 1) * depth, :] = narrow(coded(value, power))
            power_ref[at : at + 1, :] = power
        last_tiles.append(middle[main - 1])
    base = count * main * depth
    code_ref[base : base + count * main, :] = narrow(power_ref[...])
    if more is not None:
        owner_ref, tail, extra_ref = more
        base += count * main
        both = []
        for f in range(fields):
            if f < count:
                stepped = last_tiles[f]
            else:
                stepped = drift_ref[1, f, :, before] + pieces.piece(fields + f)(before) * box_ref[f, :, before]
            both.append(jnp.where(lane >= 96, u_ref[1, f, :, before], pltpu.roll(stepped, 96, 1)))
        for g in range(fields // 2):
            pair = jnp.where(lane >= 64, both[2 * g], pltpu.roll(both[2 * g + 1], 64, 1))
            power = power_of(jnp.max(jnp.abs(pair), axis=0, keepdims=True))
            code_ref[base : base + depth, :] = narrow(coded(pair, power))
            extra_ref[g : g + 1, :] = power
            base += depth
        near = y_ref[4, 0:16, before].astype(F32)
        kinds = []
        for rows in (near[4:8], near[12:16], tail):
            kind = jnp.zeros((1, LANES), F32)
            for f in range(fields):
                shift = (32 * f + 32) % LANES
                row = rows[f : f + 1]
                kind = jnp.where(lane // 32 == f, pltpu.roll(row, shift, 1) if shift else row, kind)
            kinds.append(kind)
        power = power_of(jnp.maximum(jnp.maximum(jnp.abs(kinds[0]), jnp.abs(kinds[1])), jnp.abs(kinds[2])))
        extra_ref[2:3, :] = power
        for i, kind in enumerate(kinds):
            extra_ref[3 + i : 4 + i, :] = coded(kind, power)
        moves = jnp.where(owner_ref[1] != lax.axis_index("blk"), 1.0, 0.0)
        extra_ref[6:7, :] = jnp.zeros((1, LANES), F32) + moves
        extra_ref[7:8, :] = jnp.zeros((1, LANES), F32)
        code_ref[base : base + 8, :] = narrow(extra_ref[...])


def first_row_body(map_ref, u_ref, coef_ref, y_ref, box_ref, box1_ref, drift_ref, sums_ref, row_ref):
    fields, depth, width = u_ref.shape[1:]
    main = width // LANES
    lane = lane_ids()
    row_id = lax.broadcasted_iota(jnp.int32, (depth, 1), 0)
    pieces = Pieces(map_ref, coef_ref, y_ref)
    lower = pieces.region == 0
    after = slice(0, LANES)
    for f in range(fields):
        coef = pieces.piece(f)
        coefs = [coef(tile_at(t)) for t in range(main)]
        now = [drift_ref[0, f, :, tile_at(t)] + coefs[t] * box_ref[f, :, tile_at(t)] for t in range(main)]
        local = drift_ref[1, f, :, after] + pieces.piece(fields + f)(after) * box1_ref[f, :, after]
        sums = nine_sum(now + [local], lane)
        for t in range(1, main):
            lanes = tile_at(t)
            row = sums_ref[f : f + 1, lanes]
            row_ref[f, :, lanes] = second_step(now[t], u_ref[0, f, :, lanes], sums[t], coefs[t], row_id, row, lower)


def arrival(code_ref):
    rows = code_ref.shape[0]
    return jnp.max(wide(code_ref[rows - 8 : rows, :])[6:7]) > 0.5


def code_copies(first, row_ref, out_ref, sems, base):
    count, depth, _ = row_ref.shape
    part = depth // 2
    copies = []
    for f in range(count):
        for h in range(2):
            rows = slice(h * part, (h + 1) * part)
            sem = sems.at[base + 2 * f + h]
            copies.append(pltpu.make_async_copy(row_ref.at[f, rows], out_ref.at[0, first + f, rows], sem))
    return copies


def decode(code_ref, row_ref):
    count, depth, width = row_ref.shape
    main = width // LANES
    base = count * main * depth
    scale = scale_of(wide(code_ref[base : base + count * main, :]))
    for f in range(count):
        for t in range(main):
            at = f * main + t
            row_ref[f, :, tile_at(t)] = wide(code_ref[at * depth : (at + 1) * depth, :]) * scale[at : at + 1]


def first_copies(row_ref, out_ref, at, sems, base):
    fields, _, width = row_ref.shape
    rest = slice(LANES, width)
    return [
        pltpu.make_async_copy(row_ref.at[f, :, rest], out_ref.at[at, f, :, rest], sems.at[base + f])
        for f in range(fields)
    ]


def last_copies(last_a_ref, last_b_ref, out_ref, at, sems, base):
    half = last_a_ref.shape[0]
    sources = [last_a_ref.at[f] for f in range(half)] + [last_b_ref.at[f] for f in range(half)]
    return [pltpu.make_async_copy(source, out_ref.at[at, f], sems.at[base + f]) for f, source in enumerate(sources)]


def rows_body(owner_ref, row_ref, last_a_ref, last_b_ref, out_ref, zero_ref, sems):
    fields = row_ref.shape[0]
    keeps = owner_ref[1] == lax.axis_index("blk")
    zero_ref[...] = jnp.zeros(zero_ref.shape, F32)

    def zeros(at, base):
        return [pltpu.make_async_copy(zero_ref, out_ref.at[at, f], sems.at[base + f]) for f in range(fields)]

    always = first_copies(row_ref, out_ref, 0, sems, 0) + zeros(2, fields)
    kept = last_copies(last_a_ref, last_b_ref, out_ref, 1, sems, 2 * fields)
    gone = zeros(1, 2 * fields)

    def all_of(act):
        for copy in always:
            act(copy)

        @pl.when(keeps)
        def _():
            for copy in kept:
                act(copy)

        @pl.when(jnp.logical_not(keeps))
        def _():
            for copy in gone:
                act(copy)

    all_of(lambda copy: copy.start())
    all_of(lambda copy: copy.wait())


def finish_body(
    owner_any, map_any, u_ref, coef_ref, y_ref, box_ref, drift_ref, tail_ref, code_ref, row_ref,
    last_a_ref, last_b_ref, partial_ref, out_ref, tile_ref, arrived_ref, map_ref, owner_ref, sems
):
    fields, depth, width = u_ref.shape[1:]
    main = width // LANES
    half = arrived_ref.shape[0]
    copies = [load_map(map_any, map_ref, sems.at[0]), load_map(owner_any, owner_ref, sems.at[1])]
    arrives = arrival(code_ref)
    lane = lane_ids()
    row_id = lax.broadcasted_iota(jnp.int32, (depth, 1), 0)
    base = half * main * (depth + 1)
    column = ColumnEdge(coef_ref, y_ref)
    extra = wide(code_ref[base + depth * fields // 2 : base + depth * fields // 2 + 8, :])
    tile0, tile1 = tile_at(0), tile_at(1)
    near = column.near(0, tile0)
    before = []
    for g in range(fields // 2):
        pair = wide(code_ref[base + g * depth : base + (g + 1) * depth, :]) * scale_of(extra[g : g + 1])
        before += [pair, pltpu.roll(pair, 64, 1)]
    corners = []
    for kind in range(3):
        row = extra[3 + kind : 4 + kind] * scale_of(extra[2:3])
        shifts = [(96 - 32 * f) % LANES for f in range(fields)]
        corners.append(jnp.concatenate([pltpu.roll(row, shift, 1) if shift else row for shift in shifts], axis=0))
    near_sum = nine_sum([corners[0], near, column.near(0, tile1)], lane)[1]
    beyond_sum = nine_sum([corners[1], column.beyond(0, tile0), column.beyond(0, tile1)], lane)[1]
    for copy in copies:
        copy.wait()
    pieces = Pieces(map_ref, coef_ref, y_ref)
    rims, stepped, nexts, coefs = [], [], [], []
    for f in range(fields):
        now = u_ref[0, f, :, tile0]
        total = nine_sum([before[f], now, u_ref[0, f, :, tile1]], lane)[1]
        rims.append(column.own(total))
        low_row, high_row = column.rows(near_sum[f : f + 1])
        lap = column_sum(total, row_id, low_row, high_row) - 27.0 * now
        coef = pieces.piece(f)
        coefs.append(coef(tile0))
        stepped.append(drift_ref[0, f, :, tile0] + coefs[f] * lap)
        nexts.append(drift_ref[0, f, :, tile1] + coef(tile1) * box_ref[f, :, tile1])
    box = near_sum + beyond_sum + jnp.concatenate(rims, axis=0)
    edge = column.ahead(0, tile0) + column.coefs(0, tile0) * (box - 27.0 * near)
    edge_sum = nine_sum([corners[2], edge, tail_ref[0:4, :]], lane)[1]
    for f in range(fields):
        total = nine_sum([pltpu.roll(before[f], 32, 1), stepped[f], nexts[f]], lane)[1]
        row = edge_sum[f : f + 1]
        tile_ref[f] = second_step(stepped[f], u_ref[0, f, :, tile0], total, coefs[f], row_id, row, column.lower)
    decode(code_ref, arrived_ref)

    slot = jnp.where(arrives, 1, 0)
    moves_on = jnp.logical_and(arrives, owner_ref[1] == lax.axis_index("blk"))
    last = pltpu.make_async_copy(tile_ref, out_ref.at[slot, :, :, tile0], sems.at[2])
    coming = code_copies(0, arrived_ref, out_ref, sems, 3) + first_copies(row_ref, out_ref, 1, sems, 3 + 2 * half)
    lasts = last_copies(last_a_ref, last_b_ref, out_ref, 2, sems, 3 + 2 * half + fields)
    last.start()

    @pl.when(arrives)
    def _():
        for copy in coming:
            copy.start()

    @pl.when(moves_on)
    def _():
        for copy in lasts:
            copy.start()
        for copy in lasts:
            copy.wait()

    @pl.when(arrives)
    def _():
        for copy in coming:
            copy.wait()

    last.wait()


def place_body(first, code_a_ref, code_ref, partial_ref, out_ref, row_ref, sems):
    arrives = arrival(code_a_ref)
    decode(code_ref, row_ref)
    copies = code_copies(first, row_ref, out_ref, sems, 0)

    @pl.when(arrives)
    def _():
        for copy in copies:
            copy.start()
        for copy in copies:
            copy.wait()


def fast_on_device(u_now, u_prev, coef_store, store_map, new_owner):
    blocks, _, fields, depth, width = u_now.shape
    now = u_now.reshape(blocks, fields, depth, width)
    prev = u_prev.reshape(blocks, fields, depth, width)
    coef = coef_store[0, 0]
    count = lax.axis_size("blk")
    order = store_map.reshape(-1)
    order_hbm, now_hbm, prev_hbm, coef_hbm = (
        pltpu.with_memory_space_constraint(array, pltpu.HBM) for array in (order, now, prev, coef)
    )
    params = pltpu.CompilerParams(vmem_limit_bytes=48 * 1024 * 1024)

    def call(body, name, out_shape, in_specs, out_specs, scratch, args, **options):
        return pl.pallas_call(
            body,
            out_shape=out_shape,
            in_specs=in_specs,
            out_specs=out_specs,
            scratch_shapes=scratch,
            compiler_params=params,
            name=name,
            **options,
        )(*args)

    straight = jax.ShapeDtypeStruct((fields * depth + 16, LANES), BF16)
    diag = jax.ShapeDtypeStruct((depth + 32, LANES), BF16)
    sources = (order_hbm, now_hbm, prev_hbm, coef_hbm)
    y_out = call(
        pack_region_body,
        "pack_region",
        jax.ShapeDtypeStruct((5, depth, width), BF16),
        [HBM] * 4,
        VMEM,
        [
            pltpu.VMEM((depth, width), F32),
            pltpu.VMEM((blocks, fields, 8, width), F32),
            pltpu.VMEM((blocks, fields, 8, width), F32),
            pltpu.VMEM((4, 16, width), BF16),
            pltpu.SMEM(order.shape, jnp.int32),
            pltpu.SemaphoreType.DMA((12,)),
        ],
        sources,
    )
    left, dleft = call(
        pack_back_body,
        "pack_back",
        (straight, diag),
        [HBM] * 4,
        (VMEM,) * 2,
        [
            pltpu.VMEM((1, fields, 8, LANES), F32),
            pltpu.VMEM((1, fields, 8, LANES), F32),
            pltpu.VMEM((4, 16, LANES), BF16),
            pltpu.VMEM((fields, depth, LANES), F32),
            pltpu.VMEM((fields, depth, LANES), F32),
            pltpu.VMEM((2, 4, depth, LANES), BF16),
            pltpu.SMEM(order.shape, jnp.int32),
            pltpu.SemaphoreType.DMA((7,)),
        ],
        sources,
    )
    swap = [(0, 1), (1, 0)]
    forward = [(i, (i + 1) % count) for i in range(count)]
    backward = [(i, (i - 1) % count) for i in range(count)]
    crossed = [(r * count + i, (1 - r) * count + (i - 1) % count) for r in range(2) for i in range(count)]
    y_in = lax.ppermute(y_out, "region", swap)
    from_right = lax.ppermute(left, "blk", backward)
    from_dright = lax.ppermute(dleft, ("region", "blk"), crossed)

    row = jax.ShapeDtypeStruct((fields, depth, width), F32)
    box0, box1, drift, rim = call(
        local_body,
        "local",
        (row, row, jax.ShapeDtypeStruct(now.shape, F32), jax.ShapeDtypeStruct((blocks, 8, width), F32)),
        [VMEM] * 2,
        (VMEM,) * 4,
        [],
        (now, prev),
    )
    tiles = jax.ShapeDtypeStruct((fields, depth, LANES), F32)
    sums = jax.ShapeDtypeStruct((8, width), F32)
    tail = jax.ShapeDtypeStruct((8, LANES), F32)
    box1, side_lap, side_coef, side_rim = call(
        border_body,
        "border",
        (row, tiles, tiles, jax.ShapeDtypeStruct((2, 8, LANES), F32)),
        [VMEM] * 4,
        (VMEM,) * 4,
        [],
        (now, from_right, from_dright, box1),
        input_output_aliases={3: 0},
        cost_estimate=pl.CostEstimate(flops=0, transcendentals=0, bytes_accessed=40_000_000),
    )
    half = fields // 2
    part = jax.ShapeDtypeStruct((half, depth, width), F32)
    tiled = half * width // LANES
    codes = jax.ShapeDtypeStruct((tiled * (depth + 1), LANES), jnp.int16)
    more_codes = jax.ShapeDtypeStruct((tiled * (depth + 1) + half * depth + 8, LANES), jnp.int16)
    scalars = [pltpu.SMEM(order.shape, jnp.int32), pltpu.SMEM(new_owner.shape, jnp.int32)]
    powers = pltpu.VMEM((tiled, LANES), F32)
    box1, lap1, side1, sums1, last_a, code_a = call(
        last_row_a_body,
        "last_row",
        (row, tiles, tiles, sums, part, more_codes),
        [ANY] * 2 + [VMEM] * 12,
        (VMEM,) * 6,
        [powers, pltpu.VMEM((8, LANES), F32)] + scalars + [pltpu.SemaphoreType.DMA((2,))],
        (order, new_owner, now, coef, y_in, from_right, from_dright, box0, rim, side_lap, side_coef, side_rim, drift, box1),
        input_output_aliases={13: 0},
    )
    arrived_a = lax.ppermute(code_a, "blk", forward)
    last_b, code_b = call(
        functools.partial(last_row_b_body, half),
        "last_row",
        (part, codes),
        [ANY] + [VMEM] * 8,
        (VMEM,) * 2,
        [powers, scalars[0], pltpu.SemaphoreType.DMA],
        (order, now, coef, y_in, box1, drift, lap1, side1, sums1),
    )
    arrived_b = lax.ppermute(code_b, "blk", forward)
    box0, sums0, tail0 = call(
        first_edges_body,
        "first_edges",
        (row, sums, tail),
        [VMEM] * 6,
        (VMEM,) * 3,
        [],
        (now, coef, y_in, box1, rim, box0),
        input_output_aliases={5: 0},
    )
    first = call(
        first_row_body,
        "first_row",
        row,
        [SMEM] + [VMEM] * 7,
        VMEM,
        [],
        (order, now, coef, y_in, box0, box1, drift, sums0),
    )
    whole = jax.ShapeDtypeStruct((blocks + 1, fields, depth, width), F32)
    placed = call(
        rows_body,
        "rows",
        whole,
        [SMEM] + [VMEM] * 3,
        ANY,
        [pltpu.VMEM((depth, width), F32), pltpu.SemaphoreType.DMA((3 * fields,))],
        (new_owner, first, last_a, last_b),
    )
    arrived_half = pltpu.VMEM((half, depth, width), F32)
    placed = call(
        finish_body,
        "finish",
        whole,
        [ANY] * 2 + [VMEM] * 10 + [ANY],
        ANY,
        [pltpu.VMEM((fields, depth, LANES), F32), arrived_half]
        + scalars
        + [pltpu.SemaphoreType.DMA((3 + 2 * half + 2 * fields,))],
        (new_owner, order, now, coef, y_in, box0, drift, tail0, arrived_a, first, last_a, last_b, placed),
        input_output_aliases={12: 0},
    )
    placed = call(
        functools.partial(place_body, half),
        "place",
        whole,
        [VMEM, VMEM, ANY],
        ANY,
        [arrived_half, pltpu.SemaphoreType.DMA((2 * half,))],
        (arrived_a, arrived_b, placed),
        input_output_aliases={2: 0},
    )
    return placed[:, None]


def solution(mesh):
    def on_device(*args):
        blocks = args[0].shape[0]
        if lax.axis_size("region") == 2 and blocks == 2:
            return fast_on_device(*args)
        return general_on_device(*args)

    return jax.shard_map(
        on_device,
        mesh=mesh,
        in_specs=(
            P("blk", "region", None, None, None),
            P("blk", "region", None, None, None),
            P("blk", "region", None, None, None, None),
            P("blk", "region", None),
            P("blk"),
        ),
        out_specs=P("blk", "region", None, None, None),
        check_vma=False,
    )
```

```python
import functools

import jax
import jax.numpy as jnp
from jax import lax
from jax.experimental import pallas as pl
from jax.experimental.pallas import tpu as pltpu
from jax.sharding import PartitionSpec as P

STEPS = 2
LANES = 128
F32 = jnp.float32
BF16 = jnp.bfloat16
VMEM = pl.BlockSpec(memory_space=pltpu.VMEM)
SMEM = pl.BlockSpec(memory_space=pltpu.SMEM)
ANY = pl.BlockSpec(memory_space=pl.ANY)
HBM = pl.BlockSpec(memory_space=pltpu.HBM)


def extended_2(block, sides, width, periodic):
    for axis, dim in sides:
        count = lax.axis_size(axis)
        forward = [(i, i + 1) for i in range(count - 1)]
        if periodic:
            forward.append((count - 1, 0))
        backward = [(target, source) for source, target in forward]
        low = lax.ppermute(
            lax.slice_in_dim(block, block.shape[dim] - width, None, axis=dim), axis, forward
        )
        high = lax.ppermute(lax.slice_in_dim(block, 0, width, axis=dim), axis, backward)
        block = jnp.concatenate([low, block, high], axis=dim)
    return block


def shifted_2(value, axis, by):
    devices = lax.axis_size(axis)
    return lax.ppermute(value, axis, [(i, (i + by) % devices) for i in range(devices)])


def stencil_step(state_now, state_prev, coefficient, live_count):
    slot_count, field_count, edge_cells, plane_cells = state_now.shape
    padded = extended_2(state_now, (("region", 2),), 1, False)
    first_planes = padded[..., :edge_cells]
    last_planes = padded[..., plane_cells - edge_cells :]
    last_live = jnp.take(last_planes, live_count - 1, axis=0)
    rim_pair = jnp.stack([first_planes[0], last_live], axis=2)
    spread = extended_2(rim_pair.astype(jnp.bfloat16), (("blk", 2),), 1, True).astype(
        rim_pair.dtype
    )
    left_rim = spread[:, :, 0]
    right_rim = spread[:, :, 3]
    before_planes = jnp.concatenate([left_rim[None], last_planes[:-1]], axis=0)
    after_planes = jnp.pad(first_planes[1:], ((0, 1), (0, 0), (0, 0), (0, 0)))
    slot_ids = jnp.arange(slot_count)
    after_planes = jnp.where(
        (slot_ids == live_count - 1)[:, None, None, None], right_rim[None], after_planes
    )
    extended = jnp.concatenate([before_planes, padded, after_planes], axis=-1)
    width = extended.shape[-1]
    column = jnp.arange(width) % edge_cells
    lower_mask = (column != 0).astype(jnp.float32)
    upper_mask = (column != edge_cells - 1).astype(jnp.float32)
    margin = ((0, 0), (0, 0), (0, 0), (1, 1))
    shifted = jnp.pad(extended, margin)
    summed = shifted[..., :width] * lower_mask + extended + shifted[..., 2:] * upper_mask
    summed = (
        summed[..., : -2 * edge_cells]
        + summed[..., edge_cells:-edge_cells]
        + summed[..., 2 * edge_cells :]
    )
    box_sum = summed[:, :, :-2] + summed[:, :, 1:-1] + summed[:, :, 2:]
    laplace = box_sum - 27.0 * state_now
    return 2.0 * state_now - state_prev + coefficient.astype(jnp.float32) * laplace


def compact(members, valid_flags):
    slot_count = valid_flags.shape[0]
    place_index = jnp.cumsum(valid_flags) - 1
    target = jnp.arange(slot_count)
    chooser = (valid_flags[None, :] == 1) & (place_index[None, :] == target[:, None])
    source = jnp.sum(jnp.where(chooser, target[None, :], 0), axis=1)
    filled = jnp.sum(chooser.astype(jnp.int32), axis=1) > 0
    placed = tuple(
        (
            jnp.where(
                filled.reshape((slot_count,) + (1,) * (member.ndim - 1)),
                jnp.take(member, source, axis=0),
                jnp.zeros_like(member),
            )
            for member in members
        )
    )
    return (placed, jnp.sum(valid_flags))


def general_on_device(u_now, u_prev, coef_store, store_map, new_owner):
    state_now = u_now[:, 0]
    state_prev = u_prev[:, 0]
    blocks, fields, edge_cells, plane_cells = state_now.shape
    store_local = coef_store[0, 0]
    arrived = lax.all_to_all(store_local, "region", split_axis=0, concat_axis=0, tiled=True)
    flattened = arrived.reshape((-1,) + arrived.shape[2:])
    inverse = jnp.argsort(store_map[0, 0])
    coefficient = jnp.take(flattened, inverse, axis=0).reshape(
        blocks, fields, edge_cells, plane_cells
    )
    own_index = lax.axis_index("blk")
    goes_right = new_owner[blocks - 1] != own_index
    mark_right = goes_right.astype(jnp.float32).reshape(1)
    middle_flags = jnp.ones((blocks - 2,), jnp.int32)
    keep_first = (new_owner[0] == own_index).astype(jnp.int32).reshape(1)
    keep_last = (new_owner[blocks - 1] == own_index).astype(jnp.int32).reshape(1)
    for step_index in range(STEPS):
        state_now, state_prev = (
            stencil_step(state_now, state_prev, coefficient, blocks),
            state_now,
        )
    from_left = shifted_2((state_now[blocks - 1], mark_right), "blk", 1)
    valid_flags = jnp.concatenate(
        [(from_left[1] > 0.5).astype(jnp.int32), keep_first, middle_flags, keep_last]
    )
    stacked_now = jnp.concatenate([from_left[0][None], state_now], axis=0)
    placed, live_count = compact((stacked_now,), valid_flags)
    result = placed[0]
    return result[:, None]


def lane_ids():
    return lax.broadcasted_iota(jnp.int32, (1, LANES), 1)


def edge_start(lower, depth, size):
    return pl.multiple_of(jnp.where(lower, depth - size, 0), size)


def pack_region_body(
    map_hbm, u_ref, p_ref, coef_ref, y_ref, edges_ref, ua_ref, pa_ref, ca_ref, ue_ref, pe_ref, ce_ref, map_ref, sems
):
    fields, depth, width = u_ref.shape[1:]
    region = lax.axis_index("region")
    lower = region == 0
    other = 1 - region
    half = depth // 2
    front = slice(0, LANES)
    edge8 = edge_start(lower, depth, 8)
    edge16 = edge_start(lower, depth, 16)
    slab = []
    for s in range(4):
        for h in range(2):
            part = slice(h * half, (h + 1) * half)
            slab.append(pltpu.make_async_copy(coef_ref.at[other, s, part], y_ref.at[s, part], sems.at[7 + 2 * s + h]))
    copies = [
        pltpu.make_async_copy(map_hbm, map_ref, sems.at[0]),
        pltpu.make_async_copy(u_ref.at[:, :, pl.ds(edge8, 8), :], ue_ref, sems.at[1]),
        pltpu.make_async_copy(p_ref.at[:, :, pl.ds(edge8, 8), :], pe_ref, sems.at[2]),
        pltpu.make_async_copy(coef_ref.at[region, :, pl.ds(edge16, 16), :], ce_ref, sems.at[3]),
    ]
    beside = [
        pltpu.make_async_copy(u_ref.at[0, :, :, front], ua_ref, sems.at[4]),
        pltpu.make_async_copy(p_ref.at[0, :, :, front], pa_ref, sems.at[5]),
        pltpu.make_async_copy(coef_ref.at[:, :, :, front], ca_ref, sems.at[6]),
    ]
    for copy in copies + slab + beside:
        copy.start()
    for copy in copies:
        copy.wait()
    own_edge = jnp.where(lower, 7, 0)
    own_next = jnp.where(lower, 6, 1)
    for m in range(2):
        for f in range(fields):
            at = m * fields + f
            near = ue_ref[m, f, pl.ds(own_edge, 1), :]
            edges_ref[at : at + 1, :] = near
            edges_ref[8 + at : 9 + at, :] = ue_ref[m, f, pl.ds(own_next, 1), :]
            edges_ref[16 + at : 17 + at, :] = 2.0 * near - pe_ref[m, f, pl.ds(own_edge, 1), :]
    for s in range(4):
        piece = ce_ref[s].astype(F32)
        edges_ref[24 + s : 25 + s, :] = jnp.where(lower, piece[15:16], piece[0:1])
    numbers = [map_ref[region * 4 + s] for s in range(4)] + [map_ref[other * 4 + s] for s in range(4)]
    for i, number in enumerate(numbers):
        edges_ref[28:29, tile_at(i)] = jnp.zeros((1, LANES), F32) + number.astype(F32)
    edges_ref[29:32, :] = jnp.zeros((3, width), F32)
    y_ref[4] = edges_ref[...].astype(BF16)
    for copy in slab + beside:
        copy.wait()


def pack_back_body(edges_ref, ua_ref, pa_ref, ca_ref, straight_ref, diag_ref):
    fields, depth, _ = ua_ref.shape
    region = lax.axis_index("region")
    lower = region == 0
    other = 1 - region
    lane = lane_ids()
    tag_rows = [edges_ref[28:29, tile_at(i)] for i in range(8)]
    blank = jnp.zeros((1, LANES), F32)
    for f in range(fields):
        now = ua_ref[f]
        ahead = 2.0 * now - pa_ref[f]
        piece = ca_ref[region, f].astype(F32)
        tile = jnp.where(
            lane < 64, now, jnp.where(lane < 96, pltpu.roll(ahead, 64, 1), pltpu.roll(piece, 96, 1))
        )
        straight_ref[f * depth : (f + 1) * depth, :] = tile.astype(BF16)
    far = [ca_ref[other, s].astype(F32) for s in range(4)]
    extra = [jnp.where(lower, piece[0:1], piece[depth - 1 : depth]) for piece in far] + tag_rows + [blank] * 4
    straight_ref[fields * depth : fields * depth + 16, :] = jnp.concatenate(extra, axis=0).astype(BF16)
    plane = jnp.zeros((depth, LANES), F32)
    for s in range(4):
        moved = pltpu.roll(far[s], 32 * s, 1) if s else far[s]
        plane = jnp.where((lane >= 32 * s) & (lane < 32 * s + 32), moved, plane)
    diag_ref[0:depth, :] = plane.astype(BF16)
    rows = [edges_ref[base : base + 4, 0:LANES] for base in (0, 8, 16, 24)]
    diag_ref[depth : depth + 32, :] = jnp.concatenate(rows + tag_rows + [blank] * 8, axis=0).astype(BF16)


def nine_sum(tiles, lane, first=0):
    inside = lane % 32
    low = inside != 0
    high = inside != 31
    rows = []
    for tile in tiles:
        rows.append(
            tile
            + jnp.where(low, pltpu.roll(tile, 1, 1), 0.0)
            + jnp.where(high, pltpu.roll(tile, LANES - 1, 1), 0.0)
        )
    up = [pltpu.roll(row, 32, 1) for row in rows]
    down = [pltpu.roll(row, LANES - 32, 1) for row in rows]
    count = len(tiles)
    result = []
    for t in range(count):
        before = up[t] if t == 0 else jnp.where(lane < 32, up[t - 1], up[t])
        after = down[t] if t == count - 1 else jnp.where(lane >= 96, down[t + 1], down[t])
        result.append(rows[t] + before + after)
    return result


def column_sum(tile, row_id, low_row, high_row):
    depth = tile.shape[0]
    above = pltpu.roll(tile, 1, 0)
    below = pltpu.roll(tile, depth - 1, 0)
    return tile + jnp.where(row_id == 0, low_row, above) + jnp.where(row_id == depth - 1, high_row, below)


def local_body(u_ref, p_ref, box0_ref, box1_ref, drift_ref, rim_ref):
    fields, depth, width = u_ref.shape[1:]
    main = width // LANES
    lower = lax.axis_index("region") == 0
    lane = lane_ids()
    row_id = lax.broadcasted_iota(jnp.int32, (depth, 1), 0)
    boxes = (box0_ref, box1_ref)
    for f in range(fields):
        now = [u_ref[m, f, :, tile_at(t)] for m in range(2) for t in range(main)]
        sums = nine_sum(now, lane)
        for i, (tile, total) in enumerate(zip(now, sums)):
            m, t = divmod(i, main)
            lanes = tile_at(t)
            rim_ref[m, f : f + 1, lanes] = jnp.where(lower, total[depth - 1 : depth], total[0:1])
            boxes[m][f, :, lanes] = column_sum(total, row_id, 0.0, 0.0) - 27.0 * tile
            drift_ref[m, f, :, lanes] = 2.0 * tile - p_ref[m, f, :, lanes]
    rim_ref[:, 4:8, :] = jnp.zeros((2, 4, width), F32)


def tile_at(t):
    return slice(t * LANES, (t + 1) * LANES)


class ColumnEdge:
    def __init__(self, coef_ref, y_ref):
        self.region = lax.axis_index("region")
        self.lower = self.region == 0
        self.coef = coef_ref
        self.depth = coef_ref.shape[2]
        self.extra = y_ref[4].astype(F32)
        self.tags = [self.extra[28:29, i * LANES : (i + 1) * LANES] for i in range(8)]
        self.field_id = lax.broadcasted_iota(jnp.int32, (4, LANES), 0).astype(F32)

    def near(self, m, lanes):
        return self.extra[4 * m : 4 * m + 4, lanes]

    def beyond(self, m, lanes):
        return self.extra[8 + 4 * m : 12 + 4 * m, lanes]

    def ahead(self, m, lanes):
        return self.extra[16 + 4 * m : 20 + 4 * m, lanes]

    def coefs(self, m, lanes):
        total = jnp.zeros((4, LANES), F32)
        for s in range(4):
            piece = self.coef[1 - self.region, s, :, lanes].astype(F32)
            held = jnp.where(self.lower, piece[0:1], piece[self.depth - 1 : self.depth])
            total = total + jnp.where(self.tags[s] == self.field_id + 4 * m, self.extra[24 + s : 25 + s, lanes], 0.0)
            total = total + jnp.where(self.tags[4 + s] == self.field_id + 4 * m, held, 0.0)
        return total

    def own(self, tile):
        return jnp.where(self.lower, tile[self.depth - 1 : self.depth], tile[0:1])

    def rows(self, row):
        return jnp.where(self.lower, 0.0, row), jnp.where(self.lower, row, 0.0)


def border_body(u_ref, straight_ref, diag_ref, box_in, box_ref, side_lap_ref, side_coef_ref, rim_ref):
    fields, depth, width = u_ref.shape[1:]
    lane = lane_ids()
    row_id = lax.broadcasted_iota(jnp.int32, (depth, 1), 0)
    lower = lax.axis_index("region") == 0
    before = slice(width - LANES, width)
    facing = lane >= 96
    tags = [straight_ref[fields * depth : fields * depth + 16, :].astype(F32)[4 + i : 5 + i] for i in range(8)]
    planes = []
    for s in range(4):
        planes.append(pltpu.roll(straight_ref[s * depth : (s + 1) * depth, :].astype(F32), 32, 1))
    diag_tile = diag_ref[0:depth, :].astype(F32)
    for s in range(4):
        planes.append(pltpu.roll(diag_tile, LANES - 32 * s, 1) if s else diag_tile)
    for f in range(fields):
        inner = u_ref[1, f, :, before]
        remote = straight_ref[f * depth : (f + 1) * depth, :].astype(F32)
        inner_sum, remote_sum = nine_sum([inner, remote], lane)
        for i, tile in enumerate((inner_sum, remote_sum)):
            rim_ref[i, f : f + 1, :] = jnp.where(lower, tile[depth - 1 : depth], tile[0:1])
        halo_c = jnp.zeros((depth, LANES), F32)
        for i in range(8):
            halo_c = halo_c + jnp.where(tags[i] == F32(f), planes[i], 0.0)
        side_coef_ref[f] = halo_c
        side_lap_ref[f] = column_sum(remote_sum, row_id, 0.0, 0.0) - 27.0 * remote
        whole = column_sum(inner_sum, row_id, 0.0, 0.0) - 27.0 * inner
        box_ref[f, :, before] = jnp.where(facing, whole, box_in[f, :, before])
    rim_ref[:, 4:8, :] = jnp.zeros((2, 4, LANES), F32)


def last_edges(
    coef_ref, y_ref, straight_ref, diag_ref, box0_ref, rim_ref, side_lap_ref, side_coef_ref, side_rim_ref, box_in,
    box_ref, lap_ref, side_ref, sums_ref
):
    fields, depth, width = box_in.shape
    main = width // LANES
    lane = lane_ids()
    column = ColumnEdge(coef_ref, y_ref)
    before = slice(width - LANES, width)
    extra_s = straight_ref[fields * depth : fields * depth + 16, :].astype(F32)
    extra_d = diag_ref[depth : depth + 32, :].astype(F32)
    tags_d = [extra_d[16 + i : 17 + i] for i in range(8)]

    def edge_tiles(of, base):
        return [of(0, before)] + [of(1, tile_at(t)) for t in range(main)] + [extra_d[base : base + 4]]

    near = edge_tiles(column.near, 0)
    beyond = edge_tiles(column.beyond, 4)
    ahead = edge_tiles(column.ahead, 8)
    corner = jnp.zeros((4, LANES), F32)
    for s in range(4):
        corner = corner + jnp.where(tags_d[s] == column.field_id, extra_d[12 + s : 13 + s], 0.0)
        corner = corner + jnp.where(tags_d[4 + s] == column.field_id, extra_s[s : s + 1], 0.0)
    edge_c = [column.coefs(0, before)] + [column.coefs(1, tile_at(t)) for t in range(main)] + [corner]
    near_sum = nine_sum(near, lane)
    beyond_sum = nine_sum(beyond, lane)
    top = slice(0, 1)
    bottom = slice(depth - 1, depth)
    for f in range(fields):
        for t in range(main):
            low_row, high_row = column.rows(near_sum[t + 1][f : f + 1])
            lanes = tile_at(t)
            box_ref[f, top, lanes] = box_in[f, top, lanes] + low_row
            box_ref[f, bottom, lanes] = box_in[f, bottom, lanes] + high_row
        remote = straight_ref[f * depth : (f + 1) * depth, :].astype(F32)
        side_ref[f] = pltpu.roll(remote, 64, 1) + side_coef_ref[f] * side_lap_ref[f]
        low_row, high_row = column.rows(near_sum[main + 1][f : f + 1])
        side_ref[f, top] += side_coef_ref[f, top] * low_row
        side_ref[f, bottom] += side_coef_ref[f, bottom] * high_row
        low_row, high_row = column.rows(near_sum[0][f : f + 1])
        lap_ref[f] = box0_ref[f, :, before]
        lap_ref[f, top] += low_row
        lap_ref[f, bottom] += high_row
    rims = [rim_ref[0, 0:4, before]] + [rim_ref[1, 0:4, tile_at(t)] for t in range(main)] + [side_rim_ref[1, 0:4, :]]
    rims[main] = jnp.where(lane >= 96, side_rim_ref[0, 0:4, :], rims[main])
    stepped = []
    for t in range(main + 2):
        box = near_sum[t] + beyond_sum[t] + rims[t]
        stepped.append(ahead[t] + edge_c[t] * (box - 27.0 * near[t]))
    stepped_sum = nine_sum(stepped, lane)
    for t in range(main):
        sums_ref[0:4, tile_at(t)] = stepped_sum[t + 1]
    sums_ref[4:8, :] = jnp.zeros((4, width), F32)
    return stepped[main]


def first_edges_body(
    u_ref, coef_ref, y_ref, box1_ref, rim_ref, box_in, box_ref, sums_ref, tail_ref
):
    fields, depth, width = u_ref.shape[1:]
    main = width // LANES
    lane = lane_ids()
    column = ColumnEdge(coef_ref, y_ref)
    after = slice(0, LANES)

    def edge_tiles(of):
        return [of(0, tile_at(t)) for t in range(main)] + [of(1, after)]

    near = edge_tiles(column.near)
    near_sum = nine_sum(near, lane)
    beyond_sum = nine_sum(edge_tiles(column.beyond), lane)
    ahead = edge_tiles(column.ahead)
    edge_c = edge_tiles(column.coefs)
    for f in range(fields):
        for t in range(main):
            low_row, high_row = column.rows(near_sum[t][f : f + 1])
            lanes = tile_at(t)
            box_ref[f, 0:1, lanes] = box_in[f, 0:1, lanes] + low_row
            box_ref[f, depth - 1 : depth, lanes] = box_in[f, depth - 1 : depth, lanes] + high_row
    rims = [rim_ref[0, 0:4, tile_at(t)] for t in range(main)] + [rim_ref[1, 0:4, after]]
    stepped = []
    for t in range(main + 1):
        box = near_sum[t] + beyond_sum[t] + rims[t]
        stepped.append(ahead[t] + edge_c[t] * (box - 27.0 * near[t]))
    stepped_sum = nine_sum(stepped, lane)
    for t in range(main):
        sums_ref[0:4, tile_at(t)] = stepped_sum[t]
    sums_ref[4:8, :] = jnp.zeros((4, width), F32)
    tail_ref[0:4, :] = stepped[1]
    tail_ref[4:8, :] = jnp.zeros((4, LANES), F32)


def load_map(map_any, map_ref, sem):
    copy = pltpu.make_async_copy(map_any, map_ref, sem)
    copy.start()
    return copy


class Pieces:
    def __init__(self, map_ref, coef_ref, slab_ref):
        self.coef, self.slab = coef_ref, slab_ref
        self.region = lax.axis_index("region")
        self.numbers = [map_ref[q] for q in range(8)]

    def piece(self, number):
        place = jnp.int32(0)
        for q in range(8):
            place = jnp.where(self.numbers[q] == number, q, place)
        slot = place & 3
        held = (place >> 2) == self.region

        def tile(lanes):
            return jnp.where(held, self.coef[self.region, slot, :, lanes], self.slab[slot, :, lanes]).astype(F32)

        return tile


def second_step(now, before, total, coef, row_id, row, lower):
    low_row, high_row = jnp.where(lower, 0.0, row), jnp.where(lower, row, 0.0)
    lap = column_sum(total, row_id, low_row, high_row) - 27.0 * now
    return 2.0 * now - before + coef * lap


CODES = 32000.0


def power_of(size):
    return jnp.ceil(jnp.log2(jnp.maximum(size, 1e-30)))


def coded(value, power):
    return jnp.floor(value * (CODES * jnp.exp2(-power)) + 0.5)


def narrow(value):
    return value.astype(jnp.int32).astype(jnp.int16)


def wide(code):
    return code.astype(jnp.int32).astype(F32)


def scale_of(power):
    return jnp.exp2(power) * (1.0 / CODES)


def last_row_a_body(
    map_any, owner_any, u_ref, coef_ref, y_ref, straight_ref, diag_ref, box0_ref, rim_ref, side_lap_ref, side_coef_ref,
    side_rim_ref, drift_ref, box_in, box_ref, lap_ref, side_ref, sums_ref, row_ref, code_ref, power_ref, extra_ref,
    map_ref, owner_ref, sems
):
    copies = [load_map(map_any, map_ref, sems.at[0]), load_map(owner_any, owner_ref, sems.at[1])]
    tail = last_edges(
        coef_ref, y_ref, straight_ref, diag_ref, box0_ref, rim_ref, side_lap_ref, side_coef_ref, side_rim_ref, box_in,
        box_ref, lap_ref, side_ref, sums_ref
    )
    for copy in copies:
        copy.wait()
    more = (owner_ref, tail, extra_ref)
    refs = (map_ref, u_ref, coef_ref, y_ref, box_ref, drift_ref, lap_ref, side_ref, sums_ref, row_ref, code_ref, power_ref)
    last_row(0, *refs, more=more)


def last_row_b_body(first, map_any, *refs):
    map_ref, sem = refs[-2:]
    load_map(map_any, map_ref, sem).wait()
    last_row(first, map_ref, *refs[:-2])


def last_row(
    first, map_ref, u_ref, coef_ref, y_ref, box_ref, drift_ref, lap_ref, side_ref, sums_ref, row_ref, code_ref, power_ref,
    more=None
):
    count, depth, width = row_ref.shape
    fields = u_ref.shape[1]
    main = width // LANES
    lane = lane_ids()
    row_id = lax.broadcasted_iota(jnp.int32, (depth, 1), 0)
    pieces = Pieces(map_ref, coef_ref, y_ref)
    lower = pieces.region == 0
    before = slice(width - LANES, width)
    last_tiles = []
    for f in range(first, first + count):
        coef = pieces.piece(fields + f)
        coefs = [coef(tile_at(t)) for t in range(main)]
        middle = [drift_ref[1, f, :, tile_at(t)] + coefs[t] * box_ref[f, :, tile_at(t)] for t in range(main)]
        local = drift_ref[0, f, :, before] + pieces.piece(f)(before) * lap_ref[f]
        sums = nine_sum([local] + middle + [side_ref[f]], lane)
        for t in range(main):
            lanes = tile_at(t)
            row = sums_ref[f : f + 1, lanes]
            value = second_step(middle[t], u_ref[1, f, :, lanes], sums[t + 1], coefs[t], row_id, row, lower)
            row_ref[f - first, :, lanes] = value
            power = power_of(jnp.max(jnp.abs(value), axis=0, keepdims=True))
            at = (f - first) * main + t
            code_ref[at * depth : (at + 1) * depth, :] = narrow(coded(value, power))
            power_ref[at : at + 1, :] = power
        last_tiles.append(middle[main - 1])
    base = count * main * depth
    code_ref[base : base + count * main, :] = narrow(power_ref[...])
    if more is not None:
        owner_ref, tail, extra_ref = more
        base += count * main
        both = []
        for f in range(fields):
            if f < count:
                stepped = last_tiles[f]
            else:
                stepped = drift_ref[1, f, :, before] + pieces.piece(fields + f)(before) * box_ref[f, :, before]
            both.append(jnp.where(lane >= 96, u_ref[1, f, :, before], pltpu.roll(stepped, 96, 1)))
        for g in range(fields // 2):
            pair = jnp.where(lane >= 64, both[2 * g], pltpu.roll(both[2 * g + 1], 64, 1))
            power = power_of(jnp.max(jnp.abs(pair), axis=0, keepdims=True))
            code_ref[base : base + depth, :] = narrow(coded(pair, power))
            extra_ref[g : g + 1, :] = power
            base += depth
        near = y_ref[4, 0:16, before].astype(F32)
        kinds = []
        for rows in (near[4:8], near[12:16], tail):
            kind = jnp.zeros((1, LANES), F32)
            for f in range(fields):
                shift = (32 * f + 32) % LANES
                row = rows[f : f + 1]
                kind = jnp.where(lane // 32 == f, pltpu.roll(row, shift, 1) if shift else row, kind)
            kinds.append(kind)
        power = power_of(jnp.maximum(jnp.maximum(jnp.abs(kinds[0]), jnp.abs(kinds[1])), jnp.abs(kinds[2])))
        extra_ref[2:3, :] = power
        for i, kind in enumerate(kinds):
            extra_ref[3 + i : 4 + i, :] = coded(kind, power)
        moves = jnp.where(owner_ref[1] != lax.axis_index("blk"), 1.0, 0.0)
        extra_ref[6:7, :] = jnp.zeros((1, LANES), F32) + moves
        extra_ref[7:8, :] = jnp.zeros((1, LANES), F32)
        code_ref[base : base + 8, :] = narrow(extra_ref[...])


def first_row_body(map_ref, u_ref, coef_ref, y_ref, box_ref, box1_ref, drift_ref, sums_ref, row_ref):
    fields, depth, width = u_ref.shape[1:]
    main = width // LANES
    lane = lane_ids()
    row_id = lax.broadcasted_iota(jnp.int32, (depth, 1), 0)
    pieces = Pieces(map_ref, coef_ref, y_ref)
    lower = pieces.region == 0
    after = slice(0, LANES)
    for f in range(fields):
        coef = pieces.piece(f)
        coefs = [coef(tile_at(t)) for t in range(main)]
        now = [drift_ref[0, f, :, tile_at(t)] + coefs[t] * box_ref[f, :, tile_at(t)] for t in range(main)]
        local = drift_ref[1, f, :, after] + pieces.piece(fields + f)(after) * box1_ref[f, :, after]
        sums = nine_sum(now + [local], lane)
        for t in range(1, main):
            lanes = tile_at(t)
            row = sums_ref[f : f + 1, lanes]
            row_ref[f, :, lanes] = second_step(now[t], u_ref[0, f, :, lanes], sums[t], coefs[t], row_id, row, lower)


def arrival(code_ref):
    rows = code_ref.shape[0]
    return jnp.max(wide(code_ref[rows - 8 : rows, :])[6:7]) > 0.5


def code_copies(first, row_ref, out_ref, sems, base):
    count, depth, _ = row_ref.shape
    part = depth // 2
    copies = []
    for f in range(count):
        for h in range(2):
            rows = slice(h * part, (h + 1) * part)
            sem = sems.at[base + 2 * f + h]
            copies.append(pltpu.make_async_copy(row_ref.at[f, rows], out_ref.at[0, first + f, rows], sem))
    return copies


def decode(code_ref, row_ref):
    count, depth, width = row_ref.shape
    main = width // LANES
    base = count * main * depth
    scale = scale_of(wide(code_ref[base : base + count * main, :]))
    for f in range(count):
        for t in range(main):
            at = f * main + t
            row_ref[f, :, tile_at(t)] = wide(code_ref[at * depth : (at + 1) * depth, :]) * scale[at : at + 1]


def row_copies(owner_ref, row_ref, last_a_ref, last_b_ref, zero_ref, out_ref, at, sems, base):
    fields, _, width = row_ref.shape
    half = last_a_ref.shape[0]
    keeps = owner_ref[1] == lax.axis_index("blk")
    rest = slice(LANES, width)
    sources = [last_a_ref.at[f] for f in range(half)] + [last_b_ref.at[f] for f in range(half)]

    def copies(sources, at, base):
        return [pltpu.make_async_copy(source, out_ref.at[at, f], sems.at[base + f]) for f, source in enumerate(sources)]

    firsts = [
        pltpu.make_async_copy(row_ref.at[f, :, rest], out_ref.at[at, f, :, rest], sems.at[base + f])
        for f in range(fields)
    ]
    kept = copies(sources, at + 1, base + fields)
    gone = copies([zero_ref] * fields, at + 1, base + fields)

    def apply(act):
        for copy in firsts:
            act(copy)

        @pl.when(keeps)
        def _():
            for copy in kept:
                act(copy)

        @pl.when(jnp.logical_not(keeps))
        def _():
            for copy in gone:
                act(copy)

    return apply


def rows_body(owner_ref, row_ref, last_a_ref, last_b_ref, out_ref, zero_ref, sems):
    zero_ref[...] = jnp.zeros(zero_ref.shape, F32)
    apply = row_copies(owner_ref, row_ref, last_a_ref, last_b_ref, zero_ref, out_ref, 1, sems, 0)
    apply(lambda copy: copy.start())
    apply(lambda copy: copy.wait())


def finish_body(
    owner_any, map_any, u_ref, coef_ref, y_ref, box_ref, drift_ref, tail_ref, code_ref, row_ref,
    last_a_ref, last_b_ref, partial_ref, out_ref, tile_ref, arrived_ref, zero_ref, map_ref, owner_ref, sems
):
    fields, depth, width = u_ref.shape[1:]
    main = width // LANES
    half = arrived_ref.shape[0]
    copies = [load_map(map_any, map_ref, sems.at[0]), load_map(owner_any, owner_ref, sems.at[1])]
    arrives = arrival(code_ref)
    lane = lane_ids()
    row_id = lax.broadcasted_iota(jnp.int32, (depth, 1), 0)
    base = half * main * (depth + 1)
    column = ColumnEdge(coef_ref, y_ref)
    extra = wide(code_ref[base + depth * fields // 2 : base + depth * fields // 2 + 8, :])
    tile0, tile1 = tile_at(0), tile_at(1)
    near = column.near(0, tile0)
    before = []
    for g in range(fields // 2):
        pair = wide(code_ref[base + g * depth : base + (g + 1) * depth, :]) * scale_of(extra[g : g + 1])
        before += [pair, pltpu.roll(pair, 64, 1)]
    corners = []
    for kind in range(3):
        row = extra[3 + kind : 4 + kind] * scale_of(extra[2:3])
        shifts = [(96 - 32 * f) % LANES for f in range(fields)]
        corners.append(jnp.concatenate([pltpu.roll(row, shift, 1) if shift else row for shift in shifts], axis=0))
    near_sum = nine_sum([corners[0], near, column.near(0, tile1)], lane)[1]
    beyond_sum = nine_sum([corners[1], column.beyond(0, tile0), column.beyond(0, tile1)], lane)[1]
    for copy in copies:
        copy.wait()
    pieces = Pieces(map_ref, coef_ref, y_ref)
    rims, stepped, nexts, coefs = [], [], [], []
    for f in range(fields):
        now = u_ref[0, f, :, tile0]
        total = nine_sum([before[f], now, u_ref[0, f, :, tile1]], lane)[1]
        rims.append(column.own(total))
        low_row, high_row = column.rows(near_sum[f : f + 1])
        lap = column_sum(total, row_id, low_row, high_row) - 27.0 * now
        coef = pieces.piece(f)
        coefs.append(coef(tile0))
        stepped.append(drift_ref[0, f, :, tile0] + coefs[f] * lap)
        nexts.append(drift_ref[0, f, :, tile1] + coef(tile1) * box_ref[f, :, tile1])
    box = near_sum + beyond_sum + jnp.concatenate(rims, axis=0)
    edge = column.ahead(0, tile0) + column.coefs(0, tile0) * (box - 27.0 * near)
    edge_sum = nine_sum([corners[2], edge, tail_ref[0:4, :]], lane)[1]
    for f in range(fields):
        total = nine_sum([pltpu.roll(before[f], 32, 1), stepped[f], nexts[f]], lane)[1]
        row = edge_sum[f : f + 1]
        tile_ref[f] = second_step(stepped[f], u_ref[0, f, :, tile0], total, coefs[f], row_id, row, column.lower)

    slot = jnp.where(arrives, 1, 0)
    last = pltpu.make_async_copy(tile_ref, out_ref.at[slot, :, :, tile0], sems.at[2])
    last.start()

    @pl.when(arrives)
    def _():
        decode(code_ref, arrived_ref)
        coming = code_copies(0, arrived_ref, out_ref, sems, 3)
        for copy in coming:
            copy.start()
        for copy in coming:
            copy.wait()

    @pl.when(jnp.logical_not(arrives))
    def _():
        zero_ref[...] = jnp.zeros(zero_ref.shape, F32)
        apply = row_copies(owner_ref, row_ref, last_a_ref, last_b_ref, zero_ref, out_ref, 0, sems, 3)
        blank = [
            pltpu.make_async_copy(zero_ref, out_ref.at[2, f], sems.at[3 + 2 * fields + f]) for f in range(fields)
        ]
        apply(lambda copy: copy.start())
        for copy in blank:
            copy.start()
        for copy in blank:
            copy.wait()
        apply(lambda copy: copy.wait())

    last.wait()


def place_body(first, code_a_ref, code_ref, partial_ref, out_ref, row_ref, sems):
    arrives = arrival(code_a_ref)
    decode(code_ref, row_ref)
    copies = code_copies(first, row_ref, out_ref, sems, 0)

    @pl.when(arrives)
    def _():
        for copy in copies:
            copy.start()
        for copy in copies:
            copy.wait()


def fast_on_device(u_now, u_prev, coef_store, store_map, new_owner):
    blocks, _, fields, depth, width = u_now.shape
    now = u_now.reshape(blocks, fields, depth, width)
    prev = u_prev.reshape(blocks, fields, depth, width)
    coef = coef_store[0, 0]
    count = lax.axis_size("blk")
    order = store_map.reshape(-1)
    order_hbm, now_hbm, prev_hbm, coef_hbm = (
        pltpu.with_memory_space_constraint(array, pltpu.HBM) for array in (order, now, prev, coef)
    )
    params = pltpu.CompilerParams(vmem_limit_bytes=48 * 1024 * 1024)

    def call(body, name, out_shape, in_specs, out_specs, scratch, args, **options):
        return pl.pallas_call(
            body,
            out_shape=out_shape,
            in_specs=in_specs,
            out_specs=out_specs,
            scratch_shapes=scratch,
            compiler_params=params,
            name=name,
            **options,
        )(*args)

    straight = jax.ShapeDtypeStruct((fields * depth + 16, LANES), BF16)
    diag = jax.ShapeDtypeStruct((depth + 32, LANES), BF16)
    tiles = jax.ShapeDtypeStruct((fields, depth, LANES), F32)
    y_out, edges, front, front_prev, front_coef = call(
        pack_region_body,
        "pack_region",
        (
            jax.ShapeDtypeStruct((5, depth, width), BF16),
            jax.ShapeDtypeStruct((depth, width), F32),
            tiles,
            tiles,
            jax.ShapeDtypeStruct((2, 4, depth, LANES), BF16),
        ),
        [HBM] * 4,
        (VMEM,) * 5,
        [
            pltpu.VMEM((blocks, fields, 8, width), F32),
            pltpu.VMEM((blocks, fields, 8, width), F32),
            pltpu.VMEM((4, 16, width), BF16),
            pltpu.SMEM(order.shape, jnp.int32),
            pltpu.SemaphoreType.DMA((15,)),
        ],
        (order_hbm, now_hbm, prev_hbm, coef_hbm),
    )
    left, dleft = call(
        pack_back_body, "pack_back", (straight, diag), [VMEM] * 4, (VMEM,) * 2, [], (edges, front, front_prev, front_coef)
    )

    swap = [(0, 1), (1, 0)]
    forward = [(i, (i + 1) % count) for i in range(count)]
    backward = [(i, (i - 1) % count) for i in range(count)]
    crossed = [(r * count + i, (1 - r) * count + (i - 1) % count) for r in range(2) for i in range(count)]
    y_in = lax.ppermute(y_out, "region", swap)
    from_right = lax.ppermute(left, "blk", backward)
    from_dright = lax.ppermute(dleft, ("region", "blk"), crossed)

    row = jax.ShapeDtypeStruct((fields, depth, width), F32)
    box0, box1, drift, rim = call(
        local_body,
        "local",
        (row, row, jax.ShapeDtypeStruct(now.shape, F32), jax.ShapeDtypeStruct((blocks, 8, width), F32)),
        [VMEM] * 2,
        (VMEM,) * 4,
        [],
        (now, prev),
    )
    sums = jax.ShapeDtypeStruct((8, width), F32)
    tail = jax.ShapeDtypeStruct((8, LANES), F32)
    box1, side_lap, side_coef, side_rim = call(
        border_body,
        "border",
        (row, tiles, tiles, jax.ShapeDtypeStruct((2, 8, LANES), F32)),
        [VMEM] * 4,
        (VMEM,) * 4,
        [],
        (now, from_right, from_dright, box1),
        input_output_aliases={3: 0},
        cost_estimate=pl.CostEstimate(flops=0, transcendentals=0, bytes_accessed=40_000_000),
    )
    half = fields // 2
    part = jax.ShapeDtypeStruct((half, depth, width), F32)
    tiled = half * width // LANES
    codes = jax.ShapeDtypeStruct((tiled * (depth + 1), LANES), jnp.int16)
    more_codes = jax.ShapeDtypeStruct((tiled * (depth + 1) + half * depth + 8, LANES), jnp.int16)
    scalars = [pltpu.SMEM(order.shape, jnp.int32), pltpu.SMEM(new_owner.shape, jnp.int32)]
    powers = pltpu.VMEM((tiled, LANES), F32)
    box1, lap1, side1, sums1, last_a, code_a = call(
        last_row_a_body,
        "last_row",
        (row, tiles, tiles, sums, part, more_codes),
        [ANY] * 2 + [VMEM] * 12,
        (VMEM,) * 6,
        [powers, pltpu.VMEM((8, LANES), F32)] + scalars + [pltpu.SemaphoreType.DMA((2,))],
        (order, new_owner, now, coef, y_in, from_right, from_dright, box0, rim, side_lap, side_coef, side_rim, drift, box1),
        input_output_aliases={13: 0},
    )
    arrived_a = lax.ppermute(code_a, "blk", forward)
    last_b, code_b = call(
        functools.partial(last_row_b_body, half),
        "last_row",
        (part, codes),
        [ANY] + [VMEM] * 8,
        (VMEM,) * 2,
        [powers, scalars[0], pltpu.SemaphoreType.DMA],
        (order, now, coef, y_in, box1, drift, lap1, side1, sums1),
    )
    arrived_b = lax.ppermute(code_b, "blk", forward)
    box0, sums0, tail0 = call(
        first_edges_body,
        "first_edges",
        (row, sums, tail),
        [VMEM] * 6,
        (VMEM,) * 3,
        [],
        (now, coef, y_in, box1, rim, box0),
        input_output_aliases={5: 0},
    )
    first = call(
        first_row_body,
        "first_row",
        row,
        [SMEM] + [VMEM] * 7,
        VMEM,
        [],
        (order, now, coef, y_in, box0, box1, drift, sums0),
    )
    whole = jax.ShapeDtypeStruct((blocks + 1, fields, depth, width), F32)
    placed = call(
        rows_body,
        "rows",
        whole,
        [SMEM] + [VMEM] * 3,
        ANY,
        [pltpu.VMEM((depth, width), F32), pltpu.SemaphoreType.DMA((2 * fields,))],
        (new_owner, first, last_a, last_b),
    )
    arrived_half = pltpu.VMEM((half, depth, width), F32)
    placed = call(
        finish_body,
        "finish",
        whole,
        [ANY] * 2 + [VMEM] * 10 + [ANY],
        ANY,
        [pltpu.VMEM((fields, depth, LANES), F32), arrived_half, pltpu.VMEM((depth, width), F32)]
        + scalars
        + [pltpu.SemaphoreType.DMA((3 + 3 * fields,))],
        (new_owner, order, now, coef, y_in, box0, drift, tail0, arrived_a, first, last_a, last_b, placed),
        input_output_aliases={12: 0},
    )
    placed = call(
        functools.partial(place_body, half),
        "place",
        whole,
        [VMEM, VMEM, ANY],
        ANY,
        [arrived_half, pltpu.SemaphoreType.DMA((2 * half,))],
        (arrived_a, arrived_b, placed),
        input_output_aliases={2: 0},
    )
    return placed[:, None]


def solution(mesh):
    def on_device(*args):
        blocks = args[0].shape[0]
        if lax.axis_size("region") == 2 and blocks == 2:
            return fast_on_device(*args)
        return general_on_device(*args)

    return jax.shard_map(
        on_device,
        mesh=mesh,
        in_specs=(
            P("blk", "region", None, None, None),
            P("blk", "region", None, None, None),
            P("blk", "region", None, None, None, None),
            P("blk", "region", None),
            P("blk"),
        ),
        out_specs=P("blk", "region", None, None, None),
        check_vma=False,
    )
```

```python
import functools

import jax
import jax.numpy as jnp
from jax import lax
from jax.experimental import pallas as pl
from jax.experimental.pallas import tpu as pltpu
from jax.sharding import PartitionSpec as P

STEPS = 2
LANES = 128
F32 = jnp.float32
BF16 = jnp.bfloat16
VMEM = pl.BlockSpec(memory_space=pltpu.VMEM)
SMEM = pl.BlockSpec(memory_space=pltpu.SMEM)
ANY = pl.BlockSpec(memory_space=pl.ANY)
HBM = pl.BlockSpec(memory_space=pltpu.HBM)


def extended_2(block, sides, width, periodic):
    for axis, dim in sides:
        count = lax.axis_size(axis)
        forward = [(i, i + 1) for i in range(count - 1)]
        if periodic:
            forward.append((count - 1, 0))
        backward = [(target, source) for source, target in forward]
        low = lax.ppermute(
            lax.slice_in_dim(block, block.shape[dim] - width, None, axis=dim), axis, forward
        )
        high = lax.ppermute(lax.slice_in_dim(block, 0, width, axis=dim), axis, backward)
        block = jnp.concatenate([low, block, high], axis=dim)
    return block


def shifted_2(value, axis, by):
    devices = lax.axis_size(axis)
    return lax.ppermute(value, axis, [(i, (i + by) % devices) for i in range(devices)])


def stencil_step(state_now, state_prev, coefficient, live_count):
    slot_count, field_count, edge_cells, plane_cells = state_now.shape
    padded = extended_2(state_now, (("region", 2),), 1, False)
    first_planes = padded[..., :edge_cells]
    last_planes = padded[..., plane_cells - edge_cells :]
    last_live = jnp.take(last_planes, live_count - 1, axis=0)
    rim_pair = jnp.stack([first_planes[0], last_live], axis=2)
    spread = extended_2(rim_pair.astype(jnp.bfloat16), (("blk", 2),), 1, True).astype(
        rim_pair.dtype
    )
    left_rim = spread[:, :, 0]
    right_rim = spread[:, :, 3]
    before_planes = jnp.concatenate([left_rim[None], last_planes[:-1]], axis=0)
    after_planes = jnp.pad(first_planes[1:], ((0, 1), (0, 0), (0, 0), (0, 0)))
    slot_ids = jnp.arange(slot_count)
    after_planes = jnp.where(
        (slot_ids == live_count - 1)[:, None, None, None], right_rim[None], after_planes
    )
    extended = jnp.concatenate([before_planes, padded, after_planes], axis=-1)
    width = extended.shape[-1]
    column = jnp.arange(width) % edge_cells
    lower_mask = (column != 0).astype(jnp.float32)
    upper_mask = (column != edge_cells - 1).astype(jnp.float32)
    margin = ((0, 0), (0, 0), (0, 0), (1, 1))
    shifted = jnp.pad(extended, margin)
    summed = shifted[..., :width] * lower_mask + extended + shifted[..., 2:] * upper_mask
    summed = (
        summed[..., : -2 * edge_cells]
        + summed[..., edge_cells:-edge_cells]
        + summed[..., 2 * edge_cells :]
    )
    box_sum = summed[:, :, :-2] + summed[:, :, 1:-1] + summed[:, :, 2:]
    laplace = box_sum - 27.0 * state_now
    return 2.0 * state_now - state_prev + coefficient.astype(jnp.float32) * laplace


def compact(members, valid_flags):
    slot_count = valid_flags.shape[0]
    place_index = jnp.cumsum(valid_flags) - 1
    target = jnp.arange(slot_count)
    chooser = (valid_flags[None, :] == 1) & (place_index[None, :] == target[:, None])
    source = jnp.sum(jnp.where(chooser, target[None, :], 0), axis=1)
    filled = jnp.sum(chooser.astype(jnp.int32), axis=1) > 0
    placed = tuple(
        (
            jnp.where(
                filled.reshape((slot_count,) + (1,) * (member.ndim - 1)),
                jnp.take(member, source, axis=0),
                jnp.zeros_like(member),
            )
            for member in members
        )
    )
    return (placed, jnp.sum(valid_flags))


def general_on_device(u_now, u_prev, coef_store, store_map, new_owner):
    state_now = u_now[:, 0]
    state_prev = u_prev[:, 0]
    blocks, fields, edge_cells, plane_cells = state_now.shape
    store_local = coef_store[0, 0]
    arrived = lax.all_to_all(store_local, "region", split_axis=0, concat_axis=0, tiled=True)
    flattened = arrived.reshape((-1,) + arrived.shape[2:])
    inverse = jnp.argsort(store_map[0, 0])
    coefficient = jnp.take(flattened, inverse, axis=0).reshape(
        blocks, fields, edge_cells, plane_cells
    )
    own_index = lax.axis_index("blk")
    goes_right = new_owner[blocks - 1] != own_index
    mark_right = goes_right.astype(jnp.float32).reshape(1)
    middle_flags = jnp.ones((blocks - 2,), jnp.int32)
    keep_first = (new_owner[0] == own_index).astype(jnp.int32).reshape(1)
    keep_last = (new_owner[blocks - 1] == own_index).astype(jnp.int32).reshape(1)
    for step_index in range(STEPS):
        state_now, state_prev = (
            stencil_step(state_now, state_prev, coefficient, blocks),
            state_now,
        )
    from_left = shifted_2((state_now[blocks - 1], mark_right), "blk", 1)
    valid_flags = jnp.concatenate(
        [(from_left[1] > 0.5).astype(jnp.int32), keep_first, middle_flags, keep_last]
    )
    stacked_now = jnp.concatenate([from_left[0][None], state_now], axis=0)
    placed, live_count = compact((stacked_now,), valid_flags)
    result = placed[0]
    return result[:, None]


def lane_ids():
    return lax.broadcasted_iota(jnp.int32, (1, LANES), 1)


def edge_start(lower, depth, size):
    return pl.multiple_of(jnp.where(lower, depth - size, 0), size)


def pack_region_body(
    map_hbm, u_ref, p_ref, coef_ref, y_ref, edges_ref, ua_ref, pa_ref, ca_ref, ue_ref, pe_ref, ce_ref, map_ref, sems
):
    fields, depth, width = u_ref.shape[1:]
    region = lax.axis_index("region")
    lower = region == 0
    other = 1 - region
    half = depth // 2
    front = slice(0, LANES)
    edge8 = edge_start(lower, depth, 8)
    edge16 = edge_start(lower, depth, 16)
    slab = []
    for s in range(4):
        for h in range(2):
            part = slice(h * half, (h + 1) * half)
            slab.append(pltpu.make_async_copy(coef_ref.at[other, s, part], y_ref.at[s, part], sems.at[7 + 2 * s + h]))
    copies = [
        pltpu.make_async_copy(map_hbm, map_ref, sems.at[0]),
        pltpu.make_async_copy(u_ref.at[:, :, pl.ds(edge8, 8), :], ue_ref, sems.at[1]),
        pltpu.make_async_copy(p_ref.at[:, :, pl.ds(edge8, 8), :], pe_ref, sems.at[2]),
        pltpu.make_async_copy(coef_ref.at[region, :, pl.ds(edge16, 16), :], ce_ref, sems.at[3]),
    ]
    beside = [
        pltpu.make_async_copy(u_ref.at[0, :, :, front], ua_ref, sems.at[4]),
        pltpu.make_async_copy(p_ref.at[0, :, :, front], pa_ref, sems.at[5]),
        pltpu.make_async_copy(coef_ref.at[:, :, :, front], ca_ref, sems.at[6]),
    ]
    for copy in copies + slab + beside:
        copy.start()
    for copy in copies:
        copy.wait()
    own_edge = jnp.where(lower, 7, 0)
    own_next = jnp.where(lower, 6, 1)
    for m in range(2):
        for f in range(fields):
            at = m * fields + f
            near = ue_ref[m, f, pl.ds(own_edge, 1), :]
            edges_ref[at : at + 1, :] = near
            edges_ref[8 + at : 9 + at, :] = ue_ref[m, f, pl.ds(own_next, 1), :]
            edges_ref[16 + at : 17 + at, :] = 2.0 * near - pe_ref[m, f, pl.ds(own_edge, 1), :]
    for s in range(4):
        piece = ce_ref[s].astype(F32)
        edges_ref[24 + s : 25 + s, :] = jnp.where(lower, piece[15:16], piece[0:1])
    numbers = [map_ref[region * 4 + s] for s in range(4)] + [map_ref[other * 4 + s] for s in range(4)]
    for i, number in enumerate(numbers):
        edges_ref[28:29, tile_at(i)] = jnp.zeros((1, LANES), F32) + number.astype(F32)
    edges_ref[29:32, :] = jnp.zeros((3, width), F32)
    y_ref[4] = edges_ref[...].astype(BF16)
    for copy in slab + beside:
        copy.wait()


def pack_back_body(edges_ref, ua_ref, pa_ref, ca_ref, straight_ref, diag_ref):
    fields, depth, _ = ua_ref.shape
    region = lax.axis_index("region")
    lower = region == 0
    other = 1 - region
    lane = lane_ids()
    tag_rows = [edges_ref[28:29, tile_at(i)] for i in range(8)]
    blank = jnp.zeros((1, LANES), F32)
    for f in range(fields):
        now = ua_ref[f]
        ahead = 2.0 * now - pa_ref[f]
        piece = ca_ref[region, f].astype(F32)
        tile = jnp.where(
            lane < 64, now, jnp.where(lane < 96, pltpu.roll(ahead, 64, 1), pltpu.roll(piece, 96, 1))
        )
        straight_ref[f * depth : (f + 1) * depth, :] = tile.astype(BF16)
    far = [ca_ref[other, s].astype(F32) for s in range(4)]
    extra = [jnp.where(lower, piece[0:1], piece[depth - 1 : depth]) for piece in far] + tag_rows + [blank] * 4
    straight_ref[fields * depth : fields * depth + 16, :] = jnp.concatenate(extra, axis=0).astype(BF16)
    plane = jnp.zeros((depth, LANES), F32)
    for s in range(4):
        moved = pltpu.roll(far[s], 32 * s, 1) if s else far[s]
        plane = jnp.where((lane >= 32 * s) & (lane < 32 * s + 32), moved, plane)
    diag_ref[0:depth, :] = plane.astype(BF16)
    rows = [edges_ref[base : base + 4, 0:LANES] for base in (0, 8, 16, 24)]
    diag_ref[depth : depth + 32, :] = jnp.concatenate(rows + tag_rows + [blank] * 8, axis=0).astype(BF16)


def lane_sum(tile, lane):
    inside = lane % 32
    return (
        tile
        + jnp.where(inside != 0, pltpu.roll(tile, 1, 1), 0.0)
        + jnp.where(inside != 31, pltpu.roll(tile, LANES - 1, 1), 0.0)
    )


def nine_sum(tiles, lane):
    rows = [lane_sum(tile, lane) for tile in tiles]
    up = [pltpu.roll(row, 32, 1) for row in rows]
    down = [pltpu.roll(row, LANES - 32, 1) for row in rows]
    count = len(tiles)
    result = []
    for t in range(count):
        before = jnp.where(lane < 32, up[t - 1] if t else 0.0, up[t])
        after = jnp.where(lane >= 96, down[t + 1] if t < count - 1 else 0.0, down[t])
        result.append(rows[t] + before + after)
    return result


def column_sum(tile, row_id, low_row, high_row):
    depth = tile.shape[0]
    above = pltpu.roll(tile, 1, 0)
    below = pltpu.roll(tile, depth - 1, 0)
    return tile + jnp.where(row_id == 0, low_row, above) + jnp.where(row_id == depth - 1, high_row, below)


def local_body(u_hbm, p_hbm, u_ref, box0_ref, box1_ref, drift_ref, rim_ref, p_ref, sems):
    fields, depth, width = u_ref.shape[1:]
    main = width // LANES
    copies = []
    for f in range(fields):
        copies.append(
            (
                pltpu.make_async_copy(u_hbm.at[:, f], u_ref.at[:, f], sems.at[2 * f]),
                pltpu.make_async_copy(p_hbm.at[:, f], p_ref.at[:, f], sems.at[2 * f + 1]),
            )
        )
    for pair in copies:
        for copy in pair:
            copy.start()
    lower = lax.axis_index("region") == 0
    lane = lane_ids()
    row_id = lax.broadcasted_iota(jnp.int32, (depth, 1), 0)
    boxes = (box0_ref, box1_ref)
    for f in range(fields):
        for copy in copies[f]:
            copy.wait()
        now = [u_ref[m, f, :, tile_at(t)] for m in range(2) for t in range(main)]
        sums = nine_sum(now, lane)
        for i, (tile, total) in enumerate(zip(now, sums)):
            m, t = divmod(i, main)
            lanes = tile_at(t)
            rim_ref[m, f : f + 1, lanes] = jnp.where(lower, total[depth - 1 : depth], total[0:1])
            boxes[m][f, :, lanes] = column_sum(total, row_id, 0.0, 0.0) - 27.0 * tile
            drift_ref[m, f, :, lanes] = 2.0 * tile - p_ref[m, f, :, lanes]
    rim_ref[:, 4:8, :] = jnp.zeros((2, 4, width), F32)


def tile_at(t):
    return slice(t * LANES, (t + 1) * LANES)


class ColumnEdge:
    def __init__(self, coef_ref, y_ref):
        self.region = lax.axis_index("region")
        self.lower = self.region == 0
        self.coef = coef_ref
        self.depth = coef_ref.shape[2]
        self.extra = y_ref[4].astype(F32)
        self.tags = [self.extra[28:29, i * LANES : (i + 1) * LANES] for i in range(8)]
        self.field_id = lax.broadcasted_iota(jnp.int32, (4, LANES), 0).astype(F32)

    def near(self, m, lanes):
        return self.extra[4 * m : 4 * m + 4, lanes]

    def beyond(self, m, lanes):
        return self.extra[8 + 4 * m : 12 + 4 * m, lanes]

    def ahead(self, m, lanes):
        return self.extra[16 + 4 * m : 20 + 4 * m, lanes]

    def coefs(self, m, lanes):
        total = jnp.zeros((4, LANES), F32)
        for s in range(4):
            piece = self.coef[1 - self.region, s, :, lanes].astype(F32)
            held = jnp.where(self.lower, piece[0:1], piece[self.depth - 1 : self.depth])
            total = total + jnp.where(self.tags[s] == self.field_id + 4 * m, self.extra[24 + s : 25 + s, lanes], 0.0)
            total = total + jnp.where(self.tags[4 + s] == self.field_id + 4 * m, held, 0.0)
        return total

    def own(self, tile):
        return jnp.where(self.lower, tile[self.depth - 1 : self.depth], tile[0:1])

    def rows(self, row):
        return jnp.where(self.lower, 0.0, row), jnp.where(self.lower, row, 0.0)


def border_body(u_ref, straight_ref, diag_ref, box_in, box_ref, side_lap_ref, side_coef_ref, rim_ref):
    fields, depth, width = u_ref.shape[1:]
    lane = lane_ids()
    row_id = lax.broadcasted_iota(jnp.int32, (depth, 1), 0)
    lower = lax.axis_index("region") == 0
    before = slice(width - LANES, width)
    facing = lane >= 96
    tags = [straight_ref[fields * depth : fields * depth + 16, :].astype(F32)[4 + i : 5 + i] for i in range(8)]
    planes = []
    for s in range(4):
        planes.append(pltpu.roll(straight_ref[s * depth : (s + 1) * depth, :].astype(F32), 32, 1))
    diag_tile = diag_ref[0:depth, :].astype(F32)
    for s in range(4):
        planes.append(pltpu.roll(diag_tile, LANES - 32 * s, 1) if s else diag_tile)
    for f in range(fields):
        inner = u_ref[1, f, :, before]
        remote = straight_ref[f * depth : (f + 1) * depth, :].astype(F32)
        inner_sum, remote_sum = nine_sum([inner, remote], lane)
        for i, tile in enumerate((inner_sum, remote_sum)):
            rim_ref[i, f : f + 1, :] = jnp.where(lower, tile[depth - 1 : depth], tile[0:1])
        halo_c = jnp.zeros((depth, LANES), F32)
        for i in range(8):
            halo_c = halo_c + jnp.where(tags[i] == F32(f), planes[i], 0.0)
        side_coef_ref[f] = halo_c
        side_lap_ref[f] = column_sum(remote_sum, row_id, 0.0, 0.0) - 27.0 * remote
        whole = column_sum(inner_sum, row_id, 0.0, 0.0) - 27.0 * inner
        box_ref[f, :, before] = jnp.where(facing, whole, box_in[f, :, before])
    rim_ref[:, 4:8, :] = jnp.zeros((2, 4, LANES), F32)


def last_edges(
    coef_ref, y_ref, straight_ref, diag_ref, box0_ref, rim_ref, side_lap_ref, side_coef_ref, side_rim_ref, box_in,
    box_ref, lap_ref, side_ref, sums_ref
):
    fields, depth, width = box_in.shape
    main = width // LANES
    lane = lane_ids()
    column = ColumnEdge(coef_ref, y_ref)
    before = slice(width - LANES, width)
    extra_s = straight_ref[fields * depth : fields * depth + 16, :].astype(F32)
    extra_d = diag_ref[depth : depth + 32, :].astype(F32)
    tags_d = [extra_d[16 + i : 17 + i] for i in range(8)]

    def edge_tiles(of, base):
        return [of(0, before)] + [of(1, tile_at(t)) for t in range(main)] + [extra_d[base : base + 4]]

    near = edge_tiles(column.near, 0)
    beyond = edge_tiles(column.beyond, 4)
    ahead = edge_tiles(column.ahead, 8)
    corner = jnp.zeros((4, LANES), F32)
    for s in range(4):
        corner = corner + jnp.where(tags_d[s] == column.field_id, extra_d[12 + s : 13 + s], 0.0)
        corner = corner + jnp.where(tags_d[4 + s] == column.field_id, extra_s[s : s + 1], 0.0)
    edge_c = [column.coefs(0, before)] + [column.coefs(1, tile_at(t)) for t in range(main)] + [corner]
    near_sum = nine_sum(near, lane)
    beyond_sum = nine_sum(beyond, lane)
    top = slice(0, 1)
    bottom = slice(depth - 1, depth)
    for f in range(fields):
        for t in range(main):
            low_row, high_row = column.rows(near_sum[t + 1][f : f + 1])
            lanes = tile_at(t)
            box_ref[f, top, lanes] = box_in[f, top, lanes] + low_row
            box_ref[f, bottom, lanes] = box_in[f, bottom, lanes] + high_row
        remote = straight_ref[f * depth : (f + 1) * depth, :].astype(F32)
        side_ref[f] = pltpu.roll(remote, 64, 1) + side_coef_ref[f] * side_lap_ref[f]
        low_row, high_row = column.rows(near_sum[main + 1][f : f + 1])
        side_ref[f, top] += side_coef_ref[f, top] * low_row
        side_ref[f, bottom] += side_coef_ref[f, bottom] * high_row
        low_row, high_row = column.rows(near_sum[0][f : f + 1])
        lap_ref[f] = box0_ref[f, :, before]
        lap_ref[f, top] += low_row
        lap_ref[f, bottom] += high_row
    rims = [rim_ref[0, 0:4, before]] + [rim_ref[1, 0:4, tile_at(t)] for t in range(main)] + [side_rim_ref[1, 0:4, :]]
    rims[main] = jnp.where(lane >= 96, side_rim_ref[0, 0:4, :], rims[main])
    stepped = []
    for t in range(main + 2):
        box = near_sum[t] + beyond_sum[t] + rims[t]
        stepped.append(ahead[t] + edge_c[t] * (box - 27.0 * near[t]))
    stepped_sum = nine_sum(stepped, lane)
    for t in range(main):
        sums_ref[0:4, tile_at(t)] = stepped_sum[t + 1]
    sums_ref[4:8, :] = jnp.zeros((4, width), F32)
    return stepped[main]


def first_edges_body(coef_ref, y_ref, rim_ref, box1_ref, box_in, box_ref, sums_ref, edge_c_ref):
    fields, depth, width = box_in.shape
    main = width // LANES
    lane = lane_ids()
    column = ColumnEdge(coef_ref, y_ref)
    after = slice(0, LANES)

    def edge_tiles(of):
        return [of(0, tile_at(t)) for t in range(main)] + [of(1, after)]

    near = edge_tiles(column.near)
    near_sum = nine_sum(near, lane)
    beyond_sum = nine_sum(edge_tiles(column.beyond), lane)
    ahead = edge_tiles(column.ahead)
    edge_c = edge_tiles(column.coefs)
    for f in range(fields):
        for t in range(main):
            low_row, high_row = column.rows(near_sum[t][f : f + 1])
            lanes = tile_at(t)
            box_ref[f, 0:1, lanes] = box_in[f, 0:1, lanes] + low_row
            box_ref[f, depth - 1 : depth, lanes] = box_in[f, depth - 1 : depth, lanes] + high_row
    rims = [rim_ref[0, 0:4, tile_at(t)] for t in range(main)] + [rim_ref[1, 0:4, after]]
    stepped = []
    for t in range(main + 1):
        box = near_sum[t] + beyond_sum[t] + rims[t]
        stepped.append(ahead[t] + edge_c[t] * (box - 27.0 * near[t]))
    stepped_sum = nine_sum(stepped, lane)
    for t in range(main):
        sums_ref[0:4, tile_at(t)] = stepped_sum[t]
    sums_ref[4:8, :] = jnp.zeros((4, width), F32)
    edge_c_ref[0:4, :] = edge_c[0]
    edge_c_ref[4:8, :] = jnp.zeros((4, LANES), F32)


def load_map(map_any, map_ref, sem):
    copy = pltpu.make_async_copy(map_any, map_ref, sem)
    copy.start()
    return copy


class Pieces:
    def __init__(self, map_ref, coef_ref, slab_ref):
        self.coef, self.slab = coef_ref, slab_ref
        self.region = lax.axis_index("region")
        self.numbers = [map_ref[q] for q in range(8)]

    def piece(self, number):
        place = jnp.int32(0)
        for q in range(8):
            place = jnp.where(self.numbers[q] == number, q, place)
        slot = place & 3
        held = (place >> 2) == self.region

        def tile(lanes):
            return jnp.where(held, self.coef[self.region, slot, :, lanes], self.slab[slot, :, lanes]).astype(F32)

        return tile


def second_step(now, before, total, coef, row_id, row, lower):
    low_row, high_row = jnp.where(lower, 0.0, row), jnp.where(lower, row, 0.0)
    lap = column_sum(total, row_id, low_row, high_row) - 27.0 * now
    return 2.0 * now - before + coef * lap


CODES = 32000.0


def power_of(size):
    return jnp.ceil(jnp.log2(jnp.maximum(size, 1e-30)))


def coded(value, power):
    return jnp.floor(value * (CODES * jnp.exp2(-power)) + 0.5)


def narrow(value):
    return value.astype(jnp.int32).astype(jnp.int16)


def wide(code):
    return code.astype(jnp.int32).astype(F32)


def scale_of(power):
    return jnp.exp2(power) * (1.0 / CODES)


def last_row_a_body(
    map_any, owner_any, u_ref, coef_ref, y_ref, straight_ref, diag_ref, box0_ref, rim_ref, side_lap_ref, side_coef_ref,
    side_rim_ref, drift_ref, box_in, box_ref, lap_ref, side_ref, sums_ref, row_ref, code_ref, power_ref, extra_ref,
    map_ref, owner_ref, sems
):
    copies = [load_map(map_any, map_ref, sems.at[0]), load_map(owner_any, owner_ref, sems.at[1])]
    tail = last_edges(
        coef_ref, y_ref, straight_ref, diag_ref, box0_ref, rim_ref, side_lap_ref, side_coef_ref, side_rim_ref, box_in,
        box_ref, lap_ref, side_ref, sums_ref
    )
    for copy in copies:
        copy.wait()
    more = (owner_ref, tail, extra_ref)
    refs = (map_ref, u_ref, coef_ref, y_ref, box_ref, drift_ref, lap_ref, side_ref, sums_ref, row_ref, code_ref, power_ref)
    last_row(0, *refs, more=more)


def last_row_b_body(first, map_any, *refs):
    map_ref, sem = refs[-2:]
    load_map(map_any, map_ref, sem).wait()
    last_row(first, map_ref, *refs[:-2])


def last_row(
    first, map_ref, u_ref, coef_ref, y_ref, box_ref, drift_ref, lap_ref, side_ref, sums_ref, row_ref, code_ref, power_ref,
    more=None
):
    count, depth, width = row_ref.shape
    fields = u_ref.shape[1]
    main = width // LANES
    lane = lane_ids()
    row_id = lax.broadcasted_iota(jnp.int32, (depth, 1), 0)
    pieces = Pieces(map_ref, coef_ref, y_ref)
    lower = pieces.region == 0
    before = slice(width - LANES, width)
    last_tiles = []
    for f in range(first, first + count):
        coef = pieces.piece(fields + f)
        coefs = [coef(tile_at(t)) for t in range(main)]
        middle = [drift_ref[1, f, :, tile_at(t)] + coefs[t] * box_ref[f, :, tile_at(t)] for t in range(main)]
        local = drift_ref[0, f, :, before] + pieces.piece(f)(before) * lap_ref[f]
        sums = nine_sum([local] + middle + [side_ref[f]], lane)
        for t in range(main):
            lanes = tile_at(t)
            row = sums_ref[f : f + 1, lanes]
            value = second_step(middle[t], u_ref[1, f, :, lanes], sums[t + 1], coefs[t], row_id, row, lower)
            row_ref[f - first, :, lanes] = value
            power = power_of(jnp.max(jnp.abs(value), axis=0, keepdims=True))
            at = (f - first) * main + t
            code_ref[at * depth : (at + 1) * depth, :] = narrow(coded(value, power))
            power_ref[at : at + 1, :] = power
        last_tiles.append(middle[main - 1])
    base = count * main * depth
    code_ref[base : base + count * main, :] = narrow(power_ref[...])
    if more is not None:
        owner_ref, tail, extra_ref = more
        base += count * main
        both = []
        for f in range(fields):
            if f < count:
                stepped = last_tiles[f]
            else:
                stepped = drift_ref[1, f, :, before] + pieces.piece(fields + f)(before) * box_ref[f, :, before]
            both.append(jnp.where(lane >= 96, u_ref[1, f, :, before], pltpu.roll(stepped, 96, 1)))
        for g in range(fields // 2):
            pair = jnp.where(lane >= 64, both[2 * g], pltpu.roll(both[2 * g + 1], 64, 1))
            power = power_of(jnp.max(jnp.abs(pair), axis=0, keepdims=True))
            code_ref[base : base + depth, :] = narrow(coded(pair, power))
            extra_ref[g : g + 1, :] = power
            base += depth
        near = y_ref[4, 0:16, before].astype(F32)
        kinds = []
        for rows in (near[4:8], near[12:16], tail):
            kind = jnp.zeros((1, LANES), F32)
            for f in range(fields):
                shift = (32 * f + 32) % LANES
                row = rows[f : f + 1]
                kind = jnp.where(lane // 32 == f, pltpu.roll(row, shift, 1) if shift else row, kind)
            kinds.append(kind)
        power = power_of(jnp.maximum(jnp.maximum(jnp.abs(kinds[0]), jnp.abs(kinds[1])), jnp.abs(kinds[2])))
        extra_ref[2:3, :] = power
        for i, kind in enumerate(kinds):
            extra_ref[3 + i : 4 + i, :] = coded(kind, power)
        moves = jnp.where(owner_ref[1] != lax.axis_index("blk"), 1.0, 0.0)
        extra_ref[6:7, :] = jnp.zeros((1, LANES), F32) + moves
        extra_ref[7:8, :] = jnp.zeros((1, LANES), F32)
        code_ref[base : base + 8, :] = narrow(extra_ref[...])


def first_row_body(map_ref, u_ref, coef_ref, y_ref, box_ref, box1_ref, drift_ref, sums_ref, row_ref, coef0_ref):
    fields, depth, width = u_ref.shape[1:]
    main = width // LANES
    lane = lane_ids()
    row_id = lax.broadcasted_iota(jnp.int32, (depth, 1), 0)
    pieces = Pieces(map_ref, coef_ref, y_ref)
    lower = pieces.region == 0
    after = slice(0, LANES)
    for f in range(fields):
        coef = pieces.piece(f)
        coefs = [coef(tile_at(t)) for t in range(main)]
        now = [drift_ref[0, f, :, tile_at(t)] + coefs[t] * box_ref[f, :, tile_at(t)] for t in range(main)]
        local = drift_ref[1, f, :, after] + pieces.piece(fields + f)(after) * box1_ref[f, :, after]
        sums = nine_sum(now + [local], lane)
        coef0_ref[f] = coefs[0]
        for t in range(main):
            lanes = tile_at(t)
            row = sums_ref[f : f + 1, lanes]
            row_ref[f, :, lanes] = second_step(now[t], u_ref[0, f, :, lanes], sums[t], coefs[t], row_id, row, lower)


def arrival(code_ref):
    rows = code_ref.shape[0]
    return jnp.max(wide(code_ref[rows - 8 : rows, :])[6:7]) > 0.5


def code_copies(first, row_ref, out_ref, sems, base):
    count, depth, _ = row_ref.shape
    part = depth // 2
    copies = []
    for f in range(count):
        for h in range(2):
            rows = slice(h * part, (h + 1) * part)
            sem = sems.at[base + 2 * f + h]
            copies.append(pltpu.make_async_copy(row_ref.at[f, rows], out_ref.at[0, first + f, rows], sem))
    return copies


def decode(code_ref, row_ref):
    count, depth, width = row_ref.shape
    main = width // LANES
    base = count * main * depth
    scale = scale_of(wide(code_ref[base : base + count * main, :]))
    for f in range(count):
        for t in range(main):
            at = f * main + t
            row_ref[f, :, tile_at(t)] = wide(code_ref[at * depth : (at + 1) * depth, :]) * scale[at : at + 1]


def row_copies(owner_ref, row_ref, last_a_ref, last_b_ref, zero_ref, out_ref, at, sems, base):
    fields, _, width = row_ref.shape
    half = last_a_ref.shape[0]
    keeps = owner_ref[1] == lax.axis_index("blk")
    rest = slice(LANES, width)
    sources = [last_a_ref.at[f] for f in range(half)] + [last_b_ref.at[f] for f in range(half)]

    def copies(sources, at, base):
        return [pltpu.make_async_copy(source, out_ref.at[at, f], sems.at[base + f]) for f, source in enumerate(sources)]

    firsts = [
        pltpu.make_async_copy(row_ref.at[f, :, rest], out_ref.at[at, f, :, rest], sems.at[base + f])
        for f in range(fields)
    ]
    kept = copies(sources, at + 1, base + fields)
    gone = copies([zero_ref] * fields, at + 1, base + fields)

    def apply(act):
        for copy in firsts:
            act(copy)

        @pl.when(keeps)
        def _():
            for copy in kept:
                act(copy)

        @pl.when(jnp.logical_not(keeps))
        def _():
            for copy in gone:
                act(copy)

    return apply


def rows_body(owner_ref, row_ref, last_a_ref, last_b_ref, out_ref, zero_ref, sems):
    zero_ref[...] = jnp.zeros(zero_ref.shape, F32)
    apply = row_copies(owner_ref, row_ref, last_a_ref, last_b_ref, zero_ref, out_ref, 1, sems, 0)
    apply(lambda copy: copy.start())
    apply(lambda copy: copy.wait())


def finish_body(
    owner_any, coef_ref, edge_c_ref, code_ref, row_ref, last_a_ref, last_b_ref, partial_ref,
    out_ref, tile_ref, arrived_ref, zero_ref, owner_ref, sems
):
    fields, depth, width = row_ref.shape
    main = width // LANES
    half = arrived_ref.shape[0]
    arrives = arrival(code_ref)
    lane = lane_ids()
    row_id = lax.broadcasted_iota(jnp.int32, (depth, 1), 0)
    lower = lax.axis_index("region") == 0
    first = lane < 32
    base = half * main * (depth + 1)
    extra = wide(code_ref[base + depth * fields // 2 : base + depth * fields // 2 + 8, :])
    tile0 = tile_at(0)

    def beside(total, shift):
        return jnp.where(first, pltpu.roll(total, shift, 1), 0.0)

    def rows(row):
        return jnp.where(lower, 0.0, row), jnp.where(lower, row, 0.0)

    corners = []
    for kind in range(3):
        row = lane_sum(extra[3 + kind : 4 + kind] * scale_of(extra[2:3]), lane)
        places = [pltpu.roll(row, LANES - 32 * f, 1) if f else row for f in range(fields)]
        corners.append(jnp.where(first, jnp.concatenate(places, axis=0), 0.0))
    planes = []
    for g in range(fields // 2):
        pair = wide(code_ref[base + g * depth : base + (g + 1) * depth, :]) * scale_of(extra[g : g + 1])
        total = lane_sum(pair, lane)
        planes += [(beside(total, 32), beside(total, 64)), (beside(total, 96), total)]
    planes = [(now, jnp.where(first, then, 0.0)) for now, then in planes]
    own = [jnp.where(lower, now[depth - 1 : depth], now[0:1]) for now, _ in planes]
    edge_change = edge_c_ref[0:4, :] * (corners[0] + corners[1] + jnp.concatenate(own, axis=0))
    edge_sum = lane_sum(edge_change, lane)
    edge_sum = edge_sum + corners[2] + pltpu.roll(edge_sum, 32, 1)
    for f in range(fields):
        now, then = planes[f]
        low_row, high_row = rows(corners[0][f : f + 1])
        coef = coef_ref[f]
        change = coef * column_sum(now, row_id, low_row, high_row)
        total = lane_sum(change, lane)
        total = total + then + pltpu.roll(total, 32, 1)
        low_row, high_row = rows(edge_sum[f : f + 1])
        lap = column_sum(total, row_id, low_row, high_row) - 27.0 * change
        tile_ref[f] = row_ref[f, :, tile0] + 2.0 * change + coef * lap

    slot = jnp.where(arrives, 1, 0)
    last = pltpu.make_async_copy(tile_ref, out_ref.at[slot, :, :, tile0], sems.at[0])
    last.start()

    @pl.when(arrives)
    def _():
        decode(code_ref, arrived_ref)
        coming = code_copies(0, arrived_ref, out_ref, sems, 1)
        for copy in coming:
            copy.start()
        for copy in coming:
            copy.wait()

    @pl.when(jnp.logical_not(arrives))
    def _():
        load_map(owner_any, owner_ref, sems.at[1]).wait()
        zero_ref[...] = jnp.zeros(zero_ref.shape, F32)
        apply = row_copies(owner_ref, row_ref, last_a_ref, last_b_ref, zero_ref, out_ref, 0, sems, 1)
        blank = [
            pltpu.make_async_copy(zero_ref, out_ref.at[2, f], sems.at[1 + 2 * fields + f]) for f in range(fields)
        ]
        apply(lambda copy: copy.start())
        for copy in blank:
            copy.start()
        for copy in blank:
            copy.wait()
        apply(lambda copy: copy.wait())

    last.wait()


def place_body(first, code_a_ref, code_ref, partial_ref, out_ref, row_ref, sems):
    arrives = arrival(code_a_ref)
    decode(code_ref, row_ref)
    copies = code_copies(first, row_ref, out_ref, sems, 0)

    @pl.when(arrives)
    def _():
        for copy in copies:
            copy.start()
        for copy in copies:
            copy.wait()


def fast_on_device(u_now, u_prev, coef_store, store_map, new_owner):
    blocks, _, fields, depth, width = u_now.shape
    now = u_now.reshape(blocks, fields, depth, width)
    prev = u_prev.reshape(blocks, fields, depth, width)
    coef = coef_store[0, 0]
    count = lax.axis_size("blk")
    order = store_map.reshape(-1)
    order_hbm, now_hbm, prev_hbm, coef_hbm = (
        pltpu.with_memory_space_constraint(array, pltpu.HBM) for array in (order, now, prev, coef)
    )
    params = pltpu.CompilerParams(vmem_limit_bytes=48 * 1024 * 1024)

    def call(body, name, out_shape, in_specs, out_specs, scratch, args, **options):
        return pl.pallas_call(
            body,
            out_shape=out_shape,
            in_specs=in_specs,
            out_specs=out_specs,
            scratch_shapes=scratch,
            compiler_params=params,
            name=name,
            **options,
        )(*args)

    straight = jax.ShapeDtypeStruct((fields * depth + 16, LANES), BF16)
    diag = jax.ShapeDtypeStruct((depth + 32, LANES), BF16)
    tiles = jax.ShapeDtypeStruct((fields, depth, LANES), F32)
    y_out, edges, front, front_prev, front_coef = call(
        pack_region_body,
        "pack_region",
        (
            jax.ShapeDtypeStruct((5, depth, width), BF16),
            jax.ShapeDtypeStruct((depth, width), F32),
            tiles,
            tiles,
            jax.ShapeDtypeStruct((2, 4, depth, LANES), BF16),
        ),
        [HBM] * 4,
        (VMEM,) * 5,
        [
            pltpu.VMEM((blocks, fields, 8, width), F32),
            pltpu.VMEM((blocks, fields, 8, width), F32),
            pltpu.VMEM((4, 16, width), BF16),
            pltpu.SMEM(order.shape, jnp.int32),
            pltpu.SemaphoreType.DMA((15,)),
        ],
        (order_hbm, now_hbm, prev_hbm, coef_hbm),
    )
    left, dleft = call(
        pack_back_body, "pack_back", (straight, diag), [VMEM] * 4, (VMEM,) * 2, [], (edges, front, front_prev, front_coef)
    )

    swap = [(0, 1), (1, 0)]
    forward = [(i, (i + 1) % count) for i in range(count)]
    backward = [(i, (i - 1) % count) for i in range(count)]
    crossed = [(r * count + i, (1 - r) * count + (i - 1) % count) for r in range(2) for i in range(count)]
    y_in = lax.ppermute(y_out, "region", swap)
    from_right = lax.ppermute(left, "blk", backward)
    from_dright = lax.ppermute(dleft, ("region", "blk"), crossed)

    row = jax.ShapeDtypeStruct((fields, depth, width), F32)
    both = jax.ShapeDtypeStruct(now.shape, F32)
    now, box0, box1, drift, rim = call(
        local_body,
        "local",
        (both, row, row, both, jax.ShapeDtypeStruct((blocks, 8, width), F32)),
        [HBM] * 2,
        (VMEM,) * 5,
        [pltpu.VMEM(now.shape, F32), pltpu.SemaphoreType.DMA((2 * fields,))],
        (now_hbm, prev_hbm),
    )
    sums = jax.ShapeDtypeStruct((8, width), F32)
    edge = jax.ShapeDtypeStruct((8, LANES), F32)
    box1, side_lap, side_coef, side_rim = call(
        border_body,
        "border",
        (row, tiles, tiles, jax.ShapeDtypeStruct((2, 8, LANES), F32)),
        [VMEM] * 4,
        (VMEM,) * 4,
        [],
        (now, from_right, from_dright, box1),
        input_output_aliases={3: 0},
        cost_estimate=pl.CostEstimate(flops=0, transcendentals=0, bytes_accessed=40_000_000),
    )
    half = fields // 2
    part = jax.ShapeDtypeStruct((half, depth, width), F32)
    tiled = half * width // LANES
    codes = jax.ShapeDtypeStruct((tiled * (depth + 1), LANES), jnp.int16)
    more_codes = jax.ShapeDtypeStruct((tiled * (depth + 1) + half * depth + 8, LANES), jnp.int16)
    scalars = [pltpu.SMEM(order.shape, jnp.int32), pltpu.SMEM(new_owner.shape, jnp.int32)]
    powers = pltpu.VMEM((tiled, LANES), F32)
    box1, lap1, side1, sums1, last_a, code_a = call(
        last_row_a_body,
        "last_row",
        (row, tiles, tiles, sums, part, more_codes),
        [ANY] * 2 + [VMEM] * 12,
        (VMEM,) * 6,
        [powers, pltpu.VMEM((8, LANES), F32)] + scalars + [pltpu.SemaphoreType.DMA((2,))],
        (order, new_owner, now, coef, y_in, from_right, from_dright, box0, rim, side_lap, side_coef, side_rim, drift, box1),
        input_output_aliases={13: 0},
    )
    arrived_a = lax.ppermute(code_a, "blk", forward)
    last_b, code_b = call(
        functools.partial(last_row_b_body, half),
        "last_row",
        (part, codes),
        [ANY] + [VMEM] * 8,
        (VMEM,) * 2,
        [powers, scalars[0], pltpu.SemaphoreType.DMA],
        (order, now, coef, y_in, box1, drift, lap1, side1, sums1),
    )
    arrived_b = lax.ppermute(code_b, "blk", forward)
    box0, sums0, edge_c0 = call(
        first_edges_body,
        "first_edges",
        (row, sums, edge),
        [VMEM] * 3 + [ANY, VMEM],
        (VMEM,) * 3,
        [],
        (coef, y_in, rim, box1, box0),
        input_output_aliases={4: 0},
    )
    first, coef0 = call(
        first_row_body,
        "first_row",
        (row, tiles),
        [SMEM] + [VMEM] * 7,
        (VMEM,) * 2,
        [],
        (order, now, coef, y_in, box0, box1, drift, sums0),
    )
    whole = jax.ShapeDtypeStruct((blocks + 1, fields, depth, width), F32)
    placed = call(
        rows_body,
        "rows",
        whole,
        [SMEM] + [VMEM] * 3,
        ANY,
        [pltpu.VMEM((depth, width), F32), pltpu.SemaphoreType.DMA((2 * fields,))],
        (new_owner, first, last_a, last_b),
    )
    arrived_half = pltpu.VMEM((half, depth, width), F32)
    placed = call(
        finish_body,
        "finish",
        whole,
        [ANY] + [VMEM] * 6 + [ANY],
        ANY,
        [
            pltpu.VMEM((fields, depth, LANES), F32),
            arrived_half,
            pltpu.VMEM((depth, width), F32),
            scalars[1],
            pltpu.SemaphoreType.DMA((1 + 3 * fields,)),
        ],
        (new_owner, coef0, edge_c0, arrived_a, first, last_a, last_b, placed),
        input_output_aliases={7: 0},
    )
    placed = call(
        functools.partial(place_body, half),
        "place",
        whole,
        [VMEM, VMEM, ANY],
        ANY,
        [arrived_half, pltpu.SemaphoreType.DMA((2 * half,))],
        (arrived_a, arrived_b, placed),
        input_output_aliases={2: 0},
    )
    return placed[:, None]


def solution(mesh):
    def on_device(*args):
        blocks = args[0].shape[0]
        if lax.axis_size("region") == 2 and blocks == 2:
            return fast_on_device(*args)
        return general_on_device(*args)

    return jax.shard_map(
        on_device,
        mesh=mesh,
        in_specs=(
            P("blk", "region", None, None, None),
            P("blk", "region", None, None, None),
            P("blk", "region", None, None, None, None),
            P("blk", "region", None),
            P("blk"),
        ),
        out_specs=P("blk", "region", None, None, None),
        check_vma=False,
    )
```

```python
import functools

import jax
import jax.numpy as jnp
from jax import lax
from jax.experimental import pallas as pl
from jax.experimental.pallas import tpu as pltpu
from jax.sharding import PartitionSpec as P

STEPS = 2
LANES = 128
F32 = jnp.float32
BF16 = jnp.bfloat16
VMEM = pl.BlockSpec(memory_space=pltpu.VMEM)
SMEM = pl.BlockSpec(memory_space=pltpu.SMEM)
ANY = pl.BlockSpec(memory_space=pl.ANY)
HBM = pl.BlockSpec(memory_space=pltpu.HBM)


def extended_2(block, sides, width, periodic):
    for axis, dim in sides:
        count = lax.axis_size(axis)
        forward = [(i, i + 1) for i in range(count - 1)]
        if periodic:
            forward.append((count - 1, 0))
        backward = [(target, source) for source, target in forward]
        low = lax.ppermute(
            lax.slice_in_dim(block, block.shape[dim] - width, None, axis=dim), axis, forward
        )
        high = lax.ppermute(lax.slice_in_dim(block, 0, width, axis=dim), axis, backward)
        block = jnp.concatenate([low, block, high], axis=dim)
    return block


def shifted_2(value, axis, by):
    devices = lax.axis_size(axis)
    return lax.ppermute(value, axis, [(i, (i + by) % devices) for i in range(devices)])


def stencil_step(state_now, state_prev, coefficient, live_count):
    slot_count, field_count, edge_cells, plane_cells = state_now.shape
    padded = extended_2(state_now, (("region", 2),), 1, False)
    first_planes = padded[..., :edge_cells]
    last_planes = padded[..., plane_cells - edge_cells :]
    last_live = jnp.take(last_planes, live_count - 1, axis=0)
    rim_pair = jnp.stack([first_planes[0], last_live], axis=2)
    spread = extended_2(rim_pair.astype(jnp.bfloat16), (("blk", 2),), 1, True).astype(
        rim_pair.dtype
    )
    left_rim = spread[:, :, 0]
    right_rim = spread[:, :, 3]
    before_planes = jnp.concatenate([left_rim[None], last_planes[:-1]], axis=0)
    after_planes = jnp.pad(first_planes[1:], ((0, 1), (0, 0), (0, 0), (0, 0)))
    slot_ids = jnp.arange(slot_count)
    after_planes = jnp.where(
        (slot_ids == live_count - 1)[:, None, None, None], right_rim[None], after_planes
    )
    extended = jnp.concatenate([before_planes, padded, after_planes], axis=-1)
    width = extended.shape[-1]
    column = jnp.arange(width) % edge_cells
    lower_mask = (column != 0).astype(jnp.float32)
    upper_mask = (column != edge_cells - 1).astype(jnp.float32)
    margin = ((0, 0), (0, 0), (0, 0), (1, 1))
    shifted = jnp.pad(extended, margin)
    summed = shifted[..., :width] * lower_mask + extended + shifted[..., 2:] * upper_mask
    summed = (
        summed[..., : -2 * edge_cells]
        + summed[..., edge_cells:-edge_cells]
        + summed[..., 2 * edge_cells :]
    )
    box_sum = summed[:, :, :-2] + summed[:, :, 1:-1] + summed[:, :, 2:]
    laplace = box_sum - 27.0 * state_now
    return 2.0 * state_now - state_prev + coefficient.astype(jnp.float32) * laplace


def compact(members, valid_flags):
    slot_count = valid_flags.shape[0]
    place_index = jnp.cumsum(valid_flags) - 1
    target = jnp.arange(slot_count)
    chooser = (valid_flags[None, :] == 1) & (place_index[None, :] == target[:, None])
    source = jnp.sum(jnp.where(chooser, target[None, :], 0), axis=1)
    filled = jnp.sum(chooser.astype(jnp.int32), axis=1) > 0
    placed = tuple(
        (
            jnp.where(
                filled.reshape((slot_count,) + (1,) * (member.ndim - 1)),
                jnp.take(member, source, axis=0),
                jnp.zeros_like(member),
            )
            for member in members
        )
    )
    return (placed, jnp.sum(valid_flags))


def general_on_device(u_now, u_prev, coef_store, store_map, new_owner):
    state_now = u_now[:, 0]
    state_prev = u_prev[:, 0]
    blocks, fields, edge_cells, plane_cells = state_now.shape
    store_local = coef_store[0, 0]
    arrived = lax.all_to_all(store_local, "region", split_axis=0, concat_axis=0, tiled=True)
    flattened = arrived.reshape((-1,) + arrived.shape[2:])
    inverse = jnp.argsort(store_map[0, 0])
    coefficient = jnp.take(flattened, inverse, axis=0).reshape(
        blocks, fields, edge_cells, plane_cells
    )
    own_index = lax.axis_index("blk")
    goes_right = new_owner[blocks - 1] != own_index
    mark_right = goes_right.astype(jnp.float32).reshape(1)
    middle_flags = jnp.ones((blocks - 2,), jnp.int32)
    keep_first = (new_owner[0] == own_index).astype(jnp.int32).reshape(1)
    keep_last = (new_owner[blocks - 1] == own_index).astype(jnp.int32).reshape(1)
    for step_index in range(STEPS):
        state_now, state_prev = (
            stencil_step(state_now, state_prev, coefficient, blocks),
            state_now,
        )
    from_left = shifted_2((state_now[blocks - 1], mark_right), "blk", 1)
    valid_flags = jnp.concatenate(
        [(from_left[1] > 0.5).astype(jnp.int32), keep_first, middle_flags, keep_last]
    )
    stacked_now = jnp.concatenate([from_left[0][None], state_now], axis=0)
    placed, live_count = compact((stacked_now,), valid_flags)
    result = placed[0]
    return result[:, None]


def lane_ids():
    return lax.broadcasted_iota(jnp.int32, (1, LANES), 1)


def edge_start(lower, depth, size):
    return pl.multiple_of(jnp.where(lower, depth - size, 0), size)


def pack_region_body(
    map_hbm, owner_hbm, u_ref, p_ref, coef_ref, y_ref, edges_ref, ua_ref, pa_ref, ca_ref, ue_ref, pe_ref, ce_ref,
    map_ref, owner_ref, sems
):
    fields, depth, width = u_ref.shape[1:]
    region = lax.axis_index("region")
    lower = region == 0
    other = 1 - region
    half = depth // 2
    front = slice(0, LANES)
    edge8 = edge_start(lower, depth, 8)
    pair = jnp.where(lower, depth - 2, 0)
    slab = []
    for s in range(4):
        for h in range(2):
            part = slice(h * half, (h + 1) * half)
            slab.append(pltpu.make_async_copy(coef_ref.at[other, s, part], y_ref.at[s, part], sems.at[7 + 2 * s + h]))
    copies = [
        pltpu.make_async_copy(map_hbm, map_ref, sems.at[0]),
        pltpu.make_async_copy(owner_hbm, owner_ref, sems.at[15]),
        pltpu.make_async_copy(u_ref.at[:, :, pl.ds(pair, 2), :], ue_ref, sems.at[1]),
        pltpu.make_async_copy(p_ref.at[:, :, pl.ds(pair, 2), :], pe_ref, sems.at[2]),
        pltpu.make_async_copy(coef_ref.at[region, :, pl.ds(edge8, 8), :], ce_ref, sems.at[3]),
    ]
    beside = [
        pltpu.make_async_copy(u_ref.at[0, :, :, front], ua_ref, sems.at[4]),
        pltpu.make_async_copy(p_ref.at[0, :, :, front], pa_ref, sems.at[5]),
        pltpu.make_async_copy(coef_ref.at[:, :, :, front], ca_ref, sems.at[6]),
    ]
    for copy in copies + slab + beside:
        copy.start()
    for copy in copies:
        copy.wait()
    own_edge = jnp.where(lower, 1, 0)
    own_next = 1 - own_edge
    for m in range(2):
        for f in range(fields):
            at = m * fields + f
            near = ue_ref[m, f, pl.ds(own_edge, 1), :]
            edges_ref[at : at + 1, :] = near
            edges_ref[8 + at : 9 + at, :] = ue_ref[m, f, pl.ds(own_next, 1), :]
            edges_ref[16 + at : 17 + at, :] = 2.0 * near - pe_ref[m, f, pl.ds(own_edge, 1), :]
    for s in range(4):
        piece = ce_ref[s].astype(F32)
        edges_ref[24 + s : 25 + s, :] = jnp.where(lower, piece[7:8], piece[0:1])
    numbers = [map_ref[region * 4 + s] for s in range(4)] + [map_ref[other * 4 + s] for s in range(4)]
    for i, number in enumerate(numbers):
        edges_ref[28:29, tile_at(i)] = jnp.zeros((1, LANES), F32) + number.astype(F32)
    edges_ref[29:30, :] = jnp.zeros((1, width), F32) + jnp.where(owner_ref[1] != lax.axis_index("blk"), 1.0, 0.0)
    edges_ref[30:32, :] = jnp.zeros((2, width), F32)
    y_ref[4] = edges_ref[...].astype(BF16)
    for copy in slab + beside:
        copy.wait()


def pack_back_body(edges_ref, ua_ref, pa_ref, ca_ref, straight_ref, diag_ref):
    fields, depth, _ = ua_ref.shape
    region = lax.axis_index("region")
    lower = region == 0
    other = 1 - region
    lane = lane_ids()
    tag_rows = [edges_ref[28:29, tile_at(i)] for i in range(8)]
    blank = jnp.zeros((1, LANES), F32)
    for f in range(fields):
        now = ua_ref[f]
        ahead = 2.0 * now - pa_ref[f]
        piece = ca_ref[region, f].astype(F32)
        tile = jnp.where(
            lane < 64, now, jnp.where(lane < 96, pltpu.roll(ahead, 64, 1), pltpu.roll(piece, 96, 1))
        )
        straight_ref[f * depth : (f + 1) * depth, :] = tile.astype(BF16)
    far = [ca_ref[other, s].astype(F32) for s in range(4)]
    extra = [jnp.where(lower, piece[0:1], piece[depth - 1 : depth]) for piece in far] + tag_rows + [blank] * 4
    straight_ref[fields * depth : fields * depth + 16, :] = jnp.concatenate(extra, axis=0).astype(BF16)
    plane = jnp.zeros((depth, LANES), F32)
    for s in range(4):
        moved = pltpu.roll(far[s], 32 * s, 1) if s else far[s]
        plane = jnp.where((lane >= 32 * s) & (lane < 32 * s + 32), moved, plane)
    diag_ref[0:depth, :] = plane.astype(BF16)
    rows = [edges_ref[base : base + 4, 0:LANES] for base in (0, 8, 16, 24)]
    diag_ref[depth : depth + 32, :] = jnp.concatenate(rows + tag_rows + [blank] * 8, axis=0).astype(BF16)


def lane_sum(tile, lane):
    return sum_along_c(tile, *c_masks(lane))


def c_masks(lane):
    inside = lane & 31
    return inside != 0, inside != 31


def sum_along_c(tile, low, high):
    return (
        tile
        + jnp.where(low, pltpu.roll(tile, 1, 1), 0.0)
        + jnp.where(high, pltpu.roll(tile, LANES - 1, 1), 0.0)
    )


def nine_sum(tiles, lane):
    low, high = c_masks(lane)
    rows = [sum_along_c(tile, low, high) for tile in tiles]
    up = [pltpu.roll(row, 32, 1) for row in rows]
    down = [pltpu.roll(row, LANES - 32, 1) for row in rows]
    count = len(tiles)
    result = []
    for t in range(count):
        before = jnp.where(lane < 32, up[t - 1] if t else 0.0, up[t])
        after = jnp.where(lane >= 96, down[t + 1] if t < count - 1 else 0.0, down[t])
        result.append(rows[t] + before + after)
    return result


def column_sum(tile, row_id, low_row, high_row):
    depth = tile.shape[0]
    above = pltpu.roll(tile, 1, 0)
    below = pltpu.roll(tile, depth - 1, 0)
    return tile + jnp.where(row_id == 0, low_row, above) + jnp.where(row_id == depth - 1, high_row, below)


def local_body(
    map_hbm, u_hbm, p_hbm, coef_ref, u_ref, box0_ref, box1_ref, drift_ref, rim_ref, held_ref, p_ref, map_ref, sems
):
    fields, depth, width = u_ref.shape[1:]
    main = width // LANES
    copies = []
    for f in range(fields):
        copies.append(
            (
                pltpu.make_async_copy(u_hbm.at[:, f], u_ref.at[:, f], sems.at[2 * f]),
                pltpu.make_async_copy(p_hbm.at[:, f], p_ref.at[:, f], sems.at[2 * f + 1]),
            )
        )
    numbers = load_map(map_hbm, map_ref, sems.at[2 * fields])
    for pair in copies:
        for copy in pair:
            copy.start()
    held_ref[...] = jnp.zeros(held_ref.shape, held_ref.dtype)
    numbers.wait()
    region = lax.axis_index("region")
    for s in range(4):
        held_ref[map_ref[region * 4 + s]] = coef_ref[region, s]
    lower = lax.axis_index("region") == 0
    lane = lane_ids()
    row_id = lax.broadcasted_iota(jnp.int32, (depth, 1), 0)
    boxes = (box0_ref, box1_ref)
    for f in range(fields):
        for copy in copies[f]:
            copy.wait()
        now = [u_ref[m, f, :, tile_at(t)] for m in range(2) for t in range(main)]
        sums = nine_sum(now, lane)
        for i, (tile, total) in enumerate(zip(now, sums)):
            m, t = divmod(i, main)
            lanes = tile_at(t)
            rim_ref[m, f : f + 1, lanes] = jnp.where(lower, total[depth - 1 : depth], total[0:1])
            boxes[m][f, :, lanes] = column_sum(total, row_id, 0.0, 0.0) - 27.0 * tile
            drift_ref[m, f, :, lanes] = 2.0 * tile - p_ref[m, f, :, lanes]
    rim_ref[:, 4:8, :] = jnp.zeros((2, 4, width), F32)


def tile_at(t):
    return slice(t * LANES, (t + 1) * LANES)


class ColumnEdge:
    def __init__(self, coef_ref, y_ref):
        self.region = lax.axis_index("region")
        self.lower = self.region == 0
        self.coef = coef_ref
        self.depth = coef_ref.shape[2]
        self.extra = y_ref[4].astype(F32)
        self.tags = [self.extra[28:29, i * LANES : (i + 1) * LANES] for i in range(8)]
        self.field_id = lax.broadcasted_iota(jnp.int32, (4, LANES), 0).astype(F32)

    def near(self, m, lanes):
        return self.extra[4 * m : 4 * m + 4, lanes]

    def beyond(self, m, lanes):
        return self.extra[8 + 4 * m : 12 + 4 * m, lanes]

    def ahead(self, m, lanes):
        return self.extra[16 + 4 * m : 20 + 4 * m, lanes]

    def coefs(self, m, lanes):
        total = jnp.zeros((4, LANES), F32)
        for s in range(4):
            piece = self.coef[1 - self.region, s, :, lanes].astype(F32)
            held = jnp.where(self.lower, piece[0:1], piece[self.depth - 1 : self.depth])
            total = total + jnp.where(self.tags[s] == self.field_id + 4 * m, self.extra[24 + s : 25 + s, lanes], 0.0)
            total = total + jnp.where(self.tags[4 + s] == self.field_id + 4 * m, held, 0.0)
        return total

    def own(self, tile):
        return jnp.where(self.lower, tile[self.depth - 1 : self.depth], tile[0:1])

    def rows(self, row):
        return jnp.where(self.lower, 0.0, row), jnp.where(self.lower, row, 0.0)


def border_body(u_ref, straight_ref, diag_ref, box_in, box_ref, side_lap_ref, side_coef_ref, rim_ref):
    fields, depth, width = u_ref.shape[1:]
    lane = lane_ids()
    row_id = lax.broadcasted_iota(jnp.int32, (depth, 1), 0)
    lower = lax.axis_index("region") == 0
    before = slice(width - LANES, width)
    facing = lane >= 96
    tags = [straight_ref[fields * depth : fields * depth + 16, :].astype(F32)[4 + i : 5 + i] for i in range(8)]
    planes = []
    for s in range(4):
        planes.append(pltpu.roll(straight_ref[s * depth : (s + 1) * depth, :].astype(F32), 32, 1))
    diag_tile = diag_ref[0:depth, :].astype(F32)
    for s in range(4):
        planes.append(pltpu.roll(diag_tile, LANES - 32 * s, 1) if s else diag_tile)
    for f in range(fields):
        inner = u_ref[1, f, :, before]
        remote = straight_ref[f * depth : (f + 1) * depth, :].astype(F32)
        inner_sum, remote_sum = nine_sum([inner, remote], lane)
        for i, tile in enumerate((inner_sum, remote_sum)):
            rim_ref[i, f : f + 1, :] = jnp.where(lower, tile[depth - 1 : depth], tile[0:1])
        halo_c = jnp.zeros((depth, LANES), F32)
        for i in range(8):
            halo_c = halo_c + jnp.where(tags[i] == F32(f), planes[i], 0.0)
        side_coef_ref[f] = halo_c
        side_lap_ref[f] = column_sum(remote_sum, row_id, 0.0, 0.0) - 27.0 * remote
        whole = column_sum(inner_sum, row_id, 0.0, 0.0) - 27.0 * inner
        box_ref[f, :, before] = jnp.where(facing, whole, box_in[f, :, before])
    rim_ref[:, 4:8, :] = jnp.zeros((2, 4, LANES), F32)


def last_edges(
    coef_ref, y_ref, straight_ref, diag_ref, box0_ref, rim_ref, side_lap_ref, side_coef_ref, side_rim_ref, box_in,
    box_ref, lap_ref, side_ref, sums_ref
):
    fields, depth, width = box_in.shape
    main = width // LANES
    lane = lane_ids()
    column = ColumnEdge(coef_ref, y_ref)
    before = slice(width - LANES, width)
    extra_s = straight_ref[fields * depth : fields * depth + 16, :].astype(F32)
    extra_d = diag_ref[depth : depth + 32, :].astype(F32)
    tags_d = [extra_d[16 + i : 17 + i] for i in range(8)]

    def edge_tiles(of, base):
        return [of(0, before)] + [of(1, tile_at(t)) for t in range(main)] + [extra_d[base : base + 4]]

    near = edge_tiles(column.near, 0)
    beyond = edge_tiles(column.beyond, 4)
    ahead = edge_tiles(column.ahead, 8)
    corner = jnp.zeros((4, LANES), F32)
    for s in range(4):
        corner = corner + jnp.where(tags_d[s] == column.field_id, extra_d[12 + s : 13 + s], 0.0)
        corner = corner + jnp.where(tags_d[4 + s] == column.field_id, extra_s[s : s + 1], 0.0)
    edge_c = [column.coefs(0, before)] + [column.coefs(1, tile_at(t)) for t in range(main)] + [corner]
    near_sum = nine_sum(near, lane)
    beyond_sum = nine_sum(beyond, lane)
    top = slice(0, 1)
    bottom = slice(depth - 1, depth)
    for f in range(fields):
        for t in range(main):
            low_row, high_row = column.rows(near_sum[t + 1][f : f + 1])
            lanes = tile_at(t)
            box_ref[f, top, lanes] = box_in[f, top, lanes] + low_row
            box_ref[f, bottom, lanes] = box_in[f, bottom, lanes] + high_row
        remote = straight_ref[f * depth : (f + 1) * depth, :].astype(F32)
        side_ref[f] = pltpu.roll(remote, 64, 1) + side_coef_ref[f] * side_lap_ref[f]
        low_row, high_row = column.rows(near_sum[main + 1][f : f + 1])
        side_ref[f, top] += side_coef_ref[f, top] * low_row
        side_ref[f, bottom] += side_coef_ref[f, bottom] * high_row
        low_row, high_row = column.rows(near_sum[0][f : f + 1])
        lap_ref[f] = box0_ref[f, :, before]
        lap_ref[f, top] += low_row
        lap_ref[f, bottom] += high_row
    rims = [rim_ref[0, 0:4, before]] + [rim_ref[1, 0:4, tile_at(t)] for t in range(main)] + [side_rim_ref[1, 0:4, :]]
    rims[main] = jnp.where(lane >= 96, side_rim_ref[0, 0:4, :], rims[main])
    stepped = []
    for t in range(main + 2):
        box = near_sum[t] + beyond_sum[t] + rims[t]
        stepped.append(ahead[t] + edge_c[t] * (box - 27.0 * near[t]))
    stepped_sum = nine_sum(stepped, lane)
    for t in range(main):
        sums_ref[0:4, tile_at(t)] = stepped_sum[t + 1]
    sums_ref[4:8, :] = jnp.zeros((4, width), F32)
    return stepped[main]


def first_edges_body(coef_ref, y_ref, rim_ref, box1_ref, box_in, box_ref, sums_ref, edge_c_ref):
    fields, depth, width = box_in.shape
    main = width // LANES
    lane = lane_ids()
    column = ColumnEdge(coef_ref, y_ref)
    after = slice(0, LANES)

    def edge_tiles(of):
        return [of(0, tile_at(t)) for t in range(main)] + [of(1, after)]

    near = edge_tiles(column.near)
    near_sum = nine_sum(near, lane)
    beyond_sum = nine_sum(edge_tiles(column.beyond), lane)
    ahead = edge_tiles(column.ahead)
    edge_c = edge_tiles(column.coefs)
    for f in range(fields):
        for t in range(main):
            low_row, high_row = column.rows(near_sum[t][f : f + 1])
            lanes = tile_at(t)
            box_ref[f, 0:1, lanes] = box_in[f, 0:1, lanes] + low_row
            box_ref[f, depth - 1 : depth, lanes] = box_in[f, depth - 1 : depth, lanes] + high_row
    rims = [rim_ref[0, 0:4, tile_at(t)] for t in range(main)] + [rim_ref[1, 0:4, after]]
    stepped = []
    for t in range(main + 1):
        box = near_sum[t] + beyond_sum[t] + rims[t]
        stepped.append(ahead[t] + edge_c[t] * (box - 27.0 * near[t]))
    stepped_sum = nine_sum(stepped, lane)
    for t in range(main):
        sums_ref[0:4, tile_at(t)] = stepped_sum[t]
    sums_ref[4:8, :] = jnp.zeros((4, width), F32)
    edge_c_ref[0:4, :] = edge_c[0]
    edge_c_ref[4:8, :] = jnp.zeros((4, LANES), F32)


def load_map(map_any, map_ref, sem):
    copy = pltpu.make_async_copy(map_any, map_ref, sem)
    copy.start()
    return copy


class Pieces:
    def __init__(self, edges_ref, held_ref, slab_ref):
        self.held, self.slab = held_ref, slab_ref
        self.tags = [edges_ref[28:29, tile_at(4 + s)] for s in range(4)]

    def piece(self, number):
        here = [tag == F32(number) for tag in self.tags]

        def tile(lanes):
            total = self.held[number, :, lanes].astype(F32)
            for s, mask in enumerate(here):
                total = jnp.where(mask, self.slab[s, :, lanes].astype(F32), total)
            return total

        return tile


def second_step(now, before, total, coef, row_id, row, lower):
    low_row, high_row = jnp.where(lower, 0.0, row), jnp.where(lower, row, 0.0)
    lap = column_sum(total, row_id, low_row, high_row) - 27.0 * now
    return 2.0 * now - before + coef * lap


CODES = 32000.0


def power_of(size):
    return jnp.ceil(jnp.log2(jnp.maximum(size, 1e-30)))


def coded(value, power):
    return jnp.floor(value * (CODES * jnp.exp2(-power)) + 0.5)


def narrow(value):
    return value.astype(jnp.int32).astype(jnp.int16)


def wide(code):
    return code.astype(jnp.int32).astype(F32)


def scale_of(power):
    return jnp.exp2(power) * (1.0 / CODES)


def last_row_a_body(
    edges_ref, u_ref, coef_ref, held_ref, y_ref, straight_ref, diag_ref, box0_ref, rim_ref, side_lap_ref, side_coef_ref,
    side_rim_ref, drift_ref, box_in, box_ref, lap_ref, side_ref, sums_ref, row_ref, code_ref, power_ref, extra_ref
):
    tail = last_edges(
        coef_ref, y_ref, straight_ref, diag_ref, box0_ref, rim_ref, side_lap_ref, side_coef_ref, side_rim_ref, box_in,
        box_ref, lap_ref, side_ref, sums_ref
    )
    refs = (edges_ref, u_ref, held_ref, y_ref, box_ref, drift_ref, lap_ref, side_ref, sums_ref, row_ref, code_ref, power_ref)
    last_row(0, *refs, more=(tail, extra_ref))


def last_row_b_body(first, *refs):
    last_row(first, *refs)


def last_row(
    first, edges_ref, u_ref, held_ref, y_ref, box_ref, drift_ref, lap_ref, side_ref, sums_ref, row_ref, code_ref, power_ref,
    more=None
):
    count, depth, width = row_ref.shape
    fields = u_ref.shape[1]
    main = width // LANES
    lane = lane_ids()
    row_id = lax.broadcasted_iota(jnp.int32, (depth, 1), 0)
    pieces = Pieces(edges_ref, held_ref, y_ref)
    lower = lax.axis_index("region") == 0
    before = slice(width - LANES, width)
    last_tiles = []
    for f in range(first, first + count):
        coef = pieces.piece(fields + f)
        coefs = [coef(tile_at(t)) for t in range(main)]
        middle = [drift_ref[1, f, :, tile_at(t)] + coefs[t] * box_ref[f, :, tile_at(t)] for t in range(main)]
        local = drift_ref[0, f, :, before] + pieces.piece(f)(before) * lap_ref[f]
        sums = nine_sum([local] + middle + [side_ref[f]], lane)
        for t in range(main):
            lanes = tile_at(t)
            row = sums_ref[f : f + 1, lanes]
            value = second_step(middle[t], u_ref[1, f, :, lanes], sums[t + 1], coefs[t], row_id, row, lower)
            row_ref[f - first, :, lanes] = value
            power = power_of(jnp.max(jnp.abs(value), axis=0, keepdims=True))
            at = (f - first) * main + t
            code_ref[at * depth : (at + 1) * depth, :] = narrow(coded(value, power))
            power_ref[at : at + 1, :] = power
        last_tiles.append(middle[main - 1])
    base = count * main * depth
    code_ref[base : base + count * main, :] = narrow(power_ref[...])
    if more is not None:
        tail, extra_ref = more
        base += count * main
        both = []
        for f in range(fields):
            if f < count:
                stepped = last_tiles[f]
            else:
                stepped = drift_ref[1, f, :, before] + pieces.piece(fields + f)(before) * box_ref[f, :, before]
            both.append(jnp.where(lane >= 96, u_ref[1, f, :, before], pltpu.roll(stepped, 96, 1)))
        for g in range(fields // 2):
            pair = jnp.where(lane >= 64, both[2 * g], pltpu.roll(both[2 * g + 1], 64, 1))
            power = power_of(jnp.max(jnp.abs(pair), axis=0, keepdims=True))
            code_ref[base : base + depth, :] = narrow(coded(pair, power))
            extra_ref[g : g + 1, :] = power
            base += depth
        near = y_ref[4, 0:16, before].astype(F32)
        kinds = []
        for rows in (near[4:8], near[12:16], tail):
            kind = jnp.zeros((1, LANES), F32)
            for f in range(fields):
                shift = (32 * f + 32) % LANES
                row = rows[f : f + 1]
                kind = jnp.where(lane // 32 == f, pltpu.roll(row, shift, 1) if shift else row, kind)
            kinds.append(kind)
        power = power_of(jnp.maximum(jnp.maximum(jnp.abs(kinds[0]), jnp.abs(kinds[1])), jnp.abs(kinds[2])))
        extra_ref[2:3, :] = power
        for i, kind in enumerate(kinds):
            extra_ref[3 + i : 4 + i, :] = coded(kind, power)
        extra_ref[6:7, :] = edges_ref[29:30, 0:LANES]
        extra_ref[7:8, :] = jnp.zeros((1, LANES), F32)
        code_ref[base : base + 8, :] = narrow(extra_ref[...])


def first_row_body(edges_ref, u_ref, held_ref, y_ref, box_ref, box1_ref, drift_ref, sums_ref, row_ref, coef0_ref):
    fields, depth, width = u_ref.shape[1:]
    main = width // LANES
    lane = lane_ids()
    row_id = lax.broadcasted_iota(jnp.int32, (depth, 1), 0)
    pieces = Pieces(edges_ref, held_ref, y_ref)
    lower = lax.axis_index("region") == 0
    after = slice(0, LANES)
    for f in range(fields):
        coef = pieces.piece(f)
        coefs = [coef(tile_at(t)) for t in range(main)]
        now = [drift_ref[0, f, :, tile_at(t)] + coefs[t] * box_ref[f, :, tile_at(t)] for t in range(main)]
        local = drift_ref[1, f, :, after] + pieces.piece(fields + f)(after) * box1_ref[f, :, after]
        sums = nine_sum(now + [local], lane)
        coef0_ref[f] = coefs[0]
        for t in range(main):
            lanes = tile_at(t)
            row = sums_ref[f : f + 1, lanes]
            row_ref[f, :, lanes] = second_step(now[t], u_ref[0, f, :, lanes], sums[t], coefs[t], row_id, row, lower)


def arrival(code_ref):
    rows = code_ref.shape[0]
    return wide(code_ref[rows - 8 : rows, :])[6, 0] > 0.5


def code_copies(first, row_ref, out_ref, sems, base):
    count, depth, _ = row_ref.shape
    part = depth // 2
    copies = []
    for f in range(count):
        for h in range(2):
            rows = slice(h * part, (h + 1) * part)
            sem = sems.at[base + 2 * f + h]
            copies.append(pltpu.make_async_copy(row_ref.at[f, rows], out_ref.at[0, first + f, rows], sem))
    return copies


def decode(code_ref, row_ref):
    count, depth, width = row_ref.shape
    main = width // LANES
    base = count * main * depth
    scale = scale_of(wide(code_ref[base : base + count * main, :]))
    for f in range(count):
        for t in range(main):
            at = f * main + t
            row_ref[f, :, tile_at(t)] = wide(code_ref[at * depth : (at + 1) * depth, :]) * scale[at : at + 1]


def row_copies(owner_ref, row_ref, last_a_ref, last_b_ref, zero_ref, out_ref, at, sems, base):
    fields, _, width = row_ref.shape
    half = last_a_ref.shape[0]
    keeps = owner_ref[1] == lax.axis_index("blk")
    rest = slice(LANES, width)
    sources = [last_a_ref.at[f] for f in range(half)] + [last_b_ref.at[f] for f in range(half)]

    def copies(sources, at, base):
        return [pltpu.make_async_copy(source, out_ref.at[at, f], sems.at[base + f]) for f, source in enumerate(sources)]

    firsts = [
        pltpu.make_async_copy(row_ref.at[f, :, rest], out_ref.at[at, f, :, rest], sems.at[base + f])
        for f in range(fields)
    ]
    kept = copies(sources, at + 1, base + fields)
    gone = copies([zero_ref] * fields, at + 1, base + fields)

    def apply(act):
        for copy in firsts:
            act(copy)

        @pl.when(keeps)
        def _():
            for copy in kept:
                act(copy)

        @pl.when(jnp.logical_not(keeps))
        def _():
            for copy in gone:
                act(copy)

    return apply


def rows_body(owner_ref, row_ref, last_a_ref, last_b_ref, out_ref, zero_ref, sems):
    zero_ref[...] = jnp.zeros(zero_ref.shape, F32)
    apply = row_copies(owner_ref, row_ref, last_a_ref, last_b_ref, zero_ref, out_ref, 1, sems, 0)
    apply(lambda copy: copy.start())
    apply(lambda copy: copy.wait())


def finish_body(
    owner_any, coef_ref, edge_c_ref, code_ref, row_ref, last_a_ref, last_b_ref, partial_ref,
    out_ref, tile_ref, arrived_ref, zero_ref, owner_ref, sems
):
    fields, depth, width = row_ref.shape
    main = width // LANES
    half = arrived_ref.shape[0]
    arrives = arrival(code_ref)
    lane = lane_ids()
    row_id = lax.broadcasted_iota(jnp.int32, (depth, 1), 0)
    lower = lax.axis_index("region") == 0
    first = lane < 32
    base = half * main * (depth + 1)
    extra = wide(code_ref[base + depth * fields // 2 : base + depth * fields // 2 + 8, :])
    tile0 = tile_at(0)

    def beside(total, shift):
        return jnp.where(first, pltpu.roll(total, shift, 1), 0.0)

    def rows(row):
        return jnp.where(lower, 0.0, row), jnp.where(lower, row, 0.0)

    corners = []
    for kind in range(3):
        row = lane_sum(extra[3 + kind : 4 + kind] * scale_of(extra[2:3]), lane)
        places = [pltpu.roll(row, LANES - 32 * f, 1) if f else row for f in range(fields)]
        corners.append(jnp.where(first, jnp.concatenate(places, axis=0), 0.0))
    planes = []
    for g in range(fields // 2):
        pair = wide(code_ref[base + g * depth : base + (g + 1) * depth, :]) * scale_of(extra[g : g + 1])
        total = lane_sum(pair, lane)
        planes += [(beside(total, 32), beside(total, 64)), (beside(total, 96), total)]
    planes = [(now, jnp.where(first, then, 0.0)) for now, then in planes]
    own = [jnp.where(lower, now[depth - 1 : depth], now[0:1]) for now, _ in planes]
    edge_change = edge_c_ref[0:4, :] * (corners[0] + corners[1] + jnp.concatenate(own, axis=0))
    edge_sum = lane_sum(edge_change, lane)
    edge_sum = edge_sum + corners[2] + pltpu.roll(edge_sum, 32, 1)
    for f in range(fields):
        now, then = planes[f]
        low_row, high_row = rows(corners[0][f : f + 1])
        coef = coef_ref[f]
        change = coef * column_sum(now, row_id, low_row, high_row)
        total = lane_sum(change, lane)
        total = total + then + pltpu.roll(total, 32, 1)
        low_row, high_row = rows(edge_sum[f : f + 1])
        lap = column_sum(total, row_id, low_row, high_row) - 27.0 * change
        tile_ref[f] = row_ref[f, :, tile0] + 2.0 * change + coef * lap

    slot = jnp.where(arrives, 1, 0)
    last = pltpu.make_async_copy(tile_ref, out_ref.at[slot, :, :, tile0], sems.at[0])
    last.start()

    @pl.when(arrives)
    def _():
        decode(code_ref, arrived_ref)
        coming = code_copies(0, arrived_ref, out_ref, sems, 1)
        for copy in coming:
            copy.start()
        for copy in coming:
            copy.wait()

    @pl.when(jnp.logical_not(arrives))
    def _():
        load_map(owner_any, owner_ref, sems.at[1]).wait()
        zero_ref[...] = jnp.zeros(zero_ref.shape, F32)
        apply = row_copies(owner_ref, row_ref, last_a_ref, last_b_ref, zero_ref, out_ref, 0, sems, 1)
        blank = [
            pltpu.make_async_copy(zero_ref, out_ref.at[2, f], sems.at[1 + 2 * fields + f]) for f in range(fields)
        ]
        apply(lambda copy: copy.start())
        for copy in blank:
            copy.start()
        for copy in blank:
            copy.wait()
        apply(lambda copy: copy.wait())

    last.wait()


def place_body(first, code_a_ref, code_ref, partial_ref, out_ref, row_ref, sems):
    arrives = arrival(code_a_ref)
    decode(code_ref, row_ref)
    copies = code_copies(first, row_ref, out_ref, sems, 0)

    @pl.when(arrives)
    def _():
        for copy in copies:
            copy.start()
        for copy in copies:
            copy.wait()


def fast_on_device(u_now, u_prev, coef_store, store_map, new_owner):
    blocks, _, fields, depth, width = u_now.shape
    now = u_now.reshape(blocks, fields, depth, width)
    prev = u_prev.reshape(blocks, fields, depth, width)
    coef = coef_store[0, 0]
    count = lax.axis_size("blk")
    order = store_map.reshape(-1)
    order_hbm, owner_hbm, now_hbm, prev_hbm, coef_hbm = (
        pltpu.with_memory_space_constraint(array, pltpu.HBM) for array in (order, new_owner, now, prev, coef)
    )
    params = pltpu.CompilerParams(vmem_limit_bytes=48 * 1024 * 1024)

    def call(body, name, out_shape, in_specs, out_specs, scratch, args, **options):
        return pl.pallas_call(
            body,
            out_shape=out_shape,
            in_specs=in_specs,
            out_specs=out_specs,
            scratch_shapes=scratch,
            compiler_params=params,
            name=name,
            **options,
        )(*args)

    straight = jax.ShapeDtypeStruct((fields * depth + 16, LANES), BF16)
    diag = jax.ShapeDtypeStruct((depth + 32, LANES), BF16)
    tiles = jax.ShapeDtypeStruct((fields, depth, LANES), F32)
    y_out, edges, front, front_prev, front_coef = call(
        pack_region_body,
        "pack_region",
        (
            jax.ShapeDtypeStruct((5, depth, width), BF16),
            jax.ShapeDtypeStruct((depth, width), F32),
            tiles,
            tiles,
            jax.ShapeDtypeStruct((2, 4, depth, LANES), BF16),
        ),
        [HBM] * 5,
        (VMEM,) * 5,
        [
            pltpu.VMEM((blocks, fields, 2, width), F32),
            pltpu.VMEM((blocks, fields, 2, width), F32),
            pltpu.VMEM((4, 8, width), BF16),
            pltpu.SMEM(order.shape, jnp.int32),
            pltpu.SMEM(new_owner.shape, jnp.int32),
            pltpu.SemaphoreType.DMA((16,)),
        ],
        (order_hbm, owner_hbm, now_hbm, prev_hbm, coef_hbm),
    )
    left, dleft = call(
        pack_back_body, "pack_back", (straight, diag), [VMEM] * 4, (VMEM,) * 2, [], (edges, front, front_prev, front_coef)
    )

    swap = [(0, 1), (1, 0)]
    forward = [(i, (i + 1) % count) for i in range(count)]
    backward = [(i, (i - 1) % count) for i in range(count)]
    crossed = [(r * count + i, (1 - r) * count + (i - 1) % count) for r in range(2) for i in range(count)]
    y_in = lax.ppermute(y_out, "region", swap)
    from_right = lax.ppermute(left, "blk", backward)
    from_dright = lax.ppermute(dleft, ("region", "blk"), crossed)

    row = jax.ShapeDtypeStruct((fields, depth, width), F32)
    both = jax.ShapeDtypeStruct(now.shape, F32)
    now, box0, box1, drift, rim, held = call(
        local_body,
        "local",
        (
            both,
            row,
            row,
            both,
            jax.ShapeDtypeStruct((blocks, 8, width), F32),
            jax.ShapeDtypeStruct((blocks * fields, depth, width), BF16),
        ),
        [HBM] * 3 + [VMEM],
        (VMEM,) * 6,
        [
            pltpu.VMEM(now.shape, F32),
            pltpu.SMEM(order.shape, jnp.int32),
            pltpu.SemaphoreType.DMA((2 * fields + 1,)),
        ],
        (order_hbm, now_hbm, prev_hbm, coef),
    )
    sums = jax.ShapeDtypeStruct((8, width), F32)
    edge = jax.ShapeDtypeStruct((8, LANES), F32)
    box1, side_lap, side_coef, side_rim = call(
        border_body,
        "border",
        (row, tiles, tiles, jax.ShapeDtypeStruct((2, 8, LANES), F32)),
        [VMEM] * 4,
        (VMEM,) * 4,
        [],
        (now, from_right, from_dright, box1),
        input_output_aliases={3: 0},
        cost_estimate=pl.CostEstimate(flops=0, transcendentals=0, bytes_accessed=40_000_000),
    )
    half = fields // 2
    part = jax.ShapeDtypeStruct((half, depth, width), F32)
    tiled = half * width // LANES
    codes = jax.ShapeDtypeStruct((tiled * (depth + 1), LANES), jnp.int16)
    more_codes = jax.ShapeDtypeStruct((tiled * (depth + 1) + half * depth + 8, LANES), jnp.int16)
    powers = pltpu.VMEM((tiled, LANES), F32)
    box1, lap1, side1, sums1, last_a, code_a = call(
        last_row_a_body,
        "last_row",
        (row, tiles, tiles, sums, part, more_codes),
        [VMEM] * 14,
        (VMEM,) * 6,
        [powers, pltpu.VMEM((8, LANES), F32)],
        (edges, now, coef, held, y_in, from_right, from_dright, box0, rim, side_lap, side_coef, side_rim, drift, box1),
        input_output_aliases={13: 0},
    )
    arrived_a = lax.ppermute(code_a, "blk", forward)
    last_b, code_b = call(
        functools.partial(last_row_b_body, half),
        "last_row",
        (part, codes),
        [VMEM] * 9,
        (VMEM,) * 2,
        [powers],
        (edges, now, held, y_in, box1, drift, lap1, side1, sums1),
    )
    arrived_b = lax.ppermute(code_b, "blk", forward)
    box0, sums0, edge_c0 = call(
        first_edges_body,
        "first_edges",
        (row, sums, edge),
        [VMEM] * 3 + [ANY, VMEM],
        (VMEM,) * 3,
        [],
        (coef, y_in, rim, box1, box0),
        input_output_aliases={4: 0},
    )
    first, coef0 = call(
        first_row_body,
        "first_row",
        (row, tiles),
        [VMEM] * 8,
        (VMEM,) * 2,
        [],
        (edges, now, held, y_in, box0, box1, drift, sums0),
    )
    whole = jax.ShapeDtypeStruct((blocks + 1, fields, depth, width), F32)
    placed = call(
        rows_body,
        "rows",
        whole,
        [SMEM] + [VMEM] * 3,
        ANY,
        [pltpu.VMEM((depth, width), F32), pltpu.SemaphoreType.DMA((2 * fields,))],
        (new_owner, first, last_a, last_b),
    )
    arrived_half = pltpu.VMEM((half, depth, width), F32)
    placed = call(
        finish_body,
        "finish",
        whole,
        [ANY] + [VMEM] * 6 + [ANY],
        ANY,
        [
            pltpu.VMEM((fields, depth, LANES), F32),
            arrived_half,
            pltpu.VMEM((depth, width), F32),
            pltpu.SMEM(new_owner.shape, jnp.int32),
            pltpu.SemaphoreType.DMA((1 + 3 * fields,)),
        ],
        (new_owner, coef0, edge_c0, arrived_a, first, last_a, last_b, placed),
        input_output_aliases={7: 0},
    )
    placed = call(
        functools.partial(place_body, half),
        "place",
        whole,
        [VMEM, VMEM, ANY],
        ANY,
        [arrived_half, pltpu.SemaphoreType.DMA((2 * half,))],
        (arrived_a, arrived_b, placed),
        input_output_aliases={2: 0},
    )
    return placed[:, None]


def solution(mesh):
    def on_device(*args):
        blocks = args[0].shape[0]
        if lax.axis_size("region") == 2 and blocks == 2:
            return fast_on_device(*args)
        return general_on_device(*args)

    return jax.shard_map(
        on_device,
        mesh=mesh,
        in_specs=(
            P("blk", "region", None, None, None),
            P("blk", "region", None, None, None),
            P("blk", "region", None, None, None, None),
            P("blk", "region", None),
            P("blk"),
        ),
        out_specs=P("blk", "region", None, None, None),
        check_vma=False,
    )
```

```python
import functools

import jax
import jax.numpy as jnp
from jax import lax
from jax.experimental import pallas as pl
from jax.experimental.pallas import tpu as pltpu
from jax.sharding import PartitionSpec as P

STEPS = 2
LANES = 128
F32 = jnp.float32
BF16 = jnp.bfloat16
VMEM = pl.BlockSpec(memory_space=pltpu.VMEM)
SMEM = pl.BlockSpec(memory_space=pltpu.SMEM)
ANY = pl.BlockSpec(memory_space=pl.ANY)
HBM = pl.BlockSpec(memory_space=pltpu.HBM)


def extended_2(block, sides, width, periodic):
    for axis, dim in sides:
        count = lax.axis_size(axis)
        forward = [(i, i + 1) for i in range(count - 1)]
        if periodic:
            forward.append((count - 1, 0))
        backward = [(target, source) for source, target in forward]
        low = lax.ppermute(
            lax.slice_in_dim(block, block.shape[dim] - width, None, axis=dim), axis, forward
        )
        high = lax.ppermute(lax.slice_in_dim(block, 0, width, axis=dim), axis, backward)
        block = jnp.concatenate([low, block, high], axis=dim)
    return block


def shifted_2(value, axis, by):
    devices = lax.axis_size(axis)
    return lax.ppermute(value, axis, [(i, (i + by) % devices) for i in range(devices)])


def stencil_step(state_now, state_prev, coefficient, live_count):
    slot_count, field_count, edge_cells, plane_cells = state_now.shape
    padded = extended_2(state_now, (("region", 2),), 1, False)
    first_planes = padded[..., :edge_cells]
    last_planes = padded[..., plane_cells - edge_cells :]
    last_live = jnp.take(last_planes, live_count - 1, axis=0)
    rim_pair = jnp.stack([first_planes[0], last_live], axis=2)
    spread = extended_2(rim_pair.astype(jnp.bfloat16), (("blk", 2),), 1, True).astype(
        rim_pair.dtype
    )
    left_rim = spread[:, :, 0]
    right_rim = spread[:, :, 3]
    before_planes = jnp.concatenate([left_rim[None], last_planes[:-1]], axis=0)
    after_planes = jnp.pad(first_planes[1:], ((0, 1), (0, 0), (0, 0), (0, 0)))
    slot_ids = jnp.arange(slot_count)
    after_planes = jnp.where(
        (slot_ids == live_count - 1)[:, None, None, None], right_rim[None], after_planes
    )
    extended = jnp.concatenate([before_planes, padded, after_planes], axis=-1)
    width = extended.shape[-1]
    column = jnp.arange(width) % edge_cells
    lower_mask = (column != 0).astype(jnp.float32)
    upper_mask = (column != edge_cells - 1).astype(jnp.float32)
    margin = ((0, 0), (0, 0), (0, 0), (1, 1))
    shifted = jnp.pad(extended, margin)
    summed = shifted[..., :width] * lower_mask + extended + shifted[..., 2:] * upper_mask
    summed = (
        summed[..., : -2 * edge_cells]
        + summed[..., edge_cells:-edge_cells]
        + summed[..., 2 * edge_cells :]
    )
    box_sum = summed[:, :, :-2] + summed[:, :, 1:-1] + summed[:, :, 2:]
    laplace = box_sum - 27.0 * state_now
    return 2.0 * state_now - state_prev + coefficient.astype(jnp.float32) * laplace


def compact(members, valid_flags):
    slot_count = valid_flags.shape[0]
    place_index = jnp.cumsum(valid_flags) - 1
    target = jnp.arange(slot_count)
    chooser = (valid_flags[None, :] == 1) & (place_index[None, :] == target[:, None])
    source = jnp.sum(jnp.where(chooser, target[None, :], 0), axis=1)
    filled = jnp.sum(chooser.astype(jnp.int32), axis=1) > 0
    placed = tuple(
        (
            jnp.where(
                filled.reshape((slot_count,) + (1,) * (member.ndim - 1)),
                jnp.take(member, source, axis=0),
                jnp.zeros_like(member),
            )
            for member in members
        )
    )
    return (placed, jnp.sum(valid_flags))


def general_on_device(u_now, u_prev, coef_store, store_map, new_owner):
    state_now = u_now[:, 0]
    state_prev = u_prev[:, 0]
    blocks, fields, edge_cells, plane_cells = state_now.shape
    store_local = coef_store[0, 0]
    arrived = lax.all_to_all(store_local, "region", split_axis=0, concat_axis=0, tiled=True)
    flattened = arrived.reshape((-1,) + arrived.shape[2:])
    inverse = jnp.argsort(store_map[0, 0])
    coefficient = jnp.take(flattened, inverse, axis=0).reshape(
        blocks, fields, edge_cells, plane_cells
    )
    own_index = lax.axis_index("blk")
    goes_right = new_owner[blocks - 1] != own_index
    mark_right = goes_right.astype(jnp.float32).reshape(1)
    middle_flags = jnp.ones((blocks - 2,), jnp.int32)
    keep_first = (new_owner[0] == own_index).astype(jnp.int32).reshape(1)
    keep_last = (new_owner[blocks - 1] == own_index).astype(jnp.int32).reshape(1)
    for step_index in range(STEPS):
        state_now, state_prev = (
            stencil_step(state_now, state_prev, coefficient, blocks),
            state_now,
        )
    from_left = shifted_2((state_now[blocks - 1], mark_right), "blk", 1)
    valid_flags = jnp.concatenate(
        [(from_left[1] > 0.5).astype(jnp.int32), keep_first, middle_flags, keep_last]
    )
    stacked_now = jnp.concatenate([from_left[0][None], state_now], axis=0)
    placed, live_count = compact((stacked_now,), valid_flags)
    result = placed[0]
    return result[:, None]


def lane_ids():
    return lax.broadcasted_iota(jnp.int32, (1, LANES), 1)


def edge_start(lower, depth, size):
    return pl.multiple_of(jnp.where(lower, depth - size, 0), size)


def pack_region_body(
    map_hbm, owner_hbm, u_ref, p_ref, coef_ref, y_ref, edges_ref, ua_ref, pa_ref, ca_ref, ue_ref, pe_ref, ce_ref,
    map_ref, owner_ref, sems
):
    fields, depth, width = u_ref.shape[1:]
    region = lax.axis_index("region")
    lower = region == 0
    other = 1 - region
    front = slice(0, LANES)
    edge8 = edge_start(lower, depth, 8)
    pair = jnp.where(lower, depth - 2, 0)
    slab = [pltpu.make_async_copy(coef_ref.at[other], y_ref.at[0:4], sems.at[7])]
    copies = [
        pltpu.make_async_copy(map_hbm, map_ref, sems.at[0]),
        pltpu.make_async_copy(owner_hbm, owner_ref, sems.at[8]),
        pltpu.make_async_copy(u_ref.at[:, :, pl.ds(pair, 2), :], ue_ref, sems.at[1]),
        pltpu.make_async_copy(p_ref.at[:, :, pl.ds(jnp.where(lower, depth - 1, 0), 1), :], pe_ref, sems.at[2]),
        pltpu.make_async_copy(coef_ref.at[region, :, pl.ds(edge8, 8), :], ce_ref, sems.at[3]),
    ]
    beside = [
        pltpu.make_async_copy(u_ref.at[0, :, :, front], ua_ref, sems.at[4]),
        pltpu.make_async_copy(p_ref.at[0, :, :, front], pa_ref, sems.at[5]),
        pltpu.make_async_copy(coef_ref.at[:, :, :, front], ca_ref, sems.at[6]),
    ]
    for copy in copies + slab + beside:
        copy.start()
    for copy in copies:
        copy.wait()
    own_edge = jnp.where(lower, 1, 0)
    own_next = 1 - own_edge
    for m in range(2):
        for f in range(fields):
            at = m * fields + f
            near = ue_ref[m, f, pl.ds(own_edge, 1), :]
            pair_at = 8 * m + f
            edges_ref[pair_at : pair_at + 1, :] = near
            edges_ref[pair_at + 4 : pair_at + 5, :] = ue_ref[m, f, pl.ds(own_next, 1), :]
            edges_ref[16 + at : 17 + at, :] = 2.0 * near - pe_ref[m, f]
    for s in range(4):
        piece = ce_ref[s].astype(F32)
        edges_ref[24 + s : 25 + s, :] = jnp.where(lower, piece[7:8], piece[0:1])
    numbers = [map_ref[region * 4 + s] for s in range(4)] + [map_ref[other * 4 + s] for s in range(4)]
    for i, number in enumerate(numbers):
        edges_ref[28:29, tile_at(i)] = jnp.zeros((1, LANES), F32) + number.astype(F32)
    edges_ref[29:30, :] = jnp.zeros((1, width), F32) + jnp.where(owner_ref[1] != lax.axis_index("blk"), 1.0, 0.0)
    edges_ref[30:32, :] = jnp.zeros((2, width), F32)
    y_ref[4] = edges_ref[...].astype(BF16)
    for copy in slab + beside:
        copy.wait()


def pack_back_body(edges_ref, ua_ref, pa_ref, ca_ref, straight_ref, diag_ref):
    fields, depth, _ = ua_ref.shape
    region = lax.axis_index("region")
    lower = region == 0
    other = 1 - region
    lane = lane_ids()
    tag_rows = [edges_ref[28:29, tile_at(i)] for i in range(8)]
    blank = jnp.zeros((1, LANES), F32)
    for f in range(fields):
        now = ua_ref[f]
        ahead = 2.0 * now - pa_ref[f]
        piece = ca_ref[region, f].astype(F32)
        tile = jnp.where(
            lane < 64, now, jnp.where(lane < 96, pltpu.roll(ahead, 64, 1), pltpu.roll(piece, 96, 1))
        )
        straight_ref[f * depth : (f + 1) * depth, :] = tile.astype(BF16)
    far = [ca_ref[other, s].astype(F32) for s in range(4)]
    extra = [jnp.where(lower, piece[0:1], piece[depth - 1 : depth]) for piece in far] + tag_rows + [blank] * 4
    straight_ref[fields * depth : fields * depth + 16, :] = jnp.concatenate(extra, axis=0).astype(BF16)
    plane = jnp.zeros((depth, LANES), F32)
    for s in range(4):
        moved = pltpu.roll(far[s], 32 * s, 1) if s else far[s]
        plane = jnp.where((lane >= 32 * s) & (lane < 32 * s + 32), moved, plane)
    diag_ref[0:depth, :] = plane.astype(BF16)
    rows = [edges_ref[base : base + 4, 0:LANES] for base in (0, 4, 16, 24)]
    diag_ref[depth : depth + 32, :] = jnp.concatenate(rows + tag_rows + [blank] * 8, axis=0).astype(BF16)


def lane_sum(tile, lane):
    return sum_along_c(tile, *c_masks(lane))


def c_masks(lane):
    inside = lane & 31
    return inside != 0, inside != 31


def sum_along_c(tile, low, high):
    return (
        tile
        + jnp.where(low, pltpu.roll(tile, 1, 1), 0.0)
        + jnp.where(high, pltpu.roll(tile, LANES - 1, 1), 0.0)
    )


def nine_sum(tiles, lane):
    low, high = c_masks(lane)
    rows = [sum_along_c(tile, low, high) for tile in tiles]
    up = [pltpu.roll(row, 32, 1) for row in rows]
    down = [pltpu.roll(row, LANES - 32, 1) for row in rows]
    count = len(tiles)
    result = []
    for t in range(count):
        before = jnp.where(lane < 32, up[t - 1] if t else 0.0, up[t])
        after = jnp.where(lane >= 96, down[t + 1] if t < count - 1 else 0.0, down[t])
        result.append(rows[t] + before + after)
    return result


def column_sum(tile, row_id, low_row, high_row):
    depth = tile.shape[0]
    above = pltpu.roll(tile, 1, 0)
    below = pltpu.roll(tile, depth - 1, 0)
    return tile + jnp.where(row_id == 0, low_row, above) + jnp.where(row_id == depth - 1, high_row, below)


def local_body(
    map_hbm, u_hbm, p_hbm, coef_ref, u_ref, box0_ref, box1_ref, drift_ref, rim_ref, held_ref, p_ref, map_ref, sems
):
    fields, depth, width = u_ref.shape[1:]
    main = width // LANES
    copies = []
    for f in range(fields):
        copies.append(
            (
                pltpu.make_async_copy(u_hbm.at[:, f], u_ref.at[:, f], sems.at[2 * f]),
                pltpu.make_async_copy(p_hbm.at[:, f], p_ref.at[:, f], sems.at[2 * f + 1]),
            )
        )
    numbers = load_map(map_hbm, map_ref, sems.at[2 * fields])
    for pair in copies:
        for copy in pair:
            copy.start()
    held_ref[...] = jnp.zeros(held_ref.shape, held_ref.dtype)
    numbers.wait()
    region = lax.axis_index("region")
    for s in range(4):
        held_ref[map_ref[region * 4 + s]] = coef_ref[region, s]
    lower = lax.axis_index("region") == 0
    lane = lane_ids()
    row_id = lax.broadcasted_iota(jnp.int32, (depth, 1), 0)
    boxes = (box0_ref, box1_ref)
    for f in range(fields):
        for copy in copies[f]:
            copy.wait()
        now = [u_ref[m, f, :, tile_at(t)] for m in range(2) for t in range(main)]
        sums = nine_sum(now, lane)
        for i, (tile, total) in enumerate(zip(now, sums)):
            m, t = divmod(i, main)
            lanes = tile_at(t)
            rim_ref[m, f : f + 1, lanes] = jnp.where(lower, total[depth - 1 : depth], total[0:1])
            boxes[m][f, :, lanes] = column_sum(total, row_id, 0.0, 0.0) - 27.0 * tile
            drift_ref[m, f, :, lanes] = 2.0 * tile - p_ref[m, f, :, lanes]
    rim_ref[:, 4:8, :] = jnp.zeros((2, 4, width), F32)


def tile_at(t):
    return slice(t * LANES, (t + 1) * LANES)


class ColumnEdge:
    def __init__(self, coef_ref, y_ref):
        self.region = lax.axis_index("region")
        self.lower = self.region == 0
        self.coef = coef_ref
        self.depth = coef_ref.shape[2]
        self.extra = y_ref[4].astype(F32)
        self.tags = [self.extra[28:29, i * LANES : (i + 1) * LANES] for i in range(8)]
        self.field_id = lax.broadcasted_iota(jnp.int32, (4, LANES), 0).astype(F32)

    def pair(self, m, lanes):
        return self.extra[8 * m : 8 * m + 8, lanes]

    def ahead(self, m, lanes):
        return self.extra[16 + 4 * m : 20 + 4 * m, lanes]

    def coefs(self, m, lanes):
        total = jnp.zeros((4, LANES), F32)
        for s in range(4):
            piece = self.coef[1 - self.region, s, :, lanes].astype(F32)
            held = jnp.where(self.lower, piece[0:1], piece[self.depth - 1 : self.depth])
            total = total + jnp.where(self.tags[s] == self.field_id + 4 * m, self.extra[24 + s : 25 + s, lanes], 0.0)
            total = total + jnp.where(self.tags[4 + s] == self.field_id + 4 * m, held, 0.0)
        return total

    def own(self, tile):
        return jnp.where(self.lower, tile[self.depth - 1 : self.depth], tile[0:1])

    def rows(self, row):
        return jnp.where(self.lower, 0.0, row), jnp.where(self.lower, row, 0.0)


def border_body(u_ref, straight_ref, diag_ref, box_in, box_ref, side_lap_ref, side_coef_ref, rim_ref):
    fields, depth, width = u_ref.shape[1:]
    lane = lane_ids()
    row_id = lax.broadcasted_iota(jnp.int32, (depth, 1), 0)
    lower = lax.axis_index("region") == 0
    before = slice(width - LANES, width)
    facing = lane >= 96
    tags = [straight_ref[fields * depth : fields * depth + 16, :].astype(F32)[4 + i : 5 + i] for i in range(8)]
    planes = []
    for s in range(4):
        planes.append(pltpu.roll(straight_ref[s * depth : (s + 1) * depth, :].astype(F32), 32, 1))
    diag_tile = diag_ref[0:depth, :].astype(F32)
    for s in range(4):
        planes.append(pltpu.roll(diag_tile, LANES - 32 * s, 1) if s else diag_tile)
    for f in range(fields):
        inner = u_ref[1, f, :, before]
        remote = straight_ref[f * depth : (f + 1) * depth, :].astype(F32)
        inner_sum, remote_sum = nine_sum([inner, remote], lane)
        for i, tile in enumerate((inner_sum, remote_sum)):
            rim_ref[i, f : f + 1, :] = jnp.where(lower, tile[depth - 1 : depth], tile[0:1])
        halo_c = jnp.zeros((depth, LANES), F32)
        for i in range(8):
            halo_c = halo_c + jnp.where(tags[i] == F32(f), planes[i], 0.0)
        side_coef_ref[f] = halo_c
        side_lap_ref[f] = column_sum(remote_sum, row_id, 0.0, 0.0) - 27.0 * remote
        whole = column_sum(inner_sum, row_id, 0.0, 0.0) - 27.0 * inner
        box_ref[f, :, before] = jnp.where(facing, whole, box_in[f, :, before])
    rim_ref[:, 4:8, :] = jnp.zeros((2, 4, LANES), F32)


def last_edges(
    coef_ref, y_ref, straight_ref, diag_ref, box0_ref, rim_ref, side_lap_ref, side_coef_ref, side_rim_ref, box_in,
    box_ref, lap_ref, side_ref, sums_ref
):
    fields, depth, width = box_in.shape
    main = width // LANES
    lane = lane_ids()
    column = ColumnEdge(coef_ref, y_ref)
    before = slice(width - LANES, width)
    extra_s = straight_ref[fields * depth : fields * depth + 16, :].astype(F32)
    extra_d = diag_ref[depth : depth + 32, :].astype(F32)
    tags_d = [extra_d[16 + i : 17 + i] for i in range(8)]

    def edge_tiles(of, remote):
        return [of(0, before)] + [of(1, tile_at(t)) for t in range(main)] + [remote]

    pairs = edge_tiles(column.pair, extra_d[0:8])
    near = [pair[0:4] for pair in pairs]
    ahead = edge_tiles(column.ahead, extra_d[8:12])
    corner = jnp.zeros((4, LANES), F32)
    for s in range(4):
        corner = corner + jnp.where(tags_d[s] == column.field_id, extra_d[12 + s : 13 + s], 0.0)
        corner = corner + jnp.where(tags_d[4 + s] == column.field_id, extra_s[s : s + 1], 0.0)
    edge_c = [column.coefs(0, before)] + [column.coefs(1, tile_at(t)) for t in range(main)] + [corner]
    pair_sum = nine_sum(pairs, lane)
    near_sum = [total[0:4] for total in pair_sum]
    both_sum = [total[0:4] + total[4:8] for total in pair_sum]
    top = slice(0, 1)
    bottom = slice(depth - 1, depth)
    for f in range(fields):
        for t in range(main):
            low_row, high_row = column.rows(near_sum[t + 1][f : f + 1])
            lanes = tile_at(t)
            box_ref[f, top, lanes] = box_in[f, top, lanes] + low_row
            box_ref[f, bottom, lanes] = box_in[f, bottom, lanes] + high_row
        remote = straight_ref[f * depth : (f + 1) * depth, :].astype(F32)
        side_ref[f] = pltpu.roll(remote, 64, 1) + side_coef_ref[f] * side_lap_ref[f]
        low_row, high_row = column.rows(near_sum[main + 1][f : f + 1])
        side_ref[f, top] += side_coef_ref[f, top] * low_row
        side_ref[f, bottom] += side_coef_ref[f, bottom] * high_row
        low_row, high_row = column.rows(near_sum[0][f : f + 1])
        lap_ref[f] = box0_ref[f, :, before]
        lap_ref[f, top] += low_row
        lap_ref[f, bottom] += high_row
    rims = [rim_ref[0, 0:4, before]] + [rim_ref[1, 0:4, tile_at(t)] for t in range(main)] + [side_rim_ref[1, 0:4, :]]
    rims[main] = jnp.where(lane >= 96, side_rim_ref[0, 0:4, :], rims[main])
    stepped = []
    for t in range(main + 2):
        box = both_sum[t] + rims[t]
        stepped.append(ahead[t] + edge_c[t] * (box - 27.0 * near[t]))
    stepped_sum = nine_sum(stepped, lane)
    for t in range(main):
        sums_ref[0:4, tile_at(t)] = stepped_sum[t + 1]
    sums_ref[4:8, :] = jnp.zeros((4, width), F32)
    return stepped[main], stepped_sum[1 : main + 1]


def first_edges_body(coef_ref, y_ref, rim_ref, box1_ref, box_in, box_ref, sums_ref, edge_c_ref):
    fields, depth, width = box_in.shape
    main = width // LANES
    lane = lane_ids()
    column = ColumnEdge(coef_ref, y_ref)
    after = slice(0, LANES)

    def edge_tiles(of):
        return [of(0, tile_at(t)) for t in range(main)] + [of(1, after)]

    pairs = edge_tiles(column.pair)
    near = [pair[0:4] for pair in pairs]
    pair_sum = nine_sum(pairs, lane)
    near_sum = [total[0:4] for total in pair_sum]
    both_sum = [total[0:4] + total[4:8] for total in pair_sum]
    ahead = edge_tiles(column.ahead)
    edge_c = edge_tiles(column.coefs)
    for f in range(fields):
        for t in range(main):
            low_row, high_row = column.rows(near_sum[t][f : f + 1])
            lanes = tile_at(t)
            box_ref[f, 0:1, lanes] = box_in[f, 0:1, lanes] + low_row
            box_ref[f, depth - 1 : depth, lanes] = box_in[f, depth - 1 : depth, lanes] + high_row
    rims = [rim_ref[0, 0:4, tile_at(t)] for t in range(main)] + [rim_ref[1, 0:4, after]]
    stepped = []
    for t in range(main + 1):
        box = both_sum[t] + rims[t]
        stepped.append(ahead[t] + edge_c[t] * (box - 27.0 * near[t]))
    stepped_sum = nine_sum(stepped, lane)
    for t in range(main):
        sums_ref[0:4, tile_at(t)] = stepped_sum[t]
    sums_ref[4:8, :] = jnp.zeros((4, width), F32)
    edge_c_ref[0:4, :] = edge_c[0]
    edge_c_ref[4:8, :] = jnp.zeros((4, LANES), F32)


def load_map(map_any, map_ref, sem):
    copy = pltpu.make_async_copy(map_any, map_ref, sem)
    copy.start()
    return copy


class Pieces:
    def __init__(self, edges_ref, held_ref, slab_ref):
        self.held, self.slab = held_ref, slab_ref
        self.tags = [edges_ref[28:29, tile_at(4 + s)] for s in range(4)]

    def piece(self, number):
        here = [tag == F32(number) for tag in self.tags]

        def tile(lanes):
            total = self.held[number, :, lanes].astype(F32)
            for s, mask in enumerate(here):
                total = jnp.where(mask, self.slab[s, :, lanes].astype(F32), total)
            return total

        return tile


def second_step(now, before, total, coef, row_id, row, lower):
    low_row, high_row = jnp.where(lower, 0.0, row), jnp.where(lower, row, 0.0)
    lap = column_sum(total, row_id, low_row, high_row) - 27.0 * now
    return 2.0 * now - before + coef * lap


CODES = 32000.0


def power_of(size):
    return jnp.ceil(jnp.log2(jnp.maximum(size, 1e-30)))


def coded(value, power):
    return jnp.floor(value * (CODES * jnp.exp2(-power)) + 0.5)


def narrow(value):
    return value.astype(jnp.int32).astype(jnp.int16)


def wide(code):
    return code.astype(jnp.int32).astype(F32)


def scale_of(power):
    return jnp.exp2(power) * (1.0 / CODES)


def last_row_a_body(
    edges_ref, u_ref, coef_ref, held_ref, y_ref, straight_ref, diag_ref, box0_ref, rim_ref, side_lap_ref, side_coef_ref,
    side_rim_ref, drift_ref, box_in, box_ref, lap_ref, side_ref, sums_ref, row_ref, code_ref, power_ref, extra_ref
):
    tail, edge_sums = last_edges(
        coef_ref, y_ref, straight_ref, diag_ref, box0_ref, rim_ref, side_lap_ref, side_coef_ref, side_rim_ref, box_in,
        box_ref, lap_ref, side_ref, sums_ref
    )
    refs = (edges_ref, u_ref, held_ref, y_ref, box_ref, drift_ref, lap_ref, side_ref, sums_ref, row_ref, code_ref, power_ref)
    last_row(0, *refs, more=(tail, edge_sums, extra_ref))


def last_row_b_body(first, *refs):
    last_row(first, *refs)


def last_row(
    first, edges_ref, u_ref, held_ref, y_ref, box_ref, drift_ref, lap_ref, side_ref, sums_ref, row_ref, code_ref, power_ref,
    more=None
):
    count, depth, width = row_ref.shape
    fields = u_ref.shape[1]
    main = width // LANES
    lane = lane_ids()
    row_id = lax.broadcasted_iota(jnp.int32, (depth, 1), 0)
    pieces = Pieces(edges_ref, held_ref, y_ref)
    lower = lax.axis_index("region") == 0
    before = slice(width - LANES, width)
    last_tiles = []
    for f in range(first, first + count):
        coef = pieces.piece(fields + f)
        coefs = [coef(tile_at(t)) for t in range(main)]
        middle = [drift_ref[1, f, :, tile_at(t)] + coefs[t] * box_ref[f, :, tile_at(t)] for t in range(main)]
        local = drift_ref[0, f, :, before] + pieces.piece(f)(before) * lap_ref[f]
        sums = nine_sum([local] + middle + [side_ref[f]], lane)
        for t in range(main):
            lanes = tile_at(t)
            row = sums_ref[f : f + 1, lanes] if more is None else more[1][t][f : f + 1]
            value = second_step(middle[t], u_ref[1, f, :, lanes], sums[t + 1], coefs[t], row_id, row, lower)
            row_ref[f - first, :, lanes] = value
            power = power_of(jnp.max(jnp.abs(value), axis=0, keepdims=True))
            at = (f - first) * main + t
            code_ref[at * depth : (at + 1) * depth, :] = narrow(coded(value, power))
            power_ref[at : at + 1, :] = power
        last_tiles.append(middle[main - 1])
    base = count * main * depth
    code_ref[base : base + count * main, :] = narrow(power_ref[...])
    if more is not None:
        tail, _, extra_ref = more
        base += count * main
        both = []
        for f in range(fields):
            if f < count:
                stepped = last_tiles[f]
            else:
                stepped = drift_ref[1, f, :, before] + pieces.piece(fields + f)(before) * box_ref[f, :, before]
            both.append(jnp.where(lane >= 96, u_ref[1, f, :, before], pltpu.roll(stepped, 96, 1)))
        for g in range(fields // 2):
            pair = jnp.where(lane >= 64, both[2 * g], pltpu.roll(both[2 * g + 1], 64, 1))
            power = power_of(jnp.max(jnp.abs(pair), axis=0, keepdims=True))
            code_ref[base : base + depth, :] = narrow(coded(pair, power))
            extra_ref[g : g + 1, :] = power
            base += depth
        near = y_ref[4, 0:16, before].astype(F32)
        kinds = []
        for rows in (near[8:12], near[12:16], tail):
            kind = jnp.zeros((1, LANES), F32)
            for f in range(fields):
                shift = (32 * f + 32) % LANES
                row = rows[f : f + 1]
                kind = jnp.where(lane // 32 == f, pltpu.roll(row, shift, 1) if shift else row, kind)
            kinds.append(kind)
        power = power_of(jnp.maximum(jnp.maximum(jnp.abs(kinds[0]), jnp.abs(kinds[1])), jnp.abs(kinds[2])))
        extra_ref[2:3, :] = power
        for i, kind in enumerate(kinds):
            extra_ref[3 + i : 4 + i, :] = coded(kind, power)
        extra_ref[6:7, :] = edges_ref[29:30, 0:LANES]
        extra_ref[7:8, :] = jnp.zeros((1, LANES), F32)
        code_ref[base : base + 8, :] = narrow(extra_ref[...])


def first_row_body(edges_ref, u_ref, held_ref, y_ref, box_ref, box1_ref, drift_ref, sums_ref, row_ref, coef0_ref):
    fields, depth, width = u_ref.shape[1:]
    main = width // LANES
    lane = lane_ids()
    row_id = lax.broadcasted_iota(jnp.int32, (depth, 1), 0)
    pieces = Pieces(edges_ref, held_ref, y_ref)
    lower = lax.axis_index("region") == 0
    after = slice(0, LANES)
    for f in range(fields):
        coef = pieces.piece(f)
        coefs = [coef(tile_at(t)) for t in range(main)]
        now = [drift_ref[0, f, :, tile_at(t)] + coefs[t] * box_ref[f, :, tile_at(t)] for t in range(main)]
        local = drift_ref[1, f, :, after] + pieces.piece(fields + f)(after) * box1_ref[f, :, after]
        sums = nine_sum(now + [local], lane)
        coef0_ref[f] = coefs[0]
        for t in range(main):
            lanes = tile_at(t)
            row = sums_ref[f : f + 1, lanes]
            row_ref[f, :, lanes] = second_step(now[t], u_ref[0, f, :, lanes], sums[t], coefs[t], row_id, row, lower)


def arrival(code_ref):
    rows = code_ref.shape[0]
    return wide(code_ref[rows - 8 : rows, :])[6, 0] > 0.5


def code_copies(first, row_ref, out_ref, sems, base):
    count = row_ref.shape[0]
    return [pltpu.make_async_copy(row_ref, out_ref.at[0, first : first + count], sems.at[base])]


def decode(code_ref, row_ref):
    count, depth, width = row_ref.shape
    main = width // LANES
    base = count * main * depth
    scale = scale_of(wide(code_ref[base : base + count * main, :]))
    for f in range(count):
        for t in range(main):
            at = f * main + t
            row_ref[f, :, tile_at(t)] = wide(code_ref[at * depth : (at + 1) * depth, :]) * scale[at : at + 1]


def row_copies(owner_ref, row_ref, last_refs, zero_ref, out_ref, at, sems, base):
    fields, _, width = row_ref.shape
    keeps = owner_ref[1] == lax.axis_index("blk")
    rest = slice(LANES, width)
    sources = [ref.at[f] for ref in last_refs for f in range(ref.shape[0])]

    def copies(sources, at, base):
        return [pltpu.make_async_copy(source, out_ref.at[at, f], sems.at[base + f]) for f, source in enumerate(sources)]

    firsts = [
        pltpu.make_async_copy(row_ref.at[f, :, rest], out_ref.at[at, f, :, rest], sems.at[base + f])
        for f in range(fields)
    ]
    kept = copies(sources, at + 1, base + fields)
    gone = copies([zero_ref] * fields, at + 1, base + fields)

    def apply(act):
        for copy in firsts:
            act(copy)

        @pl.when(keeps)
        def _():
            for copy in kept:
                act(copy)

        @pl.when(jnp.logical_not(keeps))
        def _():
            for copy in gone:
                act(copy)

    return apply


def rows_body(owner_ref, row_ref, *refs):
    last_refs, (out_ref, zero_ref, sems) = refs[:-3], refs[-3:]
    zero_ref[...] = jnp.zeros(zero_ref.shape, F32)
    apply = row_copies(owner_ref, row_ref, last_refs, zero_ref, out_ref, 1, sems, 0)
    apply(lambda copy: copy.start())
    apply(lambda copy: copy.wait())


def finish_body(owner_any, coef_ref, edge_c_ref, code_ref, row_ref, *refs):
    last_refs, (partial_ref, out_ref, tile_ref, arrived_ref, zero_ref, owner_ref, sems) = refs[:-7], refs[-7:]
    fields, depth, width = row_ref.shape
    main = width // LANES
    arrives = arrival(code_ref)
    lane = lane_ids()
    row_id = lax.broadcasted_iota(jnp.int32, (depth, 1), 0)
    lower = lax.axis_index("region") == 0
    first = lane < 32
    base = arrived_ref.shape[0] * main * (depth + 1)
    extra = wide(code_ref[base + depth * fields // 2 : base + depth * fields // 2 + 8, :])
    tile0 = tile_at(0)

    def beside(total, shift):
        return jnp.where(first, pltpu.roll(total, shift, 1), 0.0)

    def rows(row):
        return jnp.where(lower, 0.0, row), jnp.where(lower, row, 0.0)

    corners = []
    for kind in range(3):
        row = lane_sum(extra[3 + kind : 4 + kind] * scale_of(extra[2:3]), lane)
        places = [pltpu.roll(row, LANES - 32 * f, 1) if f else row for f in range(fields)]
        corners.append(jnp.where(first, jnp.concatenate(places, axis=0), 0.0))
    planes = []
    for g in range(fields // 2):
        pair = wide(code_ref[base + g * depth : base + (g + 1) * depth, :]) * scale_of(extra[g : g + 1])
        total = lane_sum(pair, lane)
        planes += [(beside(total, 32), beside(total, 64)), (beside(total, 96), total)]
    planes = [(now, jnp.where(first, then, 0.0)) for now, then in planes]
    own = [jnp.where(lower, now[depth - 1 : depth], now[0:1]) for now, _ in planes]
    edge_change = edge_c_ref[0:4, :] * (corners[0] + corners[1] + jnp.concatenate(own, axis=0))
    edge_sum = lane_sum(edge_change, lane)
    edge_sum = edge_sum + corners[2] + pltpu.roll(edge_sum, 32, 1)
    for f in range(fields):
        now, then = planes[f]
        low_row, high_row = rows(corners[0][f : f + 1])
        coef = coef_ref[f]
        change = coef * column_sum(now, row_id, low_row, high_row)
        total = lane_sum(change, lane)
        total = total + then + pltpu.roll(total, 32, 1)
        low_row, high_row = rows(edge_sum[f : f + 1])
        lap = column_sum(total, row_id, low_row, high_row) - 27.0 * change
        tile_ref[f] = row_ref[f, :, tile0] + 2.0 * change + coef * lap

    slot = jnp.where(arrives, 1, 0)
    last = pltpu.make_async_copy(tile_ref, out_ref.at[slot, :, :, tile0], sems.at[0])
    last.start()

    @pl.when(arrives)
    def _():
        decode(code_ref, arrived_ref)
        coming = code_copies(0, arrived_ref, out_ref, sems, 1)
        for copy in coming:
            copy.start()
        for copy in coming:
            copy.wait()

    @pl.when(jnp.logical_not(arrives))
    def _():
        load_map(owner_any, owner_ref, sems.at[1]).wait()
        zero_ref[...] = jnp.zeros(zero_ref.shape, F32)
        apply = row_copies(owner_ref, row_ref, last_refs, zero_ref, out_ref, 0, sems, 1)
        blank = [
            pltpu.make_async_copy(zero_ref, out_ref.at[2, f], sems.at[1 + 2 * fields + f]) for f in range(fields)
        ]
        apply(lambda copy: copy.start())
        for copy in blank:
            copy.start()
        for copy in blank:
            copy.wait()
        apply(lambda copy: copy.wait())

    last.wait()


def place_body(first, code_a_ref, code_ref, partial_ref, out_ref, row_ref, sems):
    arrives = arrival(code_a_ref)
    decode(code_ref, row_ref)
    copies = code_copies(first, row_ref, out_ref, sems, 0)

    @pl.when(arrives)
    def _():
        for copy in copies:
            copy.start()
        for copy in copies:
            copy.wait()


def fast_on_device(u_now, u_prev, coef_store, store_map, new_owner):
    blocks, _, fields, depth, width = u_now.shape
    now = u_now.reshape(blocks, fields, depth, width)
    prev = u_prev.reshape(blocks, fields, depth, width)
    coef = coef_store[0, 0]
    count = lax.axis_size("blk")
    order = store_map.reshape(-1)
    order_hbm, owner_hbm, now_hbm, prev_hbm, coef_hbm = (
        pltpu.with_memory_space_constraint(array, pltpu.HBM) for array in (order, new_owner, now, prev, coef)
    )
    params = pltpu.CompilerParams(vmem_limit_bytes=48 * 1024 * 1024)

    def call(body, name, out_shape, in_specs, out_specs, scratch, args, **options):
        return pl.pallas_call(
            body,
            out_shape=out_shape,
            in_specs=in_specs,
            out_specs=out_specs,
            scratch_shapes=scratch,
            compiler_params=params,
            name=name,
            **options,
        )(*args)

    straight = jax.ShapeDtypeStruct((fields * depth + 16, LANES), BF16)
    diag = jax.ShapeDtypeStruct((depth + 32, LANES), BF16)
    tiles = jax.ShapeDtypeStruct((fields, depth, LANES), F32)
    y_out, edges, front, front_prev, front_coef = call(
        pack_region_body,
        "pack_region",
        (
            jax.ShapeDtypeStruct((5, depth, width), BF16),
            jax.ShapeDtypeStruct((depth, width), F32),
            tiles,
            tiles,
            jax.ShapeDtypeStruct((2, 4, depth, LANES), BF16),
        ),
        [HBM] * 5,
        (VMEM,) * 5,
        [
            pltpu.VMEM((blocks, fields, 2, width), F32),
            pltpu.VMEM((blocks, fields, 1, width), F32),
            pltpu.VMEM((4, 8, width), BF16),
            pltpu.SMEM(order.shape, jnp.int32),
            pltpu.SMEM(new_owner.shape, jnp.int32),
            pltpu.SemaphoreType.DMA((9,)),
        ],
        (order_hbm, owner_hbm, now_hbm, prev_hbm, coef_hbm),
    )
    left, dleft = call(
        pack_back_body, "pack_back", (straight, diag), [VMEM] * 4, (VMEM,) * 2, [], (edges, front, front_prev, front_coef)
    )

    swap = [(0, 1), (1, 0)]
    forward = [(i, (i + 1) % count) for i in range(count)]
    backward = [(i, (i - 1) % count) for i in range(count)]
    crossed = [(r * count + i, (1 - r) * count + (i - 1) % count) for r in range(2) for i in range(count)]
    y_in = lax.ppermute(y_out, "region", swap)
    from_right = lax.ppermute(left, "blk", backward)
    from_dright = lax.ppermute(dleft, ("region", "blk"), crossed)

    row = jax.ShapeDtypeStruct((fields, depth, width), F32)
    both = jax.ShapeDtypeStruct(now.shape, F32)
    now, box0, box1, drift, rim, held = call(
        local_body,
        "local",
        (
            both,
            row,
            row,
            both,
            jax.ShapeDtypeStruct((blocks, 8, width), F32),
            jax.ShapeDtypeStruct((blocks * fields, depth, width), BF16),
        ),
        [HBM] * 3 + [VMEM],
        (VMEM,) * 6,
        [
            pltpu.VMEM(now.shape, F32),
            pltpu.SMEM(order.shape, jnp.int32),
            pltpu.SemaphoreType.DMA((2 * fields + 1,)),
        ],
        (order_hbm, now_hbm, prev_hbm, coef),
    )
    sums = jax.ShapeDtypeStruct((8, width), F32)
    edge = jax.ShapeDtypeStruct((8, LANES), F32)
    box1, side_lap, side_coef, side_rim = call(
        border_body,
        "border",
        (row, tiles, tiles, jax.ShapeDtypeStruct((2, 8, LANES), F32)),
        [VMEM] * 4,
        (VMEM,) * 4,
        [],
        (now, from_right, from_dright, box1),
        input_output_aliases={3: 0},
        cost_estimate=pl.CostEstimate(flops=0, transcendentals=0, bytes_accessed=40_000_000),
    )
    bounds = sorted({0, fields // 2, fields})
    parts = [(first, end - first) for first, end in zip(bounds, bounds[1:])]

    def part_shapes(size, more):
        tiled = size * width // LANES
        codes = tiled * (depth + 1) + more
        shapes = (jax.ShapeDtypeStruct((size, depth, width), F32), jax.ShapeDtypeStruct((codes, LANES), jnp.int16))
        return shapes, pltpu.VMEM((tiled, LANES), F32)

    shapes, powers = part_shapes(parts[0][1], fields // 2 * depth + 8)
    box1, lap1, side1, sums1, last, code = call(
        last_row_a_body,
        "last_row",
        (row, tiles, tiles, sums) + shapes,
        [VMEM] * 14,
        (VMEM,) * 6,
        [powers, pltpu.VMEM((8, LANES), F32)],
        (edges, now, coef, held, y_in, from_right, from_dright, box0, rim, side_lap, side_coef, side_rim, drift, box1),
        input_output_aliases={13: 0},
    )
    lasts = [last]
    arrived = [lax.ppermute(code, "blk", forward)]
    for first, size in parts[1:]:
        shapes, powers = part_shapes(size, 0)
        last, code = call(
            functools.partial(last_row_b_body, first),
            "last_row",
            shapes,
            [VMEM] * 9,
            (VMEM,) * 2,
            [powers],
            (edges, now, held, y_in, box1, drift, lap1, side1, sums1),
        )
        lasts.append(last)
        arrived.append(lax.ppermute(code, "blk", forward))
    box0, sums0, edge_c0 = call(
        first_edges_body,
        "first_edges",
        (row, sums, edge),
        [VMEM] * 3 + [ANY, VMEM],
        (VMEM,) * 3,
        [],
        (coef, y_in, rim, box1, box0),
        input_output_aliases={4: 0},
    )
    first_row, coef0 = call(
        first_row_body,
        "first_row",
        (row, tiles),
        [VMEM] * 8,
        (VMEM,) * 2,
        [],
        (edges, now, held, y_in, box0, box1, drift, sums0),
    )
    whole = jax.ShapeDtypeStruct((blocks + 1, fields, depth, width), F32)
    placed = call(
        rows_body,
        "rows",
        whole,
        [SMEM] + [VMEM] * (1 + len(lasts)),
        ANY,
        [pltpu.VMEM((depth, width), F32), pltpu.SemaphoreType.DMA((2 * fields,))],
        (new_owner, first_row, *lasts),
    )
    placed = call(
        finish_body,
        "finish",
        whole,
        [ANY] + [VMEM] * (4 + len(lasts)) + [ANY],
        ANY,
        [
            pltpu.VMEM((fields, depth, LANES), F32),
            pltpu.VMEM((parts[0][1], depth, width), F32),
            pltpu.VMEM((depth, width), F32),
            pltpu.SMEM(new_owner.shape, jnp.int32),
            pltpu.SemaphoreType.DMA((1 + 3 * fields,)),
        ],
        (new_owner, coef0, edge_c0, arrived[0], first_row, *lasts, placed),
        input_output_aliases={5 + len(lasts): 0},
    )
    for (first, size), codes in zip(parts[1:], arrived[1:]):
        placed = call(
            functools.partial(place_body, first),
            "place",
            whole,
            [VMEM, VMEM, ANY],
            ANY,
            [pltpu.VMEM((size, depth, width), F32), pltpu.SemaphoreType.DMA((2 * size,))],
            (arrived[0], codes, placed),
            input_output_aliases={2: 0},
        )
    return placed[:, None]


def solution(mesh):
    def on_device(*args):
        blocks = args[0].shape[0]
        if lax.axis_size("region") == 2 and blocks == 2:
            return fast_on_device(*args)
        return general_on_device(*args)

    return jax.shard_map(
        on_device,
        mesh=mesh,
        in_specs=(
            P("blk", "region", None, None, None),
            P("blk", "region", None, None, None),
            P("blk", "region", None, None, None, None),
            P("blk", "region", None),
            P("blk"),
        ),
        out_specs=P("blk", "region", None, None, None),
        check_vma=False,
    )
```

```python
import functools

import jax
import jax.numpy as jnp
from jax import lax
from jax.experimental import pallas as pl
from jax.experimental.pallas import tpu as pltpu
from jax.sharding import PartitionSpec as P

STEPS = 2
LANES = 128
F32 = jnp.float32
BF16 = jnp.bfloat16
VMEM = pl.BlockSpec(memory_space=pltpu.VMEM)
SMEM = pl.BlockSpec(memory_space=pltpu.SMEM)
ANY = pl.BlockSpec(memory_space=pl.ANY)
HBM = pl.BlockSpec(memory_space=pltpu.HBM)


def extended_2(block, sides, width, periodic):
    for axis, dim in sides:
        count = lax.axis_size(axis)
        forward = [(i, i + 1) for i in range(count - 1)]
        if periodic:
            forward.append((count - 1, 0))
        backward = [(target, source) for source, target in forward]
        low = lax.ppermute(
            lax.slice_in_dim(block, block.shape[dim] - width, None, axis=dim), axis, forward
        )
        high = lax.ppermute(lax.slice_in_dim(block, 0, width, axis=dim), axis, backward)
        block = jnp.concatenate([low, block, high], axis=dim)
    return block


def shifted_2(value, axis, by):
    devices = lax.axis_size(axis)
    return lax.ppermute(value, axis, [(i, (i + by) % devices) for i in range(devices)])


def stencil_step(state_now, state_prev, coefficient, live_count):
    slot_count, field_count, edge_cells, plane_cells = state_now.shape
    padded = extended_2(state_now, (("region", 2),), 1, False)
    first_planes = padded[..., :edge_cells]
    last_planes = padded[..., plane_cells - edge_cells :]
    last_live = jnp.take(last_planes, live_count - 1, axis=0)
    rim_pair = jnp.stack([first_planes[0], last_live], axis=2)
    spread = extended_2(rim_pair.astype(jnp.bfloat16), (("blk", 2),), 1, True).astype(
        rim_pair.dtype
    )
    left_rim = spread[:, :, 0]
    right_rim = spread[:, :, 3]
    before_planes = jnp.concatenate([left_rim[None], last_planes[:-1]], axis=0)
    after_planes = jnp.pad(first_planes[1:], ((0, 1), (0, 0), (0, 0), (0, 0)))
    slot_ids = jnp.arange(slot_count)
    after_planes = jnp.where(
        (slot_ids == live_count - 1)[:, None, None, None], right_rim[None], after_planes
    )
    extended = jnp.concatenate([before_planes, padded, after_planes], axis=-1)
    width = extended.shape[-1]
    column = jnp.arange(width) % edge_cells
    lower_mask = (column != 0).astype(jnp.float32)
    upper_mask = (column != edge_cells - 1).astype(jnp.float32)
    margin = ((0, 0), (0, 0), (0, 0), (1, 1))
    shifted = jnp.pad(extended, margin)
    summed = shifted[..., :width] * lower_mask + extended + shifted[..., 2:] * upper_mask
    summed = (
        summed[..., : -2 * edge_cells]
        + summed[..., edge_cells:-edge_cells]
        + summed[..., 2 * edge_cells :]
    )
    box_sum = summed[:, :, :-2] + summed[:, :, 1:-1] + summed[:, :, 2:]
    laplace = box_sum - 27.0 * state_now
    return 2.0 * state_now - state_prev + coefficient.astype(jnp.float32) * laplace


def compact(members, valid_flags):
    slot_count = valid_flags.shape[0]
    place_index = jnp.cumsum(valid_flags) - 1
    target = jnp.arange(slot_count)
    chooser = (valid_flags[None, :] == 1) & (place_index[None, :] == target[:, None])
    source = jnp.sum(jnp.where(chooser, target[None, :], 0), axis=1)
    filled = jnp.sum(chooser.astype(jnp.int32), axis=1) > 0
    placed = tuple(
        (
            jnp.where(
                filled.reshape((slot_count,) + (1,) * (member.ndim - 1)),
                jnp.take(member, source, axis=0),
                jnp.zeros_like(member),
            )
            for member in members
        )
    )
    return (placed, jnp.sum(valid_flags))


def general_on_device(u_now, u_prev, coef_store, store_map, new_owner):
    state_now = u_now[:, 0]
    state_prev = u_prev[:, 0]
    blocks, fields, edge_cells, plane_cells = state_now.shape
    store_local = coef_store[0, 0]
    arrived = lax.all_to_all(store_local, "region", split_axis=0, concat_axis=0, tiled=True)
    flattened = arrived.reshape((-1,) + arrived.shape[2:])
    inverse = jnp.argsort(store_map[0, 0])
    coefficient = jnp.take(flattened, inverse, axis=0).reshape(
        blocks, fields, edge_cells, plane_cells
    )
    own_index = lax.axis_index("blk")
    goes_right = new_owner[blocks - 1] != own_index
    mark_right = goes_right.astype(jnp.float32).reshape(1)
    middle_flags = jnp.ones((blocks - 2,), jnp.int32)
    keep_first = (new_owner[0] == own_index).astype(jnp.int32).reshape(1)
    keep_last = (new_owner[blocks - 1] == own_index).astype(jnp.int32).reshape(1)
    for step_index in range(STEPS):
        state_now, state_prev = (
            stencil_step(state_now, state_prev, coefficient, blocks),
            state_now,
        )
    from_left = shifted_2((state_now[blocks - 1], mark_right), "blk", 1)
    valid_flags = jnp.concatenate(
        [(from_left[1] > 0.5).astype(jnp.int32), keep_first, middle_flags, keep_last]
    )
    stacked_now = jnp.concatenate([from_left[0][None], state_now], axis=0)
    placed, live_count = compact((stacked_now,), valid_flags)
    result = placed[0]
    return result[:, None]


def lane_ids():
    return lax.broadcasted_iota(jnp.int32, (1, LANES), 1)


def edge_start(lower, depth, size):
    return pl.multiple_of(jnp.where(lower, depth - size, 0), size)


def pack_region_body(
    map_hbm, u_ref, p_ref, coef_ref, y_ref, edges_ref, ua_ref, pa_ref, ca_ref, ue_ref, pe_ref, ce_ref,
    map_ref, sems
):
    fields, depth, width = u_ref.shape[1:]
    region = lax.axis_index("region")
    lower = region == 0
    other = 1 - region
    front = slice(0, LANES)
    edge8 = edge_start(lower, depth, 8)
    pair = jnp.where(lower, depth - 2, 0)
    slab = [pltpu.make_async_copy(coef_ref.at[other], y_ref.at[0:4], sems.at[7])]
    copies = [
        pltpu.make_async_copy(map_hbm, map_ref, sems.at[0]),
        pltpu.make_async_copy(u_ref.at[:, :, pl.ds(pair, 2), :], ue_ref, sems.at[1]),
        pltpu.make_async_copy(p_ref.at[:, :, pl.ds(jnp.where(lower, depth - 1, 0), 1), :], pe_ref, sems.at[2]),
        pltpu.make_async_copy(coef_ref.at[region, :, pl.ds(edge8, 8), :], ce_ref, sems.at[3]),
    ]
    beside = [
        pltpu.make_async_copy(u_ref.at[0, :, :, front], ua_ref, sems.at[4]),
        pltpu.make_async_copy(p_ref.at[0, :, :, front], pa_ref, sems.at[5]),
        pltpu.make_async_copy(coef_ref.at[:, :, :, front], ca_ref, sems.at[6]),
    ]
    for copy in copies + slab + beside:
        copy.start()
    for copy in copies:
        copy.wait()
    own_edge = jnp.where(lower, 1, 0)
    own_next = 1 - own_edge
    for m in range(2):
        for f in range(fields):
            at = m * fields + f
            near = ue_ref[m, f, pl.ds(own_edge, 1), :]
            pair_at = 8 * m + f
            edges_ref[pair_at : pair_at + 1, :] = near
            edges_ref[pair_at + 4 : pair_at + 5, :] = ue_ref[m, f, pl.ds(own_next, 1), :]
            edges_ref[16 + at : 17 + at, :] = 2.0 * near - pe_ref[m, f]
    for s in range(4):
        piece = ce_ref[s].astype(F32)
        edges_ref[24 + s : 25 + s, :] = jnp.where(lower, piece[7:8], piece[0:1])
    numbers = [map_ref[region * 4 + s] for s in range(4)] + [map_ref[other * 4 + s] for s in range(4)]
    for i, number in enumerate(numbers):
        edges_ref[28:29, tile_at(i)] = jnp.zeros((1, LANES), F32) + number.astype(F32)
    edges_ref[29:32, :] = jnp.zeros((3, width), F32)
    y_ref[4] = edges_ref[...].astype(BF16)
    for copy in slab + beside:
        copy.wait()


def pack_back_body(edges_ref, ua_ref, pa_ref, ca_ref, straight_ref, diag_ref):
    fields, depth, _ = ua_ref.shape
    region = lax.axis_index("region")
    lower = region == 0
    other = 1 - region
    lane = lane_ids()
    tag_rows = [edges_ref[28:29, tile_at(i)] for i in range(8)]
    blank = jnp.zeros((1, LANES), F32)
    for f in range(fields):
        now = ua_ref[f]
        ahead = 2.0 * now - pa_ref[f]
        piece = ca_ref[region, f].astype(F32)
        tile = jnp.where(
            lane < 64, now, jnp.where(lane < 96, pltpu.roll(ahead, 64, 1), pltpu.roll(piece, 96, 1))
        )
        straight_ref[f * depth : (f + 1) * depth, :] = tile.astype(BF16)
    far = [ca_ref[other, s].astype(F32) for s in range(4)]
    extra = [jnp.where(lower, piece[0:1], piece[depth - 1 : depth]) for piece in far] + tag_rows + [blank] * 4
    straight_ref[fields * depth : fields * depth + 16, :] = jnp.concatenate(extra, axis=0).astype(BF16)
    plane = jnp.zeros((depth, LANES), F32)
    for s in range(4):
        moved = pltpu.roll(far[s], 32 * s, 1) if s else far[s]
        plane = jnp.where((lane >= 32 * s) & (lane < 32 * s + 32), moved, plane)
    diag_ref[0:depth, :] = plane.astype(BF16)
    rows = [edges_ref[base : base + 4, 0:LANES] for base in (0, 4, 16, 24)]
    diag_ref[depth : depth + 24, :] = jnp.concatenate(rows + tag_rows, axis=0).astype(BF16)


def lane_sum(tile, lane):
    return sum_along_c(tile, *c_masks(lane))


def c_masks(lane):
    inside = lane & 31
    return inside != 0, inside != 31


def sum_along_c(tile, low, high):
    return (
        tile
        + jnp.where(low, pltpu.roll(tile, 1, 1), 0.0)
        + jnp.where(high, pltpu.roll(tile, LANES - 1, 1), 0.0)
    )


def nine_sum(tiles, lane):
    low, high = c_masks(lane)
    rows = [sum_along_c(tile, low, high) for tile in tiles]
    up = [pltpu.roll(row, 32, 1) for row in rows]
    down = [pltpu.roll(row, LANES - 32, 1) for row in rows]
    count = len(tiles)
    result = []
    for t in range(count):
        before = jnp.where(lane < 32, up[t - 1] if t else 0.0, up[t])
        after = jnp.where(lane >= 96, down[t + 1] if t < count - 1 else 0.0, down[t])
        result.append(rows[t] + before + after)
    return result


def column_sum(tile, row_id, low_row, high_row):
    depth = tile.shape[0]
    above = pltpu.roll(tile, 1, 0)
    below = pltpu.roll(tile, depth - 1, 0)
    return tile + jnp.where(row_id == 0, low_row, above) + jnp.where(row_id == depth - 1, high_row, below)


def local_body(
    map_hbm, owner_hbm, u_hbm, p_hbm, coef_ref, u_ref, box0_ref, box1_ref, drift_ref, rim_ref, held_ref, p_ref,
    map_ref, owner_ref, sems
):
    fields, depth, width = u_ref.shape[1:]
    main = width // LANES
    copies = []
    for f in range(fields):
        copies.append(
            (
                pltpu.make_async_copy(u_hbm.at[:, f], u_ref.at[:, f], sems.at[2 * f]),
                pltpu.make_async_copy(p_hbm.at[:, f], p_ref.at[:, f], sems.at[2 * f + 1]),
            )
        )
    numbers = load_map(map_hbm, map_ref, sems.at[2 * fields])
    owners = load_map(owner_hbm, owner_ref, sems.at[2 * fields + 1])
    for pair in copies:
        for copy in pair:
            copy.start()
    held_ref[...] = jnp.zeros(held_ref.shape, held_ref.dtype)
    numbers.wait()
    region = lax.axis_index("region")
    for s in range(4):
        held_ref[map_ref[region * 4 + s]] = coef_ref[region, s]
    lower = lax.axis_index("region") == 0
    lane = lane_ids()
    row_id = lax.broadcasted_iota(jnp.int32, (depth, 1), 0)
    boxes = (box0_ref, box1_ref)
    for f in range(fields):
        for copy in copies[f]:
            copy.wait()
        now = [u_ref[m, f, :, tile_at(t)] for m in range(2) for t in range(main)]
        sums = nine_sum(now, lane)
        for i, (tile, total) in enumerate(zip(now, sums)):
            m, t = divmod(i, main)
            lanes = tile_at(t)
            rim_ref[m, f : f + 1, lanes] = jnp.where(lower, total[depth - 1 : depth], total[0:1])
            boxes[m][f, :, lanes] = column_sum(total, row_id, 0.0, 0.0) - 27.0 * tile
            drift_ref[m, f, :, lanes] = 2.0 * tile - p_ref[m, f, :, lanes]
    rim_ref[:, 4:8, :] = jnp.zeros((2, 4, width), F32)
    owners.wait()
    moves = jnp.where(owner_ref[1] != lax.axis_index("blk"), 1.0, 0.0)
    rim_ref[0, 4:5, :] = jnp.zeros((1, width), F32) + moves


def tile_at(t):
    return slice(t * LANES, (t + 1) * LANES)


class ColumnEdge:
    def __init__(self, coef_ref, y_ref):
        self.region = lax.axis_index("region")
        self.lower = self.region == 0
        self.coef = coef_ref
        self.depth = coef_ref.shape[2]
        self.extra = y_ref[4].astype(F32)
        self.tags = [self.extra[28:29, i * LANES : (i + 1) * LANES] for i in range(8)]
        self.field_id = lax.broadcasted_iota(jnp.int32, (4, LANES), 0).astype(F32)

    def pair(self, m, lanes):
        return self.extra[8 * m : 8 * m + 8, lanes]

    def ahead(self, m, lanes):
        return self.extra[16 + 4 * m : 20 + 4 * m, lanes]

    def coefs(self, m, lanes):
        total = jnp.zeros((4, LANES), F32)
        for s in range(4):
            piece = self.coef[1 - self.region, s, :, lanes].astype(F32)
            held = jnp.where(self.lower, piece[0:1], piece[self.depth - 1 : self.depth])
            total = total + jnp.where(self.tags[s] == self.field_id + 4 * m, self.extra[24 + s : 25 + s, lanes], 0.0)
            total = total + jnp.where(self.tags[4 + s] == self.field_id + 4 * m, held, 0.0)
        return total

    def own(self, tile):
        return jnp.where(self.lower, tile[self.depth - 1 : self.depth], tile[0:1])

    def rows(self, row):
        return jnp.where(self.lower, 0.0, row), jnp.where(self.lower, row, 0.0)


def border_body(u_ref, straight_ref, diag_ref, box_in, box_ref, side_lap_ref, side_coef_ref, rim_ref):
    fields, depth, width = u_ref.shape[1:]
    lane = lane_ids()
    row_id = lax.broadcasted_iota(jnp.int32, (depth, 1), 0)
    lower = lax.axis_index("region") == 0
    before = slice(width - LANES, width)
    facing = lane >= 96
    tags = [straight_ref[fields * depth : fields * depth + 16, :].astype(F32)[4 + i : 5 + i] for i in range(8)]
    planes = []
    for s in range(4):
        planes.append(pltpu.roll(straight_ref[s * depth : (s + 1) * depth, :].astype(F32), 32, 1))
    diag_tile = diag_ref[0:depth, :].astype(F32)
    for s in range(4):
        planes.append(pltpu.roll(diag_tile, LANES - 32 * s, 1) if s else diag_tile)
    for f in range(fields):
        inner = u_ref[1, f, :, before]
        remote = straight_ref[f * depth : (f + 1) * depth, :].astype(F32)
        inner_sum, remote_sum = nine_sum([inner, remote], lane)
        for i, tile in enumerate((inner_sum, remote_sum)):
            rim_ref[i, f : f + 1, :] = jnp.where(lower, tile[depth - 1 : depth], tile[0:1])
        halo_c = jnp.zeros((depth, LANES), F32)
        for i in range(8):
            halo_c = halo_c + jnp.where(tags[i] == F32(f), planes[i], 0.0)
        side_coef_ref[f] = halo_c
        side_lap_ref[f] = column_sum(remote_sum, row_id, 0.0, 0.0) - 27.0 * remote
        whole = column_sum(inner_sum, row_id, 0.0, 0.0) - 27.0 * inner
        box_ref[f, :, before] = jnp.where(facing, whole, box_in[f, :, before])
    rim_ref[:, 4:8, :] = jnp.zeros((2, 4, LANES), F32)


def last_edges(
    coef_ref, y_ref, straight_ref, diag_ref, box0_ref, rim_ref, side_lap_ref, side_coef_ref, side_rim_ref, box_in,
    box_ref, lap_ref, side_ref, sums_ref
):
    fields, depth, width = box_in.shape
    main = width // LANES
    lane = lane_ids()
    column = ColumnEdge(coef_ref, y_ref)
    before = slice(width - LANES, width)
    extra_s = straight_ref[fields * depth : fields * depth + 16, :].astype(F32)
    extra_d = diag_ref[depth : depth + 24, :].astype(F32)
    tags_d = [extra_d[16 + i : 17 + i] for i in range(8)]

    def edge_tiles(of, remote):
        return [of(0, before)] + [of(1, tile_at(t)) for t in range(main)] + [remote]

    pairs = edge_tiles(column.pair, extra_d[0:8])
    near = [pair[0:4] for pair in pairs]
    ahead = edge_tiles(column.ahead, extra_d[8:12])
    corner = jnp.zeros((4, LANES), F32)
    for s in range(4):
        corner = corner + jnp.where(tags_d[s] == column.field_id, extra_d[12 + s : 13 + s], 0.0)
        corner = corner + jnp.where(tags_d[4 + s] == column.field_id, extra_s[s : s + 1], 0.0)
    edge_c = [column.coefs(0, before)] + [column.coefs(1, tile_at(t)) for t in range(main)] + [corner]
    pair_sum = nine_sum(pairs, lane)
    near_sum = [total[0:4] for total in pair_sum]
    both_sum = [total[0:4] + total[4:8] for total in pair_sum]
    laps, sides = [], []
    row_id = lax.broadcasted_iota(jnp.int32, (depth, 1), 0)
    top = slice(0, 1)
    bottom = slice(depth - 1, depth)
    for f in range(fields):
        for t in range(main):
            low_row, high_row = column.rows(near_sum[t + 1][f : f + 1])
            lanes = tile_at(t)
            box_ref[f, top, lanes] = box_in[f, top, lanes] + low_row
            box_ref[f, bottom, lanes] = box_in[f, bottom, lanes] + high_row
        remote = straight_ref[f * depth : (f + 1) * depth, :].astype(F32)
        low_row, high_row = column.rows(near_sum[main + 1][f : f + 1])
        lap = side_lap_ref[f] + jnp.where(row_id == 0, low_row, 0.0) + jnp.where(row_id == depth - 1, high_row, 0.0)
        sides.append(pltpu.roll(remote, 64, 1) + side_coef_ref[f] * lap)
        side_ref[f] = sides[f]
        low_row, high_row = column.rows(near_sum[0][f : f + 1])
        lap = box0_ref[f, :, before]
        laps.append(lap + jnp.where(row_id == 0, low_row, 0.0) + jnp.where(row_id == depth - 1, high_row, 0.0))
        lap_ref[f] = laps[f]
    rims = [rim_ref[0, 0:4, before]] + [rim_ref[1, 0:4, tile_at(t)] for t in range(main)] + [side_rim_ref[1, 0:4, :]]
    rims[main] = jnp.where(lane >= 96, side_rim_ref[0, 0:4, :], rims[main])
    stepped = []
    for t in range(main + 2):
        box = both_sum[t] + rims[t]
        stepped.append(ahead[t] + edge_c[t] * (box - 27.0 * near[t]))
    stepped_sum = nine_sum(stepped, lane)
    for t in range(main):
        sums_ref[0:4, tile_at(t)] = stepped_sum[t + 1]
    sums_ref[4:8, :] = jnp.zeros((4, width), F32)
    return stepped[main], stepped_sum[1 : main + 1], laps, sides


def first_edges_body(coef_ref, y_ref, rim_ref, box1_ref, box_in, box_ref, sums_ref, edge_c_ref):
    fields, depth, width = box_in.shape
    main = width // LANES
    lane = lane_ids()
    column = ColumnEdge(coef_ref, y_ref)
    after = slice(0, LANES)

    def edge_tiles(of):
        return [of(0, tile_at(t)) for t in range(main)] + [of(1, after)]

    pairs = edge_tiles(column.pair)
    near = [pair[0:4] for pair in pairs]
    pair_sum = nine_sum(pairs, lane)
    near_sum = [total[0:4] for total in pair_sum]
    both_sum = [total[0:4] + total[4:8] for total in pair_sum]
    ahead = edge_tiles(column.ahead)
    edge_c = edge_tiles(column.coefs)
    for f in range(fields):
        for t in range(main):
            low_row, high_row = column.rows(near_sum[t][f : f + 1])
            lanes = tile_at(t)
            box_ref[f, 0:1, lanes] = box_in[f, 0:1, lanes] + low_row
            box_ref[f, depth - 1 : depth, lanes] = box_in[f, depth - 1 : depth, lanes] + high_row
    rims = [rim_ref[0, 0:4, tile_at(t)] for t in range(main)] + [rim_ref[1, 0:4, after]]
    stepped = []
    for t in range(main + 1):
        box = both_sum[t] + rims[t]
        stepped.append(ahead[t] + edge_c[t] * (box - 27.0 * near[t]))
    stepped_sum = nine_sum(stepped, lane)
    for t in range(main):
        sums_ref[0:4, tile_at(t)] = stepped_sum[t]
    sums_ref[4:8, :] = jnp.zeros((4, width), F32)
    edge_c_ref[0:4, :] = edge_c[0]
    edge_c_ref[4:8, :] = jnp.zeros((4, LANES), F32)


def load_map(map_any, map_ref, sem):
    copy = pltpu.make_async_copy(map_any, map_ref, sem)
    copy.start()
    return copy


class Pieces:
    def __init__(self, edges_ref, held_ref, slab_ref):
        self.held, self.slab = held_ref, slab_ref
        self.tags = [edges_ref[28:29, tile_at(4 + s)] for s in range(4)]

    def piece(self, number):
        here = [tag == F32(number) for tag in self.tags]

        def tile(lanes):
            total = self.held[number, :, lanes].astype(F32)
            for s, mask in enumerate(here):
                total = jnp.where(mask, self.slab[s, :, lanes].astype(F32), total)
            return total

        return tile


def second_step(now, before, total, coef, row_id, row, lower):
    low_row, high_row = jnp.where(lower, 0.0, row), jnp.where(lower, row, 0.0)
    lap = column_sum(total, row_id, low_row, high_row) - 27.0 * now
    return 2.0 * now - before + coef * lap


CODES = 32000.0


def power_of(size):
    return jnp.ceil(jnp.log2(jnp.maximum(size, 1e-30)))


def coded(value, power):
    return jnp.floor(value * (CODES * jnp.exp2(-power)) + 0.5)


def narrow(value):
    return value.astype(jnp.int32).astype(jnp.int16)


def wide(code):
    return code.astype(jnp.int32).astype(F32)


def scale_of(power):
    return jnp.exp2(power) * (1.0 / CODES)


def last_row_a_body(
    edges_ref, u_ref, coef_ref, held_ref, y_ref, straight_ref, diag_ref, box0_ref, rim_ref, side_lap_ref, side_coef_ref,
    side_rim_ref, drift_ref, box_in, box_ref, lap_ref, side_ref, sums_ref, row_ref, code_ref, power_ref, extra_ref
):
    tail, edge_sums, laps, sides = last_edges(
        coef_ref, y_ref, straight_ref, diag_ref, box0_ref, rim_ref, side_lap_ref, side_coef_ref, side_rim_ref, box_in,
        box_ref, lap_ref, side_ref, sums_ref
    )
    refs = (edges_ref, u_ref, held_ref, y_ref, box_ref, drift_ref, lap_ref, side_ref, sums_ref, row_ref, code_ref, power_ref)
    last_row(0, *refs, more=(tail, edge_sums, laps, sides, rim_ref[0, 4:5, 0:LANES], extra_ref))


def last_row_b_body(first, *refs):
    last_row(first, *refs)


def last_row(
    first, edges_ref, u_ref, held_ref, y_ref, box_ref, drift_ref, lap_ref, side_ref, sums_ref, row_ref, code_ref, power_ref,
    more=None
):
    count, depth, width = row_ref.shape
    fields = u_ref.shape[1]
    main = width // LANES
    lane = lane_ids()
    row_id = lax.broadcasted_iota(jnp.int32, (depth, 1), 0)
    pieces = Pieces(edges_ref, held_ref, y_ref)
    lower = lax.axis_index("region") == 0
    before = slice(width - LANES, width)
    last_tiles = []
    for f in range(first, first + count):
        coef = pieces.piece(fields + f)
        coefs = [coef(tile_at(t)) for t in range(main)]
        middle = [drift_ref[1, f, :, tile_at(t)] + coefs[t] * box_ref[f, :, tile_at(t)] for t in range(main)]
        lap, side = (lap_ref[f], side_ref[f]) if more is None else (more[2][f], more[3][f])
        local = drift_ref[0, f, :, before] + pieces.piece(f)(before) * lap
        sums = nine_sum([local] + middle + [side], lane)
        for t in range(main):
            lanes = tile_at(t)
            row = sums_ref[f : f + 1, lanes] if more is None else more[1][t][f : f + 1]
            value = second_step(middle[t], u_ref[1, f, :, lanes], sums[t + 1], coefs[t], row_id, row, lower)
            row_ref[f - first, :, lanes] = value
            power = power_of(jnp.max(jnp.abs(value), axis=0, keepdims=True))
            at = (f - first) * main + t
            code_ref[at * depth : (at + 1) * depth, :] = narrow(coded(value, power))
            power_ref[at : at + 1, :] = power
        last_tiles.append(middle[main - 1])
    base = count * main * depth
    code_ref[base : base + count * main, :] = narrow(power_ref[...])
    if more is not None:
        tail, _, _, _, flag, extra_ref = more
        base += count * main
        both = []
        for f in range(fields):
            if f < count:
                stepped = last_tiles[f]
            else:
                stepped = drift_ref[1, f, :, before] + pieces.piece(fields + f)(before) * box_ref[f, :, before]
            both.append(jnp.where(lane >= 96, u_ref[1, f, :, before], pltpu.roll(stepped, 96, 1)))
        for g in range(fields // 2):
            pair = jnp.where(lane >= 64, both[2 * g], pltpu.roll(both[2 * g + 1], 64, 1))
            power = power_of(jnp.max(jnp.abs(pair), axis=0, keepdims=True))
            code_ref[base : base + depth, :] = narrow(coded(pair, power))
            extra_ref[g : g + 1, :] = power
            base += depth
        near = y_ref[4, 0:16, before].astype(F32)
        kinds = []
        for rows in (near[8:12], near[12:16], tail):
            kind = jnp.zeros((1, LANES), F32)
            for f in range(fields):
                shift = (32 * f + 32) % LANES
                row = rows[f : f + 1]
                kind = jnp.where(lane // 32 == f, pltpu.roll(row, shift, 1) if shift else row, kind)
            kinds.append(kind)
        power = power_of(jnp.maximum(jnp.maximum(jnp.abs(kinds[0]), jnp.abs(kinds[1])), jnp.abs(kinds[2])))
        extra_ref[2:3, :] = power
        for i, kind in enumerate(kinds):
            extra_ref[3 + i : 4 + i, :] = coded(kind, power)
        extra_ref[6:7, :] = flag
        extra_ref[7:8, :] = jnp.zeros((1, LANES), F32)
        code_ref[base : base + 8, :] = narrow(extra_ref[...])


def first_row_body(edges_ref, u_ref, held_ref, y_ref, box_ref, box1_ref, drift_ref, sums_ref, row_ref, coef0_ref):
    fields, depth, width = u_ref.shape[1:]
    main = width // LANES
    lane = lane_ids()
    row_id = lax.broadcasted_iota(jnp.int32, (depth, 1), 0)
    pieces = Pieces(edges_ref, held_ref, y_ref)
    lower = lax.axis_index("region") == 0
    after = slice(0, LANES)
    for f in range(fields):
        coef = pieces.piece(f)
        coefs = [coef(tile_at(t)) for t in range(main)]
        now = [drift_ref[0, f, :, tile_at(t)] + coefs[t] * box_ref[f, :, tile_at(t)] for t in range(main)]
        local = drift_ref[1, f, :, after] + pieces.piece(fields + f)(after) * box1_ref[f, :, after]
        sums = nine_sum(now + [local], lane)
        coef0_ref[f] = coefs[0]
        for t in range(main):
            lanes = tile_at(t)
            row = sums_ref[f : f + 1, lanes]
            row_ref[f, :, lanes] = second_step(now[t], u_ref[0, f, :, lanes], sums[t], coefs[t], row_id, row, lower)


def arrival(code_ref):
    rows = code_ref.shape[0]
    return wide(code_ref[rows - 8 : rows, :])[6, 0] > 0.5


def code_copies(first, row_ref, out_ref, sems, base):
    count = row_ref.shape[0]
    return [pltpu.make_async_copy(row_ref, out_ref.at[0, first : first + count], sems.at[base])]


def decode(code_ref, row_ref):
    count, depth, width = row_ref.shape
    main = width // LANES
    base = count * main * depth
    scale = scale_of(wide(code_ref[base : base + count * main, :]))
    for f in range(count):
        for t in range(main):
            at = f * main + t
            row_ref[f, :, tile_at(t)] = wide(code_ref[at * depth : (at + 1) * depth, :]) * scale[at : at + 1]


def row_copies(owner_ref, row_ref, last_refs, zero_ref, out_ref, at, sems, base):
    fields, _, width = row_ref.shape
    keeps = owner_ref[1] == lax.axis_index("blk")
    rest = slice(LANES, width)
    sources = [ref.at[f] for ref in last_refs for f in range(ref.shape[0])]

    def copies(sources, at, base):
        return [pltpu.make_async_copy(source, out_ref.at[at, f], sems.at[base + f]) for f, source in enumerate(sources)]

    firsts = [
        pltpu.make_async_copy(row_ref.at[f, :, rest], out_ref.at[at, f, :, rest], sems.at[base + f])
        for f in range(fields)
    ]
    kept = copies(sources, at + 1, base + fields)
    gone = copies([zero_ref] * fields, at + 1, base + fields)

    def apply(act):
        for copy in firsts:
            act(copy)

        @pl.when(keeps)
        def _():
            for copy in kept:
                act(copy)

        @pl.when(jnp.logical_not(keeps))
        def _():
            for copy in gone:
                act(copy)

    return apply


def rows_body(owner_ref, row_ref, *refs):
    last_refs, (out_ref, zero_ref, sems) = refs[:-3], refs[-3:]
    zero_ref[...] = jnp.zeros(zero_ref.shape, F32)
    apply = row_copies(owner_ref, row_ref, last_refs, zero_ref, out_ref, 1, sems, 0)
    apply(lambda copy: copy.start())
    apply(lambda copy: copy.wait())


def finish_body(owner_any, coef_ref, edge_c_ref, code_ref, row_ref, *refs):
    last_refs, (partial_ref, out_ref, tile_ref, arrived_ref, zero_ref, owner_ref, sems) = refs[:-7], refs[-7:]
    fields, depth, width = row_ref.shape
    main = width // LANES
    arrives = arrival(code_ref)
    lane = lane_ids()
    row_id = lax.broadcasted_iota(jnp.int32, (depth, 1), 0)
    lower = lax.axis_index("region") == 0
    first = lane < 32
    base = arrived_ref.shape[0] * main * (depth + 1)
    extra = wide(code_ref[base + depth * fields // 2 : base + depth * fields // 2 + 8, :])
    tile0 = tile_at(0)

    def beside(total, shift):
        return jnp.where(first, pltpu.roll(total, shift, 1), 0.0)

    def rows(row):
        return jnp.where(lower, 0.0, row), jnp.where(lower, row, 0.0)

    corners = []
    for kind in range(3):
        row = lane_sum(extra[3 + kind : 4 + kind] * scale_of(extra[2:3]), lane)
        places = [pltpu.roll(row, LANES - 32 * f, 1) if f else row for f in range(fields)]
        corners.append(jnp.where(first, jnp.concatenate(places, axis=0), 0.0))
    planes = []
    for g in range(fields // 2):
        pair = wide(code_ref[base + g * depth : base + (g + 1) * depth, :]) * scale_of(extra[g : g + 1])
        total = lane_sum(pair, lane)
        planes += [(beside(total, 32), beside(total, 64)), (beside(total, 96), total)]
    planes = [(now, jnp.where(first, then, 0.0)) for now, then in planes]
    own = [jnp.where(lower, now[depth - 1 : depth], now[0:1]) for now, _ in planes]
    edge_change = edge_c_ref[0:4, :] * (corners[0] + corners[1] + jnp.concatenate(own, axis=0))
    edge_sum = lane_sum(edge_change, lane)
    edge_sum = edge_sum + corners[2] + pltpu.roll(edge_sum, 32, 1)
    for f in range(fields):
        now, then = planes[f]
        low_row, high_row = rows(corners[0][f : f + 1])
        coef = coef_ref[f]
        change = coef * column_sum(now, row_id, low_row, high_row)
        total = lane_sum(change, lane)
        total = total + then + pltpu.roll(total, 32, 1)
        low_row, high_row = rows(edge_sum[f : f + 1])
        lap = column_sum(total, row_id, low_row, high_row) - 27.0 * change
        tile_ref[f] = row_ref[f, :, tile0] + 2.0 * change + coef * lap

    slot = jnp.where(arrives, 1, 0)
    last = pltpu.make_async_copy(tile_ref, out_ref.at[slot, :, :, tile0], sems.at[0])
    last.start()

    @pl.when(arrives)
    def _():
        decode(code_ref, arrived_ref)
        coming = code_copies(0, arrived_ref, out_ref, sems, 1)
        for copy in coming:
            copy.start()
        for copy in coming:
            copy.wait()

    @pl.when(jnp.logical_not(arrives))
    def _():
        load_map(owner_any, owner_ref, sems.at[1]).wait()
        zero_ref[...] = jnp.zeros(zero_ref.shape, F32)
        apply = row_copies(owner_ref, row_ref, last_refs, zero_ref, out_ref, 0, sems, 1)
        blank = [
            pltpu.make_async_copy(zero_ref, out_ref.at[2, f], sems.at[1 + 2 * fields + f]) for f in range(fields)
        ]
        apply(lambda copy: copy.start())
        for copy in blank:
            copy.start()
        for copy in blank:
            copy.wait()
        apply(lambda copy: copy.wait())

    last.wait()


def place_body(first, code_a_ref, code_ref, partial_ref, out_ref, row_ref, sems):
    arrives = arrival(code_a_ref)
    decode(code_ref, row_ref)
    copies = code_copies(first, row_ref, out_ref, sems, 0)

    @pl.when(arrives)
    def _():
        for copy in copies:
            copy.start()
        for copy in copies:
            copy.wait()


def fast_on_device(u_now, u_prev, coef_store, store_map, new_owner):
    blocks, _, fields, depth, width = u_now.shape
    now = u_now.reshape(blocks, fields, depth, width)
    prev = u_prev.reshape(blocks, fields, depth, width)
    coef = coef_store[0, 0]
    count = lax.axis_size("blk")
    order = store_map.reshape(-1)
    order_hbm, owner_hbm, now_hbm, prev_hbm, coef_hbm = (
        pltpu.with_memory_space_constraint(array, pltpu.HBM) for array in (order, new_owner, now, prev, coef)
    )
    params = pltpu.CompilerParams(vmem_limit_bytes=48 * 1024 * 1024)

    def call(body, name, out_shape, in_specs, out_specs, scratch, args, **options):
        return pl.pallas_call(
            body,
            out_shape=out_shape,
            in_specs=in_specs,
            out_specs=out_specs,
            scratch_shapes=scratch,
            compiler_params=params,
            name=name,
            **options,
        )(*args)

    straight = jax.ShapeDtypeStruct((fields * depth + 16, LANES), BF16)
    diag = jax.ShapeDtypeStruct((depth + 24, LANES), BF16)
    tiles = jax.ShapeDtypeStruct((fields, depth, LANES), F32)
    y_out, edges, front, front_prev, front_coef = call(
        pack_region_body,
        "pack_region",
        (
            jax.ShapeDtypeStruct((5, depth, width), BF16),
            jax.ShapeDtypeStruct((depth, width), F32),
            tiles,
            tiles,
            jax.ShapeDtypeStruct((2, 4, depth, LANES), BF16),
        ),
        [HBM] * 4,
        (VMEM,) * 5,
        [
            pltpu.VMEM((blocks, fields, 2, width), F32),
            pltpu.VMEM((blocks, fields, 1, width), F32),
            pltpu.VMEM((4, 8, width), BF16),
            pltpu.SMEM(order.shape, jnp.int32),
            pltpu.SemaphoreType.DMA((8,)),
        ],
        (order_hbm, now_hbm, prev_hbm, coef_hbm),
    )
    left, dleft = call(
        pack_back_body, "pack_back", (straight, diag), [VMEM] * 4, (VMEM,) * 2, [], (edges, front, front_prev, front_coef)
    )

    swap = [(0, 1), (1, 0)]
    forward = [(i, (i + 1) % count) for i in range(count)]
    backward = [(i, (i - 1) % count) for i in range(count)]
    crossed = [(r * count + i, (1 - r) * count + (i - 1) % count) for r in range(2) for i in range(count)]
    y_in = lax.ppermute(y_out, "region", swap)
    from_right = lax.ppermute(left, "blk", backward)
    from_dright = lax.ppermute(dleft, ("region", "blk"), crossed)

    row = jax.ShapeDtypeStruct((fields, depth, width), F32)
    both = jax.ShapeDtypeStruct(now.shape, F32)
    now, box0, box1, drift, rim, held = call(
        local_body,
        "local",
        (
            both,
            row,
            row,
            both,
            jax.ShapeDtypeStruct((blocks, 8, width), F32),
            jax.ShapeDtypeStruct((blocks * fields, depth, width), BF16),
        ),
        [HBM] * 4 + [VMEM],
        (VMEM,) * 6,
        [
            pltpu.VMEM(now.shape, F32),
            pltpu.SMEM(order.shape, jnp.int32),
            pltpu.SMEM(new_owner.shape, jnp.int32),
            pltpu.SemaphoreType.DMA((2 * fields + 2,)),
        ],
        (order_hbm, owner_hbm, now_hbm, prev_hbm, coef),
    )
    sums = jax.ShapeDtypeStruct((8, width), F32)
    edge = jax.ShapeDtypeStruct((8, LANES), F32)
    box1, side_lap, side_coef, side_rim = call(
        border_body,
        "border",
        (row, tiles, tiles, jax.ShapeDtypeStruct((2, 8, LANES), F32)),
        [VMEM] * 4,
        (VMEM,) * 4,
        [],
        (now, from_right, from_dright, box1),
        input_output_aliases={3: 0},
        cost_estimate=pl.CostEstimate(flops=0, transcendentals=0, bytes_accessed=40_000_000),
    )
    bounds = sorted({0, fields // 2, fields})
    parts = [(first, end - first) for first, end in zip(bounds, bounds[1:])]

    def part_shapes(size, more):
        tiled = size * width // LANES
        codes = tiled * (depth + 1) + more
        shapes = (jax.ShapeDtypeStruct((size, depth, width), F32), jax.ShapeDtypeStruct((codes, LANES), jnp.int16))
        return shapes, pltpu.VMEM((tiled, LANES), F32)

    shapes, powers = part_shapes(parts[0][1], fields // 2 * depth + 8)
    box1, lap1, side1, sums1, last, code = call(
        last_row_a_body,
        "last_row",
        (row, tiles, tiles, sums) + shapes,
        [VMEM] * 14,
        (VMEM,) * 6,
        [powers, pltpu.VMEM((8, LANES), F32)],
        (edges, now, coef, held, y_in, from_right, from_dright, box0, rim, side_lap, side_coef, side_rim, drift, box1),
        input_output_aliases={13: 0},
    )
    lasts = [last]
    arrived = [lax.ppermute(code, "blk", forward)]
    for first, size in parts[1:]:
        shapes, powers = part_shapes(size, 0)
        last, code = call(
            functools.partial(last_row_b_body, first),
            "last_row",
            shapes,
            [VMEM] * 9,
            (VMEM,) * 2,
            [powers],
            (edges, now, held, y_in, box1, drift, lap1, side1, sums1),
        )
        lasts.append(last)
        arrived.append(lax.ppermute(code, "blk", forward))
    box0, sums0, edge_c0 = call(
        first_edges_body,
        "first_edges",
        (row, sums, edge),
        [VMEM] * 3 + [ANY, VMEM],
        (VMEM,) * 3,
        [],
        (coef, y_in, rim, box1, box0),
        input_output_aliases={4: 0},
    )
    first_row, coef0 = call(
        first_row_body,
        "first_row",
        (row, tiles),
        [VMEM] * 8,
        (VMEM,) * 2,
        [],
        (edges, now, held, y_in, box0, box1, drift, sums0),
    )
    whole = jax.ShapeDtypeStruct((blocks + 1, fields, depth, width), F32)
    placed = call(
        rows_body,
        "rows",
        whole,
        [SMEM] + [VMEM] * (1 + len(lasts)),
        ANY,
        [pltpu.VMEM((depth, width), F32), pltpu.SemaphoreType.DMA((2 * fields,))],
        (new_owner, first_row, *lasts),
    )
    placed = call(
        finish_body,
        "finish",
        whole,
        [ANY] + [VMEM] * (4 + len(lasts)) + [ANY],
        ANY,
        [
            pltpu.VMEM((fields, depth, LANES), F32),
            pltpu.VMEM((parts[0][1], depth, width), F32),
            pltpu.VMEM((depth, width), F32),
            pltpu.SMEM(new_owner.shape, jnp.int32),
            pltpu.SemaphoreType.DMA((1 + 3 * fields,)),
        ],
        (new_owner, coef0, edge_c0, arrived[0], first_row, *lasts, placed),
        input_output_aliases={5 + len(lasts): 0},
    )
    for (first, size), codes in zip(parts[1:], arrived[1:]):
        placed = call(
            functools.partial(place_body, first),
            "place",
            whole,
            [VMEM, VMEM, ANY],
            ANY,
            [pltpu.VMEM((size, depth, width), F32), pltpu.SemaphoreType.DMA((2 * size,))],
            (arrived[0], codes, placed),
            input_output_aliases={2: 0},
        )
    return placed[:, None]


def solution(mesh):
    def on_device(*args):
        blocks = args[0].shape[0]
        if lax.axis_size("region") == 2 and blocks == 2:
            return fast_on_device(*args)
        return general_on_device(*args)

    return jax.shard_map(
        on_device,
        mesh=mesh,
        in_specs=(
            P("blk", "region", None, None, None),
            P("blk", "region", None, None, None),
            P("blk", "region", None, None, None, None),
            P("blk", "region", None),
            P("blk"),
        ),
        out_specs=P("blk", "region", None, None, None),
        check_vma=False,
    )
```

```python
import functools

import jax
import jax.numpy as jnp
from jax import lax
from jax.experimental import pallas as pl
from jax.experimental.pallas import tpu as pltpu
from jax.sharding import PartitionSpec as P

STEPS = 2
LANES = 128
F32 = jnp.float32
BF16 = jnp.bfloat16
VMEM = pl.BlockSpec(memory_space=pltpu.VMEM)
SMEM = pl.BlockSpec(memory_space=pltpu.SMEM)
ANY = pl.BlockSpec(memory_space=pl.ANY)
HBM = pl.BlockSpec(memory_space=pltpu.HBM)


def extended_2(block, sides, width, periodic):
    for axis, dim in sides:
        count = lax.axis_size(axis)
        forward = [(i, i + 1) for i in range(count - 1)]
        if periodic:
            forward.append((count - 1, 0))
        backward = [(target, source) for source, target in forward]
        low = lax.ppermute(
            lax.slice_in_dim(block, block.shape[dim] - width, None, axis=dim), axis, forward
        )
        high = lax.ppermute(lax.slice_in_dim(block, 0, width, axis=dim), axis, backward)
        block = jnp.concatenate([low, block, high], axis=dim)
    return block


def shifted_2(value, axis, by):
    devices = lax.axis_size(axis)
    return lax.ppermute(value, axis, [(i, (i + by) % devices) for i in range(devices)])


def stencil_step(state_now, state_prev, coefficient, live_count):
    slot_count, field_count, edge_cells, plane_cells = state_now.shape
    padded = extended_2(state_now, (("region", 2),), 1, False)
    first_planes = padded[..., :edge_cells]
    last_planes = padded[..., plane_cells - edge_cells :]
    last_live = jnp.take(last_planes, live_count - 1, axis=0)
    rim_pair = jnp.stack([first_planes[0], last_live], axis=2)
    spread = extended_2(rim_pair.astype(jnp.bfloat16), (("blk", 2),), 1, True).astype(
        rim_pair.dtype
    )
    left_rim = spread[:, :, 0]
    right_rim = spread[:, :, 3]
    before_planes = jnp.concatenate([left_rim[None], last_planes[:-1]], axis=0)
    after_planes = jnp.pad(first_planes[1:], ((0, 1), (0, 0), (0, 0), (0, 0)))
    slot_ids = jnp.arange(slot_count)
    after_planes = jnp.where(
        (slot_ids == live_count - 1)[:, None, None, None], right_rim[None], after_planes
    )
    extended = jnp.concatenate([before_planes, padded, after_planes], axis=-1)
    width = extended.shape[-1]
    column = jnp.arange(width) % edge_cells
    lower_mask = (column != 0).astype(jnp.float32)
    upper_mask = (column != edge_cells - 1).astype(jnp.float32)
    margin = ((0, 0), (0, 0), (0, 0), (1, 1))
    shifted = jnp.pad(extended, margin)
    summed = shifted[..., :width] * lower_mask + extended + shifted[..., 2:] * upper_mask
    summed = (
        summed[..., : -2 * edge_cells]
        + summed[..., edge_cells:-edge_cells]
        + summed[..., 2 * edge_cells :]
    )
    box_sum = summed[:, :, :-2] + summed[:, :, 1:-1] + summed[:, :, 2:]
    laplace = box_sum - 27.0 * state_now
    return 2.0 * state_now - state_prev + coefficient.astype(jnp.float32) * laplace


def compact(members, valid_flags):
    slot_count = valid_flags.shape[0]
    place_index = jnp.cumsum(valid_flags) - 1
    target = jnp.arange(slot_count)
    chooser = (valid_flags[None, :] == 1) & (place_index[None, :] == target[:, None])
    source = jnp.sum(jnp.where(chooser, target[None, :], 0), axis=1)
    filled = jnp.sum(chooser.astype(jnp.int32), axis=1) > 0
    placed = tuple(
        (
            jnp.where(
                filled.reshape((slot_count,) + (1,) * (member.ndim - 1)),
                jnp.take(member, source, axis=0),
                jnp.zeros_like(member),
            )
            for member in members
        )
    )
    return (placed, jnp.sum(valid_flags))


def general_on_device(u_now, u_prev, coef_store, store_map, new_owner):
    state_now = u_now[:, 0]
    state_prev = u_prev[:, 0]
    blocks, fields, edge_cells, plane_cells = state_now.shape
    store_local = coef_store[0, 0]
    arrived = lax.all_to_all(store_local, "region", split_axis=0, concat_axis=0, tiled=True)
    flattened = arrived.reshape((-1,) + arrived.shape[2:])
    inverse = jnp.argsort(store_map[0, 0])
    coefficient = jnp.take(flattened, inverse, axis=0).reshape(
        blocks, fields, edge_cells, plane_cells
    )
    own_index = lax.axis_index("blk")
    goes_right = new_owner[blocks - 1] != own_index
    mark_right = goes_right.astype(jnp.float32).reshape(1)
    middle_flags = jnp.ones((blocks - 2,), jnp.int32)
    keep_first = (new_owner[0] == own_index).astype(jnp.int32).reshape(1)
    keep_last = (new_owner[blocks - 1] == own_index).astype(jnp.int32).reshape(1)
    for step_index in range(STEPS):
        state_now, state_prev = (
            stencil_step(state_now, state_prev, coefficient, blocks),
            state_now,
        )
    from_left = shifted_2((state_now[blocks - 1], mark_right), "blk", 1)
    valid_flags = jnp.concatenate(
        [(from_left[1] > 0.5).astype(jnp.int32), keep_first, middle_flags, keep_last]
    )
    stacked_now = jnp.concatenate([from_left[0][None], state_now], axis=0)
    placed, live_count = compact((stacked_now,), valid_flags)
    result = placed[0]
    return result[:, None]


def lane_ids():
    return lax.broadcasted_iota(jnp.int32, (1, LANES), 1)


def edge_start(lower, depth, size):
    return pl.multiple_of(jnp.where(lower, depth - size, 0), size)


def pack_region_body(
    map_hbm, owner_hbm, u_ref, p_ref, coef_ref, y_ref, edges_ref, ua_ref, pa_ref, ca_ref, ue_ref, pe_ref, ce_ref,
    map_ref, owner_ref, sems
):
    fields, depth, width = u_ref.shape[1:]
    region = lax.axis_index("region")
    lower = region == 0
    other = 1 - region
    front = slice(0, LANES)
    edge8 = edge_start(lower, depth, 8)
    pair = jnp.where(lower, depth - 2, 0)
    slab = [pltpu.make_async_copy(coef_ref.at[other], y_ref.at[0:4], sems.at[7])]
    copies = [
        pltpu.make_async_copy(map_hbm, map_ref, sems.at[0]),
        pltpu.make_async_copy(owner_hbm, owner_ref, sems.at[8]),
        pltpu.make_async_copy(u_ref.at[:, :, pl.ds(pair, 2), :], ue_ref, sems.at[1]),
        pltpu.make_async_copy(p_ref.at[:, :, pl.ds(jnp.where(lower, depth - 1, 0), 1), :], pe_ref, sems.at[2]),
        pltpu.make_async_copy(coef_ref.at[region, :, pl.ds(edge8, 8), :], ce_ref, sems.at[3]),
    ]
    beside = [
        pltpu.make_async_copy(u_ref.at[0, :, :, front], ua_ref, sems.at[4]),
        pltpu.make_async_copy(p_ref.at[0, :, :, front], pa_ref, sems.at[5]),
        pltpu.make_async_copy(coef_ref.at[:, :, :, front], ca_ref, sems.at[6]),
    ]
    for copy in copies + slab + beside:
        copy.start()
    for copy in copies:
        copy.wait()
    own_edge = jnp.where(lower, 1, 0)
    own_next = 1 - own_edge
    for m in range(2):
        for f in range(fields):
            at = m * fields + f
            near = ue_ref[m, f, pl.ds(own_edge, 1), :]
            pair_at = 8 * m + f
            edges_ref[pair_at : pair_at + 1, :] = near
            edges_ref[pair_at + 4 : pair_at + 5, :] = ue_ref[m, f, pl.ds(own_next, 1), :]
            edges_ref[16 + at : 17 + at, :] = 2.0 * near - pe_ref[m, f]
    for s in range(4):
        piece = ce_ref[s].astype(F32)
        edges_ref[24 + s : 25 + s, :] = jnp.where(lower, piece[7:8], piece[0:1])
    numbers = [map_ref[region * 4 + s] for s in range(4)] + [map_ref[other * 4 + s] for s in range(4)]
    for i, number in enumerate(numbers):
        edges_ref[28:29, tile_at(i)] = jnp.zeros((1, LANES), F32) + number.astype(F32)
    edges_ref[29:30, :] = jnp.zeros((1, width), F32) + jnp.where(owner_ref[1] != lax.axis_index("blk"), 1.0, 0.0)
    edges_ref[30:32, :] = jnp.zeros((2, width), F32)
    y_ref[4] = edges_ref[...].astype(BF16)
    for copy in slab + beside:
        copy.wait()


def pack_back_body(edges_ref, ua_ref, pa_ref, ca_ref, straight_ref, diag_ref):
    fields, depth, _ = ua_ref.shape
    region = lax.axis_index("region")
    lower = region == 0
    other = 1 - region
    lane = lane_ids()
    tag_rows = [edges_ref[28:29, tile_at(i)] for i in range(8)]
    blank = jnp.zeros((1, LANES), F32)
    for f in range(fields):
        now = ua_ref[f]
        ahead = 2.0 * now - pa_ref[f]
        piece = ca_ref[region, f].astype(F32)
        tile = jnp.where(
            lane < 64, now, jnp.where(lane < 96, pltpu.roll(ahead, 64, 1), pltpu.roll(piece, 96, 1))
        )
        straight_ref[f * depth : (f + 1) * depth, :] = tile.astype(BF16)
    far = [ca_ref[other, s].astype(F32) for s in range(4)]
    extra = [jnp.where(lower, piece[0:1], piece[depth - 1 : depth]) for piece in far] + tag_rows + [blank] * 4
    straight_ref[fields * depth : fields * depth + 16, :] = jnp.concatenate(extra, axis=0).astype(BF16)
    plane = jnp.zeros((depth, LANES), F32)
    for s in range(4):
        moved = pltpu.roll(far[s], 32 * s, 1) if s else far[s]
        plane = jnp.where((lane >= 32 * s) & (lane < 32 * s + 32), moved, plane)
    diag_ref[0:depth, :] = plane.astype(BF16)
    rows = [edges_ref[base : base + 4, 0:LANES] for base in (0, 4, 16, 24)]
    diag_ref[depth : depth + 32, :] = jnp.concatenate(rows + tag_rows + [blank] * 8, axis=0).astype(BF16)


def lane_sum(tile, lane):
    return sum_along_c(tile, *c_masks(lane))


def c_masks(lane):
    inside = lane & 31
    return inside != 0, inside != 31


def sum_along_c(tile, low, high):
    return (
        tile
        + jnp.where(low, pltpu.roll(tile, 1, 1), 0.0)
        + jnp.where(high, pltpu.roll(tile, LANES - 1, 1), 0.0)
    )


def nine_sum(tiles, lane):
    low, high = c_masks(lane)
    rows = [sum_along_c(tile, low, high) for tile in tiles]
    up = [pltpu.roll(row, 32, 1) for row in rows]
    down = [pltpu.roll(row, LANES - 32, 1) for row in rows]
    count = len(tiles)
    result = []
    for t in range(count):
        before = jnp.where(lane < 32, up[t - 1] if t else 0.0, up[t])
        after = jnp.where(lane >= 96, down[t + 1] if t < count - 1 else 0.0, down[t])
        result.append(rows[t] + before + after)
    return result


def column_sum(tile, row_id, low_row, high_row):
    depth = tile.shape[0]
    above = pltpu.roll(tile, 1, 0)
    below = pltpu.roll(tile, depth - 1, 0)
    return tile + jnp.where(row_id == 0, low_row, above) + jnp.where(row_id == depth - 1, high_row, below)


def local_body(
    map_hbm, u_hbm, p_hbm, coef_ref, u_ref, box0_ref, box1_ref, drift_ref, rim_ref, held_ref, p_ref, map_ref, sems
):
    fields, depth, width = u_ref.shape[1:]
    main = width // LANES
    copies = []
    for f in range(fields):
        copies.append(
            (
                pltpu.make_async_copy(u_hbm.at[:, f], u_ref.at[:, f], sems.at[2 * f]),
                pltpu.make_async_copy(p_hbm.at[:, f], p_ref.at[:, f], sems.at[2 * f + 1]),
            )
        )
    numbers = load_map(map_hbm, map_ref, sems.at[2 * fields])
    for pair in copies:
        for copy in pair:
            copy.start()
    held_ref[...] = jnp.zeros(held_ref.shape, held_ref.dtype)
    numbers.wait()
    region = lax.axis_index("region")
    for s in range(4):
        held_ref[map_ref[region * 4 + s]] = coef_ref[region, s]
    lower = lax.axis_index("region") == 0
    lane = lane_ids()
    row_id = lax.broadcasted_iota(jnp.int32, (depth, 1), 0)
    boxes = (box0_ref, box1_ref)
    for f in range(fields):
        for copy in copies[f]:
            copy.wait()
        now = [u_ref[m, f, :, tile_at(t)] for m in range(2) for t in range(main)]
        sums = nine_sum(now, lane)
        for i, (tile, total) in enumerate(zip(now, sums)):
            m, t = divmod(i, main)
            lanes = tile_at(t)
            rim_ref[m, f : f + 1, lanes] = jnp.where(lower, total[depth - 1 : depth], total[0:1])
            boxes[m][f, :, lanes] = column_sum(total, row_id, 0.0, 0.0) - 27.0 * tile
            drift_ref[m, f, :, lanes] = 2.0 * tile - p_ref[m, f, :, lanes]
    rim_ref[:, 4:8, :] = jnp.zeros((2, 4, width), F32)


def tile_at(t):
    return slice(t * LANES, (t + 1) * LANES)


class ColumnEdge:
    def __init__(self, coef_ref, y_ref):
        self.region = lax.axis_index("region")
        self.lower = self.region == 0
        self.coef = coef_ref
        self.depth = coef_ref.shape[2]
        self.extra = y_ref[4].astype(F32)
        self.tags = [self.extra[28:29, i * LANES : (i + 1) * LANES] for i in range(8)]
        self.field_id = lax.broadcasted_iota(jnp.int32, (4, LANES), 0).astype(F32)

    def pair(self, m, lanes):
        return self.extra[8 * m : 8 * m + 8, lanes]

    def ahead(self, m, lanes):
        return self.extra[16 + 4 * m : 20 + 4 * m, lanes]

    def coefs(self, m, lanes):
        total = jnp.zeros((4, LANES), F32)
        for s in range(4):
            piece = self.coef[1 - self.region, s, :, lanes].astype(F32)
            held = jnp.where(self.lower, piece[0:1], piece[self.depth - 1 : self.depth])
            total = total + jnp.where(self.tags[s] == self.field_id + 4 * m, self.extra[24 + s : 25 + s, lanes], 0.0)
            total = total + jnp.where(self.tags[4 + s] == self.field_id + 4 * m, held, 0.0)
        return total

    def own(self, tile):
        return jnp.where(self.lower, tile[self.depth - 1 : self.depth], tile[0:1])

    def rows(self, row):
        return jnp.where(self.lower, 0.0, row), jnp.where(self.lower, row, 0.0)


def border_body(u_ref, straight_ref, diag_ref, box_in, box_ref, side_lap_ref, side_coef_ref, rim_ref):
    fields, depth, width = u_ref.shape[1:]
    lane = lane_ids()
    row_id = lax.broadcasted_iota(jnp.int32, (depth, 1), 0)
    lower = lax.axis_index("region") == 0
    before = slice(width - LANES, width)
    facing = lane >= 96
    tags = [straight_ref[fields * depth : fields * depth + 16, :].astype(F32)[4 + i : 5 + i] for i in range(8)]
    planes = []
    for s in range(4):
        planes.append(pltpu.roll(straight_ref[s * depth : (s + 1) * depth, :].astype(F32), 32, 1))
    diag_tile = diag_ref[0:depth, :].astype(F32)
    for s in range(4):
        planes.append(pltpu.roll(diag_tile, LANES - 32 * s, 1) if s else diag_tile)
    for f in range(fields):
        inner = u_ref[1, f, :, before]
        remote = straight_ref[f * depth : (f + 1) * depth, :].astype(F32)
        inner_sum, remote_sum = nine_sum([inner, remote], lane)
        for i, tile in enumerate((inner_sum, remote_sum)):
            rim_ref[i, f : f + 1, :] = jnp.where(lower, tile[depth - 1 : depth], tile[0:1])
        halo_c = jnp.zeros((depth, LANES), F32)
        for i in range(8):
            halo_c = halo_c + jnp.where(tags[i] == F32(f), planes[i], 0.0)
        side_coef_ref[f] = halo_c
        side_lap_ref[f] = column_sum(remote_sum, row_id, 0.0, 0.0) - 27.0 * remote
        whole = column_sum(inner_sum, row_id, 0.0, 0.0) - 27.0 * inner
        box_ref[f, :, before] = jnp.where(facing, whole, box_in[f, :, before])
    rim_ref[:, 4:8, :] = jnp.zeros((2, 4, LANES), F32)


def last_edges(
    coef_ref, y_ref, straight_ref, diag_ref, box0_ref, rim_ref, side_lap_ref, side_coef_ref, side_rim_ref, box_in,
    box_ref, lap_ref, side_ref, sums_ref
):
    fields, depth, width = box_in.shape
    main = width // LANES
    lane = lane_ids()
    column = ColumnEdge(coef_ref, y_ref)
    before = slice(width - LANES, width)
    extra_s = straight_ref[fields * depth : fields * depth + 16, :].astype(F32)
    extra_d = diag_ref[depth : depth + 32, :].astype(F32)
    tags_d = [extra_d[16 + i : 17 + i] for i in range(8)]

    def edge_tiles(of, remote):
        return [of(0, before)] + [of(1, tile_at(t)) for t in range(main)] + [remote]

    pairs = edge_tiles(column.pair, extra_d[0:8])
    near = [pair[0:4] for pair in pairs]
    ahead = edge_tiles(column.ahead, extra_d[8:12])
    corner = jnp.zeros((4, LANES), F32)
    for s in range(4):
        corner = corner + jnp.where(tags_d[s] == column.field_id, extra_d[12 + s : 13 + s], 0.0)
        corner = corner + jnp.where(tags_d[4 + s] == column.field_id, extra_s[s : s + 1], 0.0)
    edge_c = [column.coefs(0, before)] + [column.coefs(1, tile_at(t)) for t in range(main)] + [corner]
    pair_sum = nine_sum(pairs, lane)
    near_sum = [total[0:4] for total in pair_sum]
    both_sum = [total[0:4] + total[4:8] for total in pair_sum]
    top = slice(0, 1)
    bottom = slice(depth - 1, depth)
    for f in range(fields):
        for t in range(main):
            low_row, high_row = column.rows(near_sum[t + 1][f : f + 1])
            lanes = tile_at(t)
            box_ref[f, top, lanes] = box_in[f, top, lanes] + low_row
            box_ref[f, bottom, lanes] = box_in[f, bottom, lanes] + high_row
        remote = straight_ref[f * depth : (f + 1) * depth, :].astype(F32)
        side_ref[f] = pltpu.roll(remote, 64, 1) + side_coef_ref[f] * side_lap_ref[f]
        low_row, high_row = column.rows(near_sum[main + 1][f : f + 1])
        side_ref[f, top] += side_coef_ref[f, top] * low_row
        side_ref[f, bottom] += side_coef_ref[f, bottom] * high_row
        low_row, high_row = column.rows(near_sum[0][f : f + 1])
        lap_ref[f] = box0_ref[f, :, before]
        lap_ref[f, top] += low_row
        lap_ref[f, bottom] += high_row
    rims = [rim_ref[0, 0:4, before]] + [rim_ref[1, 0:4, tile_at(t)] for t in range(main)] + [side_rim_ref[1, 0:4, :]]
    rims[main] = jnp.where(lane >= 96, side_rim_ref[0, 0:4, :], rims[main])
    stepped = []
    for t in range(main + 2):
        box = both_sum[t] + rims[t]
        stepped.append(ahead[t] + edge_c[t] * (box - 27.0 * near[t]))
    stepped_sum = nine_sum(stepped, lane)
    for t in range(main):
        sums_ref[0:4, tile_at(t)] = stepped_sum[t + 1]
    sums_ref[4:8, :] = jnp.zeros((4, width), F32)
    return stepped[main], stepped_sum[1 : main + 1]


def first_edges_body(coef_ref, y_ref, rim_ref, box1_ref, box_in, box_ref, sums_ref, edge_c_ref):
    fields, depth, width = box_in.shape
    main = width // LANES
    lane = lane_ids()
    column = ColumnEdge(coef_ref, y_ref)
    after = slice(0, LANES)

    def edge_tiles(of):
        return [of(0, tile_at(t)) for t in range(main)] + [of(1, after)]

    pairs = edge_tiles(column.pair)
    near = [pair[0:4] for pair in pairs]
    pair_sum = nine_sum(pairs, lane)
    near_sum = [total[0:4] for total in pair_sum]
    both_sum = [total[0:4] + total[4:8] for total in pair_sum]
    ahead = edge_tiles(column.ahead)
    edge_c = edge_tiles(column.coefs)
    for f in range(fields):
        for t in range(main):
            low_row, high_row = column.rows(near_sum[t][f : f + 1])
            lanes = tile_at(t)
            box_ref[f, 0:1, lanes] = box_in[f, 0:1, lanes] + low_row
            box_ref[f, depth - 1 : depth, lanes] = box_in[f, depth - 1 : depth, lanes] + high_row
    rims = [rim_ref[0, 0:4, tile_at(t)] for t in range(main)] + [rim_ref[1, 0:4, after]]
    stepped = []
    for t in range(main + 1):
        box = both_sum[t] + rims[t]
        stepped.append(ahead[t] + edge_c[t] * (box - 27.0 * near[t]))
    stepped_sum = nine_sum(stepped, lane)
    for t in range(main):
        sums_ref[0:4, tile_at(t)] = stepped_sum[t]
    sums_ref[4:8, :] = jnp.zeros((4, width), F32)
    edge_c_ref[0:4, :] = edge_c[0]
    edge_c_ref[4:8, :] = jnp.zeros((4, LANES), F32)


def load_map(map_any, map_ref, sem):
    copy = pltpu.make_async_copy(map_any, map_ref, sem)
    copy.start()
    return copy


class Pieces:
    def __init__(self, edges_ref, held_ref, slab_ref):
        self.held, self.slab = held_ref, slab_ref
        self.tags = [edges_ref[28:29, tile_at(4 + s)] for s in range(4)]

    def piece(self, number):
        here = [tag == F32(number) for tag in self.tags]

        def tile(lanes):
            total = self.held[number, :, lanes].astype(F32)
            for s, mask in enumerate(here):
                total = jnp.where(mask, self.slab[s, :, lanes].astype(F32), total)
            return total

        return tile


def second_step(now, before, total, coef, row_id, row, lower):
    low_row, high_row = jnp.where(lower, 0.0, row), jnp.where(lower, row, 0.0)
    lap = column_sum(total, row_id, low_row, high_row) - 27.0 * now
    return 2.0 * now - before + coef * lap


CODES = 32000.0


def power_of(size):
    return jnp.ceil(jnp.log2(jnp.maximum(size, 1e-30)))


def coded(value, power):
    return jnp.floor(value * (CODES * jnp.exp2(-power)) + 0.5)


def narrow(value):
    return value.astype(jnp.int32).astype(jnp.int16)


def wide(code):
    return code.astype(jnp.int32).astype(F32)


def scale_of(power):
    return jnp.exp2(power) * (1.0 / CODES)


def last_row_a_body(
    edges_ref, u_ref, coef_ref, held_ref, y_ref, straight_ref, diag_ref, box0_ref, rim_ref, side_lap_ref, side_coef_ref,
    side_rim_ref, drift_ref, box_in, box_ref, lap_ref, side_ref, sums_ref, row_ref, code_ref, power_ref, extra_ref
):
    tail, edge_sums = last_edges(
        coef_ref, y_ref, straight_ref, diag_ref, box0_ref, rim_ref, side_lap_ref, side_coef_ref, side_rim_ref, box_in,
        box_ref, lap_ref, side_ref, sums_ref
    )
    refs = (edges_ref, u_ref, held_ref, y_ref, box_ref, drift_ref, lap_ref, side_ref, sums_ref, row_ref, code_ref, power_ref)
    last_row(0, *refs, more=(tail, edge_sums, extra_ref))


def last_row_b_body(first, *refs):
    last_row(first, *refs)


def last_row(
    first, edges_ref, u_ref, held_ref, y_ref, box_ref, drift_ref, lap_ref, side_ref, sums_ref, row_ref, code_ref, power_ref,
    more=None
):
    count, depth, width = row_ref.shape
    fields = u_ref.shape[1]
    main = width // LANES
    lane = lane_ids()
    row_id = lax.broadcasted_iota(jnp.int32, (depth, 1), 0)
    pieces = Pieces(edges_ref, held_ref, y_ref)
    lower = lax.axis_index("region") == 0
    before = slice(width - LANES, width)
    last_tiles = []
    for f in range(first, first + count):
        coef = pieces.piece(fields + f)
        coefs = [coef(tile_at(t)) for t in range(main)]
        middle = [drift_ref[1, f, :, tile_at(t)] + coefs[t] * box_ref[f, :, tile_at(t)] for t in range(main)]
        local = drift_ref[0, f, :, before] + pieces.piece(f)(before) * lap_ref[f]
        sums = nine_sum([local] + middle + [side_ref[f]], lane)
        for t in range(main):
            lanes = tile_at(t)
            row = sums_ref[f : f + 1, lanes] if more is None else more[1][t][f : f + 1]
            value = second_step(middle[t], u_ref[1, f, :, lanes], sums[t + 1], coefs[t], row_id, row, lower)
            row_ref[f - first, :, lanes] = value
            power = power_of(jnp.max(jnp.abs(value), axis=0, keepdims=True))
            at = (f - first) * main + t
            code_ref[at * depth : (at + 1) * depth, :] = narrow(coded(value, power))
            power_ref[at : at + 1, :] = power
        last_tiles.append(middle[main - 1])
    base = count * main * depth
    code_ref[base : base + count * main, :] = narrow(power_ref[...])
    if more is not None:
        tail, _, extra_ref = more
        base += count * main
        both = []
        for f in range(fields):
            if f < count:
                stepped = last_tiles[f]
            else:
                stepped = drift_ref[1, f, :, before] + pieces.piece(fields + f)(before) * box_ref[f, :, before]
            both.append(jnp.where(lane >= 96, u_ref[1, f, :, before], pltpu.roll(stepped, 96, 1)))
        for g in range(fields // 2):
            pair = jnp.where(lane >= 64, both[2 * g], pltpu.roll(both[2 * g + 1], 64, 1))
            power = power_of(jnp.max(jnp.abs(pair), axis=0, keepdims=True))
            code_ref[base : base + depth, :] = narrow(coded(pair, power))
            extra_ref[g : g + 1, :] = power
            base += depth
        near = y_ref[4, 0:16, before].astype(F32)
        kinds = []
        for rows in (near[8:12], near[12:16], tail):
            kind = jnp.zeros((1, LANES), F32)
            for f in range(fields):
                shift = (32 * f + 32) % LANES
                row = rows[f : f + 1]
                kind = jnp.where(lane // 32 == f, pltpu.roll(row, shift, 1) if shift else row, kind)
            kinds.append(kind)
        power = power_of(jnp.maximum(jnp.maximum(jnp.abs(kinds[0]), jnp.abs(kinds[1])), jnp.abs(kinds[2])))
        extra_ref[2:3, :] = power
        for i, kind in enumerate(kinds):
            extra_ref[3 + i : 4 + i, :] = coded(kind, power)
        extra_ref[6:7, :] = edges_ref[29:30, 0:LANES]
        extra_ref[7:8, :] = jnp.zeros((1, LANES), F32)
        code_ref[base : base + 8, :] = narrow(extra_ref[...])


def first_row_body(edges_ref, u_ref, held_ref, y_ref, box_ref, box1_ref, drift_ref, sums_ref, row_ref, coef0_ref):
    fields, depth, width = u_ref.shape[1:]
    main = width // LANES
    lane = lane_ids()
    row_id = lax.broadcasted_iota(jnp.int32, (depth, 1), 0)
    pieces = Pieces(edges_ref, held_ref, y_ref)
    lower = lax.axis_index("region") == 0
    after = slice(0, LANES)
    for f in range(fields):
        coef = pieces.piece(f)
        coefs = [coef(tile_at(t)) for t in range(main)]
        now = [drift_ref[0, f, :, tile_at(t)] + coefs[t] * box_ref[f, :, tile_at(t)] for t in range(main)]
        local = drift_ref[1, f, :, after] + pieces.piece(fields + f)(after) * box1_ref[f, :, after]
        sums = nine_sum(now + [local], lane)
        coef0_ref[f] = coefs[0]
        for t in range(main):
            lanes = tile_at(t)
            row = sums_ref[f : f + 1, lanes]
            row_ref[f, :, lanes] = second_step(now[t], u_ref[0, f, :, lanes], sums[t], coefs[t], row_id, row, lower)


def arrival(code_ref):
    rows = code_ref.shape[0]
    return wide(code_ref[rows - 8 : rows, :])[6, 0] > 0.5


def code_copies(first, row_ref, out_ref, sems, base):
    count = row_ref.shape[0]
    return [pltpu.make_async_copy(row_ref, out_ref.at[0, first : first + count], sems.at[base])]


def decode(code_ref, row_ref):
    count, depth, width = row_ref.shape
    main = width // LANES
    base = count * main * depth
    scale = scale_of(wide(code_ref[base : base + count * main, :]))
    for f in range(count):
        for t in range(main):
            at = f * main + t
            row_ref[f, :, tile_at(t)] = wide(code_ref[at * depth : (at + 1) * depth, :]) * scale[at : at + 1]


def row_copies(owner_ref, row_ref, last_refs, zero_ref, out_ref, at, sems, base):
    fields, _, width = row_ref.shape
    keeps = owner_ref[1] == lax.axis_index("blk")
    rest = slice(LANES, width)
    sources = [ref.at[f] for ref in last_refs for f in range(ref.shape[0])]

    def copies(sources, at, base):
        return [pltpu.make_async_copy(source, out_ref.at[at, f], sems.at[base + f]) for f, source in enumerate(sources)]

    firsts = [
        pltpu.make_async_copy(row_ref.at[f, :, rest], out_ref.at[at, f, :, rest], sems.at[base + f])
        for f in range(fields)
    ]
    kept = copies(sources, at + 1, base + fields)
    gone = copies([zero_ref] * fields, at + 1, base + fields)

    def apply(act):
        for copy in firsts:
            act(copy)

        @pl.when(keeps)
        def _():
            for copy in kept:
                act(copy)

        @pl.when(jnp.logical_not(keeps))
        def _():
            for copy in gone:
                act(copy)

    return apply


def rows_body(owner_ref, row_ref, *refs):
    last_refs, (out_ref, zero_ref, sems) = refs[:-3], refs[-3:]
    zero_ref[...] = jnp.zeros(zero_ref.shape, F32)
    apply = row_copies(owner_ref, row_ref, last_refs, zero_ref, out_ref, 1, sems, 0)
    apply(lambda copy: copy.start())
    apply(lambda copy: copy.wait())


def finish_body(owner_any, coef_ref, edge_c_ref, code_ref, row_ref, *refs):
    last_refs, (partial_ref, out_ref, tile_ref, arrived_ref, zero_ref, owner_ref, sems) = refs[:-7], refs[-7:]
    fields, depth, width = row_ref.shape
    main = width // LANES
    arrives = arrival(code_ref)
    lane = lane_ids()
    row_id = lax.broadcasted_iota(jnp.int32, (depth, 1), 0)
    lower = lax.axis_index("region") == 0
    first = lane < 32
    base = arrived_ref.shape[0] * main * (depth + 1)
    extra = wide(code_ref[base + depth * fields // 2 : base + depth * fields // 2 + 8, :])
    tile0 = tile_at(0)

    def beside(total, shift):
        return jnp.where(first, pltpu.roll(total, shift, 1), 0.0)

    def rows(row):
        return jnp.where(lower, 0.0, row), jnp.where(lower, row, 0.0)

    corners = []
    for kind in range(3):
        row = lane_sum(extra[3 + kind : 4 + kind] * scale_of(extra[2:3]), lane)
        places = [pltpu.roll(row, LANES - 32 * f, 1) if f else row for f in range(fields)]
        corners.append(jnp.where(first, jnp.concatenate(places, axis=0), 0.0))
    planes = []
    for g in range(fields // 2):
        pair = wide(code_ref[base + g * depth : base + (g + 1) * depth, :]) * scale_of(extra[g : g + 1])
        total = lane_sum(pair, lane)
        planes += [(beside(total, 32), beside(total, 64)), (beside(total, 96), total)]
    planes = [(now, jnp.where(first, then, 0.0)) for now, then in planes]
    own = [jnp.where(lower, now[depth - 1 : depth], now[0:1]) for now, _ in planes]
    edge_change = edge_c_ref[0:4, :] * (corners[0] + corners[1] + jnp.concatenate(own, axis=0))
    edge_sum = lane_sum(edge_change, lane)
    edge_sum = edge_sum + corners[2] + pltpu.roll(edge_sum, 32, 1)
    for f in range(fields):
        now, then = planes[f]
        low_row, high_row = rows(corners[0][f : f + 1])
        coef = coef_ref[f]
        change = coef * column_sum(now, row_id, low_row, high_row)
        total = lane_sum(change, lane)
        total = total + then + pltpu.roll(total, 32, 1)
        low_row, high_row = rows(edge_sum[f : f + 1])
        lap = column_sum(total, row_id, low_row, high_row) - 27.0 * change
        tile_ref[f] = row_ref[f, :, tile0] + 2.0 * change + coef * lap

    slot = jnp.where(arrives, 1, 0)
    last = pltpu.make_async_copy(tile_ref, out_ref.at[slot, :, :, tile0], sems.at[0])
    last.start()

    @pl.when(arrives)
    def _():
        decode(code_ref, arrived_ref)
        coming = code_copies(0, arrived_ref, out_ref, sems, 1)
        for copy in coming:
            copy.start()
        for copy in coming:
            copy.wait()

    @pl.when(jnp.logical_not(arrives))
    def _():
        load_map(owner_any, owner_ref, sems.at[1]).wait()
        zero_ref[...] = jnp.zeros(zero_ref.shape, F32)
        apply = row_copies(owner_ref, row_ref, last_refs, zero_ref, out_ref, 0, sems, 1)
        blank = [
            pltpu.make_async_copy(zero_ref, out_ref.at[2, f], sems.at[1 + 2 * fields + f]) for f in range(fields)
        ]
        apply(lambda copy: copy.start())
        for copy in blank:
            copy.start()
        for copy in blank:
            copy.wait()
        apply(lambda copy: copy.wait())

    last.wait()


def place_body(first, code_a_ref, code_ref, partial_ref, out_ref, row_ref, sems):
    arrives = arrival(code_a_ref)
    decode(code_ref, row_ref)
    copies = code_copies(first, row_ref, out_ref, sems, 0)

    @pl.when(arrives)
    def _():
        for copy in copies:
            copy.start()
        for copy in copies:
            copy.wait()


def fast_on_device(u_now, u_prev, coef_store, store_map, new_owner):
    blocks, _, fields, depth, width = u_now.shape
    now = u_now.reshape(blocks, fields, depth, width)
    prev = u_prev.reshape(blocks, fields, depth, width)
    coef = coef_store[0, 0]
    count = lax.axis_size("blk")
    order = store_map.reshape(-1)
    order_hbm, owner_hbm, now_hbm, prev_hbm, coef_hbm = (
        pltpu.with_memory_space_constraint(array, pltpu.HBM) for array in (order, new_owner, now, prev, coef)
    )
    params = pltpu.CompilerParams(vmem_limit_bytes=48 * 1024 * 1024)

    def call(body, name, out_shape, in_specs, out_specs, scratch, args, **options):
        return pl.pallas_call(
            body,
            out_shape=out_shape,
            in_specs=in_specs,
            out_specs=out_specs,
            scratch_shapes=scratch,
            compiler_params=params,
            name=name,
            **options,
        )(*args)

    straight = jax.ShapeDtypeStruct((fields * depth + 16, LANES), BF16)
    diag = jax.ShapeDtypeStruct((depth + 32, LANES), BF16)
    tiles = jax.ShapeDtypeStruct((fields, depth, LANES), F32)
    y_out, edges, front, front_prev, front_coef = call(
        pack_region_body,
        "pack_region",
        (
            jax.ShapeDtypeStruct((5, depth, width), BF16),
            jax.ShapeDtypeStruct((depth, width), F32),
            tiles,
            tiles,
            jax.ShapeDtypeStruct((2, 4, depth, LANES), BF16),
        ),
        [HBM] * 5,
        (VMEM,) * 5,
        [
            pltpu.VMEM((blocks, fields, 2, width), F32),
            pltpu.VMEM((blocks, fields, 1, width), F32),
            pltpu.VMEM((4, 8, width), BF16),
            pltpu.SMEM(order.shape, jnp.int32),
            pltpu.SMEM(new_owner.shape, jnp.int32),
            pltpu.SemaphoreType.DMA((9,)),
        ],
        (order_hbm, owner_hbm, now_hbm, prev_hbm, coef_hbm),
    )
    left, dleft = call(
        pack_back_body, "pack_back", (straight, diag), [VMEM] * 4, (VMEM,) * 2, [], (edges, front, front_prev, front_coef)
    )

    swap = [(0, 1), (1, 0)]
    forward = [(i, (i + 1) % count) for i in range(count)]
    backward = [(i, (i - 1) % count) for i in range(count)]
    crossed = [(r * count + i, (1 - r) * count + (i - 1) % count) for r in range(2) for i in range(count)]
    y_in = lax.ppermute(y_out, "region", swap)
    from_right = lax.ppermute(left, "blk", backward)
    from_dright = lax.ppermute(dleft, ("region", "blk"), crossed)

    row = jax.ShapeDtypeStruct((fields, depth, width), F32)
    both = jax.ShapeDtypeStruct(now.shape, F32)
    now, box0, box1, drift, rim, held = call(
        local_body,
        "local",
        (
            both,
            row,
            row,
            both,
            jax.ShapeDtypeStruct((blocks, 8, width), F32),
            jax.ShapeDtypeStruct((blocks * fields, depth, width), BF16),
        ),
        [HBM] * 3 + [VMEM],
        (VMEM,) * 6,
        [
            pltpu.VMEM(now.shape, F32),
            pltpu.SMEM(order.shape, jnp.int32),
            pltpu.SemaphoreType.DMA((2 * fields + 1,)),
        ],
        (order_hbm, now_hbm, prev_hbm, coef),
    )
    sums = jax.ShapeDtypeStruct((8, width), F32)
    edge = jax.ShapeDtypeStruct((8, LANES), F32)
    box1, side_lap, side_coef, side_rim = call(
        border_body,
        "border",
        (row, tiles, tiles, jax.ShapeDtypeStruct((2, 8, LANES), F32)),
        [VMEM] * 4,
        (VMEM,) * 4,
        [],
        (now, from_right, from_dright, box1),
        input_output_aliases={3: 0},
        cost_estimate=pl.CostEstimate(flops=0, transcendentals=0, bytes_accessed=40_000_000),
    )
    bounds = sorted({0, 1, fields})
    parts = [(first, end - first) for first, end in zip(bounds, bounds[1:])]

    def part_shapes(size, more):
        tiled = size * width // LANES
        codes = tiled * (depth + 1) + more
        shapes = (jax.ShapeDtypeStruct((size, depth, width), F32), jax.ShapeDtypeStruct((codes, LANES), jnp.int16))
        return shapes, pltpu.VMEM((tiled, LANES), F32)

    shapes, powers = part_shapes(parts[0][1], fields // 2 * depth + 8)
    box1, lap1, side1, sums1, last, code = call(
        last_row_a_body,
        "last_row",
        (row, tiles, tiles, sums) + shapes,
        [VMEM] * 14,
        (VMEM,) * 6,
        [powers, pltpu.VMEM((8, LANES), F32)],
        (edges, now, coef, held, y_in, from_right, from_dright, box0, rim, side_lap, side_coef, side_rim, drift, box1),
        input_output_aliases={13: 0},
    )
    lasts = [last]
    arrived = [lax.ppermute(code, "blk", forward)]
    for first, size in parts[1:]:
        shapes, powers = part_shapes(size, 0)
        last, code = call(
            functools.partial(last_row_b_body, first),
            "last_row",
            shapes,
            [VMEM] * 9,
            (VMEM,) * 2,
            [powers],
            (edges, now, held, y_in, box1, drift, lap1, side1, sums1),
        )
        lasts.append(last)
        arrived.append(lax.ppermute(code, "blk", forward))
    box0, sums0, edge_c0 = call(
        first_edges_body,
        "first_edges",
        (row, sums, edge),
        [VMEM] * 3 + [ANY, VMEM],
        (VMEM,) * 3,
        [],
        (coef, y_in, rim, box1, box0),
        input_output_aliases={4: 0},
    )
    first_row, coef0 = call(
        first_row_body,
        "first_row",
        (row, tiles),
        [VMEM] * 8,
        (VMEM,) * 2,
        [],
        (edges, now, held, y_in, box0, box1, drift, sums0),
    )
    whole = jax.ShapeDtypeStruct((blocks + 1, fields, depth, width), F32)
    placed = call(
        rows_body,
        "rows",
        whole,
        [SMEM] + [VMEM] * (1 + len(lasts)),
        ANY,
        [pltpu.VMEM((depth, width), F32), pltpu.SemaphoreType.DMA((2 * fields,))],
        (new_owner, first_row, *lasts),
    )
    placed = call(
        finish_body,
        "finish",
        whole,
        [ANY] + [VMEM] * (4 + len(lasts)) + [ANY],
        ANY,
        [
            pltpu.VMEM((fields, depth, LANES), F32),
            pltpu.VMEM((parts[0][1], depth, width), F32),
            pltpu.VMEM((depth, width), F32),
            pltpu.SMEM(new_owner.shape, jnp.int32),
            pltpu.SemaphoreType.DMA((1 + 3 * fields,)),
        ],
        (new_owner, coef0, edge_c0, arrived[0], first_row, *lasts, placed),
        input_output_aliases={5 + len(lasts): 0},
        cost_estimate=pl.CostEstimate(flops=10**10, transcendentals=0, bytes_accessed=10**6),
    )
    for (first, size), codes in zip(parts[1:], arrived[1:]):
        placed = call(
            functools.partial(place_body, first),
            "place",
            whole,
            [VMEM, VMEM, ANY],
            ANY,
            [pltpu.VMEM((size, depth, width), F32), pltpu.SemaphoreType.DMA((2 * size,))],
            (arrived[0], codes, placed),
            input_output_aliases={2: 0},
        )
    return placed[:, None]


def solution(mesh):
    def on_device(*args):
        blocks = args[0].shape[0]
        if lax.axis_size("region") == 2 and blocks == 2:
            return fast_on_device(*args)
        return general_on_device(*args)

    return jax.shard_map(
        on_device,
        mesh=mesh,
        in_specs=(
            P("blk", "region", None, None, None),
            P("blk", "region", None, None, None),
            P("blk", "region", None, None, None, None),
            P("blk", "region", None),
            P("blk"),
        ),
        out_specs=P("blk", "region", None, None, None),
        check_vma=False,
    )
```
